32 devices in a mesh: dp: 8 (over y, x, core), tensor: 4 (over z).
Axes of the slice: x: 2, y: 2, z: 4, core: 2. Of those that a mesh axis runs over, the one named last changes fastest.
Arguments:
- block_input: bfloat16 [2, 512, 16, 1536], P(None, 'tensor', 'dp'), may hold values from -6 to 6
- lengths: int32 [2, 16, 3], P(None, 'dp'), may hold values from 64 to 320, as said below
- out_grad: bfloat16 [2, 512, 16, 1536], P(None, 'tensor', 'dp'), may hold values from -6 to 6
- w_query: bfloat16 [1536, 1536], P('dp', 'tensor'), may hold values from -0.15625 to 0.15625
- w_key: bfloat16 [1536, 1536], P('dp', 'tensor'), may hold values from -0.15625 to 0.15625
- w_value: bfloat16 [1536, 1536], P('dp', 'tensor'), may hold values from -0.15625 to 0.15625
- w_out: bfloat16 [1536, 1536], P('tensor', 'dp'), may hold values from -1.75 to 1.75
- w_gate: bfloat16 [1536, 4096], P('dp', 'tensor'), may hold values from -0.15625 to 0.15625
- w_up: bfloat16 [1536, 4096], P('dp', 'tensor'), may hold values from -0.15625 to 0.15625
- w_down: bfloat16 [4096, 1536], P('tensor', 'dp'), may hold values from -0.1875 to 0.1875
- attn_gain: bfloat16 [1536], P('dp'), may hold values from 0.5 to 1.5
- ffn_gain: bfloat16 [1536], P('dp'), may hold values from 0.5 to 1.5
Outputs:
- block_output: bfloat16 [2, 512, 16, 1536], P(None, 'tensor', 'dp')
- input_grad: bfloat16 [2, 512, 16, 1536], P(None, 'tensor', 'dp')
- grad_query: float32 [1536, 1536], P('dp', 'tensor')
- grad_key: float32 [1536, 1536], P('dp', 'tensor')
- grad_value: float32 [1536, 1536], P('dp', 'tensor')
- grad_out: float32 [1536, 1536], P('tensor', 'dp')
- grad_gate: float32 [1536, 4096], P('dp', 'tensor')
- grad_up: float32 [1536, 4096], P('dp', 'tensor')
- grad_down: float32 [4096, 1536], P('tensor', 'dp')
- grad_attn_gain: float32 [1536], P('dp')
- grad_ffn_gain: float32 [1536], P('dp')
The draws below stay inside these ranges and needn't reach their ends.
Inputs may be any that keep to these rules, and one draw needn't show every extreme that they name: Each group's 512 slots hold, in order, its prompt of lengths[..., 0] tokens and two continuations of lengths[..., 1] and lengths[..., 2] tokens; the three sum to 512; a prompt has 192 tokens or more.
All inputs are finite; a program needn't handle non-finite values.
Results may differ from the reference program's by a relative error of at most 0.023.
Values may be sent and summed in bfloat16 or wider, within the bound.
A program may use at most 192 MiB of HBM per device.

```python
import math
import jax
import jax.numpy as jnp
from jax import lax

D = 1536
HD = 64
FF = 4096
PROMPT = 256
CONT = 128
MB = 2
GTOK = 512
GROUPS = 16


def draw_lengths(key, part):
    table_shape = (MB, GROUPS)
    first_key, second_key = jax.random.split(key)
    extra = PROMPT // 4
    wiggle = CONT // 4
    shift_draw = jax.random.randint(first_key, table_shape, -extra, extra + 1)
    leading = jnp.arange(MB * GROUPS, dtype=jnp.int32).reshape(table_shape) == 0
    prompt_len = jnp.where(leading, PROMPT + extra, PROMPT + shift_draw)
    remaining = GTOK - prompt_len
    first_draw = remaining // 2 + jax.random.randint(second_key, table_shape, -wiggle, wiggle + 1)
    first_len = jnp.where(leading, remaining // 2 - wiggle, first_draw)
    second_len = remaining - first_len
    return jnp.stack([prompt_len, first_len, second_len], axis=-1).astype(jnp.int32)


def steps_of(rng, dims, shards, smallest, high):
    factor_of = 1.0
    for dim, blocks in shards:
        heights = jax.random.uniform(jax.random.fold_in(jax.random.fold_in(rng, 6), dim), (blocks,), jnp.float32, smallest / len(shards), high / len(shards))
        factor_of = factor_of * jnp.repeat(jnp.exp(heights), dims[dim] // blocks).reshape((-1,) + (1,) * (len(dims) - 1 - dim))
    return factor_of


def gaussian(own_key, dims, deviation, limit, shards=(), kind=jnp.bfloat16):
    gain = steps_of(own_key, dims, shards, -0.22, 0.18) if shards else 1.0
    entries = jax.random.normal(own_key, dims, jnp.float32) * deviation * gain
    return jnp.minimum(jnp.maximum(entries, -limit), limit).astype(kind)


def setup_inputs(seed: int = 0) -> dict:
    arg_keys = jax.random.split(jax.random.key(seed), 13)
    block_input = gaussian(arg_keys[0], (MB, GTOK, GROUPS, D), 1.0, 6.0, ((1, 4), (2, 8)))
    lengths = draw_lengths(jax.random.fold_in(arg_keys[12], 71), 0)
    out_grad = gaussian(arg_keys[2], (MB, GTOK, GROUPS, D), 1.0, 6.0, ((1, 4), (2, 8)))
    w_query = gaussian(arg_keys[3], (D, D), D ** -0.5, 0.15625, ((0, 8), (1, 4)))
    w_key = gaussian(arg_keys[4], (D, D), D ** -0.5, 0.15625, ((0, 8), (1, 4)))
    w_value = gaussian(arg_keys[5], (D, D), D ** -0.5, 0.15625, ((0, 8), (1, 4)))
    w_out = gaussian(arg_keys[6], (D, D), (max(D // 128, 1)) ** -0.5, 1.75, ((0, 4), (1, 8)))
    w_gate = gaussian(arg_keys[7], (D, FF), D ** -0.5, 0.15625, ((0, 8), (1, 4)))
    w_up = gaussian(arg_keys[8], (D, FF), D ** -0.5, 0.15625, ((0, 8), (1, 4)))
    w_down = gaussian(arg_keys[9], (FF, D), (FF // 4) ** -0.5, 0.1875, ((0, 4), (1, 8)))
    attn_gain = jnp.clip(1.0 + 0.1 * jax.random.normal(arg_keys[10], (D,), jnp.float32), 0.5, 1.5).astype(jnp.bfloat16)
    ffn_gain = jnp.clip(1.0 + 0.1 * jax.random.normal(arg_keys[11], (D,), jnp.float32), 0.5, 1.5).astype(jnp.bfloat16)
    return {"block_input": block_input, "lengths": lengths, "out_grad": out_grad, "w_query": w_query, "w_key": w_key, "w_value": w_value, "w_out": w_out, "w_gate": w_gate, "w_up": w_up, "w_down": w_down, "attn_gain": attn_gain, "ffn_gain": ffn_gain}


EPSILON = 1e-05
PRECISE = lax.Precision.HIGHEST
MASKED = -1e+30

@jax.custom_vjp
def low(v):
    return lax.optimization_barrier(v.astype(jnp.bfloat16)).astype(jnp.float32)

@jax.custom_vjp
def low_back(v):
    return v

def low_keep(v):
    return (low(v), None)

def low_pass(kept, grad):
    return (grad,)

def back_keep(v):
    return (v, None)

def back_low(kept, grad):
    return (low(grad),)
low.defvjp(low_keep, low_pass)
low_back.defvjp(back_keep, back_low)

def layout_tables(group_lengths):
    slot_index = jnp.arange(GTOK, dtype=jnp.int32)[:, None]
    prompt_len = group_lengths[:, 0][None, :]
    first_len = group_lengths[:, 1][None, :]
    segment = jnp.where(slot_index < prompt_len, 0, jnp.where(slot_index < prompt_len + first_len, 1, 2)).astype(jnp.int32)
    position = jnp.where(segment == 2, slot_index - first_len, slot_index).astype(jnp.int32)
    frequency = jnp.exp(jnp.arange(HD // 2, dtype=jnp.float32) * (-2.0 * math.log(10000.0) / HD))
    angles = position.astype(jnp.float32)[:, :, None] * frequency
    return (segment, jnp.cos(angles), jnp.sin(angles))

def rotate(values, cos_table, sin_table):
    half_size = values.shape[-1] // 2
    first_half = values[..., :half_size]
    second_half = values[..., half_size:]
    cos_wide = cos_table[:, :, None, :]
    sin_wide = sin_table[:, :, None, :]
    return jnp.concatenate([first_half * cos_wide - second_half * sin_wide, second_half * cos_wide + first_half * sin_wide], axis=-1)

def dense(inputs, weight_matrix):
    return jnp.einsum('tgd,de->tge', inputs, weight_matrix, precision=PRECISE)

def rms_norm(values, gain_row):
    return values * lax.rsqrt(lax.optimization_barrier(jnp.mean(values * values, axis=-1, keepdims=True)) + EPSILON) * gain_row

def attend(members):
    queries, key_rows, value_rows, segment = members
    scores = low_back(jnp.einsum('the,she->hts', queries, key_rows, precision=PRECISE) * HD ** (-0.5))
    token_index = jnp.arange(GTOK, dtype=jnp.int32)
    allowed = (token_index[None, :] <= token_index[:, None]) & ((segment[None, :] == 0) | (segment[None, :] == segment[:, None]))
    scores = jnp.where(allowed[None], scores, MASKED)
    attn_probs = jax.nn.softmax(scores, axis=-1)
    return low(low_back(jnp.einsum('hts,she->the', low(attn_probs), value_rows, precision=PRECISE)))

def forward(inputs, segment, cos_table, sin_table, w_query, w_key, w_value, w_out, w_gate, w_up, w_down, attn_gain, ffn_gain):
    group_count = inputs.shape[1]
    shape_heads = (GTOK, group_count, D // HD, HD)
    normed = low(rms_norm(inputs, attn_gain))
    queries = low(rotate(low_back(dense(normed, w_query)).reshape(shape_heads), cos_table, sin_table))
    key_rows = low(rotate(low_back(dense(normed, w_key)).reshape(shape_heads), cos_table, sin_table))
    value_rows = low(low_back(dense(normed, w_value))).reshape(shape_heads)
    attn_mix = lax.map(jax.checkpoint(attend), (jnp.transpose(queries, (1, 0, 2, 3)), jnp.transpose(key_rows, (1, 0, 2, 3)), jnp.transpose(value_rows, (1, 0, 2, 3)), segment.T))
    attn_mix = jnp.transpose(attn_mix, (1, 0, 2, 3)).reshape(GTOK, group_count, D)
    middle = inputs + low_back(dense(attn_mix, w_out))
    normed_two = low(rms_norm(middle, ffn_gain))
    gate_vals = low_back(dense(normed_two, w_gate))
    up_vals = low_back(dense(normed_two, w_up))
    hidden = low(jax.nn.silu(gate_vals) * up_vals)
    return middle + low_back(dense(hidden, w_down))

def reference(block_input, lengths, out_grad, w_query, w_key, w_value, w_out, w_gate, w_up, w_down, attn_gain, ffn_gain):
    params = tuple((weight_item.astype(jnp.float32) for weight_item in (w_query, w_key, w_value, w_out, w_gate, w_up, w_down, attn_gain, ffn_gain)))
    totals = tuple((jnp.zeros(weight_item.shape, jnp.float32) for weight_item in params))
    outputs = []
    input_grads = []
    for micro_index in range(MB):
        segment, cos_table, sin_table = layout_tables(lengths[micro_index])

        def layer_fn(inputs, *weight_items):
            return forward(inputs, segment, cos_table, sin_table, *weight_items)
        result, pullback = jax.vjp(layer_fn, block_input[micro_index].astype(jnp.float32), *params)
        all_grads = pullback(out_grad[micro_index].astype(jnp.float32))
        outputs.append(result.astype(jnp.bfloat16))
        input_grads.append(all_grads[0].astype(jnp.bfloat16))
        totals = tuple((earlier + later for earlier, later in zip(totals, all_grads[1:])))
    return (jnp.stack(outputs), jnp.stack(input_grads), totals[0], totals[1], totals[2], totals[3], totals[4], totals[5], totals[6], totals[7], totals[8])
```

```python
import math

import jax
import jax.numpy as jnp
from jax import lax
from jax.sharding import PartitionSpec as P

HD = 64
GTOK = 512


EPSILON = 1e-05
MASKED = -1e30


def layout_tables(group_lengths):
    slot_index = jnp.arange(GTOK, dtype=jnp.int32)[:, None]
    prompt_len = group_lengths[:, 0][None, :]
    first_len = group_lengths[:, 1][None, :]
    segment = jnp.where(
        slot_index < prompt_len, 0, jnp.where(slot_index < prompt_len + first_len, 1, 2)
    ).astype(jnp.int32)
    position = jnp.where(segment == 2, slot_index - first_len, slot_index)
    frequency = jnp.exp(jnp.arange(HD // 2, dtype=jnp.float32) * (-2.0 * math.log(10000.0) / HD))
    angles = position.astype(jnp.float32)[:, :, None] * frequency
    return (segment, jnp.cos(angles), jnp.sin(angles))


def rotate(values, cos_table, sin_table):
    half_size = values.shape[-1] // 2
    first_half = values[..., :half_size]
    second_half = values[..., half_size:]
    cos_wide = cos_table[:, :, None, :]
    sin_wide = sin_table[:, :, None, :]
    return jnp.concatenate(
        [
            first_half * cos_wide - second_half * sin_wide,
            second_half * cos_wide + first_half * sin_wide,
        ],
        axis=-1,
    )


def rotate_back(values, cos_table, sin_table):
    half_size = values.shape[-1] // 2
    first_half = values[..., :half_size]
    second_half = values[..., half_size:]
    cos_wide = cos_table[:, :, None, :]
    sin_wide = sin_table[:, :, None, :]
    return jnp.concatenate(
        [
            first_half * cos_wide + second_half * sin_wide,
            second_half * cos_wide - first_half * sin_wide,
        ],
        axis=-1,
    )


def rms_scale(values):
    return lax.rsqrt(jnp.mean(values * values, axis=-1, keepdims=True) + EPSILON)


def norm_back(upstream, unit_rows, gain_row, scale_rows):
    scaled = upstream * gain_row
    return scale_rows * (scaled - unit_rows * jnp.mean(scaled * unit_rows, axis=-1, keepdims=True))


def attention_scores(queries, key_rows, allowed):
    scores = jnp.einsum(
        "tghe,sghe->ghts", queries, key_rows, preferred_element_type=jnp.float32
    ) * HD ** (-0.5)
    return jnp.where(allowed[:, None], scores, MASKED)


def add_tuples(first_set, second_set):
    return tuple((earlier + later for earlier, later in zip(first_set, second_set)))


def micro_step(inputs, group_lengths, upstream, gathered):
    w_query, w_key, w_value, w_out, w_gate, w_up, w_down, attn_gain, ffn_gain = gathered
    gain_one = attn_gain.astype(jnp.float32)
    gain_two = ffn_gain.astype(jnp.float32)
    group_count = inputs.shape[1]
    head_cols = w_query.shape[1]
    hidden_cols = w_gate.shape[1]
    shape_heads = (GTOK, group_count, head_cols // HD, HD)
    segment, cos_table, sin_table = layout_tables(group_lengths)
    token_index = jnp.arange(GTOK, dtype=jnp.int32)
    seg_groups = segment.T
    allowed = (token_index[None, None, :] <= token_index[None, :, None]) & (
        (seg_groups[:, None, :] == 0) | (seg_groups[:, None, :] == seg_groups[:, :, None])
    )
    residual = inputs.astype(jnp.float32)
    scale_one = rms_scale(residual)
    unit_one = residual * scale_one
    normed_one = (unit_one * gain_one).astype(jnp.bfloat16)
    normed_all = lax.all_gather(normed_one, "tensor", axis=0, tiled=True)
    w_joint = jnp.concatenate([w_query, w_key, w_value], axis=1)
    projected = jnp.einsum("tgd,dc->tgc", normed_all, w_joint, preferred_element_type=jnp.float32)
    queries = rotate(projected[..., :head_cols].reshape(shape_heads), cos_table, sin_table).astype(
        jnp.bfloat16
    )
    key_rows = rotate(
        projected[..., head_cols : 2 * head_cols].reshape(shape_heads), cos_table, sin_table
    ).astype(jnp.bfloat16)
    value_rows = projected[..., 2 * head_cols :].reshape(shape_heads).astype(jnp.bfloat16)
    scores = attention_scores(queries, key_rows, allowed)
    row_max = jnp.max(scores, axis=-1, keepdims=True)
    log_total = row_max + jnp.log(jnp.sum(jnp.exp(scores - row_max), axis=-1, keepdims=True))
    attn_probs = jnp.exp(scores - log_total).astype(jnp.bfloat16)
    attn_mix = (
        jnp.einsum("ghts,sghe->tghe", attn_probs, value_rows, preferred_element_type=jnp.float32)
        .astype(jnp.bfloat16)
        .reshape(GTOK, group_count, head_cols)
    )
    rows_here = attn_mix
    attn_sum = lax.psum_scatter(
        jnp.einsum("tgc,cd->tgd", rows_here, w_out, preferred_element_type=jnp.float32),
        "tensor",
        scatter_dimension=0,
        tiled=True,
    )
    middle = residual + attn_sum
    scale_two = rms_scale(middle)
    unit_two = middle * scale_two
    normed_two = (unit_two * gain_two).astype(jnp.bfloat16)
    normed_more = lax.all_gather(normed_two, "tensor", axis=0, tiled=True)
    w_gate_up = jnp.concatenate([w_gate, w_up], axis=1)
    gate_up = jnp.einsum("tgd,df->tgf", normed_more, w_gate_up, preferred_element_type=jnp.float32)
    gate_vals = gate_up[..., :hidden_cols]
    up_vals = gate_up[..., hidden_cols:]
    sigmoid_gate = jax.nn.sigmoid(gate_vals)
    silu_gate = gate_vals * sigmoid_gate
    hidden = (silu_gate * up_vals).astype(jnp.bfloat16)
    rows_here = hidden
    ffn_sum = lax.psum_scatter(
        jnp.einsum("tgf,fd->tgd", rows_here, w_down, preferred_element_type=jnp.float32).astype(
            jnp.bfloat16
        ),
        "tensor",
        scatter_dimension=0,
        tiled=True,
    ).astype(jnp.float32)
    output = (middle + ffn_sum).astype(jnp.bfloat16)
    upstream_all = lax.all_gather(upstream, "tensor", axis=0, tiled=True)
    hidden_grad = jnp.einsum(
        "tgd,fd->tgf", upstream_all, w_down, preferred_element_type=jnp.float32
    )
    grad_down = jnp.einsum("tgf,tgd->fd", hidden, upstream_all, preferred_element_type=jnp.float32)
    up_grad = hidden_grad * silu_gate
    gate_grad = hidden_grad * up_vals * (sigmoid_gate * (1.0 + gate_vals * (1.0 - sigmoid_gate)))
    gate_up_grad = jnp.concatenate([gate_grad, up_grad], axis=-1).astype(jnp.bfloat16)
    grad_gate_up = jnp.einsum(
        "tgd,tgf->df", normed_more, gate_up_grad, preferred_element_type=jnp.float32
    )
    rows_here = gate_up_grad
    normed_two_grad = lax.psum_scatter(
        jnp.einsum("tgf,df->tgd", rows_here, w_gate_up, preferred_element_type=jnp.float32).astype(
            jnp.bfloat16
        ),
        "tensor",
        scatter_dimension=0,
        tiled=True,
    ).astype(jnp.float32)
    gain_two_grad = jnp.sum(normed_two_grad * unit_two, axis=(0, 1))
    middle_grad = upstream.astype(jnp.float32) + norm_back(
        normed_two_grad, unit_two, gain_two, scale_two
    )
    attn_grad = middle_grad.astype(jnp.bfloat16)
    attn_grad_all = lax.all_gather(attn_grad, "tensor", axis=0, tiled=True)
    mix_grad = (
        jnp.einsum("tgd,cd->tgc", attn_grad_all, w_out, preferred_element_type=jnp.float32)
        .astype(jnp.bfloat16)
        .reshape(shape_heads)
    )
    grad_out = jnp.einsum(
        "tgc,tgd->cd", attn_mix, attn_grad_all, preferred_element_type=jnp.float32
    )
    scores_again = attention_scores(queries, key_rows, allowed)
    probs_full = jnp.exp(scores_again - log_total)
    prob_grad = jnp.einsum(
        "tghe,sghe->ghts", mix_grad, value_rows, preferred_element_type=jnp.float32
    )
    value_grad = jnp.einsum(
        "ghts,tghe->sghe",
        probs_full.astype(jnp.bfloat16),
        mix_grad,
        preferred_element_type=jnp.float32,
    )
    centre = jnp.sum(probs_full * prob_grad, axis=-1, keepdims=True)
    score_grad = (probs_full * (prob_grad - centre)).astype(jnp.bfloat16)
    query_grad = jnp.einsum(
        "ghts,sghe->tghe", score_grad, key_rows, preferred_element_type=jnp.float32
    ) * HD ** (-0.5)
    key_grad = jnp.einsum(
        "ghts,tghe->sghe", score_grad, queries, preferred_element_type=jnp.float32
    ) * HD ** (-0.5)
    flat_shape = (GTOK, group_count, head_cols)
    joint_grad = jnp.concatenate(
        [
            rotate_back(query_grad, cos_table, sin_table).reshape(flat_shape),
            rotate_back(key_grad, cos_table, sin_table).reshape(flat_shape),
            value_grad.reshape(flat_shape),
        ],
        axis=-1,
    ).astype(jnp.bfloat16)
    grad_joint = jnp.einsum(
        "tgd,tgc->dc", normed_all, joint_grad, preferred_element_type=jnp.float32
    )
    rows_here = joint_grad
    normed_one_grad = lax.psum_scatter(
        jnp.einsum("tgc,dc->tgd", rows_here, w_joint, preferred_element_type=jnp.float32).astype(
            jnp.bfloat16
        ),
        "tensor",
        scatter_dimension=0,
        tiled=True,
    ).astype(jnp.float32)
    gain_one_grad = jnp.sum(normed_one_grad * unit_one, axis=(0, 1))
    input_grad = (middle_grad + norm_back(normed_one_grad, unit_one, gain_one, scale_one)).astype(
        jnp.bfloat16
    )
    param_grads = (
        grad_joint[:, :head_cols],
        grad_joint[:, head_cols : 2 * head_cols],
        grad_joint[:, 2 * head_cols :],
        grad_out,
        grad_gate_up[:, :hidden_cols],
        grad_gate_up[:, hidden_cols:],
        grad_down,
        gain_one_grad,
        gain_two_grad,
    )
    return (output, input_grad, param_grads)


def sharded_body(
    block_input,
    lengths,
    out_grad,
    w_query,
    w_key,
    w_value,
    w_out,
    w_gate,
    w_up,
    w_down,
    attn_gain,
    ffn_gain,
):
    outputs = []
    input_grads = []
    totals = None
    shares = None
    for micro_index in range(block_input.shape[0]):
        gathered = (
            lax.all_gather(w_query, "dp", axis=0, tiled=True),
            lax.all_gather(w_key, "dp", axis=0, tiled=True),
            lax.all_gather(w_value, "dp", axis=0, tiled=True),
            lax.all_gather(w_out, "dp", axis=1, tiled=True),
            lax.all_gather(w_gate, "dp", axis=0, tiled=True),
            lax.all_gather(w_up, "dp", axis=0, tiled=True),
            lax.all_gather(w_down, "dp", axis=1, tiled=True),
            lax.all_gather(attn_gain, "dp", axis=0, tiled=True),
            lax.all_gather(ffn_gain, "dp", axis=0, tiled=True),
        )
        output, input_grad, param_grads = micro_step(
            block_input[micro_index], lengths[micro_index], out_grad[micro_index], gathered
        )
        outputs.append(output)
        input_grads.append(input_grad)
        totals = param_grads if totals is None else add_tuples(totals, param_grads)
    shares = (
        lax.psum_scatter(
            totals[0].astype(jnp.bfloat16), "dp", scatter_dimension=0, tiled=True
        ).astype(jnp.float32),
        lax.psum_scatter(
            totals[1].astype(jnp.bfloat16), "dp", scatter_dimension=0, tiled=True
        ).astype(jnp.float32),
        lax.psum_scatter(
            totals[2].astype(jnp.bfloat16), "dp", scatter_dimension=0, tiled=True
        ).astype(jnp.float32),
        lax.psum_scatter(
            totals[3].astype(jnp.bfloat16), "dp", scatter_dimension=1, tiled=True
        ).astype(jnp.float32),
        lax.psum_scatter(
            totals[4].astype(jnp.bfloat16), "dp", scatter_dimension=0, tiled=True
        ).astype(jnp.float32),
        lax.psum_scatter(
            totals[5].astype(jnp.bfloat16), "dp", scatter_dimension=0, tiled=True
        ).astype(jnp.float32),
        lax.psum_scatter(
            totals[6].astype(jnp.bfloat16), "dp", scatter_dimension=1, tiled=True
        ).astype(jnp.float32),
        lax.psum_scatter(
            totals[7].astype(jnp.bfloat16), "dp", scatter_dimension=0, tiled=True
        ).astype(jnp.float32),
        lax.psum_scatter(
            totals[8].astype(jnp.bfloat16), "dp", scatter_dimension=0, tiled=True
        ).astype(jnp.float32),
    )
    gain_one_total, gain_two_total = lax.psum((shares[7], shares[8]), "tensor")
    return (
        jnp.stack(outputs),
        jnp.stack(input_grads),
        shares[0],
        shares[1],
        shares[2],
        shares[3],
        shares[4],
        shares[5],
        shares[6],
        gain_one_total,
        gain_two_total,
    )


def gather_full(shard):
    rows, cols = shard.shape
    dp_size = lax.axis_size("dp")
    z_size = lax.axis_size("tensor")
    full = lax.all_gather(shard, ("dp", "tensor"), axis=0, tiled=True)
    return full.reshape(dp_size, z_size, rows, cols).transpose(0, 2, 1, 3).reshape(
        dp_size * rows, z_size * cols
    )


def scatter_full(grad):
    dp_size = lax.axis_size("dp")
    z_size = lax.axis_size("tensor")
    rows = grad.shape[0] // dp_size
    cols = grad.shape[1] // z_size
    flat = (
        grad.reshape(dp_size, rows, z_size, cols)
        .transpose(0, 2, 1, 3)
        .reshape(dp_size * z_size * rows, cols)
    )
    return lax.psum_scatter(
        flat, ("dp", "tensor"), scatter_dimension=0, tiled=True
    ).astype(jnp.float32)


def to_group(values):
    micro, rows, groups, width = values.shape
    parts = values.transpose(0, 2, 1, 3).reshape(micro * groups, rows, width)
    moved = lax.all_to_all(parts, "tensor", 0, 0, tiled=True)
    return moved.reshape(micro * groups * rows, width)


def from_group(values, micro, groups):
    rows = values.shape[0] // (micro * groups)
    width = values.shape[1]
    parts = values.reshape(micro * groups, rows, width)
    moved = lax.all_to_all(parts, "tensor", 0, 0, tiled=True)
    return moved.reshape(micro, groups, rows, width).transpose(0, 2, 1, 3)


def dot_tt(left, right, dims):
    return lax.dot_general(left, right, (dims, ((), ())), preferred_element_type=jnp.float32)


def turn(values, cos_table, sin_table, sign):
    half = HD // 2
    first_half = values[..., :half]
    second_half = values[..., half:]
    return jnp.concatenate(
        [
            first_half * cos_table - sign * second_half * sin_table,
            second_half * cos_table + sign * first_half * sin_table,
        ],
        axis=-1,
    )


def group_body(
    block_input,
    lengths,
    out_grad,
    w_query,
    w_key,
    w_value,
    w_out,
    w_gate,
    w_up,
    w_down,
    attn_gain,
    ffn_gain,
):
    micro, _, groups, width = block_input.shape
    head_cols = w_query.shape[1] * lax.axis_size("tensor")
    heads = head_cols // HD
    bf16 = jnp.bfloat16
    f32 = jnp.float32
    tokens_in = to_group(block_input)
    upstream = to_group(out_grad)
    own_lengths = lax.dynamic_slice_in_dim(
        lengths.reshape(micro * groups, 3), lax.axis_index("tensor"), 1, 0
    )
    gains = lax.all_gather(jnp.stack([attn_gain, ffn_gain]), "dp", axis=1, tiled=True)
    gain_one = gains[0].astype(f32)
    gain_two = gains[1].astype(f32)
    wq = gather_full(w_query)
    wk = gather_full(w_key)
    wv = gather_full(w_value)
    wo = gather_full(w_out.T)
    wg = gather_full(w_gate)
    wu = gather_full(w_up)
    wd = gather_full(w_down.T)

    segment, cos_table, sin_table = layout_tables(own_lengths)
    seg = segment[:, 0]
    cos_table = cos_table[:, 0, None, :]
    sin_table = sin_table[:, 0, None, :]
    index = jnp.arange(GTOK, dtype=jnp.int32)
    allowed = (index[None, :] <= index[:, None]) & (
        (seg[None, :] == 0) | (seg[None, :] == seg[:, None])
    )
    residual = tokens_in.astype(f32)
    scale_one = rms_scale(residual)
    unit_one = residual * scale_one
    normed_one = (unit_one * gain_one).astype(bf16)
    contract = ((1,), (0,))
    contract_t = ((1,), (1,))
    contract_tok = ((0,), (0,))
    split = (GTOK, heads, HD)
    queries = turn(
        dot_tt(normed_one, wq, contract).reshape(split), cos_table, sin_table, 1.0
    ).astype(bf16)
    keys = turn(
        dot_tt(normed_one, wk, contract).reshape(split), cos_table, sin_table, 1.0
    ).astype(bf16)
    values = dot_tt(normed_one, wv, contract).reshape(split).astype(bf16)
    scale = HD ** (-0.5)

    def score(qs, ks):
        raw = jnp.einsum("the,she->hts", qs, ks, preferred_element_type=f32) * scale
        return jnp.where(allowed[None], raw, MASKED)

    scores = score(queries, keys)
    row_max = jnp.max(scores, axis=-1, keepdims=True)
    log_total = row_max + jnp.log(jnp.sum(jnp.exp(scores - row_max), axis=-1, keepdims=True))
    probs = jnp.exp(scores - log_total).astype(bf16)
    mix = (
        jnp.einsum("hts,she->the", probs, values, preferred_element_type=f32)
        .astype(bf16)
        .reshape(GTOK, head_cols)
    )
    middle = residual + dot_tt(mix, wo, contract_t)
    scale_two = rms_scale(middle)
    unit_two = middle * scale_two
    normed_two = (unit_two * gain_two).astype(bf16)
    gate_vals = dot_tt(normed_two, wg, contract)
    up_vals = dot_tt(normed_two, wu, contract)
    sigmoid_gate = jax.nn.sigmoid(gate_vals)
    silu_gate = gate_vals * sigmoid_gate
    hidden = (silu_gate * up_vals).astype(bf16)
    output = (middle + dot_tt(hidden, wd, contract_t)).astype(bf16)
    out_final = from_group(output, micro, groups)

    grad_down = dot_tt(upstream, hidden, contract_tok).astype(bf16)
    share_down = scatter_full(grad_down).T
    hidden_grad = dot_tt(upstream, wd, contract)
    up_grad = (hidden_grad * silu_gate).astype(bf16)
    gate_grad = (
        hidden_grad * up_vals * (sigmoid_gate * (1.0 + gate_vals * (1.0 - sigmoid_gate)))
    ).astype(bf16)
    share_gate = scatter_full(dot_tt(normed_two, gate_grad, contract_tok).astype(bf16))
    share_up = scatter_full(dot_tt(normed_two, up_grad, contract_tok).astype(bf16))
    normed_two_grad = dot_tt(gate_grad, wg, contract_t) + dot_tt(up_grad, wu, contract_t)
    gain_two_grad = jnp.sum(normed_two_grad * unit_two, axis=0)
    middle_grad = upstream.astype(f32) + norm_back(
        normed_two_grad, unit_two, gain_two, scale_two
    )
    attn_grad = middle_grad.astype(bf16)
    share_out = scatter_full(dot_tt(attn_grad, mix, contract_tok).astype(bf16)).T
    mix_grad = dot_tt(attn_grad, wo, contract).astype(bf16).reshape(split)
    probs_full = jnp.exp(score(queries, keys) - log_total)
    prob_grad = jnp.einsum("the,she->hts", mix_grad, values, preferred_element_type=f32)
    value_grad = jnp.einsum(
        "hts,the->she", probs_full.astype(bf16), mix_grad, preferred_element_type=f32
    )
    centre = jnp.sum(probs_full * prob_grad, axis=-1, keepdims=True)
    score_grad = (probs_full * (prob_grad - centre)).astype(bf16)
    query_grad = jnp.einsum("hts,she->the", score_grad, keys, preferred_element_type=f32) * scale
    key_grad = jnp.einsum("hts,the->she", score_grad, queries, preferred_element_type=f32) * scale
    flat = (GTOK, head_cols)
    dq = turn(query_grad, cos_table, sin_table, -1.0).reshape(flat).astype(bf16)
    dk = turn(key_grad, cos_table, sin_table, -1.0).reshape(flat).astype(bf16)
    dv = value_grad.reshape(flat).astype(bf16)
    normed_one_grad = (
        dot_tt(dq, wq, contract_t) + dot_tt(dk, wk, contract_t) + dot_tt(dv, wv, contract_t)
    )
    gain_one_grad = jnp.sum(normed_one_grad * unit_one, axis=0)
    input_grad = (
        middle_grad + norm_back(normed_one_grad, unit_one, gain_one, scale_one)
    ).astype(bf16)
    in_grad_final = from_group(input_grad, micro, groups)
    share_query = scatter_full(dot_tt(normed_one, dq, contract_tok).astype(bf16))
    share_key = scatter_full(dot_tt(normed_one, dk, contract_tok).astype(bf16))
    share_value = scatter_full(dot_tt(normed_one, dv, contract_tok).astype(bf16))
    gain_sums = lax.psum(jnp.stack([gain_one_grad, gain_two_grad]), ("dp", "tensor"))
    gain_rows = attn_gain.shape[0]
    own_gains = lax.dynamic_slice_in_dim(gain_sums, lax.axis_index("dp") * gain_rows, gain_rows, 1)
    return (
        out_final,
        in_grad_final,
        share_query,
        share_key,
        share_value,
        share_out,
        share_gate,
        share_up,
        share_down,
        own_gains[0],
        own_gains[1],
    )


def body(*operands):
    micro, _, groups, _ = operands[0].shape
    if micro * groups == lax.axis_size("tensor"):
        return group_body(*operands)
    return sharded_body(*operands)


def solution(mesh):
    placed = (
        P(None, "tensor", "dp", None),
        P(None, "dp", None),
        P(None, "tensor", "dp", None),
        P("dp", "tensor"),
        P("dp", "tensor"),
        P("dp", "tensor"),
        P("tensor", "dp"),
        P("dp", "tensor"),
        P("dp", "tensor"),
        P("tensor", "dp"),
        P("dp"),
        P("dp"),
    )
    return jax.shard_map(
        body,
        mesh=mesh,
        in_specs=placed,
        out_specs=(
            P(None, "tensor", "dp", None),
            P(None, "tensor", "dp", None),
            P("dp", "tensor"),
            P("dp", "tensor"),
            P("dp", "tensor"),
            P("tensor", "dp"),
            P("dp", "tensor"),
            P("dp", "tensor"),
            P("tensor", "dp"),
            P("dp"),
            P("dp"),
        ),
        check_vma=False,
    )
```

```python
import functools
import math

import jax
import jax.numpy as jnp
from jax import lax
from jax.experimental import pallas as pl
from jax.experimental.pallas import tpu as pltpu
from jax.sharding import PartitionSpec as P


HD = 64
GTOK = 512


EPSILON = 1e-05
MASKED = -1e30


def layout_tables(group_lengths):
    slot_index = jnp.arange(GTOK, dtype=jnp.int32)[:, None]
    prompt_len = group_lengths[:, 0][None, :]
    first_len = group_lengths[:, 1][None, :]
    segment = jnp.where(
        slot_index < prompt_len, 0, jnp.where(slot_index < prompt_len + first_len, 1, 2)
    ).astype(jnp.int32)
    position = jnp.where(segment == 2, slot_index - first_len, slot_index)
    frequency = jnp.exp(jnp.arange(HD // 2, dtype=jnp.float32) * (-2.0 * math.log(10000.0) / HD))
    angles = position.astype(jnp.float32)[:, :, None] * frequency
    return (segment, jnp.cos(angles), jnp.sin(angles))


def rotate(values, cos_table, sin_table):
    half_size = values.shape[-1] // 2
    first_half = values[..., :half_size]
    second_half = values[..., half_size:]
    cos_wide = cos_table[:, :, None, :]
    sin_wide = sin_table[:, :, None, :]
    return jnp.concatenate(
        [
            first_half * cos_wide - second_half * sin_wide,
            second_half * cos_wide + first_half * sin_wide,
        ],
        axis=-1,
    )


def rotate_back(values, cos_table, sin_table):
    half_size = values.shape[-1] // 2
    first_half = values[..., :half_size]
    second_half = values[..., half_size:]
    cos_wide = cos_table[:, :, None, :]
    sin_wide = sin_table[:, :, None, :]
    return jnp.concatenate(
        [
            first_half * cos_wide + second_half * sin_wide,
            second_half * cos_wide - first_half * sin_wide,
        ],
        axis=-1,
    )


def rms_scale(values):
    return lax.rsqrt(jnp.mean(values * values, axis=-1, keepdims=True) + EPSILON)


def norm_back(upstream, unit_rows, gain_row, scale_rows):
    scaled = upstream * gain_row
    return scale_rows * (scaled - unit_rows * jnp.mean(scaled * unit_rows, axis=-1, keepdims=True))


def attention_scores(queries, key_rows, allowed):
    scores = jnp.einsum(
        "tghe,sghe->ghts", queries, key_rows, preferred_element_type=jnp.float32
    ) * HD ** (-0.5)
    return jnp.where(allowed[:, None], scores, MASKED)


def add_tuples(first_set, second_set):
    return tuple((earlier + later for earlier, later in zip(first_set, second_set)))


def micro_step(inputs, group_lengths, upstream, gathered):
    w_query, w_key, w_value, w_out, w_gate, w_up, w_down, attn_gain, ffn_gain = gathered
    gain_one = attn_gain.astype(jnp.float32)
    gain_two = ffn_gain.astype(jnp.float32)
    group_count = inputs.shape[1]
    head_cols = w_query.shape[1]
    hidden_cols = w_gate.shape[1]
    shape_heads = (GTOK, group_count, head_cols // HD, HD)
    segment, cos_table, sin_table = layout_tables(group_lengths)
    token_index = jnp.arange(GTOK, dtype=jnp.int32)
    seg_groups = segment.T
    allowed = (token_index[None, None, :] <= token_index[None, :, None]) & (
        (seg_groups[:, None, :] == 0) | (seg_groups[:, None, :] == seg_groups[:, :, None])
    )
    residual = inputs.astype(jnp.float32)
    scale_one = rms_scale(residual)
    unit_one = residual * scale_one
    normed_one = (unit_one * gain_one).astype(jnp.bfloat16)
    normed_all = lax.all_gather(normed_one, "tensor", axis=0, tiled=True)
    w_joint = jnp.concatenate([w_query, w_key, w_value], axis=1)
    projected = jnp.einsum("tgd,dc->tgc", normed_all, w_joint, preferred_element_type=jnp.float32)
    queries = rotate(projected[..., :head_cols].reshape(shape_heads), cos_table, sin_table).astype(
        jnp.bfloat16
    )
    key_rows = rotate(
        projected[..., head_cols : 2 * head_cols].reshape(shape_heads), cos_table, sin_table
    ).astype(jnp.bfloat16)
    value_rows = projected[..., 2 * head_cols :].reshape(shape_heads).astype(jnp.bfloat16)
    scores = attention_scores(queries, key_rows, allowed)
    row_max = jnp.max(scores, axis=-1, keepdims=True)
    log_total = row_max + jnp.log(jnp.sum(jnp.exp(scores - row_max), axis=-1, keepdims=True))
    attn_probs = jnp.exp(scores - log_total).astype(jnp.bfloat16)
    attn_mix = (
        jnp.einsum("ghts,sghe->tghe", attn_probs, value_rows, preferred_element_type=jnp.float32)
        .astype(jnp.bfloat16)
        .reshape(GTOK, group_count, head_cols)
    )
    rows_here = attn_mix
    attn_sum = lax.psum_scatter(
        jnp.einsum("tgc,cd->tgd", rows_here, w_out, preferred_element_type=jnp.float32),
        "tensor",
        scatter_dimension=0,
        tiled=True,
    )
    middle = residual + attn_sum
    scale_two = rms_scale(middle)
    unit_two = middle * scale_two
    normed_two = (unit_two * gain_two).astype(jnp.bfloat16)
    normed_more = lax.all_gather(normed_two, "tensor", axis=0, tiled=True)
    w_gate_up = jnp.concatenate([w_gate, w_up], axis=1)
    gate_up = jnp.einsum("tgd,df->tgf", normed_more, w_gate_up, preferred_element_type=jnp.float32)
    gate_vals = gate_up[..., :hidden_cols]
    up_vals = gate_up[..., hidden_cols:]
    sigmoid_gate = jax.nn.sigmoid(gate_vals)
    silu_gate = gate_vals * sigmoid_gate
    hidden = (silu_gate * up_vals).astype(jnp.bfloat16)
    rows_here = hidden
    ffn_sum = lax.psum_scatter(
        jnp.einsum("tgf,fd->tgd", rows_here, w_down, preferred_element_type=jnp.float32).astype(
            jnp.bfloat16
        ),
        "tensor",
        scatter_dimension=0,
        tiled=True,
    ).astype(jnp.float32)
    output = (middle + ffn_sum).astype(jnp.bfloat16)
    upstream_all = lax.all_gather(upstream, "tensor", axis=0, tiled=True)
    hidden_grad = jnp.einsum(
        "tgd,fd->tgf", upstream_all, w_down, preferred_element_type=jnp.float32
    )
    grad_down = jnp.einsum("tgf,tgd->fd", hidden, upstream_all, preferred_element_type=jnp.float32)
    up_grad = hidden_grad * silu_gate
    gate_grad = hidden_grad * up_vals * (sigmoid_gate * (1.0 + gate_vals * (1.0 - sigmoid_gate)))
    gate_up_grad = jnp.concatenate([gate_grad, up_grad], axis=-1).astype(jnp.bfloat16)
    grad_gate_up = jnp.einsum(
        "tgd,tgf->df", normed_more, gate_up_grad, preferred_element_type=jnp.float32
    )
    rows_here = gate_up_grad
    normed_two_grad = lax.psum_scatter(
        jnp.einsum("tgf,df->tgd", rows_here, w_gate_up, preferred_element_type=jnp.float32).astype(
            jnp.bfloat16
        ),
        "tensor",
        scatter_dimension=0,
        tiled=True,
    ).astype(jnp.float32)
    gain_two_grad = jnp.sum(normed_two_grad * unit_two, axis=(0, 1))
    middle_grad = upstream.astype(jnp.float32) + norm_back(
        normed_two_grad, unit_two, gain_two, scale_two
    )
    attn_grad = middle_grad.astype(jnp.bfloat16)
    attn_grad_all = lax.all_gather(attn_grad, "tensor", axis=0, tiled=True)
    mix_grad = (
        jnp.einsum("tgd,cd->tgc", attn_grad_all, w_out, preferred_element_type=jnp.float32)
        .astype(jnp.bfloat16)
        .reshape(shape_heads)
    )
    grad_out = jnp.einsum(
        "tgc,tgd->cd", attn_mix, attn_grad_all, preferred_element_type=jnp.float32
    )
    scores_again = attention_scores(queries, key_rows, allowed)
    probs_full = jnp.exp(scores_again - log_total)
    prob_grad = jnp.einsum(
        "tghe,sghe->ghts", mix_grad, value_rows, preferred_element_type=jnp.float32
    )
    value_grad = jnp.einsum(
        "ghts,tghe->sghe",
        probs_full.astype(jnp.bfloat16),
        mix_grad,
        preferred_element_type=jnp.float32,
    )
    centre = jnp.sum(probs_full * prob_grad, axis=-1, keepdims=True)
    score_grad = (probs_full * (prob_grad - centre)).astype(jnp.bfloat16)
    query_grad = jnp.einsum(
        "ghts,sghe->tghe", score_grad, key_rows, preferred_element_type=jnp.float32
    ) * HD ** (-0.5)
    key_grad = jnp.einsum(
        "ghts,tghe->sghe", score_grad, queries, preferred_element_type=jnp.float32
    ) * HD ** (-0.5)
    flat_shape = (GTOK, group_count, head_cols)
    joint_grad = jnp.concatenate(
        [
            rotate_back(query_grad, cos_table, sin_table).reshape(flat_shape),
            rotate_back(key_grad, cos_table, sin_table).reshape(flat_shape),
            value_grad.reshape(flat_shape),
        ],
        axis=-1,
    ).astype(jnp.bfloat16)
    grad_joint = jnp.einsum(
        "tgd,tgc->dc", normed_all, joint_grad, preferred_element_type=jnp.float32
    )
    rows_here = joint_grad
    normed_one_grad = lax.psum_scatter(
        jnp.einsum("tgc,dc->tgd", rows_here, w_joint, preferred_element_type=jnp.float32).astype(
            jnp.bfloat16
        ),
        "tensor",
        scatter_dimension=0,
        tiled=True,
    ).astype(jnp.float32)
    gain_one_grad = jnp.sum(normed_one_grad * unit_one, axis=(0, 1))
    input_grad = (middle_grad + norm_back(normed_one_grad, unit_one, gain_one, scale_one)).astype(
        jnp.bfloat16
    )
    param_grads = (
        grad_joint[:, :head_cols],
        grad_joint[:, head_cols : 2 * head_cols],
        grad_joint[:, 2 * head_cols :],
        grad_out,
        grad_gate_up[:, :hidden_cols],
        grad_gate_up[:, hidden_cols:],
        grad_down,
        gain_one_grad,
        gain_two_grad,
    )
    return (output, input_grad, param_grads)


def sharded_body(
    block_input,
    lengths,
    out_grad,
    w_query,
    w_key,
    w_value,
    w_out,
    w_gate,
    w_up,
    w_down,
    attn_gain,
    ffn_gain,
):
    outputs = []
    input_grads = []
    totals = None
    shares = None
    for micro_index in range(block_input.shape[0]):
        gathered = (
            lax.all_gather(w_query, "dp", axis=0, tiled=True),
            lax.all_gather(w_key, "dp", axis=0, tiled=True),
            lax.all_gather(w_value, "dp", axis=0, tiled=True),
            lax.all_gather(w_out, "dp", axis=1, tiled=True),
            lax.all_gather(w_gate, "dp", axis=0, tiled=True),
            lax.all_gather(w_up, "dp", axis=0, tiled=True),
            lax.all_gather(w_down, "dp", axis=1, tiled=True),
            lax.all_gather(attn_gain, "dp", axis=0, tiled=True),
            lax.all_gather(ffn_gain, "dp", axis=0, tiled=True),
        )
        output, input_grad, param_grads = micro_step(
            block_input[micro_index], lengths[micro_index], out_grad[micro_index], gathered
        )
        outputs.append(output)
        input_grads.append(input_grad)
        totals = param_grads if totals is None else add_tuples(totals, param_grads)
    shares = (
        lax.psum_scatter(
            totals[0].astype(jnp.bfloat16), "dp", scatter_dimension=0, tiled=True
        ).astype(jnp.float32),
        lax.psum_scatter(
            totals[1].astype(jnp.bfloat16), "dp", scatter_dimension=0, tiled=True
        ).astype(jnp.float32),
        lax.psum_scatter(
            totals[2].astype(jnp.bfloat16), "dp", scatter_dimension=0, tiled=True
        ).astype(jnp.float32),
        lax.psum_scatter(
            totals[3].astype(jnp.bfloat16), "dp", scatter_dimension=1, tiled=True
        ).astype(jnp.float32),
        lax.psum_scatter(
            totals[4].astype(jnp.bfloat16), "dp", scatter_dimension=0, tiled=True
        ).astype(jnp.float32),
        lax.psum_scatter(
            totals[5].astype(jnp.bfloat16), "dp", scatter_dimension=0, tiled=True
        ).astype(jnp.float32),
        lax.psum_scatter(
            totals[6].astype(jnp.bfloat16), "dp", scatter_dimension=1, tiled=True
        ).astype(jnp.float32),
        lax.psum_scatter(
            totals[7].astype(jnp.bfloat16), "dp", scatter_dimension=0, tiled=True
        ).astype(jnp.float32),
        lax.psum_scatter(
            totals[8].astype(jnp.bfloat16), "dp", scatter_dimension=0, tiled=True
        ).astype(jnp.float32),
    )
    gain_one_total, gain_two_total = lax.psum((shares[7], shares[8]), "tensor")
    return (
        jnp.stack(outputs),
        jnp.stack(input_grads),
        shares[0],
        shares[1],
        shares[2],
        shares[3],
        shares[4],
        shares[5],
        shares[6],
        gain_one_total,
        gain_two_total,
    )


MESH = pl.DeviceIdType.MESH
RELATIVE = [4 * ((j // 2) % 2) + 2 * (j % 2) + j // 4 for j in range(8)]
RING = [(0, 1), (1, 3), (3, 2), (2, 0)]


def flip_core(d):
    return d + 1 - 2 * (d % 2)


def flip_x(d):
    return d + 2 - 4 * ((d // 2) % 2)


def flip_y(d):
    return d + 4 - 8 * ((d // 4) % 2)


def ring_next(z):
    return (2 * z + 1) % 5


def gather_kernel(sets, count, *refs):
    shards = refs[:count]
    parcels = refs[count : count + 2]
    fulls = refs[count + 2 : 2 * count + 2]
    boxes = refs[2 * count + 2 : 2 * count + 4]
    send_sem, recv_sem, box_send, box_recv, local_sem = refs[2 * count + 4 :]
    d = lax.axis_index("dp")
    z = lax.axis_index("tensor")
    place = {
        "z": (d, ring_next(z)),
        "x": (flip_x(d), z),
        "y": (flip_y(d), z),
        "c": (flip_core(d), z),
    }
    others = [(z + step) % 4 for step in (1, 2, 3)]
    barrier = pltpu.get_barrier_semaphore()
    for peer in (place["x"], place["y"], place["c"], *((d, other) for other in others)):
        pl.semaphore_signal(barrier, inc=1, device_id=peer, device_id_type=MESH)
    pl.semaphore_wait(barrier, 6)
    rows = shards[0].shape[0]

    def region(a, k, j, half):
        width = shards[a].shape[1]
        top, size = (j * rows, rows) if half is None else (j * rows + half * (rows // 2), rows // 2)
        return fulls[a].at[pl.ds(top, size), pl.ds(k * width, width)]

    sends = []

    def start(s, way, slot, src, dst, half=None):
        for a in sets[s]:
            source = shards[a] if src == (0, 0) else region(a, *src, half)
            pltpu.make_async_remote_copy(
                src_ref=source,
                dst_ref=region(a, *dst, half),
                send_sem=send_sem.at[s, slot],
                recv_sem=recv_sem.at[s, slot],
                device_id=place[way],
                device_id_type=MESH,
            ).start()
        sends.append((s, slot, half))

    def bulk(s, slot, half):
        arrs = sets[s]
        size = rows if half is None else rows // 2
        width = sum(shards[a].shape[1] for a in arrs)
        part = fulls[arrs[0]].at[pl.ds(0, size), pl.ds(0, width)]
        return pltpu.make_async_remote_copy(
            src_ref=part,
            dst_ref=part,
            send_sem=send_sem.at[s, slot],
            recv_sem=recv_sem.at[s, slot],
            device_id=place["c"],
            device_id_type=MESH,
        )

    def arrived(s, slot, half=None):
        bulk(s, slot, half).wait_recv()

    ring_slot, x_slot, y_slot, x_relay, y_relay, core_slot = 0, 3, 7, 11, 15, 19

    def core(s, k, j):
        start(s, "c", core_slot + 4 * k + j, (k, j), (k, 4 + j))

    def open_unit(s, k):
        if k > 0:
            arrived(s, ring_slot + k - 1)
        if k < 3:
            start(s, "z", ring_slot + k, (k, 0), (k + 1, 0))
        start(s, "x", x_slot + k, (k, 0), (k, 1))
        start(s, "y", y_slot + k, (k, 0), (k, 2))
        core(s, k, 0)

    def close_unit(s, k):
        arrived(s, x_slot + k)
        start(s, "y", y_relay + k, (k, 1), (k, 3), 1)
        core(s, k, 1)
        arrived(s, y_slot + k)
        start(s, "x", x_relay + k, (k, 2), (k, 3), 0)
        core(s, k, 2)

    def last_part(s, k):
        arrived(s, x_relay + k, 0)
        arrived(s, y_relay + k, 1)
        core(s, k, 3)

    def own_copies():
        for a in range(count):
            yield pltpu.make_async_copy(shards[a], region(a, 0, 0, None), local_sem.at[a])
        for p in range(2):
            yield pltpu.make_async_copy(
                parcels[p].at[z], boxes[p].at[z], local_sem.at[count + p]
            )

    def box_copy(p, step):
        return pltpu.make_async_remote_copy(
            src_ref=parcels[p].at[others[step]],
            dst_ref=boxes[p].at[z],
            send_sem=box_send.at[p, step],
            recv_sem=box_recv.at[p, step],
            device_id=(d, others[step]),
            device_id_type=MESH,
        )

    for copy in own_copies():
        copy.start()
    units = [(s, k) for s in range(len(sets)) for k in range(4)]
    open_unit(*units[0])
    for i, unit in enumerate(units):
        if i + 1 < len(units):
            open_unit(*units[i + 1])
        if i < 6:
            box_copy(i // 3, i % 3).start()
        close_unit(*unit)
        if i > 0:
            last_part(*units[i - 1])
    last_part(*units[-1])
    for s in range(len(sets)):
        for slot in range(core_slot, core_slot + 16):
            arrived(s, slot)
    for p in range(2):
        for step in range(3):
            box_copy(p, step).wait()
    for s, slot, half in sends:
        bulk(s, slot, half).wait_send()
    for copy in own_copies():
        copy.wait()


def gather_weights(shards, parcels, sets):
    count = len(shards)
    vmem = pl.BlockSpec(memory_space=pltpu.VMEM)
    anywhere = pl.BlockSpec(memory_space=pl.ANY)
    return pl.pallas_call(
        functools.partial(gather_kernel, sets, count),
        out_shape=[
            jax.ShapeDtypeStruct((8 * w.shape[0], 4 * w.shape[1]), w.dtype) for w in shards
        ]
        + [jax.ShapeDtypeStruct(p.shape, p.dtype) for p in parcels],
        in_specs=[vmem] * (count + 2),
        out_specs=[anywhere] * (count + 2),
        scratch_shapes=[
            pltpu.SemaphoreType.DMA((len(sets), 35)),
            pltpu.SemaphoreType.DMA((len(sets), 35)),
            pltpu.SemaphoreType.DMA((2, 3)),
            pltpu.SemaphoreType.DMA((2, 3)),
            pltpu.SemaphoreType.DMA((count + 2,)),
        ],
        compiler_params=pltpu.CompilerParams(collective_id=1, has_side_effects=True),
        name="gather_weights",
    )(*shards, *parcels)


def swap(values, mask):
    return lax.ppermute(values, "dp", [(d, d ^ mask) for d in range(8)])


def pass_on(values):
    return lax.ppermute(values, "tensor", RING)


def summed(kept, arrived):
    return (kept.astype(jnp.float32) + arrived.astype(jnp.float32)).astype(jnp.bfloat16)


def scatter_grad(left, right):
    half = left.shape[1] // 2
    width = right.shape[1]
    rows = half // 4
    tokens = ((0,), (0,))
    moved = swap(dot_tt(left[:, half:], right, tokens).astype(jnp.bfloat16), 1)
    total = (dot_tt(left[:, :half], right, tokens) + moved.astype(jnp.float32)).astype(
        jnp.bfloat16
    )
    parts = total.reshape(2, 2, rows, width)
    side_a = parts[..., : width // 2]
    side_b = parts[..., width // 2 :]
    step_a = swap(side_a[:, 1], 2)
    step_b = swap(side_b[1], 4)
    side_a = summed(side_a[:, 0], step_a)
    side_b = summed(side_b[0], step_b)
    step_a = swap(side_a[1], 4)
    step_b = swap(side_b[1], 2)
    side_a = summed(side_a[0], step_a)
    side_b = summed(side_b[0], step_b)
    unit = width // 4
    blocks = [side_a[:, :unit], side_a[:, unit:], side_b[:, :unit], side_b[:, unit:]]
    running = blocks[1]
    for k in (2, 3):
        running = summed(blocks[k], pass_on(running))
    return blocks[0].astype(jnp.float32) + pass_on(running).astype(jnp.float32)


def gather_gains(gains):
    parts = [gains] + [swap(gains, mask) for mask in RELATIVE[1:]]
    return jnp.concatenate(parts, axis=1)


def scatter_gains(sums):
    rows = sums.shape[1] // 8
    total = sums[:, :rows]
    for j in range(1, 8):
        total = total + swap(sums[:, j * rows : (j + 1) * rows], RELATIVE[j])
    result = total
    for step in (1, 2, 3):
        result = result + lax.ppermute(total, "tensor", [(z, (z + step) % 4) for z in range(4)])
    return result


def to_parcels(values):
    micro, rows, groups, width = values.shape
    return values.transpose(0, 2, 1, 3).reshape(micro * groups, rows, width)


def from_group(values, micro, groups):
    rows = values.shape[0] // (micro * groups)
    width = values.shape[1]
    parts = values.reshape(micro * groups, rows, width)
    moved = lax.all_to_all(parts, "tensor", 0, 0, tiled=True)
    return moved.reshape(micro, groups, rows, width).transpose(0, 2, 1, 3)


def dot_tt(left, right, dims):
    return lax.dot_general(left, right, (dims, ((), ())), preferred_element_type=jnp.float32)


def turn(values, cos_table, sin_table, sign):
    half = HD // 2
    first_half = values[..., :half]
    second_half = values[..., half:]
    return jnp.concatenate(
        [
            first_half * cos_table - sign * second_half * sin_table,
            second_half * cos_table + sign * first_half * sin_table,
        ],
        axis=-1,
    )


def order_matrix(width):
    rows = width // 8
    d = lax.axis_index("dp")
    owner = jnp.concatenate([jnp.full((rows,), mask, jnp.int32) for mask in RELATIVE])
    feature = (d ^ owner) * rows + jnp.arange(width, dtype=jnp.int32) % rows
    return (jnp.arange(width, dtype=jnp.int32)[:, None] == feature[None, :]).astype(jnp.bfloat16)


def group_body(
    block_input,
    lengths,
    out_grad,
    w_query,
    w_key,
    w_value,
    w_out,
    w_gate,
    w_up,
    w_down,
    attn_gain,
    ffn_gain,
):
    micro, _, groups, width = block_input.shape
    z_size = 4
    unit_cols = w_query.shape[1]
    head_cols = unit_cols * z_size
    heads = head_cols // HD
    bf16 = jnp.bfloat16
    f32 = jnp.float32
    contract = ((1,), (0,))
    contract_t = ((1,), (1,))
    own_lengths = lax.dynamic_slice_in_dim(
        lengths.reshape(micro * groups, 3), lax.axis_index("tensor"), 1, 0
    )
    gains = gather_gains(jnp.stack([attn_gain, ffn_gain]).astype(f32))
    w_qkv, wo, wg, wu, wd, x_box, dy_box = gather_weights(
        (jnp.concatenate([w_query, w_key, w_value], axis=1), w_out.T, w_gate, w_up, w_down.T),
        (to_parcels(block_input), to_parcels(out_grad)),
        ((0, 1), (2, 3), (4,)),
    )
    order = order_matrix(width)
    tokens_in = dot_tt(x_box.reshape(GTOK, width), order, contract)
    upstream = dot_tt(dy_box.reshape(GTOK, width), order, contract).astype(bf16)
    gain_one = gains[0]
    gain_two = gains[1]

    segment, cos_table, sin_table = layout_tables(own_lengths)
    seg = segment[:, 0]
    cos_table = cos_table[:, 0, None, :]
    sin_table = sin_table[:, 0, None, :]
    index = jnp.arange(GTOK, dtype=jnp.int32)
    allowed = (index[None, :] <= index[:, None]) & (
        (seg[None, :] == 0) | (seg[None, :] == seg[:, None])
    )
    residual = tokens_in
    scale_one = rms_scale(residual)
    unit_one = residual * scale_one
    normed_one = (unit_one * gain_one).astype(bf16)
    split = (GTOK, heads, HD)
    joint = dot_tt(normed_one, w_qkv, contract).reshape(GTOK, z_size, 3, unit_cols)
    queries = turn(joint[:, :, 0].reshape(split), cos_table, sin_table, 1.0).astype(bf16)
    keys = turn(joint[:, :, 1].reshape(split), cos_table, sin_table, 1.0).astype(bf16)
    values = joint[:, :, 2].reshape(split).astype(bf16)
    scale = HD ** (-0.5)

    def score(qs, ks):
        raw = jnp.einsum("the,she->hts", qs, ks, preferred_element_type=f32) * scale
        return jnp.where(allowed[None], raw, MASKED)

    scores = score(queries, keys)
    row_max = jnp.max(scores, axis=-1, keepdims=True)
    log_total = row_max + jnp.log(jnp.sum(jnp.exp(scores - row_max), axis=-1, keepdims=True))
    probs = jnp.exp(scores - log_total).astype(bf16)
    mix = (
        jnp.einsum("hts,she->the", probs, values, preferred_element_type=f32)
        .astype(bf16)
        .reshape(GTOK, head_cols)
    )
    middle = residual + dot_tt(mix, wo, contract_t)
    scale_two = rms_scale(middle)
    unit_two = middle * scale_two
    normed_two = (unit_two * gain_two).astype(bf16)
    gate_vals = dot_tt(normed_two, wg, contract)
    up_vals = dot_tt(normed_two, wu, contract)
    sigmoid_gate = jax.nn.sigmoid(gate_vals)
    silu_gate = gate_vals * sigmoid_gate
    hidden = (silu_gate * up_vals).astype(bf16)
    share_down = scatter_grad(upstream, hidden).T
    output = (middle + dot_tt(hidden, wd, contract_t)).astype(bf16)
    out_final = from_group(dot_tt(output, order, contract_t).astype(bf16), micro, groups)

    hidden_grad = dot_tt(upstream, wd, contract)
    up_grad = (hidden_grad * silu_gate).astype(bf16)
    gate_grad = (
        hidden_grad * up_vals * (sigmoid_gate * (1.0 + gate_vals * (1.0 - sigmoid_gate)))
    ).astype(bf16)
    share_gate = scatter_grad(normed_two, gate_grad)
    share_up = scatter_grad(normed_two, up_grad)
    normed_two_grad = dot_tt(gate_grad, wg, contract_t) + dot_tt(up_grad, wu, contract_t)
    gain_two_grad = jnp.sum(normed_two_grad * unit_two, axis=0)
    middle_grad = upstream.astype(f32) + norm_back(
        normed_two_grad, unit_two, gain_two, scale_two
    )
    attn_grad = middle_grad.astype(bf16)
    share_out = scatter_grad(attn_grad, mix).T
    mix_grad = dot_tt(attn_grad, wo, contract).astype(bf16).reshape(split)
    probs_full = jnp.exp(score(queries, keys) - log_total)
    prob_grad = jnp.einsum("the,she->hts", mix_grad, values, preferred_element_type=f32)
    value_grad = jnp.einsum(
        "hts,the->she", probs_full.astype(bf16), mix_grad, preferred_element_type=f32
    )
    centre = jnp.sum(probs_full * prob_grad, axis=-1, keepdims=True)
    score_grad = (probs_full * (prob_grad - centre)).astype(bf16)
    query_grad = jnp.einsum("hts,she->the", score_grad, keys, preferred_element_type=f32) * scale
    key_grad = jnp.einsum("hts,the->she", score_grad, queries, preferred_element_type=f32) * scale
    pieces = (GTOK, z_size, 1, unit_cols)
    joint_grad = jnp.concatenate(
        [
            turn(query_grad, cos_table, sin_table, -1.0).astype(bf16).reshape(pieces),
            turn(key_grad, cos_table, sin_table, -1.0).astype(bf16).reshape(pieces),
            value_grad.astype(bf16).reshape(pieces),
        ],
        axis=2,
    ).reshape(GTOK, 3 * head_cols)
    share_joint = scatter_grad(normed_one, joint_grad)
    normed_one_grad = dot_tt(joint_grad, w_qkv, contract_t)
    gain_one_grad = jnp.sum(normed_one_grad * unit_one, axis=0)
    input_grad = (
        middle_grad + norm_back(normed_one_grad, unit_one, gain_one, scale_one)
    ).astype(bf16)
    in_grad_final = from_group(dot_tt(input_grad, order, contract_t).astype(bf16), micro, groups)
    own_gains = scatter_gains(jnp.stack([gain_one_grad, gain_two_grad]))
    return (
        out_final,
        in_grad_final,
        share_joint[:, :unit_cols],
        share_joint[:, unit_cols : 2 * unit_cols],
        share_joint[:, 2 * unit_cols :],
        share_out,
        share_gate,
        share_up,
        share_down,
        own_gains[0],
        own_gains[1],
    )


def body(*operands):
    micro, _, groups, _ = operands[0].shape
    if lax.axis_size("dp") == 8 and micro * groups == lax.axis_size("tensor") == 4:
        return group_body(*operands)
    return sharded_body(*operands)


def solution(mesh):
    placed = (
        P(None, "tensor", "dp", None),
        P(None, "dp", None),
        P(None, "tensor", "dp", None),
        P("dp", "tensor"),
        P("dp", "tensor"),
        P("dp", "tensor"),
        P("tensor", "dp"),
        P("dp", "tensor"),
        P("dp", "tensor"),
        P("tensor", "dp"),
        P("dp"),
        P("dp"),
    )
    return jax.shard_map(
        body,
        mesh=mesh,
        in_specs=placed,
        out_specs=(
            P(None, "tensor", "dp", None),
            P(None, "tensor", "dp", None),
            P("dp", "tensor"),
            P("dp", "tensor"),
            P("dp", "tensor"),
            P("tensor", "dp"),
            P("dp", "tensor"),
            P("dp", "tensor"),
            P("tensor", "dp"),
            P("dp"),
            P("dp"),
        ),
        check_vma=False,
    )
```

```python
import functools
import math

import jax
import jax.numpy as jnp
from jax import lax
from jax.experimental import pallas as pl
from jax.experimental.pallas import tpu as pltpu
from jax.sharding import PartitionSpec as P


HD = 64
GTOK = 512


EPSILON = 1e-05
MASKED = -1e30


def layout_tables(group_lengths):
    slot_index = jnp.arange(GTOK, dtype=jnp.int32)[:, None]
    prompt_len = group_lengths[:, 0][None, :]
    first_len = group_lengths[:, 1][None, :]
    segment = jnp.where(
        slot_index < prompt_len, 0, jnp.where(slot_index < prompt_len + first_len, 1, 2)
    ).astype(jnp.int32)
    position = jnp.where(segment == 2, slot_index - first_len, slot_index)
    frequency = jnp.exp(jnp.arange(HD // 2, dtype=jnp.float32) * (-2.0 * math.log(10000.0) / HD))
    angles = position.astype(jnp.float32)[:, :, None] * frequency
    return (segment, jnp.cos(angles), jnp.sin(angles))


def rotate(values, cos_table, sin_table):
    half_size = values.shape[-1] // 2
    first_half = values[..., :half_size]
    second_half = values[..., half_size:]
    cos_wide = cos_table[:, :, None, :]
    sin_wide = sin_table[:, :, None, :]
    return jnp.concatenate(
        [
            first_half * cos_wide - second_half * sin_wide,
            second_half * cos_wide + first_half * sin_wide,
        ],
        axis=-1,
    )


def rotate_back(values, cos_table, sin_table):
    half_size = values.shape[-1] // 2
    first_half = values[..., :half_size]
    second_half = values[..., half_size:]
    cos_wide = cos_table[:, :, None, :]
    sin_wide = sin_table[:, :, None, :]
    return jnp.concatenate(
        [
            first_half * cos_wide + second_half * sin_wide,
            second_half * cos_wide - first_half * sin_wide,
        ],
        axis=-1,
    )


def rms_scale(values):
    return lax.rsqrt(jnp.mean(values * values, axis=-1, keepdims=True) + EPSILON)


def norm_back(upstream, unit_rows, gain_row, scale_rows):
    scaled = upstream * gain_row
    return scale_rows * (scaled - unit_rows * jnp.mean(scaled * unit_rows, axis=-1, keepdims=True))


def attention_scores(queries, key_rows, allowed):
    scores = jnp.einsum(
        "tghe,sghe->ghts", queries, key_rows, preferred_element_type=jnp.float32
    ) * HD ** (-0.5)
    return jnp.where(allowed[:, None], scores, MASKED)


def add_tuples(first_set, second_set):
    return tuple((earlier + later for earlier, later in zip(first_set, second_set)))


def micro_step(inputs, group_lengths, upstream, gathered):
    w_query, w_key, w_value, w_out, w_gate, w_up, w_down, attn_gain, ffn_gain = gathered
    gain_one = attn_gain.astype(jnp.float32)
    gain_two = ffn_gain.astype(jnp.float32)
    group_count = inputs.shape[1]
    head_cols = w_query.shape[1]
    hidden_cols = w_gate.shape[1]
    shape_heads = (GTOK, group_count, head_cols // HD, HD)
    segment, cos_table, sin_table = layout_tables(group_lengths)
    token_index = jnp.arange(GTOK, dtype=jnp.int32)
    seg_groups = segment.T
    allowed = (token_index[None, None, :] <= token_index[None, :, None]) & (
        (seg_groups[:, None, :] == 0) | (seg_groups[:, None, :] == seg_groups[:, :, None])
    )
    residual = inputs.astype(jnp.float32)
    scale_one = rms_scale(residual)
    unit_one = residual * scale_one
    normed_one = (unit_one * gain_one).astype(jnp.bfloat16)
    normed_all = lax.all_gather(normed_one, "tensor", axis=0, tiled=True)
    w_joint = jnp.concatenate([w_query, w_key, w_value], axis=1)
    projected = jnp.einsum("tgd,dc->tgc", normed_all, w_joint, preferred_element_type=jnp.float32)
    queries = rotate(projected[..., :head_cols].reshape(shape_heads), cos_table, sin_table).astype(
        jnp.bfloat16
    )
    key_rows = rotate(
        projected[..., head_cols : 2 * head_cols].reshape(shape_heads), cos_table, sin_table
    ).astype(jnp.bfloat16)
    value_rows = projected[..., 2 * head_cols :].reshape(shape_heads).astype(jnp.bfloat16)
    scores = attention_scores(queries, key_rows, allowed)
    row_max = jnp.max(scores, axis=-1, keepdims=True)
    log_total = row_max + jnp.log(jnp.sum(jnp.exp(scores - row_max), axis=-1, keepdims=True))
    attn_probs = jnp.exp(scores - log_total).astype(jnp.bfloat16)
    attn_mix = (
        jnp.einsum("ghts,sghe->tghe", attn_probs, value_rows, preferred_element_type=jnp.float32)
        .astype(jnp.bfloat16)
        .reshape(GTOK, group_count, head_cols)
    )
    rows_here = attn_mix
    attn_sum = lax.psum_scatter(
        jnp.einsum("tgc,cd->tgd", rows_here, w_out, preferred_element_type=jnp.float32),
        "tensor",
        scatter_dimension=0,
        tiled=True,
    )
    middle = residual + attn_sum
    scale_two = rms_scale(middle)
    unit_two = middle * scale_two
    normed_two = (unit_two * gain_two).astype(jnp.bfloat16)
    normed_more = lax.all_gather(normed_two, "tensor", axis=0, tiled=True)
    w_gate_up = jnp.concatenate([w_gate, w_up], axis=1)
    gate_up = jnp.einsum("tgd,df->tgf", normed_more, w_gate_up, preferred_element_type=jnp.float32)
    gate_vals = gate_up[..., :hidden_cols]
    up_vals = gate_up[..., hidden_cols:]
    sigmoid_gate = jax.nn.sigmoid(gate_vals)
    silu_gate = gate_vals * sigmoid_gate
    hidden = (silu_gate * up_vals).astype(jnp.bfloat16)
    rows_here = hidden
    ffn_sum = lax.psum_scatter(
        jnp.einsum("tgf,fd->tgd", rows_here, w_down, preferred_element_type=jnp.float32).astype(
            jnp.bfloat16
        ),
        "tensor",
        scatter_dimension=0,
        tiled=True,
    ).astype(jnp.float32)
    output = (middle + ffn_sum).astype(jnp.bfloat16)
    upstream_all = lax.all_gather(upstream, "tensor", axis=0, tiled=True)
    hidden_grad = jnp.einsum(
        "tgd,fd->tgf", upstream_all, w_down, preferred_element_type=jnp.float32
    )
    grad_down = jnp.einsum("tgf,tgd->fd", hidden, upstream_all, preferred_element_type=jnp.float32)
    up_grad = hidden_grad * silu_gate
    gate_grad = hidden_grad * up_vals * (sigmoid_gate * (1.0 + gate_vals * (1.0 - sigmoid_gate)))
    gate_up_grad = jnp.concatenate([gate_grad, up_grad], axis=-1).astype(jnp.bfloat16)
    grad_gate_up = jnp.einsum(
        "tgd,tgf->df", normed_more, gate_up_grad, preferred_element_type=jnp.float32
    )
    rows_here = gate_up_grad
    normed_two_grad = lax.psum_scatter(
        jnp.einsum("tgf,df->tgd", rows_here, w_gate_up, preferred_element_type=jnp.float32).astype(
            jnp.bfloat16
        ),
        "tensor",
        scatter_dimension=0,
        tiled=True,
    ).astype(jnp.float32)
    gain_two_grad = jnp.sum(normed_two_grad * unit_two, axis=(0, 1))
    middle_grad = upstream.astype(jnp.float32) + norm_back(
        normed_two_grad, unit_two, gain_two, scale_two
    )
    attn_grad = middle_grad.astype(jnp.bfloat16)
    attn_grad_all = lax.all_gather(attn_grad, "tensor", axis=0, tiled=True)
    mix_grad = (
        jnp.einsum("tgd,cd->tgc", attn_grad_all, w_out, preferred_element_type=jnp.float32)
        .astype(jnp.bfloat16)
        .reshape(shape_heads)
    )
    grad_out = jnp.einsum(
        "tgc,tgd->cd", attn_mix, attn_grad_all, preferred_element_type=jnp.float32
    )
    scores_again = attention_scores(queries, key_rows, allowed)
    probs_full = jnp.exp(scores_again - log_total)
    prob_grad = jnp.einsum(
        "tghe,sghe->ghts", mix_grad, value_rows, preferred_element_type=jnp.float32
    )
    value_grad = jnp.einsum(
        "ghts,tghe->sghe",
        probs_full.astype(jnp.bfloat16),
        mix_grad,
        preferred_element_type=jnp.float32,
    )
    centre = jnp.sum(probs_full * prob_grad, axis=-1, keepdims=True)
    score_grad = (probs_full * (prob_grad - centre)).astype(jnp.bfloat16)
    query_grad = jnp.einsum(
        "ghts,sghe->tghe", score_grad, key_rows, preferred_element_type=jnp.float32
    ) * HD ** (-0.5)
    key_grad = jnp.einsum(
        "ghts,tghe->sghe", score_grad, queries, preferred_element_type=jnp.float32
    ) * HD ** (-0.5)
    flat_shape = (GTOK, group_count, head_cols)
    joint_grad = jnp.concatenate(
        [
            rotate_back(query_grad, cos_table, sin_table).reshape(flat_shape),
            rotate_back(key_grad, cos_table, sin_table).reshape(flat_shape),
            value_grad.reshape(flat_shape),
        ],
        axis=-1,
    ).astype(jnp.bfloat16)
    grad_joint = jnp.einsum(
        "tgd,tgc->dc", normed_all, joint_grad, preferred_element_type=jnp.float32
    )
    rows_here = joint_grad
    normed_one_grad = lax.psum_scatter(
        jnp.einsum("tgc,dc->tgd", rows_here, w_joint, preferred_element_type=jnp.float32).astype(
            jnp.bfloat16
        ),
        "tensor",
        scatter_dimension=0,
        tiled=True,
    ).astype(jnp.float32)
    gain_one_grad = jnp.sum(normed_one_grad * unit_one, axis=(0, 1))
    input_grad = (middle_grad + norm_back(normed_one_grad, unit_one, gain_one, scale_one)).astype(
        jnp.bfloat16
    )
    param_grads = (
        grad_joint[:, :head_cols],
        grad_joint[:, head_cols : 2 * head_cols],
        grad_joint[:, 2 * head_cols :],
        grad_out,
        grad_gate_up[:, :hidden_cols],
        grad_gate_up[:, hidden_cols:],
        grad_down,
        gain_one_grad,
        gain_two_grad,
    )
    return (output, input_grad, param_grads)


def sharded_body(
    block_input,
    lengths,
    out_grad,
    w_query,
    w_key,
    w_value,
    w_out,
    w_gate,
    w_up,
    w_down,
    attn_gain,
    ffn_gain,
):
    outputs = []
    input_grads = []
    totals = None
    shares = None
    for micro_index in range(block_input.shape[0]):
        gathered = (
            lax.all_gather(w_query, "dp", axis=0, tiled=True),
            lax.all_gather(w_key, "dp", axis=0, tiled=True),
            lax.all_gather(w_value, "dp", axis=0, tiled=True),
            lax.all_gather(w_out, "dp", axis=1, tiled=True),
            lax.all_gather(w_gate, "dp", axis=0, tiled=True),
            lax.all_gather(w_up, "dp", axis=0, tiled=True),
            lax.all_gather(w_down, "dp", axis=1, tiled=True),
            lax.all_gather(attn_gain, "dp", axis=0, tiled=True),
            lax.all_gather(ffn_gain, "dp", axis=0, tiled=True),
        )
        output, input_grad, param_grads = micro_step(
            block_input[micro_index], lengths[micro_index], out_grad[micro_index], gathered
        )
        outputs.append(output)
        input_grads.append(input_grad)
        totals = param_grads if totals is None else add_tuples(totals, param_grads)
    shares = (
        lax.psum_scatter(
            totals[0].astype(jnp.bfloat16), "dp", scatter_dimension=0, tiled=True
        ).astype(jnp.float32),
        lax.psum_scatter(
            totals[1].astype(jnp.bfloat16), "dp", scatter_dimension=0, tiled=True
        ).astype(jnp.float32),
        lax.psum_scatter(
            totals[2].astype(jnp.bfloat16), "dp", scatter_dimension=0, tiled=True
        ).astype(jnp.float32),
        lax.psum_scatter(
            totals[3].astype(jnp.bfloat16), "dp", scatter_dimension=1, tiled=True
        ).astype(jnp.float32),
        lax.psum_scatter(
            totals[4].astype(jnp.bfloat16), "dp", scatter_dimension=0, tiled=True
        ).astype(jnp.float32),
        lax.psum_scatter(
            totals[5].astype(jnp.bfloat16), "dp", scatter_dimension=0, tiled=True
        ).astype(jnp.float32),
        lax.psum_scatter(
            totals[6].astype(jnp.bfloat16), "dp", scatter_dimension=1, tiled=True
        ).astype(jnp.float32),
        lax.psum_scatter(
            totals[7].astype(jnp.bfloat16), "dp", scatter_dimension=0, tiled=True
        ).astype(jnp.float32),
        lax.psum_scatter(
            totals[8].astype(jnp.bfloat16), "dp", scatter_dimension=0, tiled=True
        ).astype(jnp.float32),
    )
    gain_one_total, gain_two_total = lax.psum((shares[7], shares[8]), "tensor")
    return (
        jnp.stack(outputs),
        jnp.stack(input_grads),
        shares[0],
        shares[1],
        shares[2],
        shares[3],
        shares[4],
        shares[5],
        shares[6],
        gain_one_total,
        gain_two_total,
    )


MESH = pl.DeviceIdType.MESH
RELATIVE = [4 * ((j // 2) % 2) + 2 * (j % 2) + j // 4 for j in range(8)]


def flip_core(d):
    return d + 1 - 2 * (d % 2)


def flip_x(d):
    return d + 2 - 4 * ((d // 2) % 2)


def flip_y(d):
    return d + 4 - 8 * ((d // 4) % 2)


def ring_next(z):
    return (2 * z + 1) % 5


def ring_prev(z):
    return (3 * (z + 4)) % 5


def gather_kernel(sets, count, *refs):
    shards = refs[:count]
    parcels = refs[count : count + 2]
    fulls = refs[count + 2 : 2 * count + 2]
    boxes = refs[2 * count + 2 : 2 * count + 4]
    send_sem, recv_sem, box_send, box_recv, local_sem = refs[2 * count + 4 :]
    d = lax.axis_index("dp")
    z = lax.axis_index("tensor")
    place = {
        "z": (d, ring_next(z)),
        "x": (flip_x(d), z),
        "y": (flip_y(d), z),
        "c": (flip_core(d), z),
    }
    others = [(z + step) % 4 for step in (1, 2, 3)]
    barrier = pltpu.get_barrier_semaphore()
    for peer in (place["x"], place["y"], place["c"], *((d, other) for other in others)):
        pl.semaphore_signal(barrier, inc=1, device_id=peer, device_id_type=MESH)
    pl.semaphore_wait(barrier, 6)
    rows = shards[0].shape[0]

    def region(a, k, j, half):
        width = shards[a].shape[1]
        top, size = (j * rows, rows) if half is None else (j * rows + half * (rows // 2), rows // 2)
        return fulls[a].at[pl.ds(top, size), pl.ds(k * width, width)]

    sends = []

    def start(s, way, slot, src, dst, half=None):
        for a in sets[s]:
            source = shards[a] if src == (0, 0) else region(a, *src, half)
            pltpu.make_async_remote_copy(
                src_ref=source,
                dst_ref=region(a, *dst, half),
                send_sem=send_sem.at[s, slot],
                recv_sem=recv_sem.at[s, slot],
                device_id=place[way],
                device_id_type=MESH,
            ).start()
        sends.append((s, slot, half))

    def bulk(s, slot, half):
        arrs = sets[s]
        size = rows if half is None else rows // 2
        width = sum(shards[a].shape[1] for a in arrs)
        part = fulls[arrs[0]].at[pl.ds(0, size), pl.ds(0, width)]
        return pltpu.make_async_remote_copy(
            src_ref=part,
            dst_ref=part,
            send_sem=send_sem.at[s, slot],
            recv_sem=recv_sem.at[s, slot],
            device_id=place["c"],
            device_id_type=MESH,
        )

    def arrived(s, slot, half=None):
        bulk(s, slot, half).wait_recv()

    ring_slot, x_slot, y_slot, x_relay, y_relay, core_slot = 0, 3, 7, 11, 15, 19

    def core(s, k, j):
        start(s, "c", core_slot + 4 * k + j, (k, j), (k, 4 + j))

    def open_unit(s, k):
        if k > 0:
            arrived(s, ring_slot + k - 1)
        if k < 3:
            start(s, "z", ring_slot + k, (k, 0), (k + 1, 0))
        start(s, "x", x_slot + k, (k, 0), (k, 1))
        start(s, "y", y_slot + k, (k, 0), (k, 2))
        core(s, k, 0)

    def close_unit(s, k):
        arrived(s, x_slot + k)
        start(s, "y", y_relay + k, (k, 1), (k, 3), 1)
        core(s, k, 1)
        arrived(s, y_slot + k)
        start(s, "x", x_relay + k, (k, 2), (k, 3), 0)
        core(s, k, 2)

    def last_part(s, k):
        arrived(s, x_relay + k, 0)
        arrived(s, y_relay + k, 1)
        core(s, k, 3)

    def own_copies():
        for a in range(count):
            yield pltpu.make_async_copy(shards[a], region(a, 0, 0, None), local_sem.at[a])
        for p in range(2):
            yield pltpu.make_async_copy(
                parcels[p].at[z], boxes[p].at[z], local_sem.at[count + p]
            )

    def box_copy(p, step):
        return pltpu.make_async_remote_copy(
            src_ref=parcels[p].at[others[step]],
            dst_ref=boxes[p].at[z],
            send_sem=box_send.at[p, step],
            recv_sem=box_recv.at[p, step],
            device_id=(d, others[step]),
            device_id_type=MESH,
        )

    for copy in own_copies():
        copy.start()
    units = [(s, k) for s in range(len(sets)) for k in range(4)]
    open_unit(*units[0])
    for i, unit in enumerate(units):
        if i + 1 < len(units):
            open_unit(*units[i + 1])
        if i < 6:
            box_copy(i // 3, i % 3).start()
        close_unit(*unit)
        if i > 0:
            last_part(*units[i - 1])
    last_part(*units[-1])
    for s in range(len(sets)):
        for slot in range(core_slot, core_slot + 16):
            arrived(s, slot)
    for p in range(2):
        for step in range(3):
            box_copy(p, step).wait()
    for s, slot, half in sends:
        bulk(s, slot, half).wait_send()
    for copy in own_copies():
        copy.wait()


def gather_weights(shards, parcels, sets):
    count = len(shards)
    vmem = pl.BlockSpec(memory_space=pltpu.VMEM)
    anywhere = pl.BlockSpec(memory_space=pl.ANY)
    return pl.pallas_call(
        functools.partial(gather_kernel, sets, count),
        out_shape=[
            jax.ShapeDtypeStruct((8 * w.shape[0], 4 * w.shape[1]), w.dtype) for w in shards
        ]
        + [jax.ShapeDtypeStruct(p.shape, p.dtype) for p in parcels],
        in_specs=[vmem] * (count + 2),
        out_specs=[anywhere] * (count + 2),
        scratch_shapes=[
            pltpu.SemaphoreType.DMA((len(sets), 35)),
            pltpu.SemaphoreType.DMA((len(sets), 35)),
            pltpu.SemaphoreType.DMA((2, 3)),
            pltpu.SemaphoreType.DMA((2, 3)),
            pltpu.SemaphoreType.DMA((count + 2,)),
        ],
        compiler_params=pltpu.CompilerParams(collective_id=1, has_side_effects=True),
        name="gather_weights",
    )(*shards, *parcels)


def add_rows(target, first, second, chunk=32):
    rows = target.shape[0]

    def step(i, carry):
        at = pl.ds(pl.multiple_of(i * chunk, chunk), chunk)
        target[at, :] = (
            first[at, :].astype(jnp.float32) + second[at, :].astype(jnp.float32)
        ).astype(target.dtype)
        return carry

    lax.fori_loop(0, rows // chunk, step, 0)


def scatter_kernel(count, *refs):
    grads = refs[:count]
    shares = refs[count : 2 * count]
    rest = refs[2 * count :]
    from_core, from_first, from_second, from_ring = (
        rest[i * count : (i + 1) * count] for i in range(4)
    )
    total, middle, final, send_sem, recv_sem, load_sem = rest[4 * count :]
    d = lax.axis_index("dp")
    z = lax.axis_index("tensor")
    core, east, north = (flip_core(d), z), (flip_x(d), z), (flip_y(d), z)
    onward = (d, ring_next(z))
    barrier = pltpu.get_barrier_semaphore()
    for peer in (core, east, north, onward, (d, ring_prev(z))):
        pl.semaphore_signal(barrier, inc=1, device_id=peer, device_id_type=MESH)
    pl.semaphore_wait(barrier, 5)
    rows = grads[0].shape[1]
    half = rows // 2
    units = [(g, k) for g in range(count) for k in (1, 2, 3, 0)]
    width = [grads[g].shape[2] // 4 for g in range(count)]

    def send(src, dst, u, slot, peer):
        return pltpu.make_async_remote_copy(
            src_ref=src,
            dst_ref=dst,
            send_sem=send_sem.at[u, slot],
            recv_sem=recv_sem.at[u, slot],
            device_id=peer,
            device_id_type=MESH,
        )

    def columns(u):
        g, k = units[u]
        return pl.ds(k * width[g], width[g])

    def to_core(u):
        g, k = units[u]
        return send(
            grads[g].at[pl.ds(4, 4), :, columns(u)], from_core[g].at[k], u, 0, core
        )

    def load(u):
        g, _ = units[u]
        return pltpu.make_async_copy(
            grads[g].at[pl.ds(0, 4), :, columns(u)],
            total.at[u % 3, :, :, pl.ds(0, width[g])],
            load_sem.at[u % 3],
        )

    def first_sends(u):
        g, k = units[u]
        t = total.at[u % 3]
        cols = pl.ds(0, width[g])
        return [
            send(t.at[1, pl.ds(0, half), cols], from_first[g].at[k, 0, 0], u, 1, east),
            send(t.at[3, pl.ds(0, half), cols], from_first[g].at[k, 0, 1], u, 2, east),
            send(t.at[2, pl.ds(half, half), cols], from_first[g].at[k, 1, 0], u, 3, north),
            send(t.at[3, pl.ds(half, half), cols], from_first[g].at[k, 1, 1], u, 4, north),
        ]

    def second_sends(u):
        g, k = units[u]
        m = middle.at[u % 2]
        cols = pl.ds(0, width[g])
        return [
            send(m.at[0, :, cols], from_second[g].at[k, 0], u, 5, north),
            send(m.at[1, :, cols], from_second[g].at[k, 1], u, 6, east),
        ]

    def ring_send(u):
        g, k = units[u]
        return send(
            final.at[u % 2, :, pl.ds(0, width[g])], from_ring[g].at[k], u, 7, onward
        )

    def first_stage(u):
        g, k = units[u]
        t = total.at[u % 3]
        cols = pl.ds(0, width[g])
        load(u).wait()
        to_core(u).wait_recv()
        for j in range(4):
            part = t.at[j, :, cols]
            add_rows(part, part, from_core[g].at[k, j])
        for copy in first_sends(u):
            copy.start()

    def second_stage(u):
        g, k = units[u]
        t = total.at[u % 3]
        m = middle.at[u % 2]
        cols = pl.ds(0, width[g])
        if u >= 2:
            for copy in second_sends(u - 2):
                copy.wait_send()
        sends = first_sends(u)
        sends[1].wait_recv()
        add_rows(m.at[0, :, cols], t.at[2, pl.ds(0, half), cols], from_first[g].at[k, 0, 1])
        sends[3].wait_recv()
        add_rows(m.at[1, :, cols], t.at[1, pl.ds(half, half), cols], from_first[g].at[k, 1, 1])
        for copy in second_sends(u):
            copy.start()
        sends[0].wait_recv()
        upper = t.at[0, pl.ds(0, half), cols]
        add_rows(upper, upper, from_first[g].at[k, 0, 0])
        sends[2].wait_recv()
        lower = t.at[0, pl.ds(half, half), cols]
        add_rows(lower, lower, from_first[g].at[k, 1, 0])

    def third_stage(u):
        g, k = units[u]
        t = total.at[u % 3]
        cols = pl.ds(0, width[g])
        for side, copy in enumerate(second_sends(u)):
            copy.wait_recv()
            part = t.at[0, pl.ds(side * half, half), cols]
            if k == 1:
                if side == 0 and u >= 2:
                    wait_ring(u - 2)
                add_rows(
                    final.at[u % 2, pl.ds(side * half, half), cols],
                    part,
                    from_second[g].at[k, side],
                )
            else:
                add_rows(part, part, from_second[g].at[k, side])
        if k != 1:
            ring_send(u - 1).wait_recv()
            if k == 0:
                wait_ring(u - 2)
                add_rows(shares[g], t.at[0, :, cols], from_ring[g].at[3])
            else:
                if u >= 2:
                    wait_ring(u - 2)
                add_rows(final.at[u % 2, :, cols], t.at[0, :, cols], from_ring[g].at[k - 1])
        if k != 0:
            ring_send(u).start()
        for copy in first_sends(u):
            copy.wait_send()

    def wait_ring(u):
        if units[u][1] != 0:
            ring_send(u).wait_send()

    n = len(units)
    for u in range(n):
        to_core(u).start()
        if u < 3:
            load(u).start()
    for step in range(n + 2):
        if step < n:
            first_stage(step)
        if 0 <= step - 1 < n:
            second_stage(step - 1)
        if 0 <= step - 2:
            third_stage(step - 2)
            if step + 1 < n:
                load(step + 1).start()
    for u in range(n):
        to_core(u).wait_send()
        if u >= n - 2:
            for copy in second_sends(u):
                copy.wait_send()
            wait_ring(u)


def scatter_grads(grads, cid):
    count = len(grads)
    views = [g.reshape(8, g.shape[0] // 8, g.shape[1]) for g in grads]
    rows = views[0].shape[1]
    half = rows // 2
    widths = [g.shape[1] // 4 for g in grads]
    widest = max(widths)
    bf16 = jnp.bfloat16
    return pl.pallas_call(
        functools.partial(scatter_kernel, count),
        out_shape=[jax.ShapeDtypeStruct((rows, w), jnp.float32) for w in widths],
        in_specs=[pl.BlockSpec(memory_space=pl.ANY)] * count,
        out_specs=[pl.BlockSpec(memory_space=pltpu.VMEM)] * count,
        scratch_shapes=[pltpu.VMEM((4, 4, rows, w), bf16) for w in widths]
        + [pltpu.VMEM((4, 2, 2, half, w), bf16) for w in widths]
        + [pltpu.VMEM((4, 2, half, w), bf16) for w in widths]
        + [pltpu.VMEM((4, rows, w), bf16) for w in widths]
        + [
            pltpu.VMEM((3, 4, rows, widest), bf16),
            pltpu.VMEM((2, 2, half, widest), bf16),
            pltpu.VMEM((2, rows, widest), bf16),
            pltpu.SemaphoreType.DMA((4 * count, 8)),
            pltpu.SemaphoreType.DMA((4 * count, 8)),
            pltpu.SemaphoreType.DMA((3,)),
        ],
        compiler_params=pltpu.CompilerParams(
            collective_id=cid, has_side_effects=True, vmem_limit_bytes=64000000
        ),
        name="scatter_grads",
    )(*views)


def swap(values, mask):
    return lax.ppermute(values, "dp", [(d, d ^ mask) for d in range(8)])


def grad_dot(left, right):
    return dot_tt(left, right, ((0,), (0,))).astype(jnp.bfloat16)


def gather_gains(gains):
    parts = [gains] + [swap(gains, mask) for mask in RELATIVE[1:]]
    return jnp.concatenate(parts, axis=1)


def scatter_gains(sums):
    rows = sums.shape[1] // 8
    total = sums[:, :rows]
    for j in range(1, 8):
        total = total + swap(sums[:, j * rows : (j + 1) * rows], RELATIVE[j])
    result = total
    for step in (1, 2, 3):
        result = result + lax.ppermute(total, "tensor", [(z, (z + step) % 4) for z in range(4)])
    return result


def to_parcels(values):
    micro, rows, groups, width = values.shape
    return values.transpose(0, 2, 1, 3).reshape(micro * groups, rows, width)


def from_group(values, micro, groups):
    rows = values.shape[0] // (micro * groups)
    width = values.shape[1]
    parts = values.reshape(micro * groups, rows, width)
    moved = lax.all_to_all(parts, "tensor", 0, 0, tiled=True)
    return moved.reshape(micro, groups, rows, width).transpose(0, 2, 1, 3)


def dot_tt(left, right, dims):
    return lax.dot_general(left, right, (dims, ((), ())), preferred_element_type=jnp.float32)


def turn(values, cos_table, sin_table, sign):
    half = HD // 2
    first_half = values[..., :half]
    second_half = values[..., half:]
    return jnp.concatenate(
        [
            first_half * cos_table - sign * second_half * sin_table,
            second_half * cos_table + sign * first_half * sin_table,
        ],
        axis=-1,
    )


def order_matrix(width):
    rows = width // 8
    d = lax.axis_index("dp")
    owner = jnp.concatenate([jnp.full((rows,), mask, jnp.int32) for mask in RELATIVE])
    feature = (d ^ owner) * rows + jnp.arange(width, dtype=jnp.int32) % rows
    return (jnp.arange(width, dtype=jnp.int32)[:, None] == feature[None, :]).astype(jnp.bfloat16)


def group_body(
    block_input,
    lengths,
    out_grad,
    w_query,
    w_key,
    w_value,
    w_out,
    w_gate,
    w_up,
    w_down,
    attn_gain,
    ffn_gain,
):
    micro, _, groups, width = block_input.shape
    z_size = 4
    unit_cols = w_query.shape[1]
    head_cols = unit_cols * z_size
    heads = head_cols // HD
    bf16 = jnp.bfloat16
    f32 = jnp.float32
    contract = ((1,), (0,))
    contract_t = ((1,), (1,))
    own_lengths = lax.dynamic_slice_in_dim(
        lengths.reshape(micro * groups, 3), lax.axis_index("tensor"), 1, 0
    )
    gains = gather_gains(jnp.stack([attn_gain, ffn_gain]).astype(f32))
    w_qkv, wo, wg, wu, wd, x_box, dy_box = gather_weights(
        (jnp.concatenate([w_query, w_key, w_value], axis=1), w_out.T, w_gate, w_up, w_down.T),
        (to_parcels(block_input), to_parcels(out_grad)),
        ((0, 1), (2, 3), (4,)),
    )
    order = order_matrix(width)
    tokens_in = dot_tt(x_box.reshape(GTOK, width), order, contract)
    upstream = dot_tt(dy_box.reshape(GTOK, width), order, contract).astype(bf16)
    gain_one = gains[0]
    gain_two = gains[1]

    segment, cos_table, sin_table = layout_tables(own_lengths)
    seg = segment[:, 0]
    cos_table = cos_table[:, 0, None, :]
    sin_table = sin_table[:, 0, None, :]
    index = jnp.arange(GTOK, dtype=jnp.int32)
    allowed = (index[None, :] <= index[:, None]) & (
        (seg[None, :] == 0) | (seg[None, :] == seg[:, None])
    )
    residual = tokens_in
    scale_one = rms_scale(residual)
    unit_one = residual * scale_one
    normed_one = (unit_one * gain_one).astype(bf16)
    split = (GTOK, heads, HD)
    joint = dot_tt(normed_one, w_qkv, contract).reshape(GTOK, z_size, 3, unit_cols)
    queries = turn(joint[:, :, 0].reshape(split), cos_table, sin_table, 1.0).astype(bf16)
    keys = turn(joint[:, :, 1].reshape(split), cos_table, sin_table, 1.0).astype(bf16)
    values = joint[:, :, 2].reshape(split).astype(bf16)
    scale = HD ** (-0.5)

    def score(qs, ks):
        raw = jnp.einsum("the,she->hts", qs, ks, preferred_element_type=f32) * scale
        return jnp.where(allowed[None], raw, MASKED)

    scores = score(queries, keys)
    row_max = jnp.max(scores, axis=-1, keepdims=True)
    log_total = row_max + jnp.log(jnp.sum(jnp.exp(scores - row_max), axis=-1, keepdims=True))
    probs = jnp.exp(scores - log_total).astype(bf16)
    mix = (
        jnp.einsum("hts,she->the", probs, values, preferred_element_type=f32)
        .astype(bf16)
        .reshape(GTOK, head_cols)
    )
    middle = residual + dot_tt(mix, wo, contract_t)
    scale_two = rms_scale(middle)
    unit_two = middle * scale_two
    normed_two = (unit_two * gain_two).astype(bf16)
    gate_vals = dot_tt(normed_two, wg, contract)
    up_vals = dot_tt(normed_two, wu, contract)
    sigmoid_gate = jax.nn.sigmoid(gate_vals)
    silu_gate = gate_vals * sigmoid_gate
    hidden = (silu_gate * up_vals).astype(bf16)
    output = (middle + dot_tt(hidden, wd, contract_t)).astype(bf16)
    out_final = from_group(dot_tt(output, order, contract_t).astype(bf16), micro, groups)

    hidden_grad = dot_tt(upstream, wd, contract)
    up_grad = (hidden_grad * silu_gate).astype(bf16)
    gate_grad = (
        hidden_grad * up_vals * (sigmoid_gate * (1.0 + gate_vals * (1.0 - sigmoid_gate)))
    ).astype(bf16)
    share_down, share_gate, share_up = scatter_grads(
        (
            grad_dot(upstream, hidden),
            grad_dot(normed_two, gate_grad),
            grad_dot(normed_two, up_grad),
        ),
        2,
    )
    normed_two_grad = dot_tt(gate_grad, wg, contract_t) + dot_tt(up_grad, wu, contract_t)
    gain_two_grad = jnp.sum(normed_two_grad * unit_two, axis=0)
    middle_grad = upstream.astype(f32) + norm_back(
        normed_two_grad, unit_two, gain_two, scale_two
    )
    attn_grad = middle_grad.astype(bf16)
    mix_grad = dot_tt(attn_grad, wo, contract).astype(bf16).reshape(split)
    probs_full = jnp.exp(score(queries, keys) - log_total)
    prob_grad = jnp.einsum("the,she->hts", mix_grad, values, preferred_element_type=f32)
    value_grad = jnp.einsum(
        "hts,the->she", probs_full.astype(bf16), mix_grad, preferred_element_type=f32
    )
    centre = jnp.sum(probs_full * prob_grad, axis=-1, keepdims=True)
    score_grad = (probs_full * (prob_grad - centre)).astype(bf16)
    query_grad = jnp.einsum("hts,she->the", score_grad, keys, preferred_element_type=f32) * scale
    key_grad = jnp.einsum("hts,the->she", score_grad, queries, preferred_element_type=f32) * scale
    pieces = (GTOK, z_size, 1, unit_cols)
    joint_grad = jnp.concatenate(
        [
            turn(query_grad, cos_table, sin_table, -1.0).astype(bf16).reshape(pieces),
            turn(key_grad, cos_table, sin_table, -1.0).astype(bf16).reshape(pieces),
            value_grad.astype(bf16).reshape(pieces),
        ],
        axis=2,
    ).reshape(GTOK, 3 * head_cols)
    share_out, share_joint = scatter_grads(
        (grad_dot(attn_grad, mix), grad_dot(normed_one, joint_grad)), 3
    )
    normed_one_grad = dot_tt(joint_grad, w_qkv, contract_t)
    gain_one_grad = jnp.sum(normed_one_grad * unit_one, axis=0)
    input_grad = (
        middle_grad + norm_back(normed_one_grad, unit_one, gain_one, scale_one)
    ).astype(bf16)
    in_grad_final = from_group(dot_tt(input_grad, order, contract_t).astype(bf16), micro, groups)
    own_gains = scatter_gains(jnp.stack([gain_one_grad, gain_two_grad]))
    return (
        out_final,
        in_grad_final,
        share_joint[:, :unit_cols],
        share_joint[:, unit_cols : 2 * unit_cols],
        share_joint[:, 2 * unit_cols :],
        share_out.T,
        share_gate,
        share_up,
        share_down.T,
        own_gains[0],
        own_gains[1],
    )


def body(*operands):
    micro, _, groups, _ = operands[0].shape
    if lax.axis_size("dp") == 8 and micro * groups == lax.axis_size("tensor") == 4:
        return group_body(*operands)
    return sharded_body(*operands)


def solution(mesh):
    placed = (
        P(None, "tensor", "dp", None),
        P(None, "dp", None),
        P(None, "tensor", "dp", None),
        P("dp", "tensor"),
        P("dp", "tensor"),
        P("dp", "tensor"),
        P("tensor", "dp"),
        P("dp", "tensor"),
        P("dp", "tensor"),
        P("tensor", "dp"),
        P("dp"),
        P("dp"),
    )
    return jax.shard_map(
        body,
        mesh=mesh,
        in_specs=placed,
        out_specs=(
            P(None, "tensor", "dp", None),
            P(None, "tensor", "dp", None),
            P("dp", "tensor"),
            P("dp", "tensor"),
            P("dp", "tensor"),
            P("tensor", "dp"),
            P("dp", "tensor"),
            P("dp", "tensor"),
            P("tensor", "dp"),
            P("dp"),
            P("dp"),
        ),
        check_vma=False,
    )
```

```python
import functools
import math

import jax
import jax.numpy as jnp
from jax import lax
from jax.experimental import pallas as pl
from jax.experimental.pallas import tpu as pltpu
from jax.sharding import PartitionSpec as P


HD = 64
GTOK = 512


EPSILON = 1e-05
MASKED = -1e30


def layout_tables(group_lengths):
    slot_index = jnp.arange(GTOK, dtype=jnp.int32)[:, None]
    prompt_len = group_lengths[:, 0][None, :]
    first_len = group_lengths[:, 1][None, :]
    segment = jnp.where(
        slot_index < prompt_len, 0, jnp.where(slot_index < prompt_len + first_len, 1, 2)
    ).astype(jnp.int32)
    position = jnp.where(segment == 2, slot_index - first_len, slot_index)
    frequency = jnp.exp(jnp.arange(HD // 2, dtype=jnp.float32) * (-2.0 * math.log(10000.0) / HD))
    angles = position.astype(jnp.float32)[:, :, None] * frequency
    return (segment, jnp.cos(angles), jnp.sin(angles))


def rotate(values, cos_table, sin_table):
    half_size = values.shape[-1] // 2
    first_half = values[..., :half_size]
    second_half = values[..., half_size:]
    cos_wide = cos_table[:, :, None, :]
    sin_wide = sin_table[:, :, None, :]
    return jnp.concatenate(
        [
            first_half * cos_wide - second_half * sin_wide,
            second_half * cos_wide + first_half * sin_wide,
        ],
        axis=-1,
    )


def rotate_back(values, cos_table, sin_table):
    half_size = values.shape[-1] // 2
    first_half = values[..., :half_size]
    second_half = values[..., half_size:]
    cos_wide = cos_table[:, :, None, :]
    sin_wide = sin_table[:, :, None, :]
    return jnp.concatenate(
        [
            first_half * cos_wide + second_half * sin_wide,
            second_half * cos_wide - first_half * sin_wide,
        ],
        axis=-1,
    )


def rms_scale(values):
    return lax.rsqrt(jnp.mean(values * values, axis=-1, keepdims=True) + EPSILON)


def norm_back(upstream, unit_rows, gain_row, scale_rows):
    scaled = upstream * gain_row
    return scale_rows * (scaled - unit_rows * jnp.mean(scaled * unit_rows, axis=-1, keepdims=True))


def attention_scores(queries, key_rows, allowed):
    scores = jnp.einsum(
        "tghe,sghe->ghts", queries, key_rows, preferred_element_type=jnp.float32
    ) * HD ** (-0.5)
    return jnp.where(allowed[:, None], scores, MASKED)


def add_tuples(first_set, second_set):
    return tuple((earlier + later for earlier, later in zip(first_set, second_set)))


def micro_step(inputs, group_lengths, upstream, gathered):
    w_query, w_key, w_value, w_out, w_gate, w_up, w_down, attn_gain, ffn_gain = gathered
    gain_one = attn_gain.astype(jnp.float32)
    gain_two = ffn_gain.astype(jnp.float32)
    group_count = inputs.shape[1]
    head_cols = w_query.shape[1]
    hidden_cols = w_gate.shape[1]
    shape_heads = (GTOK, group_count, head_cols // HD, HD)
    segment, cos_table, sin_table = layout_tables(group_lengths)
    token_index = jnp.arange(GTOK, dtype=jnp.int32)
    seg_groups = segment.T
    allowed = (token_index[None, None, :] <= token_index[None, :, None]) & (
        (seg_groups[:, None, :] == 0) | (seg_groups[:, None, :] == seg_groups[:, :, None])
    )
    residual = inputs.astype(jnp.float32)
    scale_one = rms_scale(residual)
    unit_one = residual * scale_one
    normed_one = (unit_one * gain_one).astype(jnp.bfloat16)
    normed_all = lax.all_gather(normed_one, "tensor", axis=0, tiled=True)
    w_joint = jnp.concatenate([w_query, w_key, w_value], axis=1)
    projected = jnp.einsum("tgd,dc->tgc", normed_all, w_joint, preferred_element_type=jnp.float32)
    queries = rotate(projected[..., :head_cols].reshape(shape_heads), cos_table, sin_table).astype(
        jnp.bfloat16
    )
    key_rows = rotate(
        projected[..., head_cols : 2 * head_cols].reshape(shape_heads), cos_table, sin_table
    ).astype(jnp.bfloat16)
    value_rows = projected[..., 2 * head_cols :].reshape(shape_heads).astype(jnp.bfloat16)
    scores = attention_scores(queries, key_rows, allowed)
    row_max = jnp.max(scores, axis=-1, keepdims=True)
    log_total = row_max + jnp.log(jnp.sum(jnp.exp(scores - row_max), axis=-1, keepdims=True))
    attn_probs = jnp.exp(scores - log_total).astype(jnp.bfloat16)
    attn_mix = (
        jnp.einsum("ghts,sghe->tghe", attn_probs, value_rows, preferred_element_type=jnp.float32)
        .astype(jnp.bfloat16)
        .reshape(GTOK, group_count, head_cols)
    )
    rows_here = attn_mix
    attn_sum = lax.psum_scatter(
        jnp.einsum("tgc,cd->tgd", rows_here, w_out, preferred_element_type=jnp.float32),
        "tensor",
        scatter_dimension=0,
        tiled=True,
    )
    middle = residual + attn_sum
    scale_two = rms_scale(middle)
    unit_two = middle * scale_two
    normed_two = (unit_two * gain_two).astype(jnp.bfloat16)
    normed_more = lax.all_gather(normed_two, "tensor", axis=0, tiled=True)
    w_gate_up = jnp.concatenate([w_gate, w_up], axis=1)
    gate_up = jnp.einsum("tgd,df->tgf", normed_more, w_gate_up, preferred_element_type=jnp.float32)
    gate_vals = gate_up[..., :hidden_cols]
    up_vals = gate_up[..., hidden_cols:]
    sigmoid_gate = jax.nn.sigmoid(gate_vals)
    silu_gate = gate_vals * sigmoid_gate
    hidden = (silu_gate * up_vals).astype(jnp.bfloat16)
    rows_here = hidden
    ffn_sum = lax.psum_scatter(
        jnp.einsum("tgf,fd->tgd", rows_here, w_down, preferred_element_type=jnp.float32).astype(
            jnp.bfloat16
        ),
        "tensor",
        scatter_dimension=0,
        tiled=True,
    ).astype(jnp.float32)
    output = (middle + ffn_sum).astype(jnp.bfloat16)
    upstream_all = lax.all_gather(upstream, "tensor", axis=0, tiled=True)
    hidden_grad = jnp.einsum(
        "tgd,fd->tgf", upstream_all, w_down, preferred_element_type=jnp.float32
    )
    grad_down = jnp.einsum("tgf,tgd->fd", hidden, upstream_all, preferred_element_type=jnp.float32)
    up_grad = hidden_grad * silu_gate
    gate_grad = hidden_grad * up_vals * (sigmoid_gate * (1.0 + gate_vals * (1.0 - sigmoid_gate)))
    gate_up_grad = jnp.concatenate([gate_grad, up_grad], axis=-1).astype(jnp.bfloat16)
    grad_gate_up = jnp.einsum(
        "tgd,tgf->df", normed_more, gate_up_grad, preferred_element_type=jnp.float32
    )
    rows_here = gate_up_grad
    normed_two_grad = lax.psum_scatter(
        jnp.einsum("tgf,df->tgd", rows_here, w_gate_up, preferred_element_type=jnp.float32).astype(
            jnp.bfloat16
        ),
        "tensor",
        scatter_dimension=0,
        tiled=True,
    ).astype(jnp.float32)
    gain_two_grad = jnp.sum(normed_two_grad * unit_two, axis=(0, 1))
    middle_grad = upstream.astype(jnp.float32) + norm_back(
        normed_two_grad, unit_two, gain_two, scale_two
    )
    attn_grad = middle_grad.astype(jnp.bfloat16)
    attn_grad_all = lax.all_gather(attn_grad, "tensor", axis=0, tiled=True)
    mix_grad = (
        jnp.einsum("tgd,cd->tgc", attn_grad_all, w_out, preferred_element_type=jnp.float32)
        .astype(jnp.bfloat16)
        .reshape(shape_heads)
    )
    grad_out = jnp.einsum(
        "tgc,tgd->cd", attn_mix, attn_grad_all, preferred_element_type=jnp.float32
    )
    scores_again = attention_scores(queries, key_rows, allowed)
    probs_full = jnp.exp(scores_again - log_total)
    prob_grad = jnp.einsum(
        "tghe,sghe->ghts", mix_grad, value_rows, preferred_element_type=jnp.float32
    )
    value_grad = jnp.einsum(
        "ghts,tghe->sghe",
        probs_full.astype(jnp.bfloat16),
        mix_grad,
        preferred_element_type=jnp.float32,
    )
    centre = jnp.sum(probs_full * prob_grad, axis=-1, keepdims=True)
    score_grad = (probs_full * (prob_grad - centre)).astype(jnp.bfloat16)
    query_grad = jnp.einsum(
        "ghts,sghe->tghe", score_grad, key_rows, preferred_element_type=jnp.float32
    ) * HD ** (-0.5)
    key_grad = jnp.einsum(
        "ghts,tghe->sghe", score_grad, queries, preferred_element_type=jnp.float32
    ) * HD ** (-0.5)
    flat_shape = (GTOK, group_count, head_cols)
    joint_grad = jnp.concatenate(
        [
            rotate_back(query_grad, cos_table, sin_table).reshape(flat_shape),
            rotate_back(key_grad, cos_table, sin_table).reshape(flat_shape),
            value_grad.reshape(flat_shape),
        ],
        axis=-1,
    ).astype(jnp.bfloat16)
    grad_joint = jnp.einsum(
        "tgd,tgc->dc", normed_all, joint_grad, preferred_element_type=jnp.float32
    )
    rows_here = joint_grad
    normed_one_grad = lax.psum_scatter(
        jnp.einsum("tgc,dc->tgd", rows_here, w_joint, preferred_element_type=jnp.float32).astype(
            jnp.bfloat16
        ),
        "tensor",
        scatter_dimension=0,
        tiled=True,
    ).astype(jnp.float32)
    gain_one_grad = jnp.sum(normed_one_grad * unit_one, axis=(0, 1))
    input_grad = (middle_grad + norm_back(normed_one_grad, unit_one, gain_one, scale_one)).astype(
        jnp.bfloat16
    )
    param_grads = (
        grad_joint[:, :head_cols],
        grad_joint[:, head_cols : 2 * head_cols],
        grad_joint[:, 2 * head_cols :],
        grad_out,
        grad_gate_up[:, :hidden_cols],
        grad_gate_up[:, hidden_cols:],
        grad_down,
        gain_one_grad,
        gain_two_grad,
    )
    return (output, input_grad, param_grads)


def sharded_body(
    block_input,
    lengths,
    out_grad,
    w_query,
    w_key,
    w_value,
    w_out,
    w_gate,
    w_up,
    w_down,
    attn_gain,
    ffn_gain,
):
    outputs = []
    input_grads = []
    totals = None
    shares = None
    for micro_index in range(block_input.shape[0]):
        gathered = (
            lax.all_gather(w_query, "dp", axis=0, tiled=True),
            lax.all_gather(w_key, "dp", axis=0, tiled=True),
            lax.all_gather(w_value, "dp", axis=0, tiled=True),
            lax.all_gather(w_out, "dp", axis=1, tiled=True),
            lax.all_gather(w_gate, "dp", axis=0, tiled=True),
            lax.all_gather(w_up, "dp", axis=0, tiled=True),
            lax.all_gather(w_down, "dp", axis=1, tiled=True),
            lax.all_gather(attn_gain, "dp", axis=0, tiled=True),
            lax.all_gather(ffn_gain, "dp", axis=0, tiled=True),
        )
        output, input_grad, param_grads = micro_step(
            block_input[micro_index], lengths[micro_index], out_grad[micro_index], gathered
        )
        outputs.append(output)
        input_grads.append(input_grad)
        totals = param_grads if totals is None else add_tuples(totals, param_grads)
    shares = (
        lax.psum_scatter(
            totals[0].astype(jnp.bfloat16), "dp", scatter_dimension=0, tiled=True
        ).astype(jnp.float32),
        lax.psum_scatter(
            totals[1].astype(jnp.bfloat16), "dp", scatter_dimension=0, tiled=True
        ).astype(jnp.float32),
        lax.psum_scatter(
            totals[2].astype(jnp.bfloat16), "dp", scatter_dimension=0, tiled=True
        ).astype(jnp.float32),
        lax.psum_scatter(
            totals[3].astype(jnp.bfloat16), "dp", scatter_dimension=1, tiled=True
        ).astype(jnp.float32),
        lax.psum_scatter(
            totals[4].astype(jnp.bfloat16), "dp", scatter_dimension=0, tiled=True
        ).astype(jnp.float32),
        lax.psum_scatter(
            totals[5].astype(jnp.bfloat16), "dp", scatter_dimension=0, tiled=True
        ).astype(jnp.float32),
        lax.psum_scatter(
            totals[6].astype(jnp.bfloat16), "dp", scatter_dimension=1, tiled=True
        ).astype(jnp.float32),
        lax.psum_scatter(
            totals[7].astype(jnp.bfloat16), "dp", scatter_dimension=0, tiled=True
        ).astype(jnp.float32),
        lax.psum_scatter(
            totals[8].astype(jnp.bfloat16), "dp", scatter_dimension=0, tiled=True
        ).astype(jnp.float32),
    )
    gain_one_total, gain_two_total = lax.psum((shares[7], shares[8]), "tensor")
    return (
        jnp.stack(outputs),
        jnp.stack(input_grads),
        shares[0],
        shares[1],
        shares[2],
        shares[3],
        shares[4],
        shares[5],
        shares[6],
        gain_one_total,
        gain_two_total,
    )


MESH = pl.DeviceIdType.MESH
RELATIVE = [4 * ((j // 2) % 2) + 2 * (j % 2) + j // 4 for j in range(8)]


def flip_core(d):
    return d + 1 - 2 * (d % 2)


def flip_x(d):
    return d + 2 - 4 * ((d // 2) % 2)


def flip_y(d):
    return d + 4 - 8 * ((d // 4) % 2)


def flip(d, mask):
    if mask & 1:
        d = flip_core(d)
    if mask & 2:
        d = flip_x(d)
    if mask & 4:
        d = flip_y(d)
    return d


def ring_next(z):
    return (2 * z + 1) % 5


def remote(src, dst, send_sem, recv_sem, peer):
    return pltpu.make_async_remote_copy(
        src_ref=src,
        dst_ref=dst,
        send_sem=send_sem,
        recv_sem=recv_sem,
        device_id=peer,
        device_id_type=MESH,
    )


def greet(d, z):
    barrier = pltpu.get_barrier_semaphore()
    for mask in range(1, 8):
        pl.semaphore_signal(barrier, inc=1, device_id=(flip(d, mask), z), device_id_type=MESH)
    for step in (1, 2, 3):
        pl.semaphore_signal(barrier, inc=1, device_id=(d, (z + step) % 4), device_id_type=MESH)
    pl.semaphore_wait(barrier, 10)


def gather_kernel(sets, count, *refs):
    shards = refs[:count]
    parcels = refs[count : count + 2]
    gains = refs[count + 2]
    fulls = refs[count + 3 : 2 * count + 3]
    boxes = refs[2 * count + 3 : 2 * count + 5]
    gain_box = refs[2 * count + 5]
    send_sem, recv_sem, box_send, box_recv, gain_send, gain_recv, local_sem = refs[2 * count + 6 :]
    d = lax.axis_index("dp")
    z = lax.axis_index("tensor")
    place = {
        "z": (d, ring_next(z)),
        "x": (flip_x(d), z),
        "y": (flip_y(d), z),
        "c": (flip_core(d), z),
    }
    others = [(z + step) % 4 for step in (1, 2, 3)]
    greet(d, z)
    rows = shards[0].shape[0]

    def region(a, k, j, half):
        width = shards[a].shape[1]
        top, size = (j * rows, rows) if half is None else (j * rows + half * (rows // 2), rows // 2)
        return fulls[a].at[pl.ds(top, size), pl.ds(k * width, width)]

    sends = []

    def start(s, way, slot, src, dst, half=None):
        for a in sets[s]:
            source = shards[a] if src == (0, 0) else region(a, *src, half)
            remote(
                source,
                region(a, *dst, half),
                send_sem.at[s, slot],
                recv_sem.at[s, slot],
                place[way],
            ).start()
        sends.append((s, slot, half))

    def bulk(s, slot, half):
        arrs = sets[s]
        size = rows if half is None else rows // 2
        width = sum(shards[a].shape[1] for a in arrs)
        part = fulls[arrs[0]].at[pl.ds(0, size), pl.ds(0, width)]
        return remote(part, part, send_sem.at[s, slot], recv_sem.at[s, slot], place["c"])

    def arrived(s, slot, half=None):
        bulk(s, slot, half).wait_recv()

    ring_slot, x_slot, y_slot, x_relay, y_relay, core_slot = 0, 3, 7, 11, 15, 19

    def core(s, k, j):
        start(s, "c", core_slot + 4 * k + j, (k, j), (k, 4 + j))

    def ring_step(s, k):
        start(s, "z", ring_slot + k, (k, 0), (k + 1, 0))

    def open_unit(s, k):
        if k > 0:
            arrived(s, ring_slot + k - 1)
            if k < 3:
                ring_step(s, k)
        start(s, "x", x_slot + k, (k, 0), (k, 1))
        start(s, "y", y_slot + k, (k, 0), (k, 2))
        core(s, k, 0)

    def close_unit(s, k):
        arrived(s, x_slot + k)
        start(s, "y", y_relay + k, (k, 1), (k, 3), 1)
        core(s, k, 1)
        arrived(s, y_slot + k)
        start(s, "x", x_relay + k, (k, 2), (k, 3), 0)
        core(s, k, 2)

    def last_part(s, k):
        arrived(s, x_relay + k, 0)
        arrived(s, y_relay + k, 1)
        core(s, k, 3)

    def own_copies():
        for a in range(count):
            yield pltpu.make_async_copy(shards[a], region(a, 0, 0, None), local_sem.at[a])
        for p in range(2):
            yield pltpu.make_async_copy(
                parcels[p].at[z], boxes[p].at[z], local_sem.at[count + p]
            )
        yield pltpu.make_async_copy(gains, gain_box.at[0], local_sem.at[count + 2])

    def box_copy(p, step):
        return remote(
            parcels[p].at[others[step]],
            boxes[p].at[z],
            box_send.at[p, step],
            box_recv.at[p, step],
            (d, others[step]),
        )

    def gain_copy(j):
        return remote(
            gains,
            gain_box.at[j],
            gain_send.at[j - 1],
            gain_recv.at[j - 1],
            (flip(d, RELATIVE[j]), z),
        )

    for j in range(1, 8):
        gain_copy(j).start()
    for copy in own_copies():
        copy.start()
    units = [(s, k) for s in range(len(sets)) for k in range(4)]
    ring_step(0, 0)
    open_unit(*units[0])
    for i, unit in enumerate(units):
        if i + 1 < len(units):
            after = units[i + 1]
            if after[1] == 0:
                ring_step(after[0], 0)
            open_unit(*after)
        if i < 6:
            box_copy(i // 3, i % 3).start()
        close_unit(*unit)
        if i > 0:
            last_part(*units[i - 1])
    last_part(*units[-1])
    for s in range(len(sets)):
        for slot in range(core_slot, core_slot + 16):
            arrived(s, slot)
    for p in range(2):
        for step in range(3):
            box_copy(p, step).wait()
    for j in range(1, 8):
        gain_copy(j).wait()
    for s, slot, half in sends:
        bulk(s, slot, half).wait_send()
    for copy in own_copies():
        copy.wait()


def gather_weights(shards, parcels, gains, sets):
    count = len(shards)
    vmem = pl.BlockSpec(memory_space=pltpu.VMEM)
    anywhere = pl.BlockSpec(memory_space=pl.ANY)
    dma = pltpu.SemaphoreType.DMA
    return pl.pallas_call(
        functools.partial(gather_kernel, sets, count),
        out_shape=[
            jax.ShapeDtypeStruct((8 * w.shape[0], 4 * w.shape[1]), w.dtype) for w in shards
        ]
        + [jax.ShapeDtypeStruct(p.shape, p.dtype) for p in parcels]
        + [jax.ShapeDtypeStruct((8, *gains.shape), gains.dtype)],
        in_specs=[vmem] * (count + 3),
        out_specs=[anywhere] * (count + 3),
        scratch_shapes=[
            dma((len(sets), 35)),
            dma((len(sets), 35)),
            dma((2, 3)),
            dma((2, 3)),
            dma((7,)),
            dma((7,)),
            dma((count + 3,)),
        ],
        compiler_params=pltpu.CompilerParams(collective_id=1, has_side_effects=True),
        name="gather_weights",
    )(*shards, *parcels, gains)


def add_rows(target, first, second, chunk=32):
    rows = target.shape[0]

    def step(i, carry):
        at = pl.ds(pl.multiple_of(i * chunk, chunk), chunk)
        target[at, :] = (
            first[at, :].astype(jnp.float32) + second[at, :].astype(jnp.float32)
        ).astype(target.dtype)
        return carry

    lax.fori_loop(0, rows // chunk, step, 0)


def scatter_kernel(count, *refs):
    grads = refs[:count]
    gains = refs[count]
    shares = refs[count + 1 : 2 * count + 1]
    gain_share = refs[2 * count + 1]
    rest = refs[2 * count + 2 :]
    from_core, from_first, from_second, from_ring = (
        rest[i * count : (i + 1) * count] for i in range(4)
    )
    total, middle, final, gain_box, gain_line = rest[4 * count : 4 * count + 5]
    send_sem, recv_sem, load_sem, gain_send, gain_recv = rest[4 * count + 5 :]
    d = lax.axis_index("dp")
    z = lax.axis_index("tensor")
    core, east, north = (flip_core(d), z), (flip_x(d), z), (flip_y(d), z)
    onward = (d, ring_next(z))
    greet(d, z)
    rows = grads[0].shape[1]
    half = rows // 2
    units = [(g, k) for g in range(count) for k in (1, 2, 3, 0)]
    width = [grads[g].shape[2] // 4 for g in range(count)]

    def send(src, dst, u, slot, peer):
        return remote(src, dst, send_sem.at[u, slot], recv_sem.at[u, slot], peer)

    def gain_copy(j):
        return remote(
            gains.at[j],
            gain_box.at[j],
            gain_send.at[j - 1],
            gain_recv.at[j - 1],
            (flip(d, RELATIVE[j]), z),
        )

    def line_copy(step):
        return remote(
            gain_line.at[z],
            gain_line.at[z],
            gain_send.at[6 + step],
            gain_recv.at[6 + step],
            (d, (z + step) % 4),
        )

    def columns(u):
        g, k = units[u]
        return pl.ds(k * width[g], width[g])

    def to_core(u):
        g, k = units[u]
        return send(
            grads[g].at[pl.ds(4, 4), :, columns(u)], from_core[g].at[k], u, 0, core
        )

    def load(u):
        g, _ = units[u]
        return pltpu.make_async_copy(
            grads[g].at[pl.ds(0, 4), :, columns(u)],
            total.at[u % 3, :, :, pl.ds(0, width[g])],
            load_sem.at[u % 3],
        )

    def first_sends(u):
        g, k = units[u]
        t = total.at[u % 3]
        cols = pl.ds(0, width[g])
        return [
            send(t.at[1, pl.ds(0, half), cols], from_first[g].at[k, 0, 0], u, 1, east),
            send(t.at[3, pl.ds(0, half), cols], from_first[g].at[k, 0, 1], u, 2, east),
            send(t.at[2, pl.ds(half, half), cols], from_first[g].at[k, 1, 0], u, 3, north),
            send(t.at[3, pl.ds(half, half), cols], from_first[g].at[k, 1, 1], u, 4, north),
        ]

    def second_sends(u):
        g, k = units[u]
        m = middle.at[u % 2]
        cols = pl.ds(0, width[g])
        return [
            send(m.at[0, :, cols], from_second[g].at[k, 0], u, 5, north),
            send(m.at[1, :, cols], from_second[g].at[k, 1], u, 6, east),
        ]

    def ring_send(u):
        g, k = units[u]
        return send(
            final.at[u % 2, :, pl.ds(0, width[g])], from_ring[g].at[k], u, 7, onward
        )

    def first_stage(u):
        g, k = units[u]
        t = total.at[u % 3]
        cols = pl.ds(0, width[g])
        load(u).wait()
        to_core(u).wait_recv()
        for j in range(4):
            part = t.at[j, :, cols]
            add_rows(part, part, from_core[g].at[k, j])
        for copy in first_sends(u):
            copy.start()

    def second_stage(u):
        g, k = units[u]
        t = total.at[u % 3]
        m = middle.at[u % 2]
        cols = pl.ds(0, width[g])
        if u >= 2:
            for copy in second_sends(u - 2):
                copy.wait_send()
        sends = first_sends(u)
        sends[1].wait_recv()
        add_rows(m.at[0, :, cols], t.at[2, pl.ds(0, half), cols], from_first[g].at[k, 0, 1])
        sends[3].wait_recv()
        add_rows(m.at[1, :, cols], t.at[1, pl.ds(half, half), cols], from_first[g].at[k, 1, 1])
        for copy in second_sends(u):
            copy.start()
        sends[0].wait_recv()
        upper = t.at[0, pl.ds(0, half), cols]
        add_rows(upper, upper, from_first[g].at[k, 0, 0])
        sends[2].wait_recv()
        lower = t.at[0, pl.ds(half, half), cols]
        add_rows(lower, lower, from_first[g].at[k, 1, 0])

    def third_stage(u):
        g, k = units[u]
        t = total.at[u % 3]
        cols = pl.ds(0, width[g])
        for side, copy in enumerate(second_sends(u)):
            copy.wait_recv()
            part = t.at[0, pl.ds(side * half, half), cols]
            if k == 1:
                if side == 0 and u >= 2:
                    wait_ring(u - 2)
                add_rows(
                    final.at[u % 2, pl.ds(side * half, half), cols],
                    part,
                    from_second[g].at[k, side],
                )
            else:
                add_rows(part, part, from_second[g].at[k, side])
        if k != 1:
            ring_send(u - 1).wait_recv()
            if k == 0:
                wait_ring(u - 2)
                add_rows(shares[g], t.at[0, :, cols], from_ring[g].at[3])
            else:
                if u >= 2:
                    wait_ring(u - 2)
                add_rows(final.at[u % 2, :, cols], t.at[0, :, cols], from_ring[g].at[k - 1])
        if k != 0:
            ring_send(u).start()
        for copy in first_sends(u):
            copy.wait_send()

    def wait_ring(u):
        if units[u][1] != 0:
            ring_send(u).wait_send()

    n = len(units)
    for j in range(1, 8):
        gain_copy(j).start()
    for u in range(n):
        to_core(u).start()
        if u < 3:
            load(u).start()
    for step in range(n + 2):
        if step < n:
            first_stage(step)
        if 0 <= step - 1 < n:
            second_stage(step - 1)
        if 0 <= step - 2:
            third_stage(step - 2)
            if step + 1 < n:
                load(step + 1).start()
        if step == 2:
            for j in range(1, 8):
                gain_copy(j).wait()
            gain_line[z] = gains[0] + sum(gain_box[j] for j in range(1, 8))
            for hop in (1, 2, 3):
                line_copy(hop).start()
    for hop in (1, 2, 3):
        line_copy(hop).wait()
    gain_share[...] = gain_line[0] + gain_line[1] + gain_line[2] + gain_line[3]
    for u in range(n):
        to_core(u).wait_send()
        if u >= n - 2:
            for copy in second_sends(u):
                copy.wait_send()
            wait_ring(u)


def scatter_grads(grads, gains):
    count = len(grads)
    views = [g.reshape(8, g.shape[0] // 8, g.shape[1]) for g in grads]
    rows = views[0].shape[1]
    half = rows // 2
    widths = [g.shape[1] // 4 for g in grads]
    widest = max(widths)
    bf16 = jnp.bfloat16
    return pl.pallas_call(
        functools.partial(scatter_kernel, count),
        out_shape=[jax.ShapeDtypeStruct((rows, w), jnp.float32) for w in widths]
        + [jax.ShapeDtypeStruct(gains.shape[1:], jnp.float32)],
        in_specs=[pl.BlockSpec(memory_space=pl.ANY)] * count + [pl.BlockSpec(memory_space=pltpu.VMEM)],
        out_specs=[pl.BlockSpec(memory_space=pltpu.VMEM)] * (count + 1),
        scratch_shapes=[pltpu.VMEM((4, 4, rows, w), bf16) for w in widths]
        + [pltpu.VMEM((4, 2, 2, half, w), bf16) for w in widths]
        + [pltpu.VMEM((4, 2, half, w), bf16) for w in widths]
        + [pltpu.VMEM((4, rows, w), bf16) for w in widths]
        + [
            pltpu.VMEM((3, 4, rows, widest), bf16),
            pltpu.VMEM((2, 2, half, widest), bf16),
            pltpu.VMEM((2, rows, widest), bf16),
            pltpu.VMEM(gains.shape, jnp.float32),
            pltpu.VMEM((4, *gains.shape[1:]), jnp.float32),
            pltpu.SemaphoreType.DMA((4 * count, 8)),
            pltpu.SemaphoreType.DMA((4 * count, 8)),
            pltpu.SemaphoreType.DMA((3,)),
            pltpu.SemaphoreType.DMA((10,)),
            pltpu.SemaphoreType.DMA((10,)),
        ],
        compiler_params=pltpu.CompilerParams(
            collective_id=2, has_side_effects=True, vmem_limit_bytes=64000000
        ),
        name="scatter_grads",
    )(*views, gains)


def grad_dot(left, right):
    return dot_tt(left, right, ((0,), (0,))).astype(jnp.bfloat16)


def scatter_plain(left, right):
    z = lax.axis_index("tensor")
    spots = jnp.array([0, 1, 3, 2], jnp.int32)
    unit = right.shape[1] // 4
    parts = [
        grad_dot(
            left,
            lax.dynamic_slice_in_dim(right, ((spots[z] - spots[other]) % 4) * unit, unit, 1),
        )
        for other in range(4)
    ]
    return lax.psum_scatter(
        jnp.concatenate(parts, axis=0), ("tensor", "dp"), scatter_dimension=0, tiled=True
    ).astype(jnp.float32)


def to_parcels(values):
    micro, rows, groups, width = values.shape
    return values.transpose(0, 2, 1, 3).reshape(micro * groups, rows, width)


def from_group(values, micro, groups):
    rows = values.shape[0] // (micro * groups)
    width = values.shape[1]
    parts = values.reshape(micro * groups, rows, width)
    moved = lax.all_to_all(parts, "tensor", 0, 0, tiled=True)
    return moved.reshape(micro, groups, rows, width).transpose(0, 2, 1, 3)


def dot_tt(left, right, dims):
    return lax.dot_general(left, right, (dims, ((), ())), preferred_element_type=jnp.float32)


ROWS = 128
PAIR = 2 * HD
NORMAL = ((1,), (0,))
RIGHT_T = ((1,), (1,))
LEFT_T = ((0,), (0,))


def head_masks(scale):
    lane = lax.broadcasted_iota(jnp.int32, (1, PAIR), 1)
    return [jnp.where((lane // HD) == h, scale, 0.0).astype(jnp.bfloat16) for h in range(2)]


def spin(values, cos_table, sin_table, sign):
    lane = lax.broadcasted_iota(jnp.int32, values.shape, 1)
    ahead = pltpu.roll(values, PAIR - HD // 2, 1)
    behind = pltpu.roll(values, HD // 2, 1)
    turned = jnp.where(lane % HD < HD // 2, -ahead, behind)
    return values * cos_table + (sign * turned) * sin_table


def attend_kernel(
    normed_ref, w_ref, wo_ref, cos_ref, sin_ref, bias_ref, joint_ref, mix_ref, log_ref, sum_ref, proj_ref
):
    tokens = normed_ref.shape[0]
    cols = wo_ref.shape[1]
    pairs = cols // PAIR
    proj_ref[...] = dot_tt(normed_ref[...], w_ref[...], NORMAL)
    for c in range(3 * pairs):
        at = slice(c * PAIR, (c + 1) * PAIR)
        part = proj_ref[:, at]
        if c < 2 * pairs:
            part = spin(part, cos_ref[...], sin_ref[...], 1.0)
        joint_ref[:, at] = part.astype(jnp.bfloat16)
    masks = head_masks(HD ** (-0.5))
    lane = lax.broadcasted_iota(jnp.int32, (ROWS, PAIR), 1)
    for pair in range(pairs):
        for i in range(tokens // ROWS):
            rows = slice(i * ROWS, (i + 1) * ROWS)
            size = (i + 1) * ROWS
            q = joint_ref[rows, pair * PAIR : (pair + 1) * PAIR]
            k = joint_ref[:size, cols + pair * PAIR : cols + (pair + 1) * PAIR]
            v = joint_ref[:size, 2 * cols + pair * PAIR : 2 * cols + (pair + 1) * PAIR]
            both = jnp.concatenate([q * masks[0], q * masks[1]], axis=0)
            bias = bias_ref[rows, :size]
            scores = dot_tt(both, k, RIGHT_T) + jnp.concatenate([bias, bias], axis=0)
            top = jnp.max(scores, axis=1, keepdims=True)
            powers = jnp.exp(scores - top)
            norm = jnp.sum(powers, axis=1, keepdims=True)
            probs = (powers * (1.0 / norm)).astype(jnp.bfloat16)
            mixed = dot_tt(probs, v, NORMAL)
            mix_ref[rows, pair * PAIR : (pair + 1) * PAIR] = jnp.where(
                lane < HD, mixed[:ROWS], mixed[ROWS:]
            ).astype(jnp.bfloat16)
            log_norm = top + jnp.log(norm)
            log_ref[0, rows, 2 * pair : 2 * pair + 1] = log_norm[:ROWS]
            log_ref[0, rows, 2 * pair + 1 : 2 * pair + 2] = log_norm[ROWS:]
    projected = dot_tt(mix_ref[...], wo_ref[...], RIGHT_T)

    @pl.when(pl.program_id(0) == 0)
    def _():
        sum_ref[...] = projected

    @pl.when(pl.program_id(0) > 0)
    def _():
        sum_ref[...] += projected


def attend(normed, w_qkv, wo, cos_wide, sin_wide, bias):
    tokens, width = normed.shape
    blocks = 4
    cols = wo.shape[1] // blocks
    fixed = lambda k: (0, 0)
    moving = lambda k: (0, k)
    return pl.pallas_call(
        attend_kernel,
        grid=(blocks,),
        out_shape=[
            jax.ShapeDtypeStruct((tokens, 3 * blocks * cols), jnp.bfloat16),
            jax.ShapeDtypeStruct((tokens, blocks * cols), jnp.bfloat16),
            jax.ShapeDtypeStruct((blocks, tokens, 8), jnp.float32),
            jax.ShapeDtypeStruct((tokens, width), jnp.float32),
        ],
        in_specs=[
            pl.BlockSpec((tokens, width), fixed),
            pl.BlockSpec((width, 3 * cols), moving),
            pl.BlockSpec((width, cols), moving),
            pl.BlockSpec((tokens, PAIR), fixed),
            pl.BlockSpec((tokens, PAIR), fixed),
            pl.BlockSpec((tokens, tokens), fixed),
        ],
        out_specs=[
            pl.BlockSpec((tokens, 3 * cols), moving),
            pl.BlockSpec((tokens, cols), moving),
            pl.BlockSpec((1, tokens, 8), lambda k: (k, 0, 0)),
            pl.BlockSpec((tokens, width), fixed),
        ],
        scratch_shapes=[pltpu.VMEM((tokens, 3 * cols), jnp.float32)],
        compiler_params=pltpu.CompilerParams(vmem_limit_bytes=60000000),
        name="attend",
    )(normed, w_qkv, wo, cos_wide, sin_wide, bias)


def attend_back_kernel(
    grad_ref,
    w_ref,
    wo_ref,
    joint_ref,
    log_ref,
    cos_ref,
    sin_ref,
    bias_ref,
    out_ref,
    sum_ref,
    mix_grad,
    q_grad,
    k_grad,
    v_grad,
):
    tokens = grad_ref.shape[0]
    cols = wo_ref.shape[1]
    pairs = cols // PAIR
    mix_grad[...] = dot_tt(grad_ref[...], wo_ref[...], NORMAL).astype(jnp.bfloat16)
    scale = HD ** (-0.5)
    masks = head_masks(scale)
    ones = head_masks(1.0)
    lane = lax.broadcasted_iota(jnp.int32, (ROWS, PAIR), 1)
    last = tokens // ROWS - 1
    for pair in range(pairs):
        for i in range(last, -1, -1):
            rows = slice(i * ROWS, (i + 1) * ROWS)
            size = (i + 1) * ROWS
            q = joint_ref[rows, pair * PAIR : (pair + 1) * PAIR]
            k = joint_ref[:size, cols + pair * PAIR : cols + (pair + 1) * PAIR]
            v = joint_ref[:size, 2 * cols + pair * PAIR : 2 * cols + (pair + 1) * PAIR]
            g = mix_grad[rows, pair * PAIR : (pair + 1) * PAIR]
            q_both = jnp.concatenate([q * masks[0], q * masks[1]], axis=0)
            g_both = jnp.concatenate([g * ones[0], g * ones[1]], axis=0)
            bias = bias_ref[:size, rows]
            logs = jnp.concatenate(
                [log_ref[0, 2 * pair : 2 * pair + 1, rows], log_ref[0, 2 * pair + 1 : 2 * pair + 2, rows]],
                axis=1,
            )
            scores = dot_tt(k, q_both, RIGHT_T) + jnp.concatenate([bias, bias], axis=1)
            probs = jnp.exp(scores - logs)
            prob_grad = dot_tt(v, g_both, RIGHT_T)
            centre = jnp.sum(probs * prob_grad, axis=0, keepdims=True)
            score_grad = (probs * (prob_grad - centre)).astype(jnp.bfloat16)
            k_part = dot_tt(score_grad, q_both, NORMAL)
            v_part = dot_tt(probs.astype(jnp.bfloat16), g_both, NORMAL)
            if i == last:
                k_grad[...] = k_part
                v_grad[...] = v_part
            else:
                k_grad[:size, :] += k_part
                v_grad[:size, :] += v_part
            q_part = dot_tt(score_grad, k, LEFT_T)
            q_grad[rows, :] = jnp.where(lane < HD, q_part[:ROWS], q_part[ROWS:]) * scale
        cos_table = cos_ref[...]
        sin_table = sin_ref[...]
        out_ref[:, pair * PAIR : (pair + 1) * PAIR] = spin(
            q_grad[...], cos_table, sin_table, -1.0
        ).astype(jnp.bfloat16)
        out_ref[:, cols + pair * PAIR : cols + (pair + 1) * PAIR] = spin(
            k_grad[...], cos_table, sin_table, -1.0
        ).astype(jnp.bfloat16)
        out_ref[:, 2 * cols + pair * PAIR : 2 * cols + (pair + 1) * PAIR] = v_grad[...].astype(
            jnp.bfloat16
        )
    projected = dot_tt(out_ref[...], w_ref[...], RIGHT_T)

    @pl.when(pl.program_id(0) == 0)
    def _():
        sum_ref[...] = projected

    @pl.when(pl.program_id(0) > 0)
    def _():
        sum_ref[...] += projected


def attend_back(grad, w_qkv, wo, joint, logs, cos_wide, sin_wide, bias_t):
    tokens, width = grad.shape
    blocks = 4
    cols = wo.shape[1] // blocks
    fixed = lambda k: (0, 0)
    moving = lambda k: (0, k)
    return pl.pallas_call(
        attend_back_kernel,
        grid=(blocks,),
        out_shape=[
            jax.ShapeDtypeStruct((tokens, 3 * blocks * cols), jnp.bfloat16),
            jax.ShapeDtypeStruct((tokens, width), jnp.float32),
        ],
        in_specs=[
            pl.BlockSpec((tokens, width), fixed),
            pl.BlockSpec((width, 3 * cols), moving),
            pl.BlockSpec((width, cols), moving),
            pl.BlockSpec((tokens, 3 * cols), moving),
            pl.BlockSpec((1, 8, tokens), lambda k: (k, 0, 0)),
            pl.BlockSpec((tokens, PAIR), fixed),
            pl.BlockSpec((tokens, PAIR), fixed),
            pl.BlockSpec((tokens, tokens), fixed),
        ],
        out_specs=[
            pl.BlockSpec((tokens, 3 * cols), moving),
            pl.BlockSpec((tokens, width), fixed),
        ],
        scratch_shapes=[
            pltpu.VMEM((tokens, cols), jnp.bfloat16),
            pltpu.VMEM((tokens, PAIR), jnp.float32),
            pltpu.VMEM((tokens, PAIR), jnp.float32),
            pltpu.VMEM((tokens, PAIR), jnp.float32),
        ],
        compiler_params=pltpu.CompilerParams(vmem_limit_bytes=60000000),
        name="attend_back",
    )(grad, w_qkv, wo, joint, logs, cos_wide, sin_wide, bias_t)


def order_matrix(width):
    rows = width // 8
    d = lax.axis_index("dp")
    owner = jnp.concatenate([jnp.full((rows,), mask, jnp.int32) for mask in RELATIVE])
    feature = (d ^ owner) * rows + jnp.arange(width, dtype=jnp.int32) % rows
    return (jnp.arange(width, dtype=jnp.int32)[:, None] == feature[None, :]).astype(jnp.bfloat16)


def group_body(
    block_input,
    lengths,
    out_grad,
    w_query,
    w_key,
    w_value,
    w_out,
    w_gate,
    w_up,
    w_down,
    attn_gain,
    ffn_gain,
):
    micro, _, groups, width = block_input.shape
    unit_cols = w_query.shape[1]
    bf16 = jnp.bfloat16
    f32 = jnp.float32
    contract = ((1,), (0,))
    contract_t = ((1,), (1,))
    own_lengths = lax.dynamic_slice_in_dim(
        lengths.reshape(micro * groups, 3), lax.axis_index("tensor"), 1, 0
    )
    rows = attn_gain.shape[0]
    gain_tile = jnp.zeros((8, 256), f32).at[0, :rows].set(attn_gain).at[1, :rows].set(ffn_gain)
    w_qkv, wo, wg, wu, wd, x_box, dy_box, gain_box = gather_weights(
        (jnp.concatenate([w_query, w_key, w_value], axis=1), w_out.T, w_gate, w_up, w_down.T),
        (to_parcels(block_input), to_parcels(out_grad)),
        gain_tile,
        ((0, 1), (2, 3), (4,)),
    )
    gains = gain_box[:, :2, :rows].transpose(1, 0, 2).reshape(2, width)
    order = order_matrix(width)
    tokens_in = dot_tt(x_box.reshape(GTOK, width), order, contract)
    upstream_plain = dy_box.reshape(GTOK, width)
    upstream = dot_tt(upstream_plain, order, contract).astype(bf16)
    gain_one = gains[0]
    gain_two = gains[1]

    segment, cos_table, sin_table = layout_tables(own_lengths)
    seg = segment[:, 0]
    cos_wide = jnp.tile(cos_table[:, 0], (1, 4))
    sin_wide = jnp.tile(sin_table[:, 0], (1, 4))
    index = jnp.arange(GTOK, dtype=jnp.int32)
    allowed = (index[None, :] <= index[:, None]) & (
        (seg[None, :] == 0) | (seg[None, :] == seg[:, None])
    )
    bias = jnp.where(allowed, 0.0, MASKED).astype(f32)
    residual = tokens_in
    scale_one = rms_scale(residual)
    unit_one = residual * scale_one
    normed_one = (unit_one * gain_one).astype(bf16)
    joint, mix, logs, attn_sum = attend(normed_one, w_qkv, wo, cos_wide, sin_wide, bias)
    middle = residual + attn_sum
    scale_two = rms_scale(middle)
    unit_two = middle * scale_two
    normed_two = (unit_two * gain_two).astype(bf16)
    gate_vals = dot_tt(normed_two, wg, contract)
    up_vals = dot_tt(normed_two, wu, contract)
    sigmoid_gate = jax.nn.sigmoid(gate_vals)
    silu_gate = gate_vals * sigmoid_gate
    hidden = (silu_gate * up_vals).astype(bf16)
    output = (middle + dot_tt(hidden, wd, contract_t)).astype(bf16)
    out_final = from_group(dot_tt(output, order, contract_t).astype(bf16), micro, groups)

    share_down = scatter_plain(upstream_plain, hidden)
    hidden_grad = dot_tt(upstream, wd, contract)
    up_grad = (hidden_grad * silu_gate).astype(bf16)
    gate_grad = (
        hidden_grad * up_vals * (sigmoid_gate * (1.0 + gate_vals * (1.0 - sigmoid_gate)))
    ).astype(bf16)
    normed_two_grad = dot_tt(gate_grad, wg, contract_t) + dot_tt(up_grad, wu, contract_t)
    gain_two_grad = jnp.sum(normed_two_grad * unit_two, axis=0)
    middle_grad = upstream.astype(f32) + norm_back(
        normed_two_grad, unit_two, gain_two, scale_two
    )
    attn_grad = middle_grad.astype(bf16)
    joint_grad, normed_one_grad = attend_back(
        attn_grad, w_qkv, wo, joint, logs.transpose(0, 2, 1), cos_wide, sin_wide, bias.T
    )
    gain_one_grad = jnp.sum(normed_one_grad * unit_one, axis=0)
    input_grad = (
        middle_grad + norm_back(normed_one_grad, unit_one, gain_one, scale_one)
    ).astype(bf16)
    in_grad_final = from_group(dot_tt(input_grad, order, contract_t).astype(bf16), micro, groups)
    gain_parts = jnp.stack([gain_one_grad, gain_two_grad]).reshape(2, 8, rows).transpose(1, 0, 2)
    gain_parts = jnp.pad(gain_parts, ((0, 0), (0, 6), (0, 256 - rows)))
    share_gate, share_up, share_out, share_joint, own_gains = scatter_grads(
        (
            grad_dot(normed_two, gate_grad),
            grad_dot(normed_two, up_grad),
            grad_dot(attn_grad, mix),
            grad_dot(normed_one, joint_grad),
        ),
        gain_parts,
    )
    return (
        out_final,
        in_grad_final,
        share_joint[:, :unit_cols],
        share_joint[:, unit_cols : 2 * unit_cols],
        share_joint[:, 2 * unit_cols :],
        share_out.T,
        share_gate,
        share_up,
        share_down.T,
        own_gains[0, :rows],
        own_gains[1, :rows],
    )


def body(*operands):
    micro, _, groups, _ = operands[0].shape
    if lax.axis_size("dp") == 8 and micro * groups == lax.axis_size("tensor") == 4:
        return group_body(*operands)
    return sharded_body(*operands)


def solution(mesh):
    placed = (
        P(None, "tensor", "dp", None),
        P(None, "dp", None),
        P(None, "tensor", "dp", None),
        P("dp", "tensor"),
        P("dp", "tensor"),
        P("dp", "tensor"),
        P("tensor", "dp"),
        P("dp", "tensor"),
        P("dp", "tensor"),
        P("tensor", "dp"),
        P("dp"),
        P("dp"),
    )
    return jax.shard_map(
        body,
        mesh=mesh,
        in_specs=placed,
        out_specs=(
            P(None, "tensor", "dp", None),
            P(None, "tensor", "dp", None),
            P("dp", "tensor"),
            P("dp", "tensor"),
            P("dp", "tensor"),
            P("tensor", "dp"),
            P("dp", "tensor"),
            P("dp", "tensor"),
            P("tensor", "dp"),
            P("dp"),
            P("dp"),
        ),
        check_vma=False,
    )
```

```python
import functools
import math

import jax
import jax.numpy as jnp
from jax import lax
from jax.experimental import pallas as pl
from jax.experimental.pallas import tpu as pltpu
from jax.sharding import PartitionSpec as P


HD = 64
GTOK = 512


EPSILON = 1e-05
MASKED = -1e30


def layout_tables(group_lengths):
    slot_index = jnp.arange(GTOK, dtype=jnp.int32)[:, None]
    prompt_len = group_lengths[:, 0][None, :]
    first_len = group_lengths[:, 1][None, :]
    segment = jnp.where(
        slot_index < prompt_len, 0, jnp.where(slot_index < prompt_len + first_len, 1, 2)
    ).astype(jnp.int32)
    position = jnp.where(segment == 2, slot_index - first_len, slot_index)
    frequency = jnp.exp(jnp.arange(HD // 2, dtype=jnp.float32) * (-2.0 * math.log(10000.0) / HD))
    angles = position.astype(jnp.float32)[:, :, None] * frequency
    return (segment, jnp.cos(angles), jnp.sin(angles))


def rotate(values, cos_table, sin_table):
    half_size = values.shape[-1] // 2
    first_half = values[..., :half_size]
    second_half = values[..., half_size:]
    cos_wide = cos_table[:, :, None, :]
    sin_wide = sin_table[:, :, None, :]
    return jnp.concatenate(
        [
            first_half * cos_wide - second_half * sin_wide,
            second_half * cos_wide + first_half * sin_wide,
        ],
        axis=-1,
    )


def rotate_back(values, cos_table, sin_table):
    half_size = values.shape[-1] // 2
    first_half = values[..., :half_size]
    second_half = values[..., half_size:]
    cos_wide = cos_table[:, :, None, :]
    sin_wide = sin_table[:, :, None, :]
    return jnp.concatenate(
        [
            first_half * cos_wide + second_half * sin_wide,
            second_half * cos_wide - first_half * sin_wide,
        ],
        axis=-1,
    )


def rms_scale(values):
    return lax.rsqrt(jnp.mean(values * values, axis=-1, keepdims=True) + EPSILON)


def norm_back(upstream, unit_rows, gain_row, scale_rows):
    scaled = upstream * gain_row
    return scale_rows * (scaled - unit_rows * jnp.mean(scaled * unit_rows, axis=-1, keepdims=True))


def attention_scores(queries, key_rows, allowed):
    scores = jnp.einsum(
        "tghe,sghe->ghts", queries, key_rows, preferred_element_type=jnp.float32
    ) * HD ** (-0.5)
    return jnp.where(allowed[:, None], scores, MASKED)


def add_tuples(first_set, second_set):
    return tuple((earlier + later for earlier, later in zip(first_set, second_set)))


def micro_step(inputs, group_lengths, upstream, gathered):
    w_query, w_key, w_value, w_out, w_gate, w_up, w_down, attn_gain, ffn_gain = gathered
    gain_one = attn_gain.astype(jnp.float32)
    gain_two = ffn_gain.astype(jnp.float32)
    group_count = inputs.shape[1]
    head_cols = w_query.shape[1]
    hidden_cols = w_gate.shape[1]
    shape_heads = (GTOK, group_count, head_cols // HD, HD)
    segment, cos_table, sin_table = layout_tables(group_lengths)
    token_index = jnp.arange(GTOK, dtype=jnp.int32)
    seg_groups = segment.T
    allowed = (token_index[None, None, :] <= token_index[None, :, None]) & (
        (seg_groups[:, None, :] == 0) | (seg_groups[:, None, :] == seg_groups[:, :, None])
    )
    residual = inputs.astype(jnp.float32)
    scale_one = rms_scale(residual)
    unit_one = residual * scale_one
    normed_one = (unit_one * gain_one).astype(jnp.bfloat16)
    normed_all = lax.all_gather(normed_one, "tensor", axis=0, tiled=True)
    w_joint = jnp.concatenate([w_query, w_key, w_value], axis=1)
    projected = jnp.einsum("tgd,dc->tgc", normed_all, w_joint, preferred_element_type=jnp.float32)
    queries = rotate(projected[..., :head_cols].reshape(shape_heads), cos_table, sin_table).astype(
        jnp.bfloat16
    )
    key_rows = rotate(
        projected[..., head_cols : 2 * head_cols].reshape(shape_heads), cos_table, sin_table
    ).astype(jnp.bfloat16)
    value_rows = projected[..., 2 * head_cols :].reshape(shape_heads).astype(jnp.bfloat16)
    scores = attention_scores(queries, key_rows, allowed)
    row_max = jnp.max(scores, axis=-1, keepdims=True)
    log_total = row_max + jnp.log(jnp.sum(jnp.exp(scores - row_max), axis=-1, keepdims=True))
    attn_probs = jnp.exp(scores - log_total).astype(jnp.bfloat16)
    attn_mix = (
        jnp.einsum("ghts,sghe->tghe", attn_probs, value_rows, preferred_element_type=jnp.float32)
        .astype(jnp.bfloat16)
        .reshape(GTOK, group_count, head_cols)
    )
    rows_here = attn_mix
    attn_sum = lax.psum_scatter(
        jnp.einsum("tgc,cd->tgd", rows_here, w_out, preferred_element_type=jnp.float32),
        "tensor",
        scatter_dimension=0,
        tiled=True,
    )
    middle = residual + attn_sum
    scale_two = rms_scale(middle)
    unit_two = middle * scale_two
    normed_two = (unit_two * gain_two).astype(jnp.bfloat16)
    normed_more = lax.all_gather(normed_two, "tensor", axis=0, tiled=True)
    w_gate_up = jnp.concatenate([w_gate, w_up], axis=1)
    gate_up = jnp.einsum("tgd,df->tgf", normed_more, w_gate_up, preferred_element_type=jnp.float32)
    gate_vals = gate_up[..., :hidden_cols]
    up_vals = gate_up[..., hidden_cols:]
    sigmoid_gate = jax.nn.sigmoid(gate_vals)
    silu_gate = gate_vals * sigmoid_gate
    hidden = (silu_gate * up_vals).astype(jnp.bfloat16)
    rows_here = hidden
    ffn_sum = lax.psum_scatter(
        jnp.einsum("tgf,fd->tgd", rows_here, w_down, preferred_element_type=jnp.float32).astype(
            jnp.bfloat16
        ),
        "tensor",
        scatter_dimension=0,
        tiled=True,
    ).astype(jnp.float32)
    output = (middle + ffn_sum).astype(jnp.bfloat16)
    upstream_all = lax.all_gather(upstream, "tensor", axis=0, tiled=True)
    hidden_grad = jnp.einsum(
        "tgd,fd->tgf", upstream_all, w_down, preferred_element_type=jnp.float32
    )
    grad_down = jnp.einsum("tgf,tgd->fd", hidden, upstream_all, preferred_element_type=jnp.float32)
    up_grad = hidden_grad * silu_gate
    gate_grad = hidden_grad * up_vals * (sigmoid_gate * (1.0 + gate_vals * (1.0 - sigmoid_gate)))
    gate_up_grad = jnp.concatenate([gate_grad, up_grad], axis=-1).astype(jnp.bfloat16)
    grad_gate_up = jnp.einsum(
        "tgd,tgf->df", normed_more, gate_up_grad, preferred_element_type=jnp.float32
    )
    rows_here = gate_up_grad
    normed_two_grad = lax.psum_scatter(
        jnp.einsum("tgf,df->tgd", rows_here, w_gate_up, preferred_element_type=jnp.float32).astype(
            jnp.bfloat16
        ),
        "tensor",
        scatter_dimension=0,
        tiled=True,
    ).astype(jnp.float32)
    gain_two_grad = jnp.sum(normed_two_grad * unit_two, axis=(0, 1))
    middle_grad = upstream.astype(jnp.float32) + norm_back(
        normed_two_grad, unit_two, gain_two, scale_two
    )
    attn_grad = middle_grad.astype(jnp.bfloat16)
    attn_grad_all = lax.all_gather(attn_grad, "tensor", axis=0, tiled=True)
    mix_grad = (
        jnp.einsum("tgd,cd->tgc", attn_grad_all, w_out, preferred_element_type=jnp.float32)
        .astype(jnp.bfloat16)
        .reshape(shape_heads)
    )
    grad_out = jnp.einsum(
        "tgc,tgd->cd", attn_mix, attn_grad_all, preferred_element_type=jnp.float32
    )
    scores_again = attention_scores(queries, key_rows, allowed)
    probs_full = jnp.exp(scores_again - log_total)
    prob_grad = jnp.einsum(
        "tghe,sghe->ghts", mix_grad, value_rows, preferred_element_type=jnp.float32
    )
    value_grad = jnp.einsum(
        "ghts,tghe->sghe",
        probs_full.astype(jnp.bfloat16),
        mix_grad,
        preferred_element_type=jnp.float32,
    )
    centre = jnp.sum(probs_full * prob_grad, axis=-1, keepdims=True)
    score_grad = (probs_full * (prob_grad - centre)).astype(jnp.bfloat16)
    query_grad = jnp.einsum(
        "ghts,sghe->tghe", score_grad, key_rows, preferred_element_type=jnp.float32
    ) * HD ** (-0.5)
    key_grad = jnp.einsum(
        "ghts,tghe->sghe", score_grad, queries, preferred_element_type=jnp.float32
    ) * HD ** (-0.5)
    flat_shape = (GTOK, group_count, head_cols)
    joint_grad = jnp.concatenate(
        [
            rotate_back(query_grad, cos_table, sin_table).reshape(flat_shape),
            rotate_back(key_grad, cos_table, sin_table).reshape(flat_shape),
            value_grad.reshape(flat_shape),
        ],
        axis=-1,
    ).astype(jnp.bfloat16)
    grad_joint = jnp.einsum(
        "tgd,tgc->dc", normed_all, joint_grad, preferred_element_type=jnp.float32
    )
    rows_here = joint_grad
    normed_one_grad = lax.psum_scatter(
        jnp.einsum("tgc,dc->tgd", rows_here, w_joint, preferred_element_type=jnp.float32).astype(
            jnp.bfloat16
        ),
        "tensor",
        scatter_dimension=0,
        tiled=True,
    ).astype(jnp.float32)
    gain_one_grad = jnp.sum(normed_one_grad * unit_one, axis=(0, 1))
    input_grad = (middle_grad + norm_back(normed_one_grad, unit_one, gain_one, scale_one)).astype(
        jnp.bfloat16
    )
    param_grads = (
        grad_joint[:, :head_cols],
        grad_joint[:, head_cols : 2 * head_cols],
        grad_joint[:, 2 * head_cols :],
        grad_out,
        grad_gate_up[:, :hidden_cols],
        grad_gate_up[:, hidden_cols:],
        grad_down,
        gain_one_grad,
        gain_two_grad,
    )
    return (output, input_grad, param_grads)


def sharded_body(
    block_input,
    lengths,
    out_grad,
    w_query,
    w_key,
    w_value,
    w_out,
    w_gate,
    w_up,
    w_down,
    attn_gain,
    ffn_gain,
):
    outputs = []
    input_grads = []
    totals = None
    shares = None
    for micro_index in range(block_input.shape[0]):
        gathered = (
            lax.all_gather(w_query, "dp", axis=0, tiled=True),
            lax.all_gather(w_key, "dp", axis=0, tiled=True),
            lax.all_gather(w_value, "dp", axis=0, tiled=True),
            lax.all_gather(w_out, "dp", axis=1, tiled=True),
            lax.all_gather(w_gate, "dp", axis=0, tiled=True),
            lax.all_gather(w_up, "dp", axis=0, tiled=True),
            lax.all_gather(w_down, "dp", axis=1, tiled=True),
            lax.all_gather(attn_gain, "dp", axis=0, tiled=True),
            lax.all_gather(ffn_gain, "dp", axis=0, tiled=True),
        )
        output, input_grad, param_grads = micro_step(
            block_input[micro_index], lengths[micro_index], out_grad[micro_index], gathered
        )
        outputs.append(output)
        input_grads.append(input_grad)
        totals = param_grads if totals is None else add_tuples(totals, param_grads)
    shares = (
        lax.psum_scatter(
            totals[0].astype(jnp.bfloat16), "dp", scatter_dimension=0, tiled=True
        ).astype(jnp.float32),
        lax.psum_scatter(
            totals[1].astype(jnp.bfloat16), "dp", scatter_dimension=0, tiled=True
        ).astype(jnp.float32),
        lax.psum_scatter(
            totals[2].astype(jnp.bfloat16), "dp", scatter_dimension=0, tiled=True
        ).astype(jnp.float32),
        lax.psum_scatter(
            totals[3].astype(jnp.bfloat16), "dp", scatter_dimension=1, tiled=True
        ).astype(jnp.float32),
        lax.psum_scatter(
            totals[4].astype(jnp.bfloat16), "dp", scatter_dimension=0, tiled=True
        ).astype(jnp.float32),
        lax.psum_scatter(
            totals[5].astype(jnp.bfloat16), "dp", scatter_dimension=0, tiled=True
        ).astype(jnp.float32),
        lax.psum_scatter(
            totals[6].astype(jnp.bfloat16), "dp", scatter_dimension=1, tiled=True
        ).astype(jnp.float32),
        lax.psum_scatter(
            totals[7].astype(jnp.bfloat16), "dp", scatter_dimension=0, tiled=True
        ).astype(jnp.float32),
        lax.psum_scatter(
            totals[8].astype(jnp.bfloat16), "dp", scatter_dimension=0, tiled=True
        ).astype(jnp.float32),
    )
    gain_one_total, gain_two_total = lax.psum((shares[7], shares[8]), "tensor")
    return (
        jnp.stack(outputs),
        jnp.stack(input_grads),
        shares[0],
        shares[1],
        shares[2],
        shares[3],
        shares[4],
        shares[5],
        shares[6],
        gain_one_total,
        gain_two_total,
    )


MESH = pl.DeviceIdType.MESH
RELATIVE = [4 * ((j // 2) % 2) + 2 * (j % 2) + j // 4 for j in range(8)]


def flip_core(d):
    return d + 1 - 2 * (d % 2)


def flip_x(d):
    return d + 2 - 4 * ((d // 2) % 2)


def flip_y(d):
    return d + 4 - 8 * ((d // 4) % 2)


def flip(d, mask):
    if mask & 1:
        d = flip_core(d)
    if mask & 2:
        d = flip_x(d)
    if mask & 4:
        d = flip_y(d)
    return d


def ring_next(z):
    return (2 * z + 1) % 5


def remote(src, dst, send_sem, recv_sem, peer):
    return pltpu.make_async_remote_copy(
        src_ref=src,
        dst_ref=dst,
        send_sem=send_sem,
        recv_sem=recv_sem,
        device_id=peer,
        device_id_type=MESH,
    )


def greet(d, z):
    barrier = pltpu.get_barrier_semaphore()
    for mask in range(1, 8):
        pl.semaphore_signal(barrier, inc=1, device_id=(flip(d, mask), z), device_id_type=MESH)
    for step in (1, 2, 3):
        pl.semaphore_signal(barrier, inc=1, device_id=(d, (z + step) % 4), device_id_type=MESH)
    pl.semaphore_wait(barrier, 10)


def gather_kernel(sets, count, *refs):
    shards = refs[:count]
    parcels = refs[count : count + 2]
    gains = refs[count + 2]
    fulls = refs[count + 3 : 2 * count + 3]
    boxes = refs[2 * count + 3 : 2 * count + 5]
    gain_box = refs[2 * count + 5]
    send_sem, recv_sem, box_send, box_recv, gain_send, gain_recv, local_sem = refs[2 * count + 6 :]
    d = lax.axis_index("dp")
    z = lax.axis_index("tensor")
    place = {
        "z": (d, ring_next(z)),
        "x": (flip_x(d), z),
        "y": (flip_y(d), z),
        "c": (flip_core(d), z),
    }
    others = [(z + step) % 4 for step in (1, 2, 3)]
    greet(d, z)
    rows = shards[0].shape[0]

    def region(a, k, j, half):
        width = shards[a].shape[1]
        top, size = (j * rows, rows) if half is None else (j * rows + half * (rows // 2), rows // 2)
        return fulls[a].at[pl.ds(top, size), pl.ds(k * width, width)]

    sends = []

    def start(s, way, slot, src, dst, half=None):
        for a in sets[s]:
            source = shards[a] if src == (0, 0) else region(a, *src, half)
            remote(
                source,
                region(a, *dst, half),
                send_sem.at[s, slot],
                recv_sem.at[s, slot],
                place[way],
            ).start()
        sends.append((s, slot, half))

    def bulk(s, slot, half):
        arrs = sets[s]
        size = rows if half is None else rows // 2
        width = sum(shards[a].shape[1] for a in arrs)
        part = fulls[arrs[0]].at[pl.ds(0, size), pl.ds(0, width)]
        return remote(part, part, send_sem.at[s, slot], recv_sem.at[s, slot], place["c"])

    def arrived(s, slot, half=None):
        bulk(s, slot, half).wait_recv()

    ring_slot, x_slot, y_slot, x_relay, y_relay, core_slot = 0, 3, 7, 11, 15, 19

    def core(s, k, j):
        start(s, "c", core_slot + 4 * k + j, (k, j), (k, 4 + j))

    def ring_step(s, k):
        start(s, "z", ring_slot + k, (k, 0), (k + 1, 0))

    def open_unit(s, k):
        if k > 0:
            arrived(s, ring_slot + k - 1)
            if k < 3:
                ring_step(s, k)
        start(s, "x", x_slot + k, (k, 0), (k, 1))
        start(s, "y", y_slot + k, (k, 0), (k, 2))
        core(s, k, 0)

    def close_unit(s, k):
        arrived(s, x_slot + k)
        start(s, "y", y_relay + k, (k, 1), (k, 3), 1)
        core(s, k, 1)
        arrived(s, y_slot + k)
        start(s, "x", x_relay + k, (k, 2), (k, 3), 0)
        core(s, k, 2)

    def last_part(s, k):
        arrived(s, x_relay + k, 0)
        arrived(s, y_relay + k, 1)
        core(s, k, 3)

    def own_copies():
        for a in range(count):
            yield pltpu.make_async_copy(shards[a], region(a, 0, 0, None), local_sem.at[a])
        for p in range(2):
            yield pltpu.make_async_copy(
                parcels[p].at[z], boxes[p].at[z], local_sem.at[count + p]
            )
        yield pltpu.make_async_copy(gains, gain_box.at[0], local_sem.at[count + 2])

    def box_copy(p, step):
        return remote(
            parcels[p].at[others[step]],
            boxes[p].at[z],
            box_send.at[p, step],
            box_recv.at[p, step],
            (d, others[step]),
        )

    def gain_copy(j):
        return remote(
            gains,
            gain_box.at[j],
            gain_send.at[j - 1],
            gain_recv.at[j - 1],
            (flip(d, RELATIVE[j]), z),
        )

    for j in range(1, 8):
        gain_copy(j).start()
    for copy in own_copies():
        copy.start()
    units = [(s, k) for s in range(len(sets)) for k in range(4)]
    ring_step(0, 0)
    open_unit(*units[0])
    for i, unit in enumerate(units):
        if i + 1 < len(units):
            after = units[i + 1]
            if after[1] == 0:
                ring_step(after[0], 0)
            open_unit(*after)
        if i < 6:
            box_copy(i // 3, i % 3).start()
        close_unit(*unit)
        if i > 0:
            last_part(*units[i - 1])
    last_part(*units[-1])
    for s in range(len(sets)):
        for slot in range(core_slot, core_slot + 16):
            arrived(s, slot)
    for p in range(2):
        for step in range(3):
            box_copy(p, step).wait()
    for j in range(1, 8):
        gain_copy(j).wait()
    for s, slot, half in sends:
        bulk(s, slot, half).wait_send()
    for copy in own_copies():
        copy.wait()


def gather_weights(shards, parcels, gains, sets):
    count = len(shards)
    vmem = pl.BlockSpec(memory_space=pltpu.VMEM)
    anywhere = pl.BlockSpec(memory_space=pl.ANY)
    dma = pltpu.SemaphoreType.DMA
    return pl.pallas_call(
        functools.partial(gather_kernel, sets, count),
        out_shape=[
            jax.ShapeDtypeStruct((8 * w.shape[0], 4 * w.shape[1]), w.dtype) for w in shards
        ]
        + [jax.ShapeDtypeStruct(p.shape, p.dtype) for p in parcels]
        + [jax.ShapeDtypeStruct((8, *gains.shape), gains.dtype)],
        in_specs=[vmem] * (count + 3),
        out_specs=[anywhere] * (count + 3),
        scratch_shapes=[
            dma((len(sets), 35)),
            dma((len(sets), 35)),
            dma((2, 3)),
            dma((2, 3)),
            dma((7,)),
            dma((7,)),
            dma((count + 3,)),
        ],
        compiler_params=pltpu.CompilerParams(collective_id=1, has_side_effects=True),
        name="gather_weights",
    )(*shards, *parcels, gains)


def add_rows(target, first, second, chunk=32):
    rows = target.shape[0]

    def step(i, carry):
        at = pl.ds(pl.multiple_of(i * chunk, chunk), chunk)
        target[at, :] = (
            first[at, :].astype(jnp.float32) + second[at, :].astype(jnp.float32)
        ).astype(target.dtype)
        return carry

    lax.fori_loop(0, rows // chunk, step, 0)


def scatter_kernel(count, *refs):
    grads = refs[:count]
    gains, *parcels = refs[count : count + 3]
    shares = refs[count + 3 : 2 * count + 3]
    gain_share, *boxes = refs[2 * count + 3 : 2 * count + 6]
    rest = refs[2 * count + 6 :]
    from_core, from_first, from_second, from_ring = (
        rest[i * count : (i + 1) * count] for i in range(4)
    )
    total, middle, final, gain_box, gain_line = rest[4 * count : 4 * count + 5]
    send_sem, recv_sem, load_sem, gain_send, gain_recv = rest[4 * count + 5 : 4 * count + 10]
    box_send, box_recv, box_own = rest[4 * count + 10 :]
    d = lax.axis_index("dp")
    z = lax.axis_index("tensor")
    core, east, north = (flip_core(d), z), (flip_x(d), z), (flip_y(d), z)
    onward = (d, ring_next(z))
    greet(d, z)
    rows = grads[0].shape[1]
    half = rows // 2
    units = [(g, k) for g in range(count) for k in (1, 2, 3, 0)]
    width = [grads[g].shape[2] // 4 for g in range(count)]

    def send(src, dst, u, slot, peer):
        return remote(src, dst, send_sem.at[u, slot], recv_sem.at[u, slot], peer)

    def gain_copy(j):
        return remote(
            gains.at[j],
            gain_box.at[j],
            gain_send.at[j - 1],
            gain_recv.at[j - 1],
            (flip(d, RELATIVE[j]), z),
        )

    def box_copy(p, step):
        other = (z + step) % 4
        return remote(
            parcels[p].at[other],
            boxes[p].at[z],
            box_send.at[p, step - 1],
            box_recv.at[p, step - 1],
            (d, other),
        )

    def own_copy(p):
        return pltpu.make_async_copy(parcels[p].at[z], boxes[p].at[z], box_own.at[p])

    def line_copy(step):
        return remote(
            gain_line.at[z],
            gain_line.at[z],
            gain_send.at[6 + step],
            gain_recv.at[6 + step],
            (d, (z + step) % 4),
        )

    def columns(u):
        g, k = units[u]
        return pl.ds(k * width[g], width[g])

    def to_core(u):
        g, k = units[u]
        return send(
            grads[g].at[pl.ds(4, 4), :, columns(u)], from_core[g].at[k], u, 0, core
        )

    def load(u):
        g, _ = units[u]
        return pltpu.make_async_copy(
            grads[g].at[pl.ds(0, 4), :, columns(u)],
            total.at[u % 3, :, :, pl.ds(0, width[g])],
            load_sem.at[u % 3],
        )

    def first_sends(u):
        g, k = units[u]
        t = total.at[u % 3]
        cols = pl.ds(0, width[g])
        return [
            send(t.at[1, pl.ds(0, half), cols], from_first[g].at[k, 0, 0], u, 1, east),
            send(t.at[3, pl.ds(0, half), cols], from_first[g].at[k, 0, 1], u, 2, east),
            send(t.at[2, pl.ds(half, half), cols], from_first[g].at[k, 1, 0], u, 3, north),
            send(t.at[3, pl.ds(half, half), cols], from_first[g].at[k, 1, 1], u, 4, north),
        ]

    def second_sends(u):
        g, k = units[u]
        m = middle.at[u % 2]
        cols = pl.ds(0, width[g])
        return [
            send(m.at[0, :, cols], from_second[g].at[k, 0], u, 5, north),
            send(m.at[1, :, cols], from_second[g].at[k, 1], u, 6, east),
        ]

    def ring_send(u):
        g, k = units[u]
        return send(
            final.at[u % 2, :, pl.ds(0, width[g])], from_ring[g].at[k], u, 7, onward
        )

    def first_stage(u):
        g, k = units[u]
        t = total.at[u % 3]
        cols = pl.ds(0, width[g])
        load(u).wait()
        to_core(u).wait_recv()
        for j in range(4):
            part = t.at[j, :, cols]
            add_rows(part, part, from_core[g].at[k, j])
        for copy in first_sends(u):
            copy.start()

    def second_stage(u):
        g, k = units[u]
        t = total.at[u % 3]
        m = middle.at[u % 2]
        cols = pl.ds(0, width[g])
        if u >= 2:
            for copy in second_sends(u - 2):
                copy.wait_send()
        sends = first_sends(u)
        sends[1].wait_recv()
        add_rows(m.at[0, :, cols], t.at[2, pl.ds(0, half), cols], from_first[g].at[k, 0, 1])
        sends[3].wait_recv()
        add_rows(m.at[1, :, cols], t.at[1, pl.ds(half, half), cols], from_first[g].at[k, 1, 1])
        for copy in second_sends(u):
            copy.start()
        sends[0].wait_recv()
        upper = t.at[0, pl.ds(0, half), cols]
        add_rows(upper, upper, from_first[g].at[k, 0, 0])
        sends[2].wait_recv()
        lower = t.at[0, pl.ds(half, half), cols]
        add_rows(lower, lower, from_first[g].at[k, 1, 0])

    def third_stage(u):
        g, k = units[u]
        t = total.at[u % 3]
        cols = pl.ds(0, width[g])
        for side, copy in enumerate(second_sends(u)):
            copy.wait_recv()
            part = t.at[0, pl.ds(side * half, half), cols]
            if k == 1:
                if side == 0 and u >= 2:
                    wait_ring(u - 2)
                add_rows(
                    final.at[u % 2, pl.ds(side * half, half), cols],
                    part,
                    from_second[g].at[k, side],
                )
            else:
                add_rows(part, part, from_second[g].at[k, side])
        if k != 1:
            ring_send(u - 1).wait_recv()
            if k == 0:
                wait_ring(u - 2)
                add_rows(shares[g], t.at[0, :, cols], from_ring[g].at[3])
            else:
                if u >= 2:
                    wait_ring(u - 2)
                add_rows(final.at[u % 2, :, cols], t.at[0, :, cols], from_ring[g].at[k - 1])
        if k != 0:
            ring_send(u).start()
        for copy in first_sends(u):
            copy.wait_send()

    def wait_ring(u):
        if units[u][1] != 0:
            ring_send(u).wait_send()

    n = len(units)
    for j in range(1, 8):
        gain_copy(j).start()
    for p in range(2):
        own_copy(p).start()
    for u in range(n):
        to_core(u).start()
        if u < 3:
            load(u).start()
    for step in range(n + 2):
        if step < n:
            first_stage(step)
        if 0 <= step - 1 < n:
            second_stage(step - 1)
        if 0 <= step - 2:
            third_stage(step - 2)
            if step + 1 < n:
                load(step + 1).start()
        if step == 2:
            for j in range(1, 8):
                gain_copy(j).wait()
            gain_line[z] = gains[0] + sum(gain_box[j] for j in range(1, 8))
            for hop in (1, 2, 3):
                line_copy(hop).start()
        if 4 <= step < 10:
            box_copy((step - 4) // 3, (step - 4) % 3 + 1).start()
    for hop in (1, 2, 3):
        line_copy(hop).wait()
        for p in range(2):
            box_copy(p, hop).wait()
    for p in range(2):
        own_copy(p).wait()
    gain_share[...] = gain_line[0] + gain_line[1] + gain_line[2] + gain_line[3]
    for u in range(n):
        to_core(u).wait_send()
        if u >= n - 2:
            for copy in second_sends(u):
                copy.wait_send()
            wait_ring(u)


def scatter_grads(grads, gains, parcels):
    count = len(grads)
    views = [g.reshape(8, g.shape[0] // 8, g.shape[1]) for g in grads]
    rows = views[0].shape[1]
    half = rows // 2
    widths = [g.shape[1] // 4 for g in grads]
    widest = max(widths)
    bf16 = jnp.bfloat16
    return pl.pallas_call(
        functools.partial(scatter_kernel, count),
        out_shape=[jax.ShapeDtypeStruct((rows, w), jnp.float32) for w in widths]
        + [jax.ShapeDtypeStruct(gains.shape[1:], jnp.float32)]
        + [jax.ShapeDtypeStruct(p.shape, p.dtype) for p in parcels],
        in_specs=[pl.BlockSpec(memory_space=pl.ANY)] * count
        + [pl.BlockSpec(memory_space=pltpu.VMEM)] * 3,
        out_specs=[pl.BlockSpec(memory_space=pltpu.VMEM)] * (count + 1)
        + [pl.BlockSpec(memory_space=pl.ANY)] * 2,
        scratch_shapes=[pltpu.VMEM((4, 4, rows, w), bf16) for w in widths]
        + [pltpu.VMEM((4, 2, 2, half, w), bf16) for w in widths]
        + [pltpu.VMEM((4, 2, half, w), bf16) for w in widths]
        + [pltpu.VMEM((4, rows, w), bf16) for w in widths]
        + [
            pltpu.VMEM((3, 4, rows, widest), bf16),
            pltpu.VMEM((2, 2, half, widest), bf16),
            pltpu.VMEM((2, rows, widest), bf16),
            pltpu.VMEM(gains.shape, jnp.float32),
            pltpu.VMEM((4, *gains.shape[1:]), jnp.float32),
            pltpu.SemaphoreType.DMA((4 * count, 8)),
            pltpu.SemaphoreType.DMA((4 * count, 8)),
            pltpu.SemaphoreType.DMA((3,)),
            pltpu.SemaphoreType.DMA((10,)),
            pltpu.SemaphoreType.DMA((10,)),
            pltpu.SemaphoreType.DMA((2, 3)),
            pltpu.SemaphoreType.DMA((2, 3)),
            pltpu.SemaphoreType.DMA((2,)),
        ],
        compiler_params=pltpu.CompilerParams(
            collective_id=2, has_side_effects=True, vmem_limit_bytes=64000000
        ),
        name="scatter_grads",
    )(*views, gains, *parcels)


def grad_dot(left, right):
    return dot_tt(left, right, ((0,), (0,))).astype(jnp.bfloat16)


def scatter_plain(left, right):
    spots = jnp.array([0, 1, 3, 2], jnp.int32)
    order = (spots[lax.axis_index("tensor")] - spots) % 4
    parts = outer(left, right, order, 4)
    return lax.psum_scatter(
        parts.reshape(-1, parts.shape[2]), ("tensor", "dp"), scatter_dimension=0, tiled=True
    ).astype(jnp.float32)


def to_parcels(values):
    micro, rows, groups, width = values.shape
    return values.transpose(0, 2, 1, 3).reshape(micro * groups, rows, width)


def from_box(box, micro, groups):
    return box.reshape(micro, groups, *box.shape[1:]).transpose(0, 2, 1, 3)


def dot_tt(left, right, dims):
    return lax.dot_general(left, right, (dims, ((), ())), preferred_element_type=jnp.float32)


ROWS = 128
PAIR = 2 * HD
NORMAL = ((1,), (0,))
RIGHT_T = ((1,), (1,))
LEFT_T = ((0,), (0,))


def head_masks(scale):
    lane = lax.broadcasted_iota(jnp.int32, (1, PAIR), 1)
    return [jnp.where((lane // HD) == h, scale, 0.0).astype(jnp.bfloat16) for h in range(2)]


def spin(values, cos_table, sin_table, sign):
    lane = lax.broadcasted_iota(jnp.int32, values.shape, 1)
    ahead = pltpu.roll(values, PAIR - HD // 2, 1)
    behind = pltpu.roll(values, HD // 2, 1)
    turned = jnp.where(lane % HD < HD // 2, -ahead, behind)
    return values * cos_table + (sign * turned) * sin_table


def attend_kernel(
    normed_ref, w_ref, wo_ref, cos_ref, sin_ref, bias_ref, joint_ref, mix_ref, log_ref, sum_ref, proj_ref
):
    tokens = normed_ref.shape[0]
    cols = wo_ref.shape[1]
    pairs = cols // PAIR
    proj_ref[...] = dot_tt(normed_ref[...], w_ref[...], NORMAL)
    for c in range(3 * pairs):
        at = slice(c * PAIR, (c + 1) * PAIR)
        part = proj_ref[:, at]
        if c < 2 * pairs:
            part = spin(part, cos_ref[...], sin_ref[...], 1.0)
        joint_ref[:, at] = part.astype(jnp.bfloat16)
    masks = head_masks(HD ** (-0.5))
    lane = lax.broadcasted_iota(jnp.int32, (ROWS, PAIR), 1)
    for pair in range(pairs):
        for i in range(tokens // ROWS):
            rows = slice(i * ROWS, (i + 1) * ROWS)
            size = (i + 1) * ROWS
            q = joint_ref[rows, pair * PAIR : (pair + 1) * PAIR]
            k = joint_ref[:size, cols + pair * PAIR : cols + (pair + 1) * PAIR]
            v = joint_ref[:size, 2 * cols + pair * PAIR : 2 * cols + (pair + 1) * PAIR]
            both = jnp.concatenate([q * masks[0], q * masks[1]], axis=0)
            bias = bias_ref[rows, :size]
            scores = dot_tt(both, k, RIGHT_T) + jnp.concatenate([bias, bias], axis=0)
            top = jnp.max(scores, axis=1, keepdims=True)
            powers = jnp.exp(scores - top)
            norm = jnp.sum(powers, axis=1, keepdims=True)
            probs = (powers * (1.0 / norm)).astype(jnp.bfloat16)
            mixed = dot_tt(probs, v, NORMAL)
            mix_ref[rows, pair * PAIR : (pair + 1) * PAIR] = jnp.where(
                lane < HD, mixed[:ROWS], mixed[ROWS:]
            ).astype(jnp.bfloat16)
            log_norm = top + jnp.log(norm)
            log_ref[0, rows, 2 * pair : 2 * pair + 1] = log_norm[:ROWS]
            log_ref[0, rows, 2 * pair + 1 : 2 * pair + 2] = log_norm[ROWS:]
    projected = dot_tt(mix_ref[...], wo_ref[...], RIGHT_T)

    @pl.when(pl.program_id(0) == 0)
    def _():
        sum_ref[...] = projected

    @pl.when(pl.program_id(0) > 0)
    def _():
        sum_ref[...] += projected


def attend(normed, w_qkv, wo, cos_wide, sin_wide, bias):
    tokens, width = normed.shape
    blocks = 4
    cols = wo.shape[1] // blocks
    fixed = lambda k: (0, 0)
    moving = lambda k: (0, k)
    return pl.pallas_call(
        attend_kernel,
        grid=(blocks,),
        out_shape=[
            jax.ShapeDtypeStruct((tokens, 3 * blocks * cols), jnp.bfloat16),
            jax.ShapeDtypeStruct((tokens, blocks * cols), jnp.bfloat16),
            jax.ShapeDtypeStruct((blocks, tokens, 8), jnp.float32),
            jax.ShapeDtypeStruct((tokens, width), jnp.float32),
        ],
        in_specs=[
            pl.BlockSpec((tokens, width), fixed),
            pl.BlockSpec((width, 3 * cols), moving),
            pl.BlockSpec((width, cols), moving),
            pl.BlockSpec((tokens, PAIR), fixed),
            pl.BlockSpec((tokens, PAIR), fixed),
            pl.BlockSpec((tokens, tokens), fixed),
        ],
        out_specs=[
            pl.BlockSpec((tokens, 3 * cols), moving),
            pl.BlockSpec((tokens, cols), moving),
            pl.BlockSpec((1, tokens, 8), lambda k: (k, 0, 0)),
            pl.BlockSpec((tokens, width), fixed),
        ],
        scratch_shapes=[pltpu.VMEM((tokens, 3 * cols), jnp.float32)],
        compiler_params=pltpu.CompilerParams(vmem_limit_bytes=60000000),
        name="attend",
    )(normed, w_qkv, wo, cos_wide, sin_wide, bias)


def attend_back_kernel(
    grad_ref,
    w_ref,
    wo_ref,
    joint_ref,
    log_ref,
    cos_ref,
    sin_ref,
    bias_ref,
    out_ref,
    sum_ref,
    mix_grad,
    q_grad,
    k_grad,
    v_grad,
):
    tokens = grad_ref.shape[0]
    cols = wo_ref.shape[1]
    pairs = cols // PAIR
    mix_grad[...] = dot_tt(grad_ref[...], wo_ref[...], NORMAL).astype(jnp.bfloat16)
    scale = HD ** (-0.5)
    masks = head_masks(scale)
    ones = head_masks(1.0)
    lane = lax.broadcasted_iota(jnp.int32, (ROWS, PAIR), 1)
    last = tokens // ROWS - 1
    for pair in range(pairs):
        for i in range(last, -1, -1):
            rows = slice(i * ROWS, (i + 1) * ROWS)
            size = (i + 1) * ROWS
            q = joint_ref[rows, pair * PAIR : (pair + 1) * PAIR]
            k = joint_ref[:size, cols + pair * PAIR : cols + (pair + 1) * PAIR]
            v = joint_ref[:size, 2 * cols + pair * PAIR : 2 * cols + (pair + 1) * PAIR]
            g = mix_grad[rows, pair * PAIR : (pair + 1) * PAIR]
            q_both = jnp.concatenate([q * masks[0], q * masks[1]], axis=0)
            g_both = jnp.concatenate([g * ones[0], g * ones[1]], axis=0)
            bias = bias_ref[:size, rows]
            logs = jnp.concatenate(
                [log_ref[0, 2 * pair : 2 * pair + 1, rows], log_ref[0, 2 * pair + 1 : 2 * pair + 2, rows]],
                axis=1,
            )
            scores = dot_tt(k, q_both, RIGHT_T) + jnp.concatenate([bias, bias], axis=1)
            probs = jnp.exp(scores - logs)
            prob_grad = dot_tt(v, g_both, RIGHT_T)
            centre = jnp.sum(probs * prob_grad, axis=0, keepdims=True)
            score_grad = (probs * (prob_grad - centre)).astype(jnp.bfloat16)
            k_part = dot_tt(score_grad, q_both, NORMAL)
            v_part = dot_tt(probs.astype(jnp.bfloat16), g_both, NORMAL)
            if i == last:
                k_grad[...] = k_part
                v_grad[...] = v_part
            else:
                k_grad[:size, :] += k_part
                v_grad[:size, :] += v_part
            q_part = dot_tt(score_grad, k, LEFT_T)
            q_grad[rows, :] = jnp.where(lane < HD, q_part[:ROWS], q_part[ROWS:]) * scale
        cos_table = cos_ref[...]
        sin_table = sin_ref[...]
        out_ref[:, pair * PAIR : (pair + 1) * PAIR] = spin(
            q_grad[...], cos_table, sin_table, -1.0
        ).astype(jnp.bfloat16)
        out_ref[:, cols + pair * PAIR : cols + (pair + 1) * PAIR] = spin(
            k_grad[...], cos_table, sin_table, -1.0
        ).astype(jnp.bfloat16)
        out_ref[:, 2 * cols + pair * PAIR : 2 * cols + (pair + 1) * PAIR] = v_grad[...].astype(
            jnp.bfloat16
        )
    projected = dot_tt(out_ref[...], w_ref[...], RIGHT_T)

    @pl.when(pl.program_id(0) == 0)
    def _():
        sum_ref[...] = projected

    @pl.when(pl.program_id(0) > 0)
    def _():
        sum_ref[...] += projected


def attend_back(grad, w_qkv, wo, joint, logs, cos_wide, sin_wide, bias_t):
    tokens, width = grad.shape
    blocks = 4
    cols = wo.shape[1] // blocks
    fixed = lambda k: (0, 0)
    moving = lambda k: (0, k)
    return pl.pallas_call(
        attend_back_kernel,
        grid=(blocks,),
        out_shape=[
            jax.ShapeDtypeStruct((tokens, 3 * blocks * cols), jnp.bfloat16),
            jax.ShapeDtypeStruct((tokens, width), jnp.float32),
        ],
        in_specs=[
            pl.BlockSpec((tokens, width), fixed),
            pl.BlockSpec((width, 3 * cols), moving),
            pl.BlockSpec((width, cols), moving),
            pl.BlockSpec((tokens, 3 * cols), moving),
            pl.BlockSpec((1, 8, tokens), lambda k: (k, 0, 0)),
            pl.BlockSpec((tokens, PAIR), fixed),
            pl.BlockSpec((tokens, PAIR), fixed),
            pl.BlockSpec((tokens, tokens), fixed),
        ],
        out_specs=[
            pl.BlockSpec((tokens, 3 * cols), moving),
            pl.BlockSpec((tokens, width), fixed),
        ],
        scratch_shapes=[
            pltpu.VMEM((tokens, cols), jnp.bfloat16),
            pltpu.VMEM((tokens, PAIR), jnp.float32),
            pltpu.VMEM((tokens, PAIR), jnp.float32),
            pltpu.VMEM((tokens, PAIR), jnp.float32),
        ],
        compiler_params=pltpu.CompilerParams(vmem_limit_bytes=60000000),
        name="attend_back",
    )(grad, w_qkv, wo, joint, logs, cos_wide, sin_wide, bias_t)


def feed_kernel(
    normed_ref, grad_ref, wg_ref, wu_ref, wd_ref, hidden_ref, dg_ref, du_ref, out_ref, back_ref
):
    normed = normed_ref[...]
    gate = dot_tt(normed, wg_ref[...], NORMAL)
    up = dot_tt(normed, wu_ref[...], NORMAL)
    hidden_grad = dot_tt(grad_ref[...], wd_ref[...], NORMAL)
    sigmoid = jax.nn.sigmoid(gate)
    silu = gate * sigmoid
    hidden_ref[...] = (silu * up).astype(jnp.bfloat16)
    du_ref[...] = (hidden_grad * silu).astype(jnp.bfloat16)
    dg_ref[...] = (hidden_grad * up * (sigmoid * (1.0 + gate * (1.0 - sigmoid)))).astype(
        jnp.bfloat16
    )
    out = dot_tt(hidden_ref[...], wd_ref[...], RIGHT_T)
    back = dot_tt(dg_ref[...], wg_ref[...], RIGHT_T) + dot_tt(du_ref[...], wu_ref[...], RIGHT_T)

    @pl.when(pl.program_id(0) == 0)
    def _():
        out_ref[...] = out
        back_ref[...] = back

    @pl.when(pl.program_id(0) > 0)
    def _():
        out_ref[...] += out
        back_ref[...] += back


def feed_forward(normed, grad, wg, wu, wd, block=1024):
    tokens, width = normed.shape
    units = wg.shape[1]
    fixed = pl.BlockSpec((tokens, width), lambda b: (0, 0))
    weight = pl.BlockSpec((width, block), lambda b: (0, b))
    moving = pl.BlockSpec((tokens, block), lambda b: (0, b))
    return pl.pallas_call(
        feed_kernel,
        grid=(units // block,),
        out_shape=[jax.ShapeDtypeStruct((tokens, units), jnp.bfloat16)] * 3
        + [jax.ShapeDtypeStruct((tokens, width), jnp.float32)] * 2,
        in_specs=[fixed, fixed, weight, weight, weight],
        out_specs=[moving, moving, moving, fixed, fixed],
        compiler_params=pltpu.CompilerParams(vmem_limit_bytes=60000000),
        name="feed_forward",
    )(normed, grad, wg, wu, wd)


def outer_kernel(order_ref, left_ref, right_ref, out_ref, turned_ref):
    @pl.when(pl.program_id(1) == 0)
    def _():
        turned_ref[...] = left_ref[...].T

    out_ref[0] = dot_tt(turned_ref[...], right_ref[...], NORMAL).astype(jnp.bfloat16)


def outer(left, right, order, blocks, block=768):
    tokens, width = left.shape
    unit = right.shape[1] // blocks
    return pl.pallas_call(
        outer_kernel,
        grid_spec=pltpu.PrefetchScalarGridSpec(
            num_scalar_prefetch=1,
            grid=(width // block, blocks),
            in_specs=[
                pl.BlockSpec((tokens, block), lambda i, b, order: (0, i)),
                pl.BlockSpec((tokens, unit), lambda i, b, order: (0, order[b])),
            ],
            out_specs=pl.BlockSpec((1, block, unit), lambda i, b, order: (b, i, 0)),
            scratch_shapes=[pltpu.VMEM((block, tokens), left.dtype)],
        ),
        out_shape=jax.ShapeDtypeStruct((blocks, width, unit), jnp.bfloat16),
        compiler_params=pltpu.CompilerParams(vmem_limit_bytes=60000000),
        name="outer",
    )(order, left, right)


def order_matrix(width):
    rows = width // 8
    d = lax.axis_index("dp")
    owner = jnp.concatenate([jnp.full((rows,), mask, jnp.int32) for mask in RELATIVE])
    feature = (d ^ owner) * rows + jnp.arange(width, dtype=jnp.int32) % rows
    return (jnp.arange(width, dtype=jnp.int32)[:, None] == feature[None, :]).astype(jnp.bfloat16)


def group_body(
    block_input,
    lengths,
    out_grad,
    w_query,
    w_key,
    w_value,
    w_out,
    w_gate,
    w_up,
    w_down,
    attn_gain,
    ffn_gain,
):
    micro, _, groups, width = block_input.shape
    unit_cols = w_query.shape[1]
    bf16 = jnp.bfloat16
    f32 = jnp.float32
    contract = ((1,), (0,))
    contract_t = ((1,), (1,))
    own_lengths = lax.dynamic_slice_in_dim(
        lengths.reshape(micro * groups, 3), lax.axis_index("tensor"), 1, 0
    )
    rows = attn_gain.shape[0]
    gain_tile = jnp.zeros((8, 256), f32).at[0, :rows].set(attn_gain).at[1, :rows].set(ffn_gain)
    w_qkv, wo, wg, wu, wd, x_box, dy_box, gain_box = gather_weights(
        (jnp.concatenate([w_query, w_key, w_value], axis=1), w_out.T, w_gate, w_up, w_down.T),
        (to_parcels(block_input), to_parcels(out_grad)),
        gain_tile,
        ((0, 1), (2, 3), (4,)),
    )
    gains = gain_box[:, :2, :rows].transpose(1, 0, 2).reshape(2, width)
    order = order_matrix(width)
    tokens_in = dot_tt(x_box.reshape(GTOK, width), order, contract)
    upstream_plain = dy_box.reshape(GTOK, width)
    upstream = dot_tt(upstream_plain, order, contract).astype(bf16)
    gain_one = gains[0]
    gain_two = gains[1]

    segment, cos_table, sin_table = layout_tables(own_lengths)
    seg = segment[:, 0]
    cos_wide = jnp.tile(cos_table[:, 0], (1, 4))
    sin_wide = jnp.tile(sin_table[:, 0], (1, 4))
    index = jnp.arange(GTOK, dtype=jnp.int32)
    allowed = (index[None, :] <= index[:, None]) & (
        (seg[None, :] == 0) | (seg[None, :] == seg[:, None])
    )
    bias = jnp.where(allowed, 0.0, MASKED).astype(f32)
    residual = tokens_in
    scale_one = rms_scale(residual)
    unit_one = residual * scale_one
    normed_one = (unit_one * gain_one).astype(bf16)
    joint, mix, logs, attn_sum = attend(normed_one, w_qkv, wo, cos_wide, sin_wide, bias)
    middle = residual + attn_sum
    scale_two = rms_scale(middle)
    unit_two = middle * scale_two
    normed_two = (unit_two * gain_two).astype(bf16)
    hidden, gate_grad, up_grad, ffn_sum, normed_two_grad = feed_forward(
        normed_two, upstream, wg, wu, wd
    )
    share_down = scatter_plain(upstream_plain, hidden)
    output = (middle + ffn_sum).astype(bf16)
    out_parcels = dot_tt(output, order, contract_t).astype(bf16).reshape(x_box.shape)
    gain_two_grad = jnp.sum(normed_two_grad * unit_two, axis=0)
    middle_grad = upstream.astype(f32) + norm_back(
        normed_two_grad, unit_two, gain_two, scale_two
    )
    attn_grad = middle_grad.astype(bf16)
    joint_grad, normed_one_grad = attend_back(
        attn_grad, w_qkv, wo, joint, logs.transpose(0, 2, 1), cos_wide, sin_wide, bias.T
    )
    gain_one_grad = jnp.sum(normed_one_grad * unit_one, axis=0)
    input_grad = (
        middle_grad + norm_back(normed_one_grad, unit_one, gain_one, scale_one)
    ).astype(bf16)
    in_parcels = dot_tt(input_grad, order, contract_t).astype(bf16).reshape(x_box.shape)
    gain_parts = jnp.stack([gain_one_grad, gain_two_grad]).reshape(2, 8, rows).transpose(1, 0, 2)
    gain_parts = jnp.pad(gain_parts, ((0, 0), (0, 6), (0, 256 - rows)))
    share_gate, share_up, share_out, share_joint, own_gains, out_box, in_box = scatter_grads(
        (
            grad_dot(normed_two, gate_grad),
            grad_dot(normed_two, up_grad),
            grad_dot(attn_grad, mix),
            grad_dot(normed_one, joint_grad),
        ),
        gain_parts,
        (out_parcels, in_parcels),
    )
    return (
        from_box(out_box, micro, groups),
        from_box(in_box, micro, groups),
        share_joint[:, :unit_cols],
        share_joint[:, unit_cols : 2 * unit_cols],
        share_joint[:, 2 * unit_cols :],
        share_out.T,
        share_gate,
        share_up,
        share_down.T,
        own_gains[0, :rows],
        own_gains[1, :rows],
    )


def body(*operands):
    micro, _, groups, _ = operands[0].shape
    if lax.axis_size("dp") == 8 and micro * groups == lax.axis_size("tensor") == 4:
        return group_body(*operands)
    return sharded_body(*operands)


def solution(mesh):
    placed = (
        P(None, "tensor", "dp", None),
        P(None, "dp", None),
        P(None, "tensor", "dp", None),
        P("dp", "tensor"),
        P("dp", "tensor"),
        P("dp", "tensor"),
        P("tensor", "dp"),
        P("dp", "tensor"),
        P("dp", "tensor"),
        P("tensor", "dp"),
        P("dp"),
        P("dp"),
    )
    return jax.shard_map(
        body,
        mesh=mesh,
        in_specs=placed,
        out_specs=(
            P(None, "tensor", "dp", None),
            P(None, "tensor", "dp", None),
            P("dp", "tensor"),
            P("dp", "tensor"),
            P("dp", "tensor"),
            P("tensor", "dp"),
            P("dp", "tensor"),
            P("dp", "tensor"),
            P("tensor", "dp"),
            P("dp"),
            P("dp"),
        ),
        check_vma=False,
    )
```

```python
import functools
import math

import jax
import jax.numpy as jnp
from jax import lax
from jax.experimental import pallas as pl
from jax.experimental.pallas import tpu as pltpu
from jax.sharding import PartitionSpec as P


HD = 64
GTOK = 512


EPSILON = 1e-05
MASKED = -1e30


def layout_tables(group_lengths):
    slot_index = jnp.arange(GTOK, dtype=jnp.int32)[:, None]
    prompt_len = group_lengths[:, 0][None, :]
    first_len = group_lengths[:, 1][None, :]
    segment = jnp.where(
        slot_index < prompt_len, 0, jnp.where(slot_index < prompt_len + first_len, 1, 2)
    ).astype(jnp.int32)
    position = jnp.where(segment == 2, slot_index - first_len, slot_index)
    frequency = jnp.exp(jnp.arange(HD // 2, dtype=jnp.float32) * (-2.0 * math.log(10000.0) / HD))
    angles = position.astype(jnp.float32)[:, :, None] * frequency
    return (segment, jnp.cos(angles), jnp.sin(angles))


def rotate(values, cos_table, sin_table):
    half_size = values.shape[-1] // 2
    first_half = values[..., :half_size]
    second_half = values[..., half_size:]
    cos_wide = cos_table[:, :, None, :]
    sin_wide = sin_table[:, :, None, :]
    return jnp.concatenate(
        [
            first_half * cos_wide - second_half * sin_wide,
            second_half * cos_wide + first_half * sin_wide,
        ],
        axis=-1,
    )


def rotate_back(values, cos_table, sin_table):
    half_size = values.shape[-1] // 2
    first_half = values[..., :half_size]
    second_half = values[..., half_size:]
    cos_wide = cos_table[:, :, None, :]
    sin_wide = sin_table[:, :, None, :]
    return jnp.concatenate(
        [
            first_half * cos_wide + second_half * sin_wide,
            second_half * cos_wide - first_half * sin_wide,
        ],
        axis=-1,
    )


def rms_scale(values):
    return lax.rsqrt(jnp.mean(values * values, axis=-1, keepdims=True) + EPSILON)


def norm_back(upstream, unit_rows, gain_row, scale_rows):
    scaled = upstream * gain_row
    return scale_rows * (scaled - unit_rows * jnp.mean(scaled * unit_rows, axis=-1, keepdims=True))


def attention_scores(queries, key_rows, allowed):
    scores = jnp.einsum(
        "tghe,sghe->ghts", queries, key_rows, preferred_element_type=jnp.float32
    ) * HD ** (-0.5)
    return jnp.where(allowed[:, None], scores, MASKED)


def add_tuples(first_set, second_set):
    return tuple((earlier + later for earlier, later in zip(first_set, second_set)))


def micro_step(inputs, group_lengths, upstream, gathered):
    w_query, w_key, w_value, w_out, w_gate, w_up, w_down, attn_gain, ffn_gain = gathered
    gain_one = attn_gain.astype(jnp.float32)
    gain_two = ffn_gain.astype(jnp.float32)
    group_count = inputs.shape[1]
    head_cols = w_query.shape[1]
    hidden_cols = w_gate.shape[1]
    shape_heads = (GTOK, group_count, head_cols // HD, HD)
    segment, cos_table, sin_table = layout_tables(group_lengths)
    token_index = jnp.arange(GTOK, dtype=jnp.int32)
    seg_groups = segment.T
    allowed = (token_index[None, None, :] <= token_index[None, :, None]) & (
        (seg_groups[:, None, :] == 0) | (seg_groups[:, None, :] == seg_groups[:, :, None])
    )
    residual = inputs.astype(jnp.float32)
    scale_one = rms_scale(residual)
    unit_one = residual * scale_one
    normed_one = (unit_one * gain_one).astype(jnp.bfloat16)
    normed_all = lax.all_gather(normed_one, "tensor", axis=0, tiled=True)
    w_joint = jnp.concatenate([w_query, w_key, w_value], axis=1)
    projected = jnp.einsum("tgd,dc->tgc", normed_all, w_joint, preferred_element_type=jnp.float32)
    queries = rotate(projected[..., :head_cols].reshape(shape_heads), cos_table, sin_table).astype(
        jnp.bfloat16
    )
    key_rows = rotate(
        projected[..., head_cols : 2 * head_cols].reshape(shape_heads), cos_table, sin_table
    ).astype(jnp.bfloat16)
    value_rows = projected[..., 2 * head_cols :].reshape(shape_heads).astype(jnp.bfloat16)
    scores = attention_scores(queries, key_rows, allowed)
    row_max = jnp.max(scores, axis=-1, keepdims=True)
    log_total = row_max + jnp.log(jnp.sum(jnp.exp(scores - row_max), axis=-1, keepdims=True))
    attn_probs = jnp.exp(scores - log_total).astype(jnp.bfloat16)
    attn_mix = (
        jnp.einsum("ghts,sghe->tghe", attn_probs, value_rows, preferred_element_type=jnp.float32)
        .astype(jnp.bfloat16)
        .reshape(GTOK, group_count, head_cols)
    )
    rows_here = attn_mix
    attn_sum = lax.psum_scatter(
        jnp.einsum("tgc,cd->tgd", rows_here, w_out, preferred_element_type=jnp.float32),
        "tensor",
        scatter_dimension=0,
        tiled=True,
    )
    middle = residual + attn_sum
    scale_two = rms_scale(middle)
    unit_two = middle * scale_two
    normed_two = (unit_two * gain_two).astype(jnp.bfloat16)
    normed_more = lax.all_gather(normed_two, "tensor", axis=0, tiled=True)
    w_gate_up = jnp.concatenate([w_gate, w_up], axis=1)
    gate_up = jnp.einsum("tgd,df->tgf", normed_more, w_gate_up, preferred_element_type=jnp.float32)
    gate_vals = gate_up[..., :hidden_cols]
    up_vals = gate_up[..., hidden_cols:]
    sigmoid_gate = jax.nn.sigmoid(gate_vals)
    silu_gate = gate_vals * sigmoid_gate
    hidden = (silu_gate * up_vals).astype(jnp.bfloat16)
    rows_here = hidden
    ffn_sum = lax.psum_scatter(
        jnp.einsum("tgf,fd->tgd", rows_here, w_down, preferred_element_type=jnp.float32).astype(
            jnp.bfloat16
        ),
        "tensor",
        scatter_dimension=0,
        tiled=True,
    ).astype(jnp.float32)
    output = (middle + ffn_sum).astype(jnp.bfloat16)
    upstream_all = lax.all_gather(upstream, "tensor", axis=0, tiled=True)
    hidden_grad = jnp.einsum(
        "tgd,fd->tgf", upstream_all, w_down, preferred_element_type=jnp.float32
    )
    grad_down = jnp.einsum("tgf,tgd->fd", hidden, upstream_all, preferred_element_type=jnp.float32)
    up_grad = hidden_grad * silu_gate
    gate_grad = hidden_grad * up_vals * (sigmoid_gate * (1.0 + gate_vals * (1.0 - sigmoid_gate)))
    gate_up_grad = jnp.concatenate([gate_grad, up_grad], axis=-1).astype(jnp.bfloat16)
    grad_gate_up = jnp.einsum(
        "tgd,tgf->df", normed_more, gate_up_grad, preferred_element_type=jnp.float32
    )
    rows_here = gate_up_grad
    normed_two_grad = lax.psum_scatter(
        jnp.einsum("tgf,df->tgd", rows_here, w_gate_up, preferred_element_type=jnp.float32).astype(
            jnp.bfloat16
        ),
        "tensor",
        scatter_dimension=0,
        tiled=True,
    ).astype(jnp.float32)
    gain_two_grad = jnp.sum(normed_two_grad * unit_two, axis=(0, 1))
    middle_grad = upstream.astype(jnp.float32) + norm_back(
        normed_two_grad, unit_two, gain_two, scale_two
    )
    attn_grad = middle_grad.astype(jnp.bfloat16)
    attn_grad_all = lax.all_gather(attn_grad, "tensor", axis=0, tiled=True)
    mix_grad = (
        jnp.einsum("tgd,cd->tgc", attn_grad_all, w_out, preferred_element_type=jnp.float32)
        .astype(jnp.bfloat16)
        .reshape(shape_heads)
    )
    grad_out = jnp.einsum(
        "tgc,tgd->cd", attn_mix, attn_grad_all, preferred_element_type=jnp.float32
    )
    scores_again = attention_scores(queries, key_rows, allowed)
    probs_full = jnp.exp(scores_again - log_total)
    prob_grad = jnp.einsum(
        "tghe,sghe->ghts", mix_grad, value_rows, preferred_element_type=jnp.float32
    )
    value_grad = jnp.einsum(
        "ghts,tghe->sghe",
        probs_full.astype(jnp.bfloat16),
        mix_grad,
        preferred_element_type=jnp.float32,
    )
    centre = jnp.sum(probs_full * prob_grad, axis=-1, keepdims=True)
    score_grad = (probs_full * (prob_grad - centre)).astype(jnp.bfloat16)
    query_grad = jnp.einsum(
        "ghts,sghe->tghe", score_grad, key_rows, preferred_element_type=jnp.float32
    ) * HD ** (-0.5)
    key_grad = jnp.einsum(
        "ghts,tghe->sghe", score_grad, queries, preferred_element_type=jnp.float32
    ) * HD ** (-0.5)
    flat_shape = (GTOK, group_count, head_cols)
    joint_grad = jnp.concatenate(
        [
            rotate_back(query_grad, cos_table, sin_table).reshape(flat_shape),
            rotate_back(key_grad, cos_table, sin_table).reshape(flat_shape),
            value_grad.reshape(flat_shape),
        ],
        axis=-1,
    ).astype(jnp.bfloat16)
    grad_joint = jnp.einsum(
        "tgd,tgc->dc", normed_all, joint_grad, preferred_element_type=jnp.float32
    )
    rows_here = joint_grad
    normed_one_grad = lax.psum_scatter(
        jnp.einsum("tgc,dc->tgd", rows_here, w_joint, preferred_element_type=jnp.float32).astype(
            jnp.bfloat16
        ),
        "tensor",
        scatter_dimension=0,
        tiled=True,
    ).astype(jnp.float32)
    gain_one_grad = jnp.sum(normed_one_grad * unit_one, axis=(0, 1))
    input_grad = (middle_grad + norm_back(normed_one_grad, unit_one, gain_one, scale_one)).astype(
        jnp.bfloat16
    )
    param_grads = (
        grad_joint[:, :head_cols],
        grad_joint[:, head_cols : 2 * head_cols],
        grad_joint[:, 2 * head_cols :],
        grad_out,
        grad_gate_up[:, :hidden_cols],
        grad_gate_up[:, hidden_cols:],
        grad_down,
        gain_one_grad,
        gain_two_grad,
    )
    return (output, input_grad, param_grads)


def sharded_body(
    block_input,
    lengths,
    out_grad,
    w_query,
    w_key,
    w_value,
    w_out,
    w_gate,
    w_up,
    w_down,
    attn_gain,
    ffn_gain,
):
    outputs = []
    input_grads = []
    totals = None
    shares = None
    for micro_index in range(block_input.shape[0]):
        gathered = (
            lax.all_gather(w_query, "dp", axis=0, tiled=True),
            lax.all_gather(w_key, "dp", axis=0, tiled=True),
            lax.all_gather(w_value, "dp", axis=0, tiled=True),
            lax.all_gather(w_out, "dp", axis=1, tiled=True),
            lax.all_gather(w_gate, "dp", axis=0, tiled=True),
            lax.all_gather(w_up, "dp", axis=0, tiled=True),
            lax.all_gather(w_down, "dp", axis=1, tiled=True),
            lax.all_gather(attn_gain, "dp", axis=0, tiled=True),
            lax.all_gather(ffn_gain, "dp", axis=0, tiled=True),
        )
        output, input_grad, param_grads = micro_step(
            block_input[micro_index], lengths[micro_index], out_grad[micro_index], gathered
        )
        outputs.append(output)
        input_grads.append(input_grad)
        totals = param_grads if totals is None else add_tuples(totals, param_grads)
    shares = (
        lax.psum_scatter(
            totals[0].astype(jnp.bfloat16), "dp", scatter_dimension=0, tiled=True
        ).astype(jnp.float32),
        lax.psum_scatter(
            totals[1].astype(jnp.bfloat16), "dp", scatter_dimension=0, tiled=True
        ).astype(jnp.float32),
        lax.psum_scatter(
            totals[2].astype(jnp.bfloat16), "dp", scatter_dimension=0, tiled=True
        ).astype(jnp.float32),
        lax.psum_scatter(
            totals[3].astype(jnp.bfloat16), "dp", scatter_dimension=1, tiled=True
        ).astype(jnp.float32),
        lax.psum_scatter(
            totals[4].astype(jnp.bfloat16), "dp", scatter_dimension=0, tiled=True
        ).astype(jnp.float32),
        lax.psum_scatter(
            totals[5].astype(jnp.bfloat16), "dp", scatter_dimension=0, tiled=True
        ).astype(jnp.float32),
        lax.psum_scatter(
            totals[6].astype(jnp.bfloat16), "dp", scatter_dimension=1, tiled=True
        ).astype(jnp.float32),
        lax.psum_scatter(
            totals[7].astype(jnp.bfloat16), "dp", scatter_dimension=0, tiled=True
        ).astype(jnp.float32),
        lax.psum_scatter(
            totals[8].astype(jnp.bfloat16), "dp", scatter_dimension=0, tiled=True
        ).astype(jnp.float32),
    )
    gain_one_total, gain_two_total = lax.psum((shares[7], shares[8]), "tensor")
    return (
        jnp.stack(outputs),
        jnp.stack(input_grads),
        shares[0],
        shares[1],
        shares[2],
        shares[3],
        shares[4],
        shares[5],
        shares[6],
        gain_one_total,
        gain_two_total,
    )


MESH = pl.DeviceIdType.MESH
RELATIVE = [4 * ((j // 2) % 2) + 2 * (j % 2) + j // 4 for j in range(8)]


def flip_core(d):
    return d + 1 - 2 * (d % 2)


def flip_x(d):
    return d + 2 - 4 * ((d // 2) % 2)


def flip_y(d):
    return d + 4 - 8 * ((d // 4) % 2)


def flip(d, mask):
    if mask & 1:
        d = flip_core(d)
    if mask & 2:
        d = flip_x(d)
    if mask & 4:
        d = flip_y(d)
    return d


def ring_next(z):
    return (2 * z + 1) % 5


def remote(src, dst, send_sem, recv_sem, peer):
    return pltpu.make_async_remote_copy(
        src_ref=src,
        dst_ref=dst,
        send_sem=send_sem,
        recv_sem=recv_sem,
        device_id=peer,
        device_id_type=MESH,
    )


def greet(d, z):
    barrier = pltpu.get_barrier_semaphore()
    for mask in range(1, 8):
        pl.semaphore_signal(barrier, inc=1, device_id=(flip(d, mask), z), device_id_type=MESH)
    for step in (1, 2, 3):
        pl.semaphore_signal(barrier, inc=1, device_id=(d, (z + step) % 4), device_id_type=MESH)
    pl.semaphore_wait(barrier, 10)


def gather_kernel(sets, count, *refs):
    shards = refs[:count]
    parcels = refs[count : count + 2]
    gains = refs[count + 2]
    fulls = refs[count + 3 : 2 * count + 3]
    boxes = refs[2 * count + 3 : 2 * count + 5]
    gain_box = refs[2 * count + 5]
    send_sem, recv_sem, box_send, box_recv, gain_send, gain_recv, local_sem = refs[2 * count + 6 :]
    d = lax.axis_index("dp")
    z = lax.axis_index("tensor")
    place = {
        "z": (d, ring_next(z)),
        "x": (flip_x(d), z),
        "y": (flip_y(d), z),
        "c": (flip_core(d), z),
    }
    others = [(z + step) % 4 for step in (1, 2, 3)]
    greet(d, z)
    rows = shards[0].shape[0]

    def region(a, k, j, half):
        width = shards[a].shape[1]
        top, size = (j * rows, rows) if half is None else (j * rows + half * (rows // 2), rows // 2)
        return fulls[a].at[pl.ds(top, size), pl.ds(k * width, width)]

    sends = []

    def start(s, way, slot, src, dst, half=None):
        for a in sets[s]:
            source = shards[a] if src == (0, 0) else region(a, *src, half)
            remote(
                source,
                region(a, *dst, half),
                send_sem.at[s, slot],
                recv_sem.at[s, slot],
                place[way],
            ).start()
        sends.append((s, slot, half))

    def bulk(s, slot, half):
        arrs = sets[s]
        size = rows if half is None else rows // 2
        width = sum(shards[a].shape[1] for a in arrs)
        part = fulls[arrs[0]].at[pl.ds(0, size), pl.ds(0, width)]
        return remote(part, part, send_sem.at[s, slot], recv_sem.at[s, slot], place["c"])

    def arrived(s, slot, half=None):
        bulk(s, slot, half).wait_recv()

    ring_slot, x_slot, y_slot, x_relay, y_relay, core_slot = 0, 3, 7, 11, 15, 19

    def core(s, k, j):
        start(s, "c", core_slot + 4 * k + j, (k, j), (k, 4 + j))

    def ring_step(s, k):
        start(s, "z", ring_slot + k, (k, 0), (k + 1, 0))

    def open_unit(s, k):
        if k > 0:
            arrived(s, ring_slot + k - 1)
            if k < 3:
                ring_step(s, k)
        start(s, "x", x_slot + k, (k, 0), (k, 1))
        start(s, "y", y_slot + k, (k, 0), (k, 2))
        core(s, k, 0)

    def close_unit(s, k):
        arrived(s, x_slot + k)
        start(s, "y", y_relay + k, (k, 1), (k, 3), 1)
        core(s, k, 1)
        arrived(s, y_slot + k)
        start(s, "x", x_relay + k, (k, 2), (k, 3), 0)
        core(s, k, 2)

    def last_part(s, k):
        arrived(s, x_relay + k, 0)
        arrived(s, y_relay + k, 1)
        core(s, k, 3)

    def own_copies():
        for a in range(count):
            yield pltpu.make_async_copy(shards[a], region(a, 0, 0, None), local_sem.at[a])
        for p in range(2):
            yield pltpu.make_async_copy(
                parcels[p].at[z], boxes[p].at[z], local_sem.at[count + p]
            )
        yield pltpu.make_async_copy(gains, gain_box.at[0], local_sem.at[count + 2])

    def box_copy(p, step):
        return remote(
            parcels[p].at[others[step]],
            boxes[p].at[z],
            box_send.at[p, step],
            box_recv.at[p, step],
            (d, others[step]),
        )

    def gain_copy(j):
        return remote(
            gains,
            gain_box.at[j],
            gain_send.at[j - 1],
            gain_recv.at[j - 1],
            (flip(d, RELATIVE[j]), z),
        )

    for j in range(1, 8):
        gain_copy(j).start()
    for copy in own_copies():
        copy.start()
    units = [(s, k) for s in range(len(sets)) for k in range(4)]
    ring_step(0, 0)
    open_unit(*units[0])
    for i, unit in enumerate(units):
        if i + 1 < len(units):
            after = units[i + 1]
            if after[1] == 0:
                ring_step(after[0], 0)
            open_unit(*after)
        if i < 6:
            box_copy(i // 3, i % 3).start()
        close_unit(*unit)
        if i > 0:
            last_part(*units[i - 1])
    last_part(*units[-1])
    for s in range(len(sets)):
        for slot in range(core_slot, core_slot + 16):
            arrived(s, slot)
    for p in range(2):
        for step in range(3):
            box_copy(p, step).wait()
    for j in range(1, 8):
        gain_copy(j).wait()
    for s, slot, half in sends:
        bulk(s, slot, half).wait_send()
    for copy in own_copies():
        copy.wait()


def gather_weights(shards, parcels, gains, sets):
    count = len(shards)
    vmem = pl.BlockSpec(memory_space=pltpu.VMEM)
    anywhere = pl.BlockSpec(memory_space=pl.ANY)
    dma = pltpu.SemaphoreType.DMA
    return pl.pallas_call(
        functools.partial(gather_kernel, sets, count),
        out_shape=[
            jax.ShapeDtypeStruct((8 * w.shape[0], 4 * w.shape[1]), w.dtype) for w in shards
        ]
        + [jax.ShapeDtypeStruct(p.shape, p.dtype) for p in parcels]
        + [jax.ShapeDtypeStruct((8, *gains.shape), gains.dtype)],
        in_specs=[vmem] * (count + 3),
        out_specs=[anywhere] * (count + 3),
        scratch_shapes=[
            dma((len(sets), 35)),
            dma((len(sets), 35)),
            dma((2, 3)),
            dma((2, 3)),
            dma((7,)),
            dma((7,)),
            dma((count + 3,)),
        ],
        compiler_params=pltpu.CompilerParams(collective_id=1, has_side_effects=True),
        name="gather_weights",
    )(*shards, *parcels, gains)


def add_rows(target, first, second, chunk=32):
    rows = target.shape[0]

    def step(i, carry):
        at = pl.ds(pl.multiple_of(i * chunk, chunk), chunk)
        target[at, :] = (
            first[at, :].astype(jnp.float32) + second[at, :].astype(jnp.float32)
        ).astype(target.dtype)
        return carry

    lax.fori_loop(0, rows // chunk, step, 0)


def scatter_steps(grads, shares, buffers, gain_refs, box_refs):
    count = len(grads)
    from_core, from_first, from_second, from_ring = (
        buffers[i * count : (i + 1) * count] for i in range(4)
    )
    total, middle, final, send_sem, recv_sem, load_sem = buffers[4 * count :]
    d = lax.axis_index("dp")
    z = lax.axis_index("tensor")
    core, east, north = (flip_core(d), z), (flip_x(d), z), (flip_y(d), z)
    onward = (d, ring_next(z))
    rows = grads[0].shape[1]
    half = rows // 2
    units = [(g, k) for g in range(count) for k in (1, 2, 3, 0)]
    width = [grads[g].shape[2] // 4 for g in range(count)]

    def send(src, dst, u, slot, peer):
        return remote(src, dst, send_sem.at[u, slot], recv_sem.at[u, slot], peer)

    def gain_copy(j):
        gains, _, gain_box, _, gain_send, gain_recv = gain_refs
        return remote(
            gains.at[j],
            gain_box.at[j],
            gain_send.at[j - 1],
            gain_recv.at[j - 1],
            (flip(d, RELATIVE[j]), z),
        )

    def line_copy(step):
        _, _, _, gain_line, gain_send, gain_recv = gain_refs
        return remote(
            gain_line.at[z],
            gain_line.at[z],
            gain_send.at[6 + step],
            gain_recv.at[6 + step],
            (d, (z + step) % 4),
        )

    def box_copy(step):
        parcel, box, box_send, box_recv, _ = box_refs
        other = (z + step) % 4
        return remote(
            parcel.at[other],
            box.at[z],
            box_send.at[step - 1],
            box_recv.at[step - 1],
            (d, other),
        )

    def own_copy():
        parcel, box, _, _, box_own = box_refs
        return pltpu.make_async_copy(parcel.at[z], box.at[z], box_own)

    def columns(u):
        g, k = units[u]
        return pl.ds(k * width[g], width[g])

    def to_core(u):
        g, k = units[u]
        return send(
            grads[g].at[pl.ds(4, 4), :, columns(u)], from_core[g].at[k], u, 0, core
        )

    def load(u):
        g, _ = units[u]
        return pltpu.make_async_copy(
            grads[g].at[pl.ds(0, 4), :, columns(u)],
            total.at[u % 3, :, :, pl.ds(0, width[g])],
            load_sem.at[u % 3],
        )

    def first_sends(u):
        g, k = units[u]
        t = total.at[u % 3]
        cols = pl.ds(0, width[g])
        return [
            send(t.at[1, pl.ds(0, half), cols], from_first[g].at[k, 0, 0], u, 1, east),
            send(t.at[3, pl.ds(0, half), cols], from_first[g].at[k, 0, 1], u, 2, east),
            send(t.at[2, pl.ds(half, half), cols], from_first[g].at[k, 1, 0], u, 3, north),
            send(t.at[3, pl.ds(half, half), cols], from_first[g].at[k, 1, 1], u, 4, north),
        ]

    def second_sends(u):
        g, k = units[u]
        m = middle.at[u % 2]
        cols = pl.ds(0, width[g])
        return [
            send(m.at[0, :, cols], from_second[g].at[k, 0], u, 5, north),
            send(m.at[1, :, cols], from_second[g].at[k, 1], u, 6, east),
        ]

    def ring_send(u):
        g, k = units[u]
        return send(
            final.at[u % 2, :, pl.ds(0, width[g])], from_ring[g].at[k], u, 7, onward
        )

    def first_stage(u):
        g, k = units[u]
        t = total.at[u % 3]
        cols = pl.ds(0, width[g])
        load(u).wait()
        to_core(u).wait_recv()
        for j in range(4):
            part = t.at[j, :, cols]
            add_rows(part, part, from_core[g].at[k, j])
        for copy in first_sends(u):
            copy.start()

    def second_stage(u):
        g, k = units[u]
        t = total.at[u % 3]
        m = middle.at[u % 2]
        cols = pl.ds(0, width[g])
        if u >= 2:
            for copy in second_sends(u - 2):
                copy.wait_send()
        sends = first_sends(u)
        sends[1].wait_recv()
        add_rows(m.at[0, :, cols], t.at[2, pl.ds(0, half), cols], from_first[g].at[k, 0, 1])
        sends[3].wait_recv()
        add_rows(m.at[1, :, cols], t.at[1, pl.ds(half, half), cols], from_first[g].at[k, 1, 1])
        for copy in second_sends(u):
            copy.start()
        sends[0].wait_recv()
        upper = t.at[0, pl.ds(0, half), cols]
        add_rows(upper, upper, from_first[g].at[k, 0, 0])
        sends[2].wait_recv()
        lower = t.at[0, pl.ds(half, half), cols]
        add_rows(lower, lower, from_first[g].at[k, 1, 0])

    def third_stage(u):
        g, k = units[u]
        t = total.at[u % 3]
        cols = pl.ds(0, width[g])
        for side, copy in enumerate(second_sends(u)):
            copy.wait_recv()
            part = t.at[0, pl.ds(side * half, half), cols]
            if k == 1:
                if side == 0 and u >= 2:
                    wait_ring(u - 2)
                add_rows(
                    final.at[u % 2, pl.ds(side * half, half), cols],
                    part,
                    from_second[g].at[k, side],
                )
            else:
                add_rows(part, part, from_second[g].at[k, side])
        if k != 1:
            ring_send(u - 1).wait_recv()
            if u >= 2:
                wait_ring(u - 2)
            if k == 0:
                add_rows(shares[g], t.at[0, :, cols], from_ring[g].at[3])
            else:
                add_rows(final.at[u % 2, :, cols], t.at[0, :, cols], from_ring[g].at[k - 1])
        if k != 0:
            ring_send(u).start()
        for copy in first_sends(u):
            copy.wait_send()

    def wait_ring(u):
        if units[u][1] != 0:
            ring_send(u).wait_send()

    n = len(units)

    def begin():
        greet(d, z)
        if gain_refs:
            for j in range(1, 8):
                gain_copy(j).start()
        own_copy().start()
        for u in range(n):
            to_core(u).start()
            if u < 3:
                load(u).start()

    def run(step):
        if step == 0:
            begin()
        if step < n:
            first_stage(step)
        if 0 <= step - 1 < n:
            second_stage(step - 1)
        if 0 <= step - 2:
            third_stage(step - 2)
            if step + 1 < n:
                load(step + 1).start()
        if step == 2 and gain_refs:
            gains, _, gain_box, gain_line, _, _ = gain_refs
            for j in range(1, 8):
                gain_copy(j).wait()
            gain_line[z] = gains[0] + sum(gain_box[j] for j in range(1, 8))
            for hop in (1, 2, 3):
                line_copy(hop).start()
        if 3 <= step < 6:
            box_copy(step - 2).start()
        if step == n + 1:
            end()

    def end():
        if gain_refs:
            _, gain_share, _, gain_line, _, _ = gain_refs
            for hop in (1, 2, 3):
                line_copy(hop).wait()
            gain_share[...] = gain_line[0] + gain_line[1] + gain_line[2] + gain_line[3]
        for hop in (1, 2, 3):
            box_copy(hop).wait()
        own_copy().wait()
        for u in range(n):
            to_core(u).wait_send()
            if u >= n - 2:
                for copy in second_sends(u):
                    copy.wait_send()
                wait_ring(u)

    return [functools.partial(run, step) for step in range(n + 2)]


def scatter_scratch(rows, widths):
    bf16 = jnp.bfloat16
    half = rows // 2
    widest = max(widths)
    dma = pltpu.SemaphoreType.DMA
    return (
        [pltpu.VMEM((4, 4, rows, w), bf16) for w in widths]
        + [pltpu.VMEM((4, 2, 2, half, w), bf16) for w in widths]
        + [pltpu.VMEM((4, 2, half, w), bf16) for w in widths]
        + [pltpu.VMEM((4, rows, w), bf16) for w in widths]
        + [
            pltpu.VMEM((3, 4, rows, widest), bf16),
            pltpu.VMEM((2, 2, half, widest), bf16),
            pltpu.VMEM((2, rows, widest), bf16),
            dma((4 * len(widths), 8)),
            dma((4 * len(widths), 8)),
            dma((3,)),
        ]
    )


def scatter_kernel(count, *refs):
    grads = refs[:count]
    gains, parcel = refs[count : count + 2]
    shares = refs[count + 2 : 2 * count + 2]
    gain_share, box = refs[2 * count + 2 : 2 * count + 4]
    rest = refs[2 * count + 4 :]
    buffers = rest[: 4 * count + 6]
    gain_box, gain_line, gain_send, gain_recv, *box_sems = rest[4 * count + 6 :]
    for step in scatter_steps(
        grads,
        shares,
        buffers,
        (gains, gain_share, gain_box, gain_line, gain_send, gain_recv),
        (parcel, box, *box_sems),
    ):
        step()


def scatter_grads(grads, gains, parcel):
    count = len(grads)
    views = [g.reshape(8, g.shape[0] // 8, g.shape[1]) for g in grads]
    rows = views[0].shape[1]
    widths = [g.shape[1] // 4 for g in grads]
    dma = pltpu.SemaphoreType.DMA
    vmem = pl.BlockSpec(memory_space=pltpu.VMEM)
    anywhere = pl.BlockSpec(memory_space=pl.ANY)
    return pl.pallas_call(
        functools.partial(scatter_kernel, count),
        out_shape=[jax.ShapeDtypeStruct((rows, w), jnp.float32) for w in widths]
        + [jax.ShapeDtypeStruct(gains.shape[1:], jnp.float32)]
        + [jax.ShapeDtypeStruct(parcel.shape, parcel.dtype)],
        in_specs=[anywhere] * count + [vmem] * 2,
        out_specs=[vmem] * (count + 1) + [anywhere],
        scratch_shapes=scatter_scratch(rows, widths)
        + [
            pltpu.VMEM(gains.shape, jnp.float32),
            pltpu.VMEM((4, *gains.shape[1:]), jnp.float32),
            dma((10,)),
            dma((10,)),
            dma((3,)),
            dma((3,)),
            dma(()),
        ],
        compiler_params=pltpu.CompilerParams(
            collective_id=2, has_side_effects=True, vmem_limit_bytes=64000000
        ),
        name="scatter_grads",
    )(*views, gains, parcel)


def grad_dot(left, right):
    return dot_tt(left, right, ((0,), (0,))).astype(jnp.bfloat16)


def to_parcels(values):
    micro, rows, groups, width = values.shape
    return values.transpose(0, 2, 1, 3).reshape(micro * groups, rows, width)


def from_box(box, micro, groups):
    return box.reshape(micro, groups, *box.shape[1:]).transpose(0, 2, 1, 3)


def dot_tt(left, right, dims):
    return lax.dot_general(left, right, (dims, ((), ())), preferred_element_type=jnp.float32)


ROWS = 128
PAIR = 2 * HD
NORMAL = ((1,), (0,))
RIGHT_T = ((1,), (1,))
LEFT_T = ((0,), (0,))


def head_masks(scale):
    lane = lax.broadcasted_iota(jnp.int32, (1, PAIR), 1)
    return [jnp.where((lane // HD) == h, scale, 0.0).astype(jnp.bfloat16) for h in range(2)]


def spin(values, cos_table, sin_table, sign):
    lane = lax.broadcasted_iota(jnp.int32, values.shape, 1)
    ahead = pltpu.roll(values, PAIR - HD // 2, 1)
    behind = pltpu.roll(values, HD // 2, 1)
    turned = jnp.where(lane % HD < HD // 2, -ahead, behind)
    return values * cos_table + (sign * turned) * sin_table


def attend_kernel(
    normed_ref, w_ref, wo_ref, cos_ref, sin_ref, bias_ref, joint_ref, mix_ref, log_ref, sum_ref, proj_ref
):
    tokens = normed_ref.shape[0]
    cols = wo_ref.shape[1]
    pairs = cols // PAIR
    proj_ref[...] = dot_tt(normed_ref[...], w_ref[...], NORMAL)
    for c in range(3 * pairs):
        at = slice(c * PAIR, (c + 1) * PAIR)
        part = proj_ref[:, at]
        if c < 2 * pairs:
            part = spin(part, cos_ref[...], sin_ref[...], 1.0)
        joint_ref[:, at] = part.astype(jnp.bfloat16)
    masks = head_masks(HD ** (-0.5))
    lane = lax.broadcasted_iota(jnp.int32, (ROWS, PAIR), 1)
    for pair in range(pairs):
        for i in range(tokens // ROWS):
            rows = slice(i * ROWS, (i + 1) * ROWS)
            size = (i + 1) * ROWS
            q = joint_ref[rows, pair * PAIR : (pair + 1) * PAIR]
            k = joint_ref[:size, cols + pair * PAIR : cols + (pair + 1) * PAIR]
            v = joint_ref[:size, 2 * cols + pair * PAIR : 2 * cols + (pair + 1) * PAIR]
            both = jnp.concatenate([q * masks[0], q * masks[1]], axis=0)
            bias = bias_ref[rows, :size]
            scores = dot_tt(both, k, RIGHT_T) + jnp.concatenate([bias, bias], axis=0)
            top = jnp.max(scores, axis=1, keepdims=True)
            powers = jnp.exp(scores - top)
            norm = jnp.sum(powers, axis=1, keepdims=True)
            probs = (powers * (1.0 / norm)).astype(jnp.bfloat16)
            mixed = dot_tt(probs, v, NORMAL)
            mix_ref[rows, pair * PAIR : (pair + 1) * PAIR] = jnp.where(
                lane < HD, mixed[:ROWS], mixed[ROWS:]
            ).astype(jnp.bfloat16)
            log_norm = top + jnp.log(norm)
            log_ref[0, rows, 2 * pair : 2 * pair + 1] = log_norm[:ROWS]
            log_ref[0, rows, 2 * pair + 1 : 2 * pair + 2] = log_norm[ROWS:]
    projected = dot_tt(mix_ref[...], wo_ref[...], RIGHT_T)

    @pl.when(pl.program_id(0) == 0)
    def _():
        sum_ref[...] = projected

    @pl.when(pl.program_id(0) > 0)
    def _():
        sum_ref[...] += projected


def attend(normed, w_qkv, wo, cos_wide, sin_wide, bias):
    tokens, width = normed.shape
    blocks = 4
    cols = wo.shape[1] // blocks
    fixed = lambda k: (0, 0)
    moving = lambda k: (0, k)
    return pl.pallas_call(
        attend_kernel,
        grid=(blocks,),
        out_shape=[
            jax.ShapeDtypeStruct((tokens, 3 * blocks * cols), jnp.bfloat16),
            jax.ShapeDtypeStruct((tokens, blocks * cols), jnp.bfloat16),
            jax.ShapeDtypeStruct((blocks, tokens, 8), jnp.float32),
            jax.ShapeDtypeStruct((tokens, width), jnp.float32),
        ],
        in_specs=[
            pl.BlockSpec((tokens, width), fixed),
            pl.BlockSpec((width, 3 * cols), moving),
            pl.BlockSpec((width, cols), moving),
            pl.BlockSpec((tokens, PAIR), fixed),
            pl.BlockSpec((tokens, PAIR), fixed),
            pl.BlockSpec((tokens, tokens), fixed),
        ],
        out_specs=[
            pl.BlockSpec((tokens, 3 * cols), moving),
            pl.BlockSpec((tokens, cols), moving),
            pl.BlockSpec((1, tokens, 8), lambda k: (k, 0, 0)),
            pl.BlockSpec((tokens, width), fixed),
        ],
        scratch_shapes=[pltpu.VMEM((tokens, 3 * cols), jnp.float32)],
        compiler_params=pltpu.CompilerParams(vmem_limit_bytes=60000000),
        name="attend",
    )(normed, w_qkv, wo, cos_wide, sin_wide, bias)


def attend_back_kernel(
    count,
    grad_ref,
    w_ref,
    wo_ref,
    joint_ref,
    log_ref,
    cos_ref,
    sin_ref,
    bias_ref,
    *refs,
):
    grads = refs[:count]
    parcel, out_ref, sum_ref = refs[count : count + 3]
    shares = refs[count + 3 : 2 * count + 3]
    box, mix_grad, q_grad, k_grad, v_grad = refs[2 * count + 3 : 2 * count + 8]
    buffers = refs[2 * count + 8 : 6 * count + 14]
    box_sems = refs[6 * count + 14 :]
    turns = scatter_steps(grads, shares, buffers, None, (parcel, box, *box_sems))
    phase = pl.program_id(0)

    def talk(first, size):
        for p in range(4):

            @pl.when(phase == p)
            def _():
                for step in turns[2 * p + first : 2 * p + first + size]:
                    step()

    tokens = grad_ref.shape[0]
    cols = wo_ref.shape[1]
    pairs = cols // PAIR
    talk(0, 1)
    mix_grad[...] = dot_tt(grad_ref[...], wo_ref[...], NORMAL).astype(jnp.bfloat16)
    scale = HD ** (-0.5)
    masks = head_masks(scale)
    ones = head_masks(1.0)
    lane = lax.broadcasted_iota(jnp.int32, (ROWS, PAIR), 1)
    last = tokens // ROWS - 1
    for pair in range(pairs):
        if pair == 1:
            talk(1, 1)
        for i in range(last, -1, -1):
            rows = slice(i * ROWS, (i + 1) * ROWS)
            size = (i + 1) * ROWS
            q = joint_ref[rows, pair * PAIR : (pair + 1) * PAIR]
            k = joint_ref[:size, cols + pair * PAIR : cols + (pair + 1) * PAIR]
            v = joint_ref[:size, 2 * cols + pair * PAIR : 2 * cols + (pair + 1) * PAIR]
            g = mix_grad[rows, pair * PAIR : (pair + 1) * PAIR]
            q_both = jnp.concatenate([q * masks[0], q * masks[1]], axis=0)
            g_both = jnp.concatenate([g * ones[0], g * ones[1]], axis=0)
            bias = bias_ref[:size, rows]
            logs = jnp.concatenate(
                [log_ref[0, 2 * pair : 2 * pair + 1, rows], log_ref[0, 2 * pair + 1 : 2 * pair + 2, rows]],
                axis=1,
            )
            scores = dot_tt(k, q_both, RIGHT_T) + jnp.concatenate([bias, bias], axis=1)
            probs = jnp.exp(scores - logs)
            prob_grad = dot_tt(v, g_both, RIGHT_T)
            centre = jnp.sum(probs * prob_grad, axis=0, keepdims=True)
            score_grad = (probs * (prob_grad - centre)).astype(jnp.bfloat16)
            k_part = dot_tt(score_grad, q_both, NORMAL)
            v_part = dot_tt(probs.astype(jnp.bfloat16), g_both, NORMAL)
            if i == last:
                k_grad[...] = k_part
                v_grad[...] = v_part
            else:
                k_grad[:size, :] += k_part
                v_grad[:size, :] += v_part
            q_part = dot_tt(score_grad, k, LEFT_T)
            q_grad[rows, :] = jnp.where(lane < HD, q_part[:ROWS], q_part[ROWS:]) * scale
        cos_table = cos_ref[...]
        sin_table = sin_ref[...]
        out_ref[:, pair * PAIR : (pair + 1) * PAIR] = spin(
            q_grad[...], cos_table, sin_table, -1.0
        ).astype(jnp.bfloat16)
        out_ref[:, cols + pair * PAIR : cols + (pair + 1) * PAIR] = spin(
            k_grad[...], cos_table, sin_table, -1.0
        ).astype(jnp.bfloat16)
        out_ref[:, 2 * cols + pair * PAIR : 2 * cols + (pair + 1) * PAIR] = v_grad[...].astype(
            jnp.bfloat16
        )
    projected = dot_tt(out_ref[...], w_ref[...], RIGHT_T)

    @pl.when(phase == 0)
    def _():
        sum_ref[...] = projected

    @pl.when(phase > 0)
    def _():
        sum_ref[...] += projected

    @pl.when(phase == 3)
    def _():
        for step in turns[8:]:
            step()


def attend_back(grad, w_qkv, wo, joint, logs, cos_wide, sin_wide, bias_t, grads, parcel):
    tokens, width = grad.shape
    count = len(grads)
    views = [g.reshape(8, g.shape[0] // 8, g.shape[1]) for g in grads]
    rows = views[0].shape[1]
    widths = [g.shape[1] // 4 for g in grads]
    blocks = 4
    cols = wo.shape[1] // blocks
    dma = pltpu.SemaphoreType.DMA
    vmem = pl.BlockSpec(memory_space=pltpu.VMEM)
    anywhere = pl.BlockSpec(memory_space=pl.ANY)
    moving = lambda k: (0, k)
    return pl.pallas_call(
        functools.partial(attend_back_kernel, count),
        grid=(blocks,),
        out_shape=[
            jax.ShapeDtypeStruct((tokens, 3 * blocks * cols), jnp.bfloat16),
            jax.ShapeDtypeStruct((tokens, width), jnp.float32),
        ]
        + [jax.ShapeDtypeStruct((rows, w), jnp.float32) for w in widths]
        + [jax.ShapeDtypeStruct(parcel.shape, parcel.dtype)],
        in_specs=[
            vmem,
            pl.BlockSpec((width, 3 * cols), moving),
            pl.BlockSpec((width, cols), moving),
            pl.BlockSpec((tokens, 3 * cols), moving),
            pl.BlockSpec((1, 8, tokens), lambda k: (k, 0, 0)),
            vmem,
            vmem,
            vmem,
        ]
        + [anywhere] * (count + 1),
        out_specs=[pl.BlockSpec((tokens, 3 * cols), moving), vmem] + [vmem] * count + [anywhere],
        scratch_shapes=[
            pltpu.VMEM((tokens, cols), jnp.bfloat16),
            pltpu.VMEM((tokens, PAIR), jnp.float32),
            pltpu.VMEM((tokens, PAIR), jnp.float32),
            pltpu.VMEM((tokens, PAIR), jnp.float32),
        ]
        + scatter_scratch(rows, widths)
        + [dma((3,)), dma((3,)), dma(())],
        compiler_params=pltpu.CompilerParams(
            collective_id=3, has_side_effects=True, vmem_limit_bytes=66500000
        ),
        name="attend_back",
    )(grad, w_qkv, wo, joint, logs, cos_wide, sin_wide, bias_t, *views, parcel)


def feed_kernel(
    normed_ref, grad_ref, wg_ref, wu_ref, wd_ref, hidden_ref, dg_ref, du_ref, out_ref, back_ref
):
    normed = normed_ref[...]
    gate = dot_tt(normed, wg_ref[...], NORMAL)
    up = dot_tt(normed, wu_ref[...], NORMAL)
    hidden_grad = dot_tt(grad_ref[...], wd_ref[...], NORMAL)
    sigmoid = jax.nn.sigmoid(gate)
    silu = gate * sigmoid
    hidden_ref[...] = (silu * up).astype(jnp.bfloat16)
    du_ref[...] = (hidden_grad * silu).astype(jnp.bfloat16)
    dg_ref[...] = (hidden_grad * up * (sigmoid * (1.0 + gate * (1.0 - sigmoid)))).astype(
        jnp.bfloat16
    )
    out = dot_tt(hidden_ref[...], wd_ref[...], RIGHT_T)
    back = dot_tt(dg_ref[...], wg_ref[...], RIGHT_T) + dot_tt(du_ref[...], wu_ref[...], RIGHT_T)

    @pl.when(pl.program_id(0) == 0)
    def _():
        out_ref[...] = out
        back_ref[...] = back

    @pl.when(pl.program_id(0) > 0)
    def _():
        out_ref[...] += out
        back_ref[...] += back


def feed_forward(normed, grad, wg, wu, wd, block=1024):
    tokens, width = normed.shape
    units = wg.shape[1]
    fixed = pl.BlockSpec((tokens, width), lambda b: (0, 0))
    weight = pl.BlockSpec((width, block), lambda b: (0, b))
    moving = pl.BlockSpec((tokens, block), lambda b: (0, b))
    return pl.pallas_call(
        feed_kernel,
        grid=(units // block,),
        out_shape=[jax.ShapeDtypeStruct((tokens, units), jnp.bfloat16)] * 3
        + [jax.ShapeDtypeStruct((tokens, width), jnp.float32)] * 2,
        in_specs=[fixed, fixed, weight, weight, weight],
        out_specs=[moving, moving, moving, fixed, fixed],
        compiler_params=pltpu.CompilerParams(vmem_limit_bytes=60000000),
        name="feed_forward",
    )(normed, grad, wg, wu, wd)


def order_matrix(width):
    rows = width // 8
    d = lax.axis_index("dp")
    owner = jnp.concatenate([jnp.full((rows,), mask, jnp.int32) for mask in RELATIVE])
    feature = (d ^ owner) * rows + jnp.arange(width, dtype=jnp.int32) % rows
    return (jnp.arange(width, dtype=jnp.int32)[:, None] == feature[None, :]).astype(jnp.bfloat16)


def group_body(
    block_input,
    lengths,
    out_grad,
    w_query,
    w_key,
    w_value,
    w_out,
    w_gate,
    w_up,
    w_down,
    attn_gain,
    ffn_gain,
):
    micro, _, groups, width = block_input.shape
    unit_cols = w_query.shape[1]
    bf16 = jnp.bfloat16
    f32 = jnp.float32
    contract = ((1,), (0,))
    contract_t = ((1,), (1,))
    own_lengths = lax.dynamic_slice_in_dim(
        lengths.reshape(micro * groups, 3), lax.axis_index("tensor"), 1, 0
    )
    rows = attn_gain.shape[0]
    gain_tile = jnp.zeros((8, 256), f32).at[0, :rows].set(attn_gain).at[1, :rows].set(ffn_gain)
    w_qkv, wo, wg, wu, wd, x_box, dy_box, gain_box = gather_weights(
        (jnp.concatenate([w_query, w_key, w_value], axis=1), w_out.T, w_gate, w_up, w_down.T),
        (to_parcels(block_input), to_parcels(out_grad)),
        gain_tile,
        ((0, 1), (2, 3), (4,)),
    )
    gains = gain_box[:, :2, :rows].transpose(1, 0, 2).reshape(2, width)
    order = order_matrix(width)
    tokens_in = dot_tt(x_box.reshape(GTOK, width), order, contract)
    upstream = dot_tt(dy_box.reshape(GTOK, width), order, contract).astype(bf16)
    gain_one = gains[0]
    gain_two = gains[1]

    segment, cos_table, sin_table = layout_tables(own_lengths)
    seg = segment[:, 0]
    cos_wide = jnp.tile(cos_table[:, 0], (1, 4))
    sin_wide = jnp.tile(sin_table[:, 0], (1, 4))
    index = jnp.arange(GTOK, dtype=jnp.int32)
    allowed = (index[None, :] <= index[:, None]) & (
        (seg[None, :] == 0) | (seg[None, :] == seg[:, None])
    )
    bias = jnp.where(allowed, 0.0, MASKED).astype(f32)
    residual = tokens_in
    scale_one = rms_scale(residual)
    unit_one = residual * scale_one
    normed_one = (unit_one * gain_one).astype(bf16)
    joint, mix, logs, attn_sum = attend(normed_one, w_qkv, wo, cos_wide, sin_wide, bias)
    middle = residual + attn_sum
    scale_two = rms_scale(middle)
    unit_two = middle * scale_two
    normed_two = (unit_two * gain_two).astype(bf16)
    hidden, gate_grad, up_grad, ffn_sum, normed_two_grad = feed_forward(
        normed_two, upstream, wg, wu, wd
    )
    output = (middle + ffn_sum).astype(bf16)
    out_parcels = dot_tt(output, order, contract_t).astype(bf16).reshape(x_box.shape)
    gain_two_grad = jnp.sum(normed_two_grad * unit_two, axis=0)
    middle_grad = upstream.astype(f32) + norm_back(
        normed_two_grad, unit_two, gain_two, scale_two
    )
    attn_grad = middle_grad.astype(bf16)
    joint_grad, normed_one_grad, share_gate, share_up, out_box = attend_back(
        attn_grad,
        w_qkv,
        wo,
        joint,
        logs.transpose(0, 2, 1),
        cos_wide,
        sin_wide,
        bias.T,
        (grad_dot(normed_two, gate_grad), grad_dot(normed_two, up_grad)),
        out_parcels,
    )
    gain_one_grad = jnp.sum(normed_one_grad * unit_one, axis=0)
    input_grad = (
        middle_grad + norm_back(normed_one_grad, unit_one, gain_one, scale_one)
    ).astype(bf16)
    in_parcels = dot_tt(input_grad, order, contract_t).astype(bf16).reshape(x_box.shape)
    gain_parts = jnp.stack([gain_one_grad, gain_two_grad]).reshape(2, 8, rows).transpose(1, 0, 2)
    gain_parts = jnp.pad(gain_parts, ((0, 0), (0, 6), (0, 256 - rows)))
    share_down, share_out, share_joint, own_gains, in_box = scatter_grads(
        (
            grad_dot(upstream, hidden),
            grad_dot(attn_grad, mix),
            grad_dot(normed_one, joint_grad),
        ),
        gain_parts,
        in_parcels,
    )
    return (
        from_box(out_box, micro, groups),
        from_box(in_box, micro, groups),
        share_joint[:, :unit_cols],
        share_joint[:, unit_cols : 2 * unit_cols],
        share_joint[:, 2 * unit_cols :],
        share_out.T,
        share_gate,
        share_up,
        share_down.T,
        own_gains[0, :rows],
        own_gains[1, :rows],
    )


def body(*operands):
    micro, _, groups, _ = operands[0].shape
    if lax.axis_size("dp") == 8 and micro * groups == lax.axis_size("tensor") == 4:
        return group_body(*operands)
    return sharded_body(*operands)


def solution(mesh):
    placed = (
        P(None, "tensor", "dp", None),
        P(None, "dp", None),
        P(None, "tensor", "dp", None),
        P("dp", "tensor"),
        P("dp", "tensor"),
        P("dp", "tensor"),
        P("tensor", "dp"),
        P("dp", "tensor"),
        P("dp", "tensor"),
        P("tensor", "dp"),
        P("dp"),
        P("dp"),
    )
    return jax.shard_map(
        body,
        mesh=mesh,
        in_specs=placed,
        out_specs=(
            P(None, "tensor", "dp", None),
            P(None, "tensor", "dp", None),
            P("dp", "tensor"),
            P("dp", "tensor"),
            P("dp", "tensor"),
            P("tensor", "dp"),
            P("dp", "tensor"),
            P("dp", "tensor"),
            P("tensor", "dp"),
            P("dp"),
            P("dp"),
        ),
        check_vma=False,
    )
```

```python
import functools
import math

import jax
import jax.numpy as jnp
from jax import lax
from jax.experimental import pallas as pl
from jax.experimental.pallas import tpu as pltpu
from jax.sharding import PartitionSpec as P


HD = 64
GTOK = 512


EPSILON = 1e-05
MASKED = -1e30


def layout_tables(group_lengths):
    slot_index = jnp.arange(GTOK, dtype=jnp.int32)[:, None]
    prompt_len = group_lengths[:, 0][None, :]
    first_len = group_lengths[:, 1][None, :]
    segment = jnp.where(
        slot_index < prompt_len, 0, jnp.where(slot_index < prompt_len + first_len, 1, 2)
    ).astype(jnp.int32)
    position = jnp.where(segment == 2, slot_index - first_len, slot_index)
    frequency = jnp.exp(jnp.arange(HD // 2, dtype=jnp.float32) * (-2.0 * math.log(10000.0) / HD))
    angles = position.astype(jnp.float32)[:, :, None] * frequency
    return (segment, jnp.cos(angles), jnp.sin(angles))


def rotate(values, cos_table, sin_table):
    half_size = values.shape[-1] // 2
    first_half = values[..., :half_size]
    second_half = values[..., half_size:]
    cos_wide = cos_table[:, :, None, :]
    sin_wide = sin_table[:, :, None, :]
    return jnp.concatenate(
        [
            first_half * cos_wide - second_half * sin_wide,
            second_half * cos_wide + first_half * sin_wide,
        ],
        axis=-1,
    )


def rotate_back(values, cos_table, sin_table):
    half_size = values.shape[-1] // 2
    first_half = values[..., :half_size]
    second_half = values[..., half_size:]
    cos_wide = cos_table[:, :, None, :]
    sin_wide = sin_table[:, :, None, :]
    return jnp.concatenate(
        [
            first_half * cos_wide + second_half * sin_wide,
            second_half * cos_wide - first_half * sin_wide,
        ],
        axis=-1,
    )


def rms_scale(values):
    return lax.rsqrt(jnp.mean(values * values, axis=-1, keepdims=True) + EPSILON)


def norm_back(upstream, unit_rows, gain_row, scale_rows):
    scaled = upstream * gain_row
    return scale_rows * (scaled - unit_rows * jnp.mean(scaled * unit_rows, axis=-1, keepdims=True))


def attention_scores(queries, key_rows, allowed):
    scores = jnp.einsum(
        "tghe,sghe->ghts", queries, key_rows, preferred_element_type=jnp.float32
    ) * HD ** (-0.5)
    return jnp.where(allowed[:, None], scores, MASKED)


def add_tuples(first_set, second_set):
    return tuple((earlier + later for earlier, later in zip(first_set, second_set)))


def micro_step(inputs, group_lengths, upstream, gathered):
    w_query, w_key, w_value, w_out, w_gate, w_up, w_down, attn_gain, ffn_gain = gathered
    gain_one = attn_gain.astype(jnp.float32)
    gain_two = ffn_gain.astype(jnp.float32)
    group_count = inputs.shape[1]
    head_cols = w_query.shape[1]
    hidden_cols = w_gate.shape[1]
    shape_heads = (GTOK, group_count, head_cols // HD, HD)
    segment, cos_table, sin_table = layout_tables(group_lengths)
    token_index = jnp.arange(GTOK, dtype=jnp.int32)
    seg_groups = segment.T
    allowed = (token_index[None, None, :] <= token_index[None, :, None]) & (
        (seg_groups[:, None, :] == 0) | (seg_groups[:, None, :] == seg_groups[:, :, None])
    )
    residual = inputs.astype(jnp.float32)
    scale_one = rms_scale(residual)
    unit_one = residual * scale_one
    normed_one = (unit_one * gain_one).astype(jnp.bfloat16)
    normed_all = lax.all_gather(normed_one, "tensor", axis=0, tiled=True)
    w_joint = jnp.concatenate([w_query, w_key, w_value], axis=1)
    projected = jnp.einsum("tgd,dc->tgc", normed_all, w_joint, preferred_element_type=jnp.float32)
    queries = rotate(projected[..., :head_cols].reshape(shape_heads), cos_table, sin_table).astype(
        jnp.bfloat16
    )
    key_rows = rotate(
        projected[..., head_cols : 2 * head_cols].reshape(shape_heads), cos_table, sin_table
    ).astype(jnp.bfloat16)
    value_rows = projected[..., 2 * head_cols :].reshape(shape_heads).astype(jnp.bfloat16)
    scores = attention_scores(queries, key_rows, allowed)
    row_max = jnp.max(scores, axis=-1, keepdims=True)
    log_total = row_max + jnp.log(jnp.sum(jnp.exp(scores - row_max), axis=-1, keepdims=True))
    attn_probs = jnp.exp(scores - log_total).astype(jnp.bfloat16)
    attn_mix = (
        jnp.einsum("ghts,sghe->tghe", attn_probs, value_rows, preferred_element_type=jnp.float32)
        .astype(jnp.bfloat16)
        .reshape(GTOK, group_count, head_cols)
    )
    rows_here = attn_mix
    attn_sum = lax.psum_scatter(
        jnp.einsum("tgc,cd->tgd", rows_here, w_out, preferred_element_type=jnp.float32),
        "tensor",
        scatter_dimension=0,
        tiled=True,
    )
    middle = residual + attn_sum
    scale_two = rms_scale(middle)
    unit_two = middle * scale_two
    normed_two = (unit_two * gain_two).astype(jnp.bfloat16)
    normed_more = lax.all_gather(normed_two, "tensor", axis=0, tiled=True)
    w_gate_up = jnp.concatenate([w_gate, w_up], axis=1)
    gate_up = jnp.einsum("tgd,df->tgf", normed_more, w_gate_up, preferred_element_type=jnp.float32)
    gate_vals = gate_up[..., :hidden_cols]
    up_vals = gate_up[..., hidden_cols:]
    sigmoid_gate = jax.nn.sigmoid(gate_vals)
    silu_gate = gate_vals * sigmoid_gate
    hidden = (silu_gate * up_vals).astype(jnp.bfloat16)
    rows_here = hidden
    ffn_sum = lax.psum_scatter(
        jnp.einsum("tgf,fd->tgd", rows_here, w_down, preferred_element_type=jnp.float32).astype(
            jnp.bfloat16
        ),
        "tensor",
        scatter_dimension=0,
        tiled=True,
    ).astype(jnp.float32)
    output = (middle + ffn_sum).astype(jnp.bfloat16)
    upstream_all = lax.all_gather(upstream, "tensor", axis=0, tiled=True)
    hidden_grad = jnp.einsum(
        "tgd,fd->tgf", upstream_all, w_down, preferred_element_type=jnp.float32
    )
    grad_down = jnp.einsum("tgf,tgd->fd", hidden, upstream_all, preferred_element_type=jnp.float32)
    up_grad = hidden_grad * silu_gate
    gate_grad = hidden_grad * up_vals * (sigmoid_gate * (1.0 + gate_vals * (1.0 - sigmoid_gate)))
    gate_up_grad = jnp.concatenate([gate_grad, up_grad], axis=-1).astype(jnp.bfloat16)
    grad_gate_up = jnp.einsum(
        "tgd,tgf->df", normed_more, gate_up_grad, preferred_element_type=jnp.float32
    )
    rows_here = gate_up_grad
    normed_two_grad = lax.psum_scatter(
        jnp.einsum("tgf,df->tgd", rows_here, w_gate_up, preferred_element_type=jnp.float32).astype(
            jnp.bfloat16
        ),
        "tensor",
        scatter_dimension=0,
        tiled=True,
    ).astype(jnp.float32)
    gain_two_grad = jnp.sum(normed_two_grad * unit_two, axis=(0, 1))
    middle_grad = upstream.astype(jnp.float32) + norm_back(
        normed_two_grad, unit_two, gain_two, scale_two
    )
    attn_grad = middle_grad.astype(jnp.bfloat16)
    attn_grad_all = lax.all_gather(attn_grad, "tensor", axis=0, tiled=True)
    mix_grad = (
        jnp.einsum("tgd,cd->tgc", attn_grad_all, w_out, preferred_element_type=jnp.float32)
        .astype(jnp.bfloat16)
        .reshape(shape_heads)
    )
    grad_out = jnp.einsum(
        "tgc,tgd->cd", attn_mix, attn_grad_all, preferred_element_type=jnp.float32
    )
    scores_again = attention_scores(queries, key_rows, allowed)
    probs_full = jnp.exp(scores_again - log_total)
    prob_grad = jnp.einsum(
        "tghe,sghe->ghts", mix_grad, value_rows, preferred_element_type=jnp.float32
    )
    value_grad = jnp.einsum(
        "ghts,tghe->sghe",
        probs_full.astype(jnp.bfloat16),
        mix_grad,
        preferred_element_type=jnp.float32,
    )
    centre = jnp.sum(probs_full * prob_grad, axis=-1, keepdims=True)
    score_grad = (probs_full * (prob_grad - centre)).astype(jnp.bfloat16)
    query_grad = jnp.einsum(
        "ghts,sghe->tghe", score_grad, key_rows, preferred_element_type=jnp.float32
    ) * HD ** (-0.5)
    key_grad = jnp.einsum(
        "ghts,tghe->sghe", score_grad, queries, preferred_element_type=jnp.float32
    ) * HD ** (-0.5)
    flat_shape = (GTOK, group_count, head_cols)
    joint_grad = jnp.concatenate(
        [
            rotate_back(query_grad, cos_table, sin_table).reshape(flat_shape),
            rotate_back(key_grad, cos_table, sin_table).reshape(flat_shape),
            value_grad.reshape(flat_shape),
        ],
        axis=-1,
    ).astype(jnp.bfloat16)
    grad_joint = jnp.einsum(
        "tgd,tgc->dc", normed_all, joint_grad, preferred_element_type=jnp.float32
    )
    rows_here = joint_grad
    normed_one_grad = lax.psum_scatter(
        jnp.einsum("tgc,dc->tgd", rows_here, w_joint, preferred_element_type=jnp.float32).astype(
            jnp.bfloat16
        ),
        "tensor",
        scatter_dimension=0,
        tiled=True,
    ).astype(jnp.float32)
    gain_one_grad = jnp.sum(normed_one_grad * unit_one, axis=(0, 1))
    input_grad = (middle_grad + norm_back(normed_one_grad, unit_one, gain_one, scale_one)).astype(
        jnp.bfloat16
    )
    param_grads = (
        grad_joint[:, :head_cols],
        grad_joint[:, head_cols : 2 * head_cols],
        grad_joint[:, 2 * head_cols :],
        grad_out,
        grad_gate_up[:, :hidden_cols],
        grad_gate_up[:, hidden_cols:],
        grad_down,
        gain_one_grad,
        gain_two_grad,
    )
    return (output, input_grad, param_grads)


def sharded_body(
    block_input,
    lengths,
    out_grad,
    w_query,
    w_key,
    w_value,
    w_out,
    w_gate,
    w_up,
    w_down,
    attn_gain,
    ffn_gain,
):
    outputs = []
    input_grads = []
    totals = None
    shares = None
    for micro_index in range(block_input.shape[0]):
        gathered = (
            lax.all_gather(w_query, "dp", axis=0, tiled=True),
            lax.all_gather(w_key, "dp", axis=0, tiled=True),
            lax.all_gather(w_value, "dp", axis=0, tiled=True),
            lax.all_gather(w_out, "dp", axis=1, tiled=True),
            lax.all_gather(w_gate, "dp", axis=0, tiled=True),
            lax.all_gather(w_up, "dp", axis=0, tiled=True),
            lax.all_gather(w_down, "dp", axis=1, tiled=True),
            lax.all_gather(attn_gain, "dp", axis=0, tiled=True),
            lax.all_gather(ffn_gain, "dp", axis=0, tiled=True),
        )
        output, input_grad, param_grads = micro_step(
            block_input[micro_index], lengths[micro_index], out_grad[micro_index], gathered
        )
        outputs.append(output)
        input_grads.append(input_grad)
        totals = param_grads if totals is None else add_tuples(totals, param_grads)
    shares = (
        lax.psum_scatter(
            totals[0].astype(jnp.bfloat16), "dp", scatter_dimension=0, tiled=True
        ).astype(jnp.float32),
        lax.psum_scatter(
            totals[1].astype(jnp.bfloat16), "dp", scatter_dimension=0, tiled=True
        ).astype(jnp.float32),
        lax.psum_scatter(
            totals[2].astype(jnp.bfloat16), "dp", scatter_dimension=0, tiled=True
        ).astype(jnp.float32),
        lax.psum_scatter(
            totals[3].astype(jnp.bfloat16), "dp", scatter_dimension=1, tiled=True
        ).astype(jnp.float32),
        lax.psum_scatter(
            totals[4].astype(jnp.bfloat16), "dp", scatter_dimension=0, tiled=True
        ).astype(jnp.float32),
        lax.psum_scatter(
            totals[5].astype(jnp.bfloat16), "dp", scatter_dimension=0, tiled=True
        ).astype(jnp.float32),
        lax.psum_scatter(
            totals[6].astype(jnp.bfloat16), "dp", scatter_dimension=1, tiled=True
        ).astype(jnp.float32),
        lax.psum_scatter(
            totals[7].astype(jnp.bfloat16), "dp", scatter_dimension=0, tiled=True
        ).astype(jnp.float32),
        lax.psum_scatter(
            totals[8].astype(jnp.bfloat16), "dp", scatter_dimension=0, tiled=True
        ).astype(jnp.float32),
    )
    gain_one_total, gain_two_total = lax.psum((shares[7], shares[8]), "tensor")
    return (
        jnp.stack(outputs),
        jnp.stack(input_grads),
        shares[0],
        shares[1],
        shares[2],
        shares[3],
        shares[4],
        shares[5],
        shares[6],
        gain_one_total,
        gain_two_total,
    )


MESH = pl.DeviceIdType.MESH
RELATIVE = [4 * ((j // 2) % 2) + 2 * (j % 2) + j // 4 for j in range(8)]


def flip_core(d):
    return d + 1 - 2 * (d % 2)


def flip_x(d):
    return d + 2 - 4 * ((d // 2) % 2)


def flip_y(d):
    return d + 4 - 8 * ((d // 4) % 2)


def flip(d, mask):
    if mask & 1:
        d = flip_core(d)
    if mask & 2:
        d = flip_x(d)
    if mask & 4:
        d = flip_y(d)
    return d


def ring_next(z):
    return (2 * z + 1) % 5


def remote(src, dst, send_sem, recv_sem, peer):
    return pltpu.make_async_remote_copy(
        src_ref=src,
        dst_ref=dst,
        send_sem=send_sem,
        recv_sem=recv_sem,
        device_id=peer,
        device_id_type=MESH,
    )


def greet(d, z):
    barrier = pltpu.get_barrier_semaphore()
    for mask in range(1, 8):
        pl.semaphore_signal(barrier, inc=1, device_id=(flip(d, mask), z), device_id_type=MESH)
    for step in (1, 2, 3):
        pl.semaphore_signal(barrier, inc=1, device_id=(d, (z + step) % 4), device_id_type=MESH)
    pl.semaphore_wait(barrier, 10)


def gather_steps(sets, shards, fulls, sems, box_refs, gain_refs):
    count = len(shards)
    send_sem, recv_sem, local_sem = sems
    d = lax.axis_index("dp")
    z = lax.axis_index("tensor")
    place = {
        "z": (d, ring_next(z)),
        "x": (flip_x(d), z),
        "y": (flip_y(d), z),
        "c": (flip_core(d), z),
    }
    rows = shards[0].shape[0]

    def region(a, k, j, half):
        width = shards[a].shape[1]
        top, size = (j * rows, rows) if half is None else (j * rows + half * (rows // 2), rows // 2)
        return fulls[a].at[pl.ds(top, size), pl.ds(k * width, width)]

    sends = []

    def start(s, way, slot, src, dst, half=None):
        for a in sets[s]:
            source = shards[a] if src == (0, 0) else region(a, *src, half)
            remote(
                source,
                region(a, *dst, half),
                send_sem.at[s, slot],
                recv_sem.at[s, slot],
                place[way],
            ).start()
        sends.append((s, slot, half))

    def bulk(s, slot, half):
        arrs = sets[s]
        size = rows if half is None else rows // 2
        width = sum(shards[a].shape[1] for a in arrs)
        part = fulls[arrs[0]].at[pl.ds(0, size), pl.ds(0, width)]
        return remote(part, part, send_sem.at[s, slot], recv_sem.at[s, slot], place["c"])

    def arrived(s, slot, half=None):
        bulk(s, slot, half).wait_recv()

    ring_slot, x_slot, y_slot, x_relay, y_relay, core_slot = 0, 3, 7, 11, 15, 19

    def core(s, k, j):
        start(s, "c", core_slot + 4 * k + j, (k, j), (k, 4 + j))

    def ring_step(s, k):
        start(s, "z", ring_slot + k, (k, 0), (k + 1, 0))

    def open_unit(s, k):
        if k > 0:
            arrived(s, ring_slot + k - 1)
            if k < 3:
                ring_step(s, k)
        start(s, "x", x_slot + k, (k, 0), (k, 1))
        start(s, "y", y_slot + k, (k, 0), (k, 2))
        core(s, k, 0)

    def close_unit(s, k):
        arrived(s, x_slot + k)
        start(s, "y", y_relay + k, (k, 1), (k, 3), 1)
        core(s, k, 1)
        arrived(s, y_slot + k)
        start(s, "x", x_relay + k, (k, 2), (k, 3), 0)
        core(s, k, 2)

    def last_part(s, k):
        arrived(s, x_relay + k, 0)
        arrived(s, y_relay + k, 1)
        core(s, k, 3)

    def own_copies():
        for a in range(count):
            yield pltpu.make_async_copy(shards[a], region(a, 0, 0, None), local_sem.at[a])
        parcel, box = box_refs[:2]
        yield pltpu.make_async_copy(parcel.at[z], box.at[z], local_sem.at[count])
        if gain_refs:
            gains, gain_box = gain_refs[:2]
            yield pltpu.make_async_copy(gains, gain_box.at[0], local_sem.at[count + 1])

    def box_copy(step):
        parcel, box, box_send, box_recv = box_refs
        other = (z + step) % 4
        return remote(
            parcel.at[other],
            box.at[z],
            box_send.at[step - 1],
            box_recv.at[step - 1],
            (d, other),
        )

    def gain_copy(j):
        gains, gain_box, gain_send, gain_recv = gain_refs
        return remote(
            gains,
            gain_box.at[j],
            gain_send.at[j - 1],
            gain_recv.at[j - 1],
            (flip(d, RELATIVE[j]), z),
        )

    units = [(s, k) for s in range(len(sets)) for k in range(4)]

    def run(i):
        if i == 0:
            greet(d, z)
            if gain_refs:
                for j in range(1, 8):
                    gain_copy(j).start()
            for copy in own_copies():
                copy.start()
            ring_step(0, 0)
            open_unit(*units[0])
        if i < len(units):
            if i + 1 < len(units):
                after = units[i + 1]
                if after[1] == 0:
                    ring_step(after[0], 0)
                open_unit(*after)
            if i < 3:
                box_copy(i + 1).start()
            close_unit(*units[i])
        if i > 0:
            last_part(*units[i - 1])
        if i == len(units):
            end()

    def end():
        for s in range(len(sets)):
            for slot in range(core_slot, core_slot + 16):
                arrived(s, slot)
        for step in (1, 2, 3):
            box_copy(step).wait()
        if gain_refs:
            for j in range(1, 8):
                gain_copy(j).wait()
        for s, slot, half in sends:
            bulk(s, slot, half).wait_send()
        for copy in own_copies():
            copy.wait()

    return [functools.partial(run, i) for i in range(len(units) + 1)]


def gather_scratch(sets, count, gains):
    dma = pltpu.SemaphoreType.DMA
    sems = [dma((len(sets), 35)), dma((len(sets), 35)), dma((count + 2,)), dma((3,)), dma((3,))]
    return sems + ([dma((7,)), dma((7,))] if gains else [])


def gather_shapes(shards):
    return [jax.ShapeDtypeStruct((8 * w.shape[0], 4 * w.shape[1]), w.dtype) for w in shards]


def gather_kernel(sets, count, *refs):
    shards = refs[:count]
    parcel, gains = refs[count : count + 2]
    fulls = refs[count + 2 : 2 * count + 2]
    box, gain_box = refs[2 * count + 2 : 2 * count + 4]
    send_sem, recv_sem, local_sem, box_send, box_recv, *gain_sems = refs[2 * count + 4 :]
    for step in gather_steps(
        sets,
        shards,
        fulls,
        (send_sem, recv_sem, local_sem),
        (parcel, box, box_send, box_recv),
        (gains, gain_box, *gain_sems),
    ):
        step()


def gather_weights(shards, parcel, gains, sets):
    count = len(shards)
    vmem = pl.BlockSpec(memory_space=pltpu.VMEM)
    anywhere = pl.BlockSpec(memory_space=pl.ANY)
    return pl.pallas_call(
        functools.partial(gather_kernel, sets, count),
        out_shape=gather_shapes(shards)
        + [jax.ShapeDtypeStruct(parcel.shape, parcel.dtype)]
        + [jax.ShapeDtypeStruct((8, *gains.shape), gains.dtype)],
        in_specs=[vmem] * (count + 2),
        out_specs=[anywhere] * (count + 2),
        scratch_shapes=gather_scratch(sets, count, True),
        compiler_params=pltpu.CompilerParams(collective_id=1, has_side_effects=True),
        name="gather_weights",
    )(*shards, parcel, gains)


def add_rows(target, first, second, chunk=32):
    rows = target.shape[0]

    def step(i, carry):
        at = pl.ds(pl.multiple_of(i * chunk, chunk), chunk)
        target[at, :] = (
            first[at, :].astype(jnp.float32) + second[at, :].astype(jnp.float32)
        ).astype(target.dtype)
        return carry

    lax.fori_loop(0, rows // chunk, step, 0)


def scatter_steps(grads, shares, buffers, gain_refs, box_refs):
    count = len(grads)
    from_core, from_first, from_second, from_ring = (
        buffers[i * count : (i + 1) * count] for i in range(4)
    )
    total, middle, final, send_sem, recv_sem, load_sem = buffers[4 * count :]
    d = lax.axis_index("dp")
    z = lax.axis_index("tensor")
    core, east, north = (flip_core(d), z), (flip_x(d), z), (flip_y(d), z)
    onward = (d, ring_next(z))
    rows = grads[0].shape[1]
    half = rows // 2
    units = [(g, k) for g in range(count) for k in (1, 2, 3, 0)]
    width = [grads[g].shape[2] // 4 for g in range(count)]

    def send(src, dst, u, slot, peer):
        return remote(src, dst, send_sem.at[u, slot], recv_sem.at[u, slot], peer)

    def gain_copy(j):
        gains, _, gain_box, _, gain_send, gain_recv = gain_refs
        return remote(
            gains.at[j],
            gain_box.at[j],
            gain_send.at[j - 1],
            gain_recv.at[j - 1],
            (flip(d, RELATIVE[j]), z),
        )

    def line_copy(step):
        _, _, _, gain_line, gain_send, gain_recv = gain_refs
        return remote(
            gain_line.at[z],
            gain_line.at[z],
            gain_send.at[6 + step],
            gain_recv.at[6 + step],
            (d, (z + step) % 4),
        )

    def box_copy(step):
        parcel, box, box_send, box_recv, _ = box_refs
        other = (z + step) % 4
        return remote(
            parcel.at[other],
            box.at[z],
            box_send.at[step - 1],
            box_recv.at[step - 1],
            (d, other),
        )

    def own_copy():
        parcel, box, _, _, box_own = box_refs
        return pltpu.make_async_copy(parcel.at[z], box.at[z], box_own)

    def columns(u):
        g, k = units[u]
        return pl.ds(k * width[g], width[g])

    def to_core(u):
        g, k = units[u]
        return send(
            grads[g].at[pl.ds(4, 4), :, columns(u)], from_core[g].at[k], u, 0, core
        )

    def load(u):
        g, _ = units[u]
        return pltpu.make_async_copy(
            grads[g].at[pl.ds(0, 4), :, columns(u)],
            total.at[u % 3, :, :, pl.ds(0, width[g])],
            load_sem.at[u % 3],
        )

    def first_sends(u):
        g, k = units[u]
        t = total.at[u % 3]
        cols = pl.ds(0, width[g])
        return [
            send(t.at[1, pl.ds(0, half), cols], from_first[g].at[k, 0, 0], u, 1, east),
            send(t.at[3, pl.ds(0, half), cols], from_first[g].at[k, 0, 1], u, 2, east),
            send(t.at[2, pl.ds(half, half), cols], from_first[g].at[k, 1, 0], u, 3, north),
            send(t.at[3, pl.ds(half, half), cols], from_first[g].at[k, 1, 1], u, 4, north),
        ]

    def second_sends(u):
        g, k = units[u]
        m = middle.at[u % 2]
        cols = pl.ds(0, width[g])
        return [
            send(m.at[0, :, cols], from_second[g].at[k, 0], u, 5, north),
            send(m.at[1, :, cols], from_second[g].at[k, 1], u, 6, east),
        ]

    def ring_send(u):
        g, k = units[u]
        return send(
            final.at[u % 2, :, pl.ds(0, width[g])], from_ring[g].at[k], u, 7, onward
        )

    def first_stage(u):
        g, k = units[u]
        t = total.at[u % 3]
        cols = pl.ds(0, width[g])
        load(u).wait()
        to_core(u).wait_recv()
        for j in range(4):
            part = t.at[j, :, cols]
            add_rows(part, part, from_core[g].at[k, j])
        for copy in first_sends(u):
            copy.start()

    def second_stage(u):
        g, k = units[u]
        t = total.at[u % 3]
        m = middle.at[u % 2]
        cols = pl.ds(0, width[g])
        if u >= 2:
            for copy in second_sends(u - 2):
                copy.wait_send()
        sends = first_sends(u)
        sends[1].wait_recv()
        add_rows(m.at[0, :, cols], t.at[2, pl.ds(0, half), cols], from_first[g].at[k, 0, 1])
        sends[3].wait_recv()
        add_rows(m.at[1, :, cols], t.at[1, pl.ds(half, half), cols], from_first[g].at[k, 1, 1])
        for copy in second_sends(u):
            copy.start()
        sends[0].wait_recv()
        upper = t.at[0, pl.ds(0, half), cols]
        add_rows(upper, upper, from_first[g].at[k, 0, 0])
        sends[2].wait_recv()
        lower = t.at[0, pl.ds(half, half), cols]
        add_rows(lower, lower, from_first[g].at[k, 1, 0])

    def third_stage(u):
        g, k = units[u]
        t = total.at[u % 3]
        cols = pl.ds(0, width[g])
        for side, copy in enumerate(second_sends(u)):
            copy.wait_recv()
            part = t.at[0, pl.ds(side * half, half), cols]
            if k == 1:
                if side == 0 and u >= 2:
                    wait_ring(u - 2)
                add_rows(
                    final.at[u % 2, pl.ds(side * half, half), cols],
                    part,
                    from_second[g].at[k, side],
                )
            else:
                add_rows(part, part, from_second[g].at[k, side])
        if k != 1:
            ring_send(u - 1).wait_recv()
            if u >= 2:
                wait_ring(u - 2)
            if k == 0:
                add_rows(shares[g], t.at[0, :, cols], from_ring[g].at[3])
            else:
                add_rows(final.at[u % 2, :, cols], t.at[0, :, cols], from_ring[g].at[k - 1])
        if k != 0:
            ring_send(u).start()
        for copy in first_sends(u):
            copy.wait_send()

    def wait_ring(u):
        if units[u][1] != 0:
            ring_send(u).wait_send()

    n = len(units)

    def begin():
        greet(d, z)
        if gain_refs:
            for j in range(1, 8):
                gain_copy(j).start()
        own_copy().start()
        for hop in (1, 2, 3):
            box_copy(hop).start()
        for u in range(n):
            to_core(u).start()
            if u < 3:
                load(u).start()

    def run(step):
        if step == 0:
            begin()
        if step < n:
            first_stage(step)
        if 0 <= step - 1 < n:
            second_stage(step - 1)
        if 0 <= step - 2:
            third_stage(step - 2)
            if step + 1 < n:
                load(step + 1).start()
        if step == 2 and gain_refs:
            gains, _, gain_box, gain_line, _, _ = gain_refs
            for j in range(1, 8):
                gain_copy(j).wait()
            gain_line[z] = gains[0] + sum(gain_box[j] for j in range(1, 8))
            for hop in (1, 2, 3):
                line_copy(hop).start()
        if step == n + 1:
            end()

    def end():
        if gain_refs:
            _, gain_share, _, gain_line, _, _ = gain_refs
            for hop in (1, 2, 3):
                line_copy(hop).wait()
            gain_share[...] = gain_line[0] + gain_line[1] + gain_line[2] + gain_line[3]
        for hop in (1, 2, 3):
            box_copy(hop).wait()
        own_copy().wait()
        for u in range(n):
            to_core(u).wait_send()
            if u >= n - 2:
                for copy in second_sends(u):
                    copy.wait_send()
                wait_ring(u)

    return [functools.partial(run, step) for step in range(n + 2)]


def scatter_scratch(rows, widths):
    bf16 = jnp.bfloat16
    half = rows // 2
    widest = max(widths)
    dma = pltpu.SemaphoreType.DMA
    return (
        [pltpu.VMEM((4, 4, rows, w), bf16) for w in widths]
        + [pltpu.VMEM((4, 2, 2, half, w), bf16) for w in widths]
        + [pltpu.VMEM((4, 2, half, w), bf16) for w in widths]
        + [pltpu.VMEM((4, rows, w), bf16) for w in widths]
        + [
            pltpu.VMEM((3, 4, rows, widest), bf16),
            pltpu.VMEM((2, 2, half, widest), bf16),
            pltpu.VMEM((2, rows, widest), bf16),
            dma((4 * len(widths), 8)),
            dma((4 * len(widths), 8)),
            dma((3,)),
        ]
    )


def scatter_kernel(count, *refs):
    grads = refs[:count]
    gains, parcel = refs[count : count + 2]
    shares = refs[count + 2 : 2 * count + 2]
    gain_share, box = refs[2 * count + 2 : 2 * count + 4]
    rest = refs[2 * count + 4 :]
    buffers = rest[: 4 * count + 6]
    gain_box, gain_line, gain_send, gain_recv, *box_sems = rest[4 * count + 6 :]
    for step in scatter_steps(
        grads,
        shares,
        buffers,
        (gains, gain_share, gain_box, gain_line, gain_send, gain_recv),
        (parcel, box, *box_sems),
    ):
        step()


def scatter_grads(grads, gains, parcel):
    count = len(grads)
    views = [g.reshape(8, g.shape[0] // 8, g.shape[1]) for g in grads]
    rows = views[0].shape[1]
    widths = [g.shape[1] // 4 for g in grads]
    dma = pltpu.SemaphoreType.DMA
    vmem = pl.BlockSpec(memory_space=pltpu.VMEM)
    anywhere = pl.BlockSpec(memory_space=pl.ANY)
    return pl.pallas_call(
        functools.partial(scatter_kernel, count),
        out_shape=[jax.ShapeDtypeStruct((rows, w), jnp.float32) for w in widths]
        + [jax.ShapeDtypeStruct(gains.shape[1:], jnp.float32)]
        + [jax.ShapeDtypeStruct(parcel.shape, parcel.dtype)],
        in_specs=[anywhere] * count + [vmem] * 2,
        out_specs=[vmem] * (count + 1) + [anywhere],
        scratch_shapes=scatter_scratch(rows, widths)
        + [
            pltpu.VMEM(gains.shape, jnp.float32),
            pltpu.VMEM((4, *gains.shape[1:]), jnp.float32),
            dma((10,)),
            dma((10,)),
            dma((3,)),
            dma((3,)),
            dma(()),
        ],
        compiler_params=pltpu.CompilerParams(
            collective_id=2, has_side_effects=True, vmem_limit_bytes=64000000
        ),
        name="scatter_grads",
    )(*views, gains, parcel)


def grad_dot(left, right):
    return dot_tt(left, right, ((0,), (0,))).astype(jnp.bfloat16)


def to_parcels(values):
    micro, rows, groups, width = values.shape
    return values.transpose(0, 2, 1, 3).reshape(micro * groups, rows, width)


def from_box(box, micro, groups):
    return box.reshape(micro, groups, *box.shape[1:]).transpose(0, 2, 1, 3)


def dot_tt(left, right, dims):
    return lax.dot_general(left, right, (dims, ((), ())), preferred_element_type=jnp.float32)


ROWS = 128
PAIR = 2 * HD
NORMAL = ((1,), (0,))
RIGHT_T = ((1,), (1,))
LEFT_T = ((0,), (0,))


def head_masks(scale):
    lane = lax.broadcasted_iota(jnp.int32, (1, PAIR), 1)
    return [jnp.where((lane // HD) == h, scale, 0.0).astype(jnp.bfloat16) for h in range(2)]


def spin(values, cos_table, sin_table, sign):
    lane = lax.broadcasted_iota(jnp.int32, values.shape, 1)
    ahead = pltpu.roll(values, PAIR - HD // 2, 1)
    behind = pltpu.roll(values, HD // 2, 1)
    turned = jnp.where(lane % HD < HD // 2, -ahead, behind)
    return values * cos_table + (sign * turned) * sin_table


def attend_kernel(sets, count, normed_ref, w_ref, wo_ref, cos_ref, sin_ref, bias_ref, *refs):
    shards = refs[:count]
    parcel, joint_ref, mix_ref, log_ref, sum_ref = refs[count : count + 5]
    fulls = refs[count + 5 : 2 * count + 5]
    box, proj_ref, send_sem, recv_sem, local_sem, box_send, box_recv = refs[2 * count + 5 :]
    turns = gather_steps(
        sets,
        shards,
        fulls,
        (send_sem, recv_sem, local_sem),
        (parcel, box, box_send, box_recv),
        None,
    )
    phase = pl.program_id(0)

    def talk(first):
        for p in range(4):

            @pl.when(phase == p)
            def _():
                turns[2 * p + first]()

    talk(0)
    tokens = normed_ref.shape[0]
    cols = wo_ref.shape[1]
    pairs = cols // PAIR
    proj_ref[...] = dot_tt(normed_ref[...], w_ref[...], NORMAL)
    for c in range(3 * pairs):
        at = slice(c * PAIR, (c + 1) * PAIR)
        part = proj_ref[:, at]
        if c < 2 * pairs:
            part = spin(part, cos_ref[...], sin_ref[...], 1.0)
        joint_ref[:, at] = part.astype(jnp.bfloat16)
    masks = head_masks(HD ** (-0.5))
    lane = lax.broadcasted_iota(jnp.int32, (ROWS, PAIR), 1)
    for pair in range(pairs):
        if pair == 1:
            talk(1)
        for i in range(tokens // ROWS):
            rows = slice(i * ROWS, (i + 1) * ROWS)
            size = (i + 1) * ROWS
            q = joint_ref[rows, pair * PAIR : (pair + 1) * PAIR]
            k = joint_ref[:size, cols + pair * PAIR : cols + (pair + 1) * PAIR]
            v = joint_ref[:size, 2 * cols + pair * PAIR : 2 * cols + (pair + 1) * PAIR]
            both = jnp.concatenate([q * masks[0], q * masks[1]], axis=0)
            bias = bias_ref[rows, :size]
            scores = dot_tt(both, k, RIGHT_T) + jnp.concatenate([bias, bias], axis=0)
            top = jnp.max(scores, axis=1, keepdims=True)
            powers = jnp.exp(scores - top)
            norm = jnp.sum(powers, axis=1, keepdims=True)
            probs = (powers * (1.0 / norm)).astype(jnp.bfloat16)
            mixed = dot_tt(probs, v, NORMAL)
            mix_ref[rows, pair * PAIR : (pair + 1) * PAIR] = jnp.where(
                lane < HD, mixed[:ROWS], mixed[ROWS:]
            ).astype(jnp.bfloat16)
            log_norm = top + jnp.log(norm)
            log_ref[0, rows, 2 * pair : 2 * pair + 1] = log_norm[:ROWS]
            log_ref[0, rows, 2 * pair + 1 : 2 * pair + 2] = log_norm[ROWS:]
    projected = dot_tt(mix_ref[...], wo_ref[...], RIGHT_T)

    @pl.when(phase == 0)
    def _():
        sum_ref[...] = projected

    @pl.when(phase > 0)
    def _():
        sum_ref[...] += projected

    @pl.when(phase == 3)
    def _():
        turns[8]()


def attend(normed, w_qkv, wo, cos_wide, sin_wide, bias, shards, parcel, sets):
    tokens, width = normed.shape
    count = len(shards)
    blocks = 4
    cols = wo.shape[1] // blocks
    vmem = pl.BlockSpec(memory_space=pltpu.VMEM)
    anywhere = pl.BlockSpec(memory_space=pl.ANY)
    moving = lambda k: (0, k)
    return pl.pallas_call(
        functools.partial(attend_kernel, sets, count),
        grid=(blocks,),
        out_shape=[
            jax.ShapeDtypeStruct((tokens, 3 * blocks * cols), jnp.bfloat16),
            jax.ShapeDtypeStruct((tokens, blocks * cols), jnp.bfloat16),
            jax.ShapeDtypeStruct((blocks, tokens, 8), jnp.float32),
            jax.ShapeDtypeStruct((tokens, width), jnp.float32),
        ]
        + gather_shapes(shards)
        + [jax.ShapeDtypeStruct(parcel.shape, parcel.dtype)],
        in_specs=[
            vmem,
            pl.BlockSpec((width, 3 * cols), moving),
            pl.BlockSpec((width, cols), moving),
            vmem,
            vmem,
            vmem,
        ]
        + [vmem] * (count + 1),
        out_specs=[
            pl.BlockSpec((tokens, 3 * cols), moving),
            pl.BlockSpec((tokens, cols), moving),
            pl.BlockSpec((1, tokens, 8), lambda k: (k, 0, 0)),
            vmem,
        ]
        + [anywhere] * (count + 1),
        scratch_shapes=[pltpu.VMEM((tokens, 3 * cols), jnp.float32)]
        + gather_scratch(sets, count, False),
        compiler_params=pltpu.CompilerParams(
            collective_id=4, has_side_effects=True, vmem_limit_bytes=60000000
        ),
        name="attend",
    )(normed, w_qkv, wo, cos_wide, sin_wide, bias, *shards, parcel)


def attend_back_kernel(
    count,
    grad_ref,
    w_ref,
    wo_ref,
    joint_ref,
    log_ref,
    cos_ref,
    sin_ref,
    bias_ref,
    *refs,
):
    grads = refs[:count]
    parcel, out_ref, sum_ref = refs[count : count + 3]
    shares = refs[count + 3 : 2 * count + 3]
    box, mix_grad, q_grad, k_grad, v_grad = refs[2 * count + 3 : 2 * count + 8]
    buffers = refs[2 * count + 8 : 6 * count + 14]
    box_sems = refs[6 * count + 14 :]
    turns = scatter_steps(grads, shares, buffers, None, (parcel, box, *box_sems))
    phase = pl.program_id(0)

    def talk(first, size):
        for p in range(4):

            @pl.when(phase == p)
            def _():
                for step in turns[2 * p + first : 2 * p + first + size]:
                    step()

    tokens = grad_ref.shape[0]
    cols = wo_ref.shape[1]
    pairs = cols // PAIR
    talk(0, 1)
    mix_grad[...] = dot_tt(grad_ref[...], wo_ref[...], NORMAL).astype(jnp.bfloat16)
    scale = HD ** (-0.5)
    masks = head_masks(scale)
    ones = head_masks(1.0)
    lane = lax.broadcasted_iota(jnp.int32, (ROWS, PAIR), 1)
    last = tokens // ROWS - 1
    for pair in range(pairs):
        if pair == 1:
            talk(1, 1)
        for i in range(last, -1, -1):
            rows = slice(i * ROWS, (i + 1) * ROWS)
            size = (i + 1) * ROWS
            q = joint_ref[rows, pair * PAIR : (pair + 1) * PAIR]
            k = joint_ref[:size, cols + pair * PAIR : cols + (pair + 1) * PAIR]
            v = joint_ref[:size, 2 * cols + pair * PAIR : 2 * cols + (pair + 1) * PAIR]
            g = mix_grad[rows, pair * PAIR : (pair + 1) * PAIR]
            q_both = jnp.concatenate([q * masks[0], q * masks[1]], axis=0)
            g_both = jnp.concatenate([g * ones[0], g * ones[1]], axis=0)
            bias = bias_ref[:size, rows]
            logs = jnp.concatenate(
                [log_ref[0, 2 * pair : 2 * pair + 1, rows], log_ref[0, 2 * pair + 1 : 2 * pair + 2, rows]],
                axis=1,
            )
            scores = dot_tt(k, q_both, RIGHT_T) + jnp.concatenate([bias, bias], axis=1)
            probs = jnp.exp(scores - logs)
            prob_grad = dot_tt(v, g_both, RIGHT_T)
            centre = jnp.sum(probs * prob_grad, axis=0, keepdims=True)
            score_grad = (probs * (prob_grad - centre)).astype(jnp.bfloat16)
            k_part = dot_tt(score_grad, q_both, NORMAL)
            v_part = dot_tt(probs.astype(jnp.bfloat16), g_both, NORMAL)
            if i == last:
                k_grad[...] = k_part
                v_grad[...] = v_part
            else:
                k_grad[:size, :] += k_part
                v_grad[:size, :] += v_part
            q_part = dot_tt(score_grad, k, LEFT_T)
            q_grad[rows, :] = jnp.where(lane < HD, q_part[:ROWS], q_part[ROWS:]) * scale
        cos_table = cos_ref[...]
        sin_table = sin_ref[...]
        out_ref[:, pair * PAIR : (pair + 1) * PAIR] = spin(
            q_grad[...], cos_table, sin_table, -1.0
        ).astype(jnp.bfloat16)
        out_ref[:, cols + pair * PAIR : cols + (pair + 1) * PAIR] = spin(
            k_grad[...], cos_table, sin_table, -1.0
        ).astype(jnp.bfloat16)
        out_ref[:, 2 * cols + pair * PAIR : 2 * cols + (pair + 1) * PAIR] = v_grad[...].astype(
            jnp.bfloat16
        )
    projected = dot_tt(out_ref[...], w_ref[...], RIGHT_T)

    @pl.when(phase == 0)
    def _():
        sum_ref[...] = projected

    @pl.when(phase > 0)
    def _():
        sum_ref[...] += projected

    @pl.when(phase == 3)
    def _():
        for step in turns[8:]:
            step()


def attend_back(grad, w_qkv, wo, joint, logs, cos_wide, sin_wide, bias_t, grads, parcel):
    tokens, width = grad.shape
    count = len(grads)
    views = [g.reshape(8, g.shape[0] // 8, g.shape[1]) for g in grads]
    rows = views[0].shape[1]
    widths = [g.shape[1] // 4 for g in grads]
    blocks = 4
    cols = wo.shape[1] // blocks
    dma = pltpu.SemaphoreType.DMA
    vmem = pl.BlockSpec(memory_space=pltpu.VMEM)
    anywhere = pl.BlockSpec(memory_space=pl.ANY)
    moving = lambda k: (0, k)
    return pl.pallas_call(
        functools.partial(attend_back_kernel, count),
        grid=(blocks,),
        out_shape=[
            jax.ShapeDtypeStruct((tokens, 3 * blocks * cols), jnp.bfloat16),
            jax.ShapeDtypeStruct((tokens, width), jnp.float32),
        ]
        + [jax.ShapeDtypeStruct((rows, w), jnp.float32) for w in widths]
        + [jax.ShapeDtypeStruct(parcel.shape, parcel.dtype)],
        in_specs=[
            vmem,
            pl.BlockSpec((width, 3 * cols), moving),
            pl.BlockSpec((width, cols), moving),
            pl.BlockSpec((tokens, 3 * cols), moving),
            pl.BlockSpec((1, 8, tokens), lambda k: (k, 0, 0)),
            vmem,
            vmem,
            vmem,
        ]
        + [anywhere] * (count + 1),
        out_specs=[pl.BlockSpec((tokens, 3 * cols), moving), vmem] + [vmem] * count + [anywhere],
        scratch_shapes=[
            pltpu.VMEM((tokens, cols), jnp.bfloat16),
            pltpu.VMEM((tokens, PAIR), jnp.float32),
            pltpu.VMEM((tokens, PAIR), jnp.float32),
            pltpu.VMEM((tokens, PAIR), jnp.float32),
        ]
        + scatter_scratch(rows, widths)
        + [dma((3,)), dma((3,)), dma(())],
        compiler_params=pltpu.CompilerParams(
            collective_id=3, has_side_effects=True, vmem_limit_bytes=66500000
        ),
        name="attend_back",
    )(grad, w_qkv, wo, joint, logs, cos_wide, sin_wide, bias_t, *views, parcel)


def feed_kernel(
    normed_ref, grad_ref, wg_ref, wu_ref, wd_ref, hidden_ref, dg_ref, du_ref, out_ref, back_ref
):
    normed = normed_ref[...]
    gate = dot_tt(normed, wg_ref[...], NORMAL)
    up = dot_tt(normed, wu_ref[...], NORMAL)
    hidden_grad = dot_tt(grad_ref[...], wd_ref[...], NORMAL)
    sigmoid = jax.nn.sigmoid(gate)
    silu = gate * sigmoid
    hidden_ref[...] = (silu * up).astype(jnp.bfloat16)
    du_ref[...] = (hidden_grad * silu).astype(jnp.bfloat16)
    dg_ref[...] = (hidden_grad * up * (sigmoid * (1.0 + gate * (1.0 - sigmoid)))).astype(
        jnp.bfloat16
    )
    out = dot_tt(hidden_ref[...], wd_ref[...], RIGHT_T)
    back = dot_tt(dg_ref[...], wg_ref[...], RIGHT_T) + dot_tt(du_ref[...], wu_ref[...], RIGHT_T)

    @pl.when(pl.program_id(0) == 0)
    def _():
        out_ref[...] = out
        back_ref[...] = back

    @pl.when(pl.program_id(0) > 0)
    def _():
        out_ref[...] += out
        back_ref[...] += back


def feed_forward(normed, grad, wg, wu, wd, block=1024):
    tokens, width = normed.shape
    units = wg.shape[1]
    fixed = pl.BlockSpec((tokens, width), lambda b: (0, 0))
    weight = pl.BlockSpec((width, block), lambda b: (0, b))
    moving = pl.BlockSpec((tokens, block), lambda b: (0, b))
    return pl.pallas_call(
        feed_kernel,
        grid=(units // block,),
        out_shape=[jax.ShapeDtypeStruct((tokens, units), jnp.bfloat16)] * 3
        + [jax.ShapeDtypeStruct((tokens, width), jnp.float32)] * 2,
        in_specs=[fixed, fixed, weight, weight, weight],
        out_specs=[moving, moving, moving, fixed, fixed],
        compiler_params=pltpu.CompilerParams(vmem_limit_bytes=60000000),
        name="feed_forward",
    )(normed, grad, wg, wu, wd)


def order_matrix(width):
    rows = width // 8
    d = lax.axis_index("dp")
    owner = jnp.concatenate([jnp.full((rows,), mask, jnp.int32) for mask in RELATIVE])
    feature = (d ^ owner) * rows + jnp.arange(width, dtype=jnp.int32) % rows
    return (jnp.arange(width, dtype=jnp.int32)[:, None] == feature[None, :]).astype(jnp.bfloat16)


def group_body(
    block_input,
    lengths,
    out_grad,
    w_query,
    w_key,
    w_value,
    w_out,
    w_gate,
    w_up,
    w_down,
    attn_gain,
    ffn_gain,
):
    micro, _, groups, width = block_input.shape
    unit_cols = w_query.shape[1]
    bf16 = jnp.bfloat16
    f32 = jnp.float32
    contract = ((1,), (0,))
    contract_t = ((1,), (1,))
    own_lengths = lax.dynamic_slice_in_dim(
        lengths.reshape(micro * groups, 3), lax.axis_index("tensor"), 1, 0
    )
    rows = attn_gain.shape[0]
    gain_tile = jnp.zeros((8, 256), f32).at[0, :rows].set(attn_gain).at[1, :rows].set(ffn_gain)
    w_qkv, wo, x_box, gain_box = gather_weights(
        (jnp.concatenate([w_query, w_key, w_value], axis=1), w_out.T),
        to_parcels(block_input),
        gain_tile,
        ((0, 1),),
    )
    gains = gain_box[:, :2, :rows].transpose(1, 0, 2).reshape(2, width)
    order = order_matrix(width)
    tokens_in = dot_tt(x_box.reshape(GTOK, width), order, contract)
    gain_one = gains[0]
    gain_two = gains[1]

    segment, cos_table, sin_table = layout_tables(own_lengths)
    seg = segment[:, 0]
    cos_wide = jnp.tile(cos_table[:, 0], (1, 4))
    sin_wide = jnp.tile(sin_table[:, 0], (1, 4))
    index = jnp.arange(GTOK, dtype=jnp.int32)
    allowed = (index[None, :] <= index[:, None]) & (
        (seg[None, :] == 0) | (seg[None, :] == seg[:, None])
    )
    bias = jnp.where(allowed, 0.0, MASKED).astype(f32)
    residual = tokens_in
    scale_one = rms_scale(residual)
    unit_one = residual * scale_one
    normed_one = (unit_one * gain_one).astype(bf16)
    joint, mix, logs, attn_sum, wg, wu, wd, dy_box = attend(
        normed_one,
        w_qkv,
        wo,
        cos_wide,
        sin_wide,
        bias,
        (w_gate, w_up, w_down.T),
        to_parcels(out_grad),
        ((0, 1), (2,)),
    )
    upstream = dot_tt(dy_box.reshape(GTOK, width), order, contract).astype(bf16)
    middle = residual + attn_sum
    scale_two = rms_scale(middle)
    unit_two = middle * scale_two
    normed_two = (unit_two * gain_two).astype(bf16)
    hidden, gate_grad, up_grad, ffn_sum, normed_two_grad = feed_forward(
        normed_two, upstream, wg, wu, wd
    )
    output = (middle + ffn_sum).astype(bf16)
    out_parcels = dot_tt(output, order, contract_t).astype(bf16).reshape(x_box.shape)
    gain_two_grad = jnp.sum(normed_two_grad * unit_two, axis=0)
    middle_grad = upstream.astype(f32) + norm_back(
        normed_two_grad, unit_two, gain_two, scale_two
    )
    attn_grad = middle_grad.astype(bf16)
    joint_grad, normed_one_grad, share_gate, share_up, out_box = attend_back(
        attn_grad,
        w_qkv,
        wo,
        joint,
        logs.transpose(0, 2, 1),
        cos_wide,
        sin_wide,
        bias.T,
        (grad_dot(normed_two, gate_grad), grad_dot(normed_two, up_grad)),
        out_parcels,
    )
    gain_one_grad = jnp.sum(normed_one_grad * unit_one, axis=0)
    input_grad = (
        middle_grad + norm_back(normed_one_grad, unit_one, gain_one, scale_one)
    ).astype(bf16)
    in_parcels = dot_tt(input_grad, order, contract_t).astype(bf16).reshape(x_box.shape)
    gain_parts = jnp.stack([gain_one_grad, gain_two_grad]).reshape(2, 8, rows).transpose(1, 0, 2)
    gain_parts = jnp.pad(gain_parts, ((0, 0), (0, 6), (0, 256 - rows)))
    share_joint, share_down, share_out, own_gains, in_box = scatter_grads(
        (
            grad_dot(normed_one, joint_grad),
            grad_dot(upstream, hidden),
            grad_dot(attn_grad, mix),
        ),
        gain_parts,
        in_parcels,
    )
    return (
        from_box(out_box, micro, groups),
        from_box(in_box, micro, groups),
        share_joint[:, :unit_cols],
        share_joint[:, unit_cols : 2 * unit_cols],
        share_joint[:, 2 * unit_cols :],
        share_out.T,
        share_gate,
        share_up,
        share_down.T,
        own_gains[0, :rows],
        own_gains[1, :rows],
    )


def body(*operands):
    micro, _, groups, _ = operands[0].shape
    if lax.axis_size("dp") == 8 and micro * groups == lax.axis_size("tensor") == 4:
        return group_body(*operands)
    return sharded_body(*operands)


def solution(mesh):
    placed = (
        P(None, "tensor", "dp", None),
        P(None, "dp", None),
        P(None, "tensor", "dp", None),
        P("dp", "tensor"),
        P("dp", "tensor"),
        P("dp", "tensor"),
        P("tensor", "dp"),
        P("dp", "tensor"),
        P("dp", "tensor"),
        P("tensor", "dp"),
        P("dp"),
        P("dp"),
    )
    return jax.shard_map(
        body,
        mesh=mesh,
        in_specs=placed,
        out_specs=(
            P(None, "tensor", "dp", None),
            P(None, "tensor", "dp", None),
            P("dp", "tensor"),
            P("dp", "tensor"),
            P("dp", "tensor"),
            P("tensor", "dp"),
            P("dp", "tensor"),
            P("dp", "tensor"),
            P("tensor", "dp"),
            P("dp"),
            P("dp"),
        ),
        check_vma=False,
    )
```

```python
import functools
import math

import jax
import jax.numpy as jnp
from jax import lax
from jax.experimental import pallas as pl
from jax.experimental.pallas import tpu as pltpu
from jax.sharding import PartitionSpec as P


HD = 64
GTOK = 512


EPSILON = 1e-05
MASKED = -1e30


def layout_tables(group_lengths):
    slot_index = jnp.arange(GTOK, dtype=jnp.int32)[:, None]
    prompt_len = group_lengths[:, 0][None, :]
    first_len = group_lengths[:, 1][None, :]
    segment = jnp.where(
        slot_index < prompt_len, 0, jnp.where(slot_index < prompt_len + first_len, 1, 2)
    ).astype(jnp.int32)
    position = jnp.where(segment == 2, slot_index - first_len, slot_index)
    frequency = jnp.exp(jnp.arange(HD // 2, dtype=jnp.float32) * (-2.0 * math.log(10000.0) / HD))
    angles = position.astype(jnp.float32)[:, :, None] * frequency
    return (segment, jnp.cos(angles), jnp.sin(angles))


def rotate(values, cos_table, sin_table):
    half_size = values.shape[-1] // 2
    first_half = values[..., :half_size]
    second_half = values[..., half_size:]
    cos_wide = cos_table[:, :, None, :]
    sin_wide = sin_table[:, :, None, :]
    return jnp.concatenate(
        [
            first_half * cos_wide - second_half * sin_wide,
            second_half * cos_wide + first_half * sin_wide,
        ],
        axis=-1,
    )


def rotate_back(values, cos_table, sin_table):
    half_size = values.shape[-1] // 2
    first_half = values[..., :half_size]
    second_half = values[..., half_size:]
    cos_wide = cos_table[:, :, None, :]
    sin_wide = sin_table[:, :, None, :]
    return jnp.concatenate(
        [
            first_half * cos_wide + second_half * sin_wide,
            second_half * cos_wide - first_half * sin_wide,
        ],
        axis=-1,
    )


def rms_scale(values):
    return lax.rsqrt(jnp.mean(values * values, axis=-1, keepdims=True) + EPSILON)


def norm_back(upstream, unit_rows, gain_row, scale_rows):
    scaled = upstream * gain_row
    return scale_rows * (scaled - unit_rows * jnp.mean(scaled * unit_rows, axis=-1, keepdims=True))


def attention_scores(queries, key_rows, allowed):
    scores = jnp.einsum(
        "tghe,sghe->ghts", queries, key_rows, preferred_element_type=jnp.float32
    ) * HD ** (-0.5)
    return jnp.where(allowed[:, None], scores, MASKED)


def add_tuples(first_set, second_set):
    return tuple((earlier + later for earlier, later in zip(first_set, second_set)))


def micro_step(inputs, group_lengths, upstream, gathered):
    w_query, w_key, w_value, w_out, w_gate, w_up, w_down, attn_gain, ffn_gain = gathered
    gain_one = attn_gain.astype(jnp.float32)
    gain_two = ffn_gain.astype(jnp.float32)
    group_count = inputs.shape[1]
    head_cols = w_query.shape[1]
    hidden_cols = w_gate.shape[1]
    shape_heads = (GTOK, group_count, head_cols // HD, HD)
    segment, cos_table, sin_table = layout_tables(group_lengths)
    token_index = jnp.arange(GTOK, dtype=jnp.int32)
    seg_groups = segment.T
    allowed = (token_index[None, None, :] <= token_index[None, :, None]) & (
        (seg_groups[:, None, :] == 0) | (seg_groups[:, None, :] == seg_groups[:, :, None])
    )
    residual = inputs.astype(jnp.float32)
    scale_one = rms_scale(residual)
    unit_one = residual * scale_one
    normed_one = (unit_one * gain_one).astype(jnp.bfloat16)
    normed_all = lax.all_gather(normed_one, "tensor", axis=0, tiled=True)
    w_joint = jnp.concatenate([w_query, w_key, w_value], axis=1)
    projected = jnp.einsum("tgd,dc->tgc", normed_all, w_joint, preferred_element_type=jnp.float32)
    queries = rotate(projected[..., :head_cols].reshape(shape_heads), cos_table, sin_table).astype(
        jnp.bfloat16
    )
    key_rows = rotate(
        projected[..., head_cols : 2 * head_cols].reshape(shape_heads), cos_table, sin_table
    ).astype(jnp.bfloat16)
    value_rows = projected[..., 2 * head_cols :].reshape(shape_heads).astype(jnp.bfloat16)
    scores = attention_scores(queries, key_rows, allowed)
    row_max = jnp.max(scores, axis=-1, keepdims=True)
    log_total = row_max + jnp.log(jnp.sum(jnp.exp(scores - row_max), axis=-1, keepdims=True))
    attn_probs = jnp.exp(scores - log_total).astype(jnp.bfloat16)
    attn_mix = (
        jnp.einsum("ghts,sghe->tghe", attn_probs, value_rows, preferred_element_type=jnp.float32)
        .astype(jnp.bfloat16)
        .reshape(GTOK, group_count, head_cols)
    )
    rows_here = attn_mix
    attn_sum = lax.psum_scatter(
        jnp.einsum("tgc,cd->tgd", rows_here, w_out, preferred_element_type=jnp.float32),
        "tensor",
        scatter_dimension=0,
        tiled=True,
    )
    middle = residual + attn_sum
    scale_two = rms_scale(middle)
    unit_two = middle * scale_two
    normed_two = (unit_two * gain_two).astype(jnp.bfloat16)
    normed_more = lax.all_gather(normed_two, "tensor", axis=0, tiled=True)
    w_gate_up = jnp.concatenate([w_gate, w_up], axis=1)
    gate_up = jnp.einsum("tgd,df->tgf", normed_more, w_gate_up, preferred_element_type=jnp.float32)
    gate_vals = gate_up[..., :hidden_cols]
    up_vals = gate_up[..., hidden_cols:]
    sigmoid_gate = jax.nn.sigmoid(gate_vals)
    silu_gate = gate_vals * sigmoid_gate
    hidden = (silu_gate * up_vals).astype(jnp.bfloat16)
    rows_here = hidden
    ffn_sum = lax.psum_scatter(
        jnp.einsum("tgf,fd->tgd", rows_here, w_down, preferred_element_type=jnp.float32).astype(
            jnp.bfloat16
        ),
        "tensor",
        scatter_dimension=0,
        tiled=True,
    ).astype(jnp.float32)
    output = (middle + ffn_sum).astype(jnp.bfloat16)
    upstream_all = lax.all_gather(upstream, "tensor", axis=0, tiled=True)
    hidden_grad = jnp.einsum(
        "tgd,fd->tgf", upstream_all, w_down, preferred_element_type=jnp.float32
    )
    grad_down = jnp.einsum("tgf,tgd->fd", hidden, upstream_all, preferred_element_type=jnp.float32)
    up_grad = hidden_grad * silu_gate
    gate_grad = hidden_grad * up_vals * (sigmoid_gate * (1.0 + gate_vals * (1.0 - sigmoid_gate)))
    gate_up_grad = jnp.concatenate([gate_grad, up_grad], axis=-1).astype(jnp.bfloat16)
    grad_gate_up = jnp.einsum(
        "tgd,tgf->df", normed_more, gate_up_grad, preferred_element_type=jnp.float32
    )
    rows_here = gate_up_grad
    normed_two_grad = lax.psum_scatter(
        jnp.einsum("tgf,df->tgd", rows_here, w_gate_up, preferred_element_type=jnp.float32).astype(
            jnp.bfloat16
        ),
        "tensor",
        scatter_dimension=0,
        tiled=True,
    ).astype(jnp.float32)
    gain_two_grad = jnp.sum(normed_two_grad * unit_two, axis=(0, 1))
    middle_grad = upstream.astype(jnp.float32) + norm_back(
        normed_two_grad, unit_two, gain_two, scale_two
    )
    attn_grad = middle_grad.astype(jnp.bfloat16)
    attn_grad_all = lax.all_gather(attn_grad, "tensor", axis=0, tiled=True)
    mix_grad = (
        jnp.einsum("tgd,cd->tgc", attn_grad_all, w_out, preferred_element_type=jnp.float32)
        .astype(jnp.bfloat16)
        .reshape(shape_heads)
    )
    grad_out = jnp.einsum(
        "tgc,tgd->cd", attn_mix, attn_grad_all, preferred_element_type=jnp.float32
    )
    scores_again = attention_scores(queries, key_rows, allowed)
    probs_full = jnp.exp(scores_again - log_total)
    prob_grad = jnp.einsum(
        "tghe,sghe->ghts", mix_grad, value_rows, preferred_element_type=jnp.float32
    )
    value_grad = jnp.einsum(
        "ghts,tghe->sghe",
        probs_full.astype(jnp.bfloat16),
        mix_grad,
        preferred_element_type=jnp.float32,
    )
    centre = jnp.sum(probs_full * prob_grad, axis=-1, keepdims=True)
    score_grad = (probs_full * (prob_grad - centre)).astype(jnp.bfloat16)
    query_grad = jnp.einsum(
        "ghts,sghe->tghe", score_grad, key_rows, preferred_element_type=jnp.float32
    ) * HD ** (-0.5)
    key_grad = jnp.einsum(
        "ghts,tghe->sghe", score_grad, queries, preferred_element_type=jnp.float32
    ) * HD ** (-0.5)
    flat_shape = (GTOK, group_count, head_cols)
    joint_grad = jnp.concatenate(
        [
            rotate_back(query_grad, cos_table, sin_table).reshape(flat_shape),
            rotate_back(key_grad, cos_table, sin_table).reshape(flat_shape),
            value_grad.reshape(flat_shape),
        ],
        axis=-1,
    ).astype(jnp.bfloat16)
    grad_joint = jnp.einsum(
        "tgd,tgc->dc", normed_all, joint_grad, preferred_element_type=jnp.float32
    )
    rows_here = joint_grad
    normed_one_grad = lax.psum_scatter(
        jnp.einsum("tgc,dc->tgd", rows_here, w_joint, preferred_element_type=jnp.float32).astype(
            jnp.bfloat16
        ),
        "tensor",
        scatter_dimension=0,
        tiled=True,
    ).astype(jnp.float32)
    gain_one_grad = jnp.sum(normed_one_grad * unit_one, axis=(0, 1))
    input_grad = (middle_grad + norm_back(normed_one_grad, unit_one, gain_one, scale_one)).astype(
        jnp.bfloat16
    )
    param_grads = (
        grad_joint[:, :head_cols],
        grad_joint[:, head_cols : 2 * head_cols],
        grad_joint[:, 2 * head_cols :],
        grad_out,
        grad_gate_up[:, :hidden_cols],
        grad_gate_up[:, hidden_cols:],
        grad_down,
        gain_one_grad,
        gain_two_grad,
    )
    return (output, input_grad, param_grads)


def sharded_body(
    block_input,
    lengths,
    out_grad,
    w_query,
    w_key,
    w_value,
    w_out,
    w_gate,
    w_up,
    w_down,
    attn_gain,
    ffn_gain,
):
    outputs = []
    input_grads = []
    totals = None
    shares = None
    for micro_index in range(block_input.shape[0]):
        gathered = (
            lax.all_gather(w_query, "dp", axis=0, tiled=True),
            lax.all_gather(w_key, "dp", axis=0, tiled=True),
            lax.all_gather(w_value, "dp", axis=0, tiled=True),
            lax.all_gather(w_out, "dp", axis=1, tiled=True),
            lax.all_gather(w_gate, "dp", axis=0, tiled=True),
            lax.all_gather(w_up, "dp", axis=0, tiled=True),
            lax.all_gather(w_down, "dp", axis=1, tiled=True),
            lax.all_gather(attn_gain, "dp", axis=0, tiled=True),
            lax.all_gather(ffn_gain, "dp", axis=0, tiled=True),
        )
        output, input_grad, param_grads = micro_step(
            block_input[micro_index], lengths[micro_index], out_grad[micro_index], gathered
        )
        outputs.append(output)
        input_grads.append(input_grad)
        totals = param_grads if totals is None else add_tuples(totals, param_grads)
    shares = (
        lax.psum_scatter(
            totals[0].astype(jnp.bfloat16), "dp", scatter_dimension=0, tiled=True
        ).astype(jnp.float32),
        lax.psum_scatter(
            totals[1].astype(jnp.bfloat16), "dp", scatter_dimension=0, tiled=True
        ).astype(jnp.float32),
        lax.psum_scatter(
            totals[2].astype(jnp.bfloat16), "dp", scatter_dimension=0, tiled=True
        ).astype(jnp.float32),
        lax.psum_scatter(
            totals[3].astype(jnp.bfloat16), "dp", scatter_dimension=1, tiled=True
        ).astype(jnp.float32),
        lax.psum_scatter(
            totals[4].astype(jnp.bfloat16), "dp", scatter_dimension=0, tiled=True
        ).astype(jnp.float32),
        lax.psum_scatter(
            totals[5].astype(jnp.bfloat16), "dp", scatter_dimension=0, tiled=True
        ).astype(jnp.float32),
        lax.psum_scatter(
            totals[6].astype(jnp.bfloat16), "dp", scatter_dimension=1, tiled=True
        ).astype(jnp.float32),
        lax.psum_scatter(
            totals[7].astype(jnp.bfloat16), "dp", scatter_dimension=0, tiled=True
        ).astype(jnp.float32),
        lax.psum_scatter(
            totals[8].astype(jnp.bfloat16), "dp", scatter_dimension=0, tiled=True
        ).astype(jnp.float32),
    )
    gain_one_total, gain_two_total = lax.psum((shares[7], shares[8]), "tensor")
    return (
        jnp.stack(outputs),
        jnp.stack(input_grads),
        shares[0],
        shares[1],
        shares[2],
        shares[3],
        shares[4],
        shares[5],
        shares[6],
        gain_one_total,
        gain_two_total,
    )


MESH = pl.DeviceIdType.MESH
RELATIVE = [4 * ((j // 2) % 2) + 2 * (j % 2) + j // 4 for j in range(8)]


def flip_core(d):
    return d + 1 - 2 * (d % 2)


def flip_x(d):
    return d + 2 - 4 * ((d // 2) % 2)


def flip_y(d):
    return d + 4 - 8 * ((d // 4) % 2)


def flip(d, mask):
    if mask & 1:
        d = flip_core(d)
    if mask & 2:
        d = flip_x(d)
    if mask & 4:
        d = flip_y(d)
    return d


def ring_next(z):
    return (2 * z + 1) % 5


def remote(src, dst, send_sem, recv_sem, peer):
    return pltpu.make_async_remote_copy(
        src_ref=src,
        dst_ref=dst,
        send_sem=send_sem,
        recv_sem=recv_sem,
        device_id=peer,
        device_id_type=MESH,
    )


def greet(d, z):
    barrier = pltpu.get_barrier_semaphore()
    for mask in range(1, 8):
        pl.semaphore_signal(barrier, inc=1, device_id=(flip(d, mask), z), device_id_type=MESH)
    for step in (1, 2, 3):
        pl.semaphore_signal(barrier, inc=1, device_id=(d, (z + step) % 4), device_id_type=MESH)
    pl.semaphore_wait(barrier, 10)


def gather_steps(sets, shards, fulls, sems, box_refs, gain_refs):
    count = len(shards)
    send_sem, recv_sem, local_sem = sems
    d = lax.axis_index("dp")
    z = lax.axis_index("tensor")
    place = {
        "z": (d, ring_next(z)),
        "x": (flip_x(d), z),
        "y": (flip_y(d), z),
        "c": (flip_core(d), z),
    }
    rows = shards[0].shape[0]

    def region(a, k, j, half):
        width = shards[a].shape[1]
        top, size = (j * rows, rows) if half is None else (j * rows + half * (rows // 2), rows // 2)
        return fulls[a].at[pl.ds(top, size), pl.ds(k * width, width)]

    sends = []

    def start(s, way, slot, src, dst, half=None):
        for a in sets[s]:
            source = shards[a] if src == (0, 0) else region(a, *src, half)
            remote(
                source,
                region(a, *dst, half),
                send_sem.at[s, slot],
                recv_sem.at[s, slot],
                place[way],
            ).start()
        sends.append((s, slot, half))

    def bulk(s, slot, half):
        arrs = sets[s]
        size = rows if half is None else rows // 2
        width = sum(shards[a].shape[1] for a in arrs)
        part = fulls[arrs[0]].at[pl.ds(0, size), pl.ds(0, width)]
        return remote(part, part, send_sem.at[s, slot], recv_sem.at[s, slot], place["c"])

    def arrived(s, slot, half=None):
        bulk(s, slot, half).wait_recv()

    ring_slot, x_slot, y_slot, x_relay, y_relay, core_slot = 0, 3, 7, 11, 15, 19

    def core(s, k, j):
        start(s, "c", core_slot + 4 * k + j, (k, j), (k, 4 + j))

    def ring_step(s, k):
        start(s, "z", ring_slot + k, (k, 0), (k + 1, 0))

    def open_unit(s, k):
        if k > 0:
            arrived(s, ring_slot + k - 1)
            if k < 3:
                ring_step(s, k)
        start(s, "x", x_slot + k, (k, 0), (k, 1))
        start(s, "y", y_slot + k, (k, 0), (k, 2))
        core(s, k, 0)

    def close_unit(s, k):
        arrived(s, x_slot + k)
        start(s, "y", y_relay + k, (k, 1), (k, 3), 1)
        core(s, k, 1)
        arrived(s, y_slot + k)
        start(s, "x", x_relay + k, (k, 2), (k, 3), 0)
        core(s, k, 2)

    def last_part(s, k):
        arrived(s, x_relay + k, 0)
        arrived(s, y_relay + k, 1)
        core(s, k, 3)

    def own_copies():
        for a in range(count):
            yield pltpu.make_async_copy(shards[a], region(a, 0, 0, None), local_sem.at[a])
        parcel, box = box_refs[:2]
        yield pltpu.make_async_copy(parcel.at[z], box.at[z], local_sem.at[count])
        if gain_refs:
            gains, gain_box = gain_refs[:2]
            yield pltpu.make_async_copy(gains, gain_box.at[0], local_sem.at[count + 1])

    def box_copy(step):
        parcel, box, box_send, box_recv = box_refs
        other = (z + step) % 4
        return remote(
            parcel.at[other],
            box.at[z],
            box_send.at[step - 1],
            box_recv.at[step - 1],
            (d, other),
        )

    def gain_copy(j):
        gains, gain_box, gain_send, gain_recv = gain_refs
        return remote(
            gains,
            gain_box.at[j],
            gain_send.at[j - 1],
            gain_recv.at[j - 1],
            (flip(d, RELATIVE[j]), z),
        )

    units = [(s, k) for s in range(len(sets)) for k in range(4)]

    def run(i):
        if i == 0:
            greet(d, z)
            if gain_refs:
                for j in range(1, 8):
                    gain_copy(j).start()
            for copy in own_copies():
                copy.start()
            ring_step(0, 0)
            open_unit(*units[0])
        if i < len(units):
            if i + 1 < len(units):
                after = units[i + 1]
                if after[1] == 0:
                    ring_step(after[0], 0)
                open_unit(*after)
            if i < 3:
                box_copy(i + 1).start()
            close_unit(*units[i])
        if i > 0:
            last_part(*units[i - 1])
        if i == len(units):
            end()

    def end():
        for s in range(len(sets)):
            for slot in range(core_slot, core_slot + 16):
                arrived(s, slot)
        for step in (1, 2, 3):
            box_copy(step).wait()
        if gain_refs:
            for j in range(1, 8):
                gain_copy(j).wait()
        for s, slot, half in sends:
            bulk(s, slot, half).wait_send()
        for copy in own_copies():
            copy.wait()

    return [functools.partial(run, i) for i in range(len(units) + 1)]


def gather_scratch(sets, count, gains):
    dma = pltpu.SemaphoreType.DMA
    sems = [dma((len(sets), 35)), dma((len(sets), 35)), dma((count + 2,)), dma((3,)), dma((3,))]
    return sems + ([dma((7,)), dma((7,))] if gains else [])


def gather_shapes(shards):
    return [jax.ShapeDtypeStruct((8 * w.shape[0], 4 * w.shape[1]), w.dtype) for w in shards]


def gather_kernel(sets, count, *refs):
    shards = refs[:count]
    parcel, gains = refs[count : count + 2]
    fulls = refs[count + 2 : 2 * count + 2]
    box, gain_box = refs[2 * count + 2 : 2 * count + 4]
    send_sem, recv_sem, local_sem, box_send, box_recv, *gain_sems = refs[2 * count + 4 :]
    for step in gather_steps(
        sets,
        shards,
        fulls,
        (send_sem, recv_sem, local_sem),
        (parcel, box, box_send, box_recv),
        (gains, gain_box, *gain_sems),
    ):
        step()


def gather_weights(shards, parcel, gains, sets):
    count = len(shards)
    vmem = pl.BlockSpec(memory_space=pltpu.VMEM)
    anywhere = pl.BlockSpec(memory_space=pl.ANY)
    return pl.pallas_call(
        functools.partial(gather_kernel, sets, count),
        out_shape=gather_shapes(shards)
        + [jax.ShapeDtypeStruct(parcel.shape, parcel.dtype)]
        + [jax.ShapeDtypeStruct((8, *gains.shape), gains.dtype)],
        in_specs=[vmem] * (count + 2),
        out_specs=[anywhere] * (count + 2),
        scratch_shapes=gather_scratch(sets, count, True),
        compiler_params=pltpu.CompilerParams(collective_id=1, has_side_effects=True),
        name="gather_weights",
    )(*shards, parcel, gains)


def add_rows(target, first, second, chunk=32):
    rows = target.shape[0]

    def step(i, carry):
        at = pl.ds(pl.multiple_of(i * chunk, chunk), chunk)
        target[at, :] = (
            first[at, :].astype(jnp.float32) + second[at, :].astype(jnp.float32)
        ).astype(target.dtype)
        return carry

    lax.fori_loop(0, rows // chunk, step, 0)


def scatter_steps(grads, width, shares, buffers, gain_refs, box_refs, staging=None):
    count = len(grads)
    from_core, from_first, from_second, from_ring = (
        buffers[i * count : (i + 1) * count] for i in range(4)
    )
    total, middle, final, send_sem, recv_sem, load_sem = buffers[4 * count :]
    d = lax.axis_index("dp")
    z = lax.axis_index("tensor")
    core, east, north = (flip_core(d), z), (flip_x(d), z), (flip_y(d), z)
    onward = (d, ring_next(z))
    rows = total.shape[2]
    half = rows // 2
    units = [(g, k) for g in range(count) for k in (1, 2, 3, 0)]

    def send(src, dst, u, slot, peer):
        return remote(src, dst, send_sem.at[u, slot], recv_sem.at[u, slot], peer)

    def gain_copy(j):
        gains, _, gain_box, _, gain_send, gain_recv = gain_refs
        return remote(
            gains.at[j],
            gain_box.at[j],
            gain_send.at[j - 1],
            gain_recv.at[j - 1],
            (flip(d, RELATIVE[j]), z),
        )

    def line_copy(step):
        _, _, _, gain_line, gain_send, gain_recv = gain_refs
        return remote(
            gain_line.at[z],
            gain_line.at[z],
            gain_send.at[6 + step],
            gain_recv.at[6 + step],
            (d, (z + step) % 4),
        )

    def box_copy(step):
        parcel, box, box_send, box_recv, _ = box_refs
        other = (z + step) % 4
        return remote(
            parcel.at[other],
            box.at[z],
            box_send.at[step - 1],
            box_recv.at[step - 1],
            (d, other),
        )

    def own_copy():
        parcel, box, _, _, box_own = box_refs
        return pltpu.make_async_copy(parcel.at[z], box.at[z], box_own)

    def columns(u):
        g, k = units[u]
        return pl.ds(k * width[g], width[g])

    def to_core(u):
        g, k = units[u]
        if staging:
            source = staging[1].at[u % 2, :, :, pl.ds(0, width[g])]
        else:
            source = grads[g].at[pl.ds(4, 4), :, columns(u)]
        return send(source, from_core[g].at[k], u, 0, core)

    def load_right(u):
        g, _ = units[u]
        return pltpu.make_async_copy(
            grads[g][1].at[:, columns(u)],
            staging[0].at[u % 2, :, pl.ds(0, width[g])],
            staging[2].at[u % 2],
        )

    def multiply(u, target, first):
        g, _ = units[u]
        cols = slice(0, width[g])
        for pair in range(2):
            at = slice((first + 2 * pair) * rows, (first + 2 * pair + 2) * rows)
            part = dot_tt(grads[g][0][:, at], staging[0][u % 2, :, cols], ((0,), (0,)))
            target[2 * pair : 2 * pair + 2, :, cols] = part.astype(jnp.bfloat16).reshape(
                2, rows, width[g]
            )

    def far_half(u):
        load_right(u).wait()
        if u >= 2:
            to_core(u - 2).wait_send()
        multiply(u, staging[1].at[u % 2], 4)
        to_core(u).start()

    def near_half(u):
        multiply(u, total.at[u % 3], 0)
        if u + 2 < len(units):
            load_right(u + 2).start()

    def load(u):
        g, _ = units[u]
        return pltpu.make_async_copy(
            grads[g].at[pl.ds(0, 4), :, columns(u)],
            total.at[u % 3, :, :, pl.ds(0, width[g])],
            load_sem.at[u % 3],
        )

    def first_sends(u):
        g, k = units[u]
        t = total.at[u % 3]
        cols = pl.ds(0, width[g])
        return [
            send(t.at[1, pl.ds(0, half), cols], from_first[g].at[k, 0, 0], u, 1, east),
            send(t.at[3, pl.ds(0, half), cols], from_first[g].at[k, 0, 1], u, 2, east),
            send(t.at[2, pl.ds(half, half), cols], from_first[g].at[k, 1, 0], u, 3, north),
            send(t.at[3, pl.ds(half, half), cols], from_first[g].at[k, 1, 1], u, 4, north),
        ]

    def second_sends(u):
        g, k = units[u]
        m = middle.at[u % 2]
        cols = pl.ds(0, width[g])
        return [
            send(m.at[0, :, cols], from_second[g].at[k, 0], u, 5, north),
            send(m.at[1, :, cols], from_second[g].at[k, 1], u, 6, east),
        ]

    def ring_send(u):
        g, k = units[u]
        return send(
            final.at[u % 2, :, pl.ds(0, width[g])], from_ring[g].at[k], u, 7, onward
        )

    def first_stage(u):
        g, k = units[u]
        t = total.at[u % 3]
        cols = pl.ds(0, width[g])
        if not staging:
            load(u).wait()
        to_core(u).wait_recv()
        for j in range(4):
            part = t.at[j, :, cols]
            add_rows(part, part, from_core[g].at[k, j])
        for copy in first_sends(u):
            copy.start()

    def second_stage(u):
        g, k = units[u]
        t = total.at[u % 3]
        m = middle.at[u % 2]
        cols = pl.ds(0, width[g])
        if u >= 2:
            for copy in second_sends(u - 2):
                copy.wait_send()
        sends = first_sends(u)
        sends[1].wait_recv()
        add_rows(m.at[0, :, cols], t.at[2, pl.ds(0, half), cols], from_first[g].at[k, 0, 1])
        sends[3].wait_recv()
        add_rows(m.at[1, :, cols], t.at[1, pl.ds(half, half), cols], from_first[g].at[k, 1, 1])
        for copy in second_sends(u):
            copy.start()
        sends[0].wait_recv()
        upper = t.at[0, pl.ds(0, half), cols]
        add_rows(upper, upper, from_first[g].at[k, 0, 0])
        sends[2].wait_recv()
        lower = t.at[0, pl.ds(half, half), cols]
        add_rows(lower, lower, from_first[g].at[k, 1, 0])

    def third_stage(u):
        g, k = units[u]
        t = total.at[u % 3]
        cols = pl.ds(0, width[g])
        for side, copy in enumerate(second_sends(u)):
            copy.wait_recv()
            part = t.at[0, pl.ds(side * half, half), cols]
            if k == 1:
                if side == 0 and u >= 2:
                    wait_ring(u - 2)
                add_rows(
                    final.at[u % 2, pl.ds(side * half, half), cols],
                    part,
                    from_second[g].at[k, side],
                )
            else:
                add_rows(part, part, from_second[g].at[k, side])
        if k != 1:
            ring_send(u - 1).wait_recv()
            if u >= 2:
                wait_ring(u - 2)
            if k == 0:
                add_rows(shares[g], t.at[0, :, cols], from_ring[g].at[3])
            else:
                add_rows(final.at[u % 2, :, cols], t.at[0, :, cols], from_ring[g].at[k - 1])
        if k != 0:
            ring_send(u).start()
        for copy in first_sends(u):
            copy.wait_send()

    def wait_ring(u):
        if units[u][1] != 0:
            ring_send(u).wait_send()

    n = len(units)

    def begin():
        greet(d, z)
        if gain_refs:
            for j in range(1, 8):
                gain_copy(j).start()
        own_copy().start()
        for hop in (1, 2, 3):
            box_copy(hop).start()
        if staging:
            load_right(0).start()
            load_right(1).start()
            far_half(0)
            near_half(0)
            far_half(1)
        else:
            for u in range(n):
                to_core(u).start()
                if u < 3:
                    load(u).start()

    def run(step):
        if step == 0:
            begin()
        if step < n:
            first_stage(step)
        if 0 <= step - 1 < n:
            second_stage(step - 1)
        if 0 <= step - 2:
            third_stage(step - 2)
            if step + 1 < n and not staging:
                load(step + 1).start()
        if staging and step + 1 < n:
            near_half(step + 1)
            if step + 2 < n:
                far_half(step + 2)
        if step == 2 and gain_refs:
            gains, _, gain_box, gain_line, _, _ = gain_refs
            for j in range(1, 8):
                gain_copy(j).wait()
            gain_line[z] = gains[0] + sum(gain_box[j] for j in range(1, 8))
            for hop in (1, 2, 3):
                line_copy(hop).start()
        if step == n + 1:
            end()

    def end():
        if gain_refs:
            _, gain_share, _, gain_line, _, _ = gain_refs
            for hop in (1, 2, 3):
                line_copy(hop).wait()
            gain_share[...] = gain_line[0] + gain_line[1] + gain_line[2] + gain_line[3]
        for hop in (1, 2, 3):
            box_copy(hop).wait()
        own_copy().wait()
        for u in range(n):
            if u >= n - 2 or not staging:
                to_core(u).wait_send()
            if u >= n - 2:
                for copy in second_sends(u):
                    copy.wait_send()
                wait_ring(u)

    return [functools.partial(run, step) for step in range(n + 2)]


def scatter_scratch(rows, widths):
    bf16 = jnp.bfloat16
    half = rows // 2
    widest = max(widths)
    dma = pltpu.SemaphoreType.DMA
    return (
        [pltpu.VMEM((4, 4, rows, w), bf16) for w in widths]
        + [pltpu.VMEM((4, 2, 2, half, w), bf16) for w in widths]
        + [pltpu.VMEM((4, 2, half, w), bf16) for w in widths]
        + [pltpu.VMEM((4, rows, w), bf16) for w in widths]
        + [
            pltpu.VMEM((3, 4, rows, widest), bf16),
            pltpu.VMEM((2, 2, half, widest), bf16),
            pltpu.VMEM((2, rows, widest), bf16),
            dma((4 * len(widths), 8)),
            dma((4 * len(widths), 8)),
            dma((3,)),
        ]
    )


def scatter_kernel(width, *refs):
    count = len(width)
    grads = [(refs[g], refs[count + g]) for g in range(count)]
    refs = refs[2 * count :]
    gains, parcel = refs[:2]
    shares = refs[2 : count + 2]
    gain_share, box = refs[count + 2 : count + 4]
    rest = refs[count + 4 :]
    buffers = rest[: 4 * count + 6]
    gain_box, gain_line, gain_send, gain_recv = rest[4 * count + 6 : 4 * count + 10]
    box_sems = rest[4 * count + 10 : 4 * count + 13]
    for step in scatter_steps(
        grads,
        width,
        shares,
        buffers,
        (gains, gain_share, gain_box, gain_line, gain_send, gain_recv),
        (parcel, box, *box_sems),
        rest[4 * count + 13 :],
    ):
        step()


def scatter_grads(pairs, gains, parcel):
    lefts = [left for left, _ in pairs]
    rights = [right for _, right in pairs]
    tokens = lefts[0].shape[0]
    rows = lefts[0].shape[1] // 8
    widths = [right.shape[1] // 4 for right in rights]
    widest = max(widths)
    count = len(pairs)
    dma = pltpu.SemaphoreType.DMA
    vmem = pl.BlockSpec(memory_space=pltpu.VMEM)
    anywhere = pl.BlockSpec(memory_space=pl.ANY)
    return pl.pallas_call(
        functools.partial(scatter_kernel, widths),
        out_shape=[jax.ShapeDtypeStruct((rows, w), jnp.float32) for w in widths]
        + [jax.ShapeDtypeStruct(gains.shape[1:], jnp.float32)]
        + [jax.ShapeDtypeStruct(parcel.shape, parcel.dtype)],
        in_specs=[vmem] * count + [anywhere] * count + [vmem] * 2,
        out_specs=[vmem] * (count + 1) + [anywhere],
        scratch_shapes=scatter_scratch(rows, widths)
        + [
            pltpu.VMEM(gains.shape, jnp.float32),
            pltpu.VMEM((4, *gains.shape[1:]), jnp.float32),
            dma((10,)),
            dma((10,)),
            dma((3,)),
            dma((3,)),
            dma(()),
            pltpu.VMEM((2, tokens, widest), jnp.bfloat16),
            pltpu.VMEM((2, 4, rows, widest), jnp.bfloat16),
            dma((2,)),
        ],
        compiler_params=pltpu.CompilerParams(
            collective_id=2, has_side_effects=True, vmem_limit_bytes=66000000
        ),
        name="scatter_grads",
    )(*lefts, *rights, gains, parcel)


def grad_dot(left, right):
    return dot_tt(left, right, ((0,), (0,))).astype(jnp.bfloat16)


def to_parcels(values):
    micro, rows, groups, width = values.shape
    return values.transpose(0, 2, 1, 3).reshape(micro * groups, rows, width)


def from_box(box, micro, groups):
    return box.reshape(micro, groups, *box.shape[1:]).transpose(0, 2, 1, 3)


def dot_tt(left, right, dims):
    return lax.dot_general(left, right, (dims, ((), ())), preferred_element_type=jnp.float32)


ROWS = 128
PAIR = 2 * HD
NORMAL = ((1,), (0,))
RIGHT_T = ((1,), (1,))
LEFT_T = ((0,), (0,))


def head_masks(scale):
    lane = lax.broadcasted_iota(jnp.int32, (1, PAIR), 1)
    return [jnp.where((lane // HD) == h, scale, 0.0).astype(jnp.bfloat16) for h in range(2)]


def spin(values, cos_table, sin_table, sign):
    lane = lax.broadcasted_iota(jnp.int32, values.shape, 1)
    ahead = pltpu.roll(values, PAIR - HD // 2, 1)
    behind = pltpu.roll(values, HD // 2, 1)
    turned = jnp.where(lane % HD < HD // 2, -ahead, behind)
    return values * cos_table + (sign * turned) * sin_table


def attend_kernel(sets, count, normed_ref, w_ref, wo_ref, cos_ref, sin_ref, bias_ref, *refs):
    shards = refs[:count]
    parcel, joint_ref, mix_ref, log_ref, sum_ref = refs[count : count + 5]
    fulls = refs[count + 5 : 2 * count + 5]
    box, proj_ref, send_sem, recv_sem, local_sem, box_send, box_recv = refs[2 * count + 5 :]
    turns = gather_steps(
        sets,
        shards,
        fulls,
        (send_sem, recv_sem, local_sem),
        (parcel, box, box_send, box_recv),
        None,
    )
    phase = pl.program_id(0)

    def talk(slot):
        for p in range(4):
            if slot == 0 or p < 2:

                @pl.when(phase == p)
                def _():
                    turns[p + min(p, 2) + slot]()

    talk(0)
    tokens = normed_ref.shape[0]
    cols = wo_ref.shape[1]
    pairs = cols // PAIR
    proj_ref[...] = dot_tt(normed_ref[...], w_ref[...], NORMAL)
    for c in range(3 * pairs):
        at = slice(c * PAIR, (c + 1) * PAIR)
        part = proj_ref[:, at]
        if c < 2 * pairs:
            part = spin(part, cos_ref[...], sin_ref[...], 1.0)
        joint_ref[:, at] = part.astype(jnp.bfloat16)
    masks = head_masks(HD ** (-0.5))
    lane = lax.broadcasted_iota(jnp.int32, (ROWS, PAIR), 1)
    for pair in range(pairs):
        if pair == 1:
            talk(1)
        for i in range(tokens // ROWS):
            rows = slice(i * ROWS, (i + 1) * ROWS)
            size = (i + 1) * ROWS
            q = joint_ref[rows, pair * PAIR : (pair + 1) * PAIR]
            k = joint_ref[:size, cols + pair * PAIR : cols + (pair + 1) * PAIR]
            v = joint_ref[:size, 2 * cols + pair * PAIR : 2 * cols + (pair + 1) * PAIR]
            both = jnp.concatenate([q * masks[0], q * masks[1]], axis=0)
            bias = bias_ref[rows, :size]
            scores = dot_tt(both, k, RIGHT_T) + jnp.concatenate([bias, bias], axis=0)
            top = jnp.max(scores, axis=1, keepdims=True)
            powers = jnp.exp(scores - top)
            norm = jnp.sum(powers, axis=1, keepdims=True)
            probs = (powers * (1.0 / norm)).astype(jnp.bfloat16)
            mixed = dot_tt(probs, v, NORMAL)
            mix_ref[rows, pair * PAIR : (pair + 1) * PAIR] = jnp.where(
                lane < HD, mixed[:ROWS], mixed[ROWS:]
            ).astype(jnp.bfloat16)
            log_norm = top + jnp.log(norm)
            log_ref[0, rows, 2 * pair : 2 * pair + 1] = log_norm[:ROWS]
            log_ref[0, rows, 2 * pair + 1 : 2 * pair + 2] = log_norm[ROWS:]
    projected = dot_tt(mix_ref[...], wo_ref[...], RIGHT_T)

    @pl.when(phase == 0)
    def _():
        sum_ref[...] = projected

    @pl.when(phase > 0)
    def _():
        sum_ref[...] += projected

    @pl.when(phase == 3)
    def _():
        for step in turns[6:]:
            step()


def attend(normed, w_qkv, wo, cos_wide, sin_wide, bias, shards, parcel, sets):
    tokens, width = normed.shape
    count = len(shards)
    blocks = 4
    cols = wo.shape[1] // blocks
    vmem = pl.BlockSpec(memory_space=pltpu.VMEM)
    anywhere = pl.BlockSpec(memory_space=pl.ANY)
    moving = lambda k: (0, k)
    return pl.pallas_call(
        functools.partial(attend_kernel, sets, count),
        grid=(blocks,),
        out_shape=[
            jax.ShapeDtypeStruct((tokens, 3 * blocks * cols), jnp.bfloat16),
            jax.ShapeDtypeStruct((tokens, blocks * cols), jnp.bfloat16),
            jax.ShapeDtypeStruct((blocks, tokens, 8), jnp.float32),
            jax.ShapeDtypeStruct((tokens, width), jnp.float32),
        ]
        + gather_shapes(shards)
        + [jax.ShapeDtypeStruct(parcel.shape, parcel.dtype)],
        in_specs=[
            vmem,
            pl.BlockSpec((width, 3 * cols), moving),
            pl.BlockSpec((width, cols), moving),
            vmem,
            vmem,
            vmem,
        ]
        + [vmem] * (count + 1),
        out_specs=[
            pl.BlockSpec((tokens, 3 * cols), moving),
            pl.BlockSpec((tokens, cols), moving),
            pl.BlockSpec((1, tokens, 8), lambda k: (k, 0, 0)),
            vmem,
        ]
        + [anywhere] * (count + 1),
        scratch_shapes=[pltpu.VMEM((tokens, 3 * cols), jnp.float32)]
        + gather_scratch(sets, count, False),
        compiler_params=pltpu.CompilerParams(
            collective_id=4, has_side_effects=True, vmem_limit_bytes=60000000
        ),
        name="attend",
    )(normed, w_qkv, wo, cos_wide, sin_wide, bias, *shards, parcel)


def attend_back_kernel(
    count,
    grad_ref,
    w_ref,
    wo_ref,
    joint_ref,
    log_ref,
    cos_ref,
    sin_ref,
    bias_ref,
    *refs,
):
    grads = refs[:count]
    parcel, out_ref, sum_ref = refs[count : count + 3]
    shares = refs[count + 3 : 2 * count + 3]
    box, mix_grad, q_grad, k_grad, v_grad = refs[2 * count + 3 : 2 * count + 8]
    buffers = refs[2 * count + 8 : 6 * count + 14]
    box_sems = refs[6 * count + 14 :]
    width = [share.shape[1] for share in shares]
    turns = scatter_steps(grads, width, shares, buffers, None, (parcel, box, *box_sems))
    phase = pl.program_id(0)

    def talk(slot):
        for p in range(4):
            if slot == 0 or p < 2:

                @pl.when(phase == p)
                def _():
                    turns[p + min(p, 2) + slot]()

    tokens = grad_ref.shape[0]
    cols = wo_ref.shape[1]
    pairs = cols // PAIR
    talk(0)
    mix_grad[...] = dot_tt(grad_ref[...], wo_ref[...], NORMAL).astype(jnp.bfloat16)
    scale = HD ** (-0.5)
    masks = head_masks(scale)
    ones = head_masks(1.0)
    lane = lax.broadcasted_iota(jnp.int32, (ROWS, PAIR), 1)
    last = tokens // ROWS - 1
    for pair in range(pairs):
        if pair == 1:
            talk(1)
        for i in range(last, -1, -1):
            rows = slice(i * ROWS, (i + 1) * ROWS)
            size = (i + 1) * ROWS
            q = joint_ref[rows, pair * PAIR : (pair + 1) * PAIR]
            k = joint_ref[:size, cols + pair * PAIR : cols + (pair + 1) * PAIR]
            v = joint_ref[:size, 2 * cols + pair * PAIR : 2 * cols + (pair + 1) * PAIR]
            g = mix_grad[rows, pair * PAIR : (pair + 1) * PAIR]
            q_both = jnp.concatenate([q * masks[0], q * masks[1]], axis=0)
            g_both = jnp.concatenate([g * ones[0], g * ones[1]], axis=0)
            bias = bias_ref[:size, rows]
            logs = jnp.concatenate(
                [log_ref[0, 2 * pair : 2 * pair + 1, rows], log_ref[0, 2 * pair + 1 : 2 * pair + 2, rows]],
                axis=1,
            )
            scores = dot_tt(k, q_both, RIGHT_T) + jnp.concatenate([bias, bias], axis=1)
            probs = jnp.exp(scores - logs)
            prob_grad = dot_tt(v, g_both, RIGHT_T)
            centre = jnp.sum(probs * prob_grad, axis=0, keepdims=True)
            score_grad = (probs * (prob_grad - centre)).astype(jnp.bfloat16)
            k_part = dot_tt(score_grad, q_both, NORMAL)
            v_part = dot_tt(probs.astype(jnp.bfloat16), g_both, NORMAL)
            if i == last:
                k_grad[...] = k_part
                v_grad[...] = v_part
            else:
                k_grad[:size, :] += k_part
                v_grad[:size, :] += v_part
            q_part = dot_tt(score_grad, k, LEFT_T)
            q_grad[rows, :] = jnp.where(lane < HD, q_part[:ROWS], q_part[ROWS:]) * scale
        cos_table = cos_ref[...]
        sin_table = sin_ref[...]
        out_ref[:, pair * PAIR : (pair + 1) * PAIR] = spin(
            q_grad[...], cos_table, sin_table, -1.0
        ).astype(jnp.bfloat16)
        out_ref[:, cols + pair * PAIR : cols + (pair + 1) * PAIR] = spin(
            k_grad[...], cos_table, sin_table, -1.0
        ).astype(jnp.bfloat16)
        out_ref[:, 2 * cols + pair * PAIR : 2 * cols + (pair + 1) * PAIR] = v_grad[...].astype(
            jnp.bfloat16
        )
    projected = dot_tt(out_ref[...], w_ref[...], RIGHT_T)

    @pl.when(phase == 0)
    def _():
        sum_ref[...] = projected

    @pl.when(phase > 0)
    def _():
        sum_ref[...] += projected

    @pl.when(phase == 3)
    def _():
        for step in turns[6:]:
            step()


def attend_back(grad, w_qkv, wo, joint, logs, cos_wide, sin_wide, bias_t, grads, parcel):
    tokens, width = grad.shape
    count = len(grads)
    views = [g.reshape(8, g.shape[0] // 8, g.shape[1]) for g in grads]
    rows = views[0].shape[1]
    widths = [g.shape[1] // 4 for g in grads]
    blocks = 4
    cols = wo.shape[1] // blocks
    dma = pltpu.SemaphoreType.DMA
    vmem = pl.BlockSpec(memory_space=pltpu.VMEM)
    anywhere = pl.BlockSpec(memory_space=pl.ANY)
    moving = lambda k: (0, k)
    return pl.pallas_call(
        functools.partial(attend_back_kernel, count),
        grid=(blocks,),
        out_shape=[
            jax.ShapeDtypeStruct((tokens, 3 * blocks * cols), jnp.bfloat16),
            jax.ShapeDtypeStruct((tokens, width), jnp.float32),
        ]
        + [jax.ShapeDtypeStruct((rows, w), jnp.float32) for w in widths]
        + [jax.ShapeDtypeStruct(parcel.shape, parcel.dtype)],
        in_specs=[
            vmem,
            pl.BlockSpec((width, 3 * cols), moving),
            pl.BlockSpec((width, cols), moving),
            pl.BlockSpec((tokens, 3 * cols), moving),
            pl.BlockSpec((1, 8, tokens), lambda k: (k, 0, 0)),
            vmem,
            vmem,
            vmem,
        ]
        + [anywhere] * (count + 1),
        out_specs=[pl.BlockSpec((tokens, 3 * cols), moving), vmem] + [vmem] * count + [anywhere],
        scratch_shapes=[
            pltpu.VMEM((tokens, cols), jnp.bfloat16),
            pltpu.VMEM((tokens, PAIR), jnp.float32),
            pltpu.VMEM((tokens, PAIR), jnp.float32),
            pltpu.VMEM((tokens, PAIR), jnp.float32),
        ]
        + scatter_scratch(rows, widths)
        + [dma((3,)), dma((3,)), dma(())],
        compiler_params=pltpu.CompilerParams(
            collective_id=3, has_side_effects=True, vmem_limit_bytes=66500000
        ),
        name="attend_back",
    )(grad, w_qkv, wo, joint, logs, cos_wide, sin_wide, bias_t, *views, parcel)


def feed_kernel(
    normed_ref, grad_ref, wg_ref, wu_ref, wd_ref, hidden_ref, dg_ref, du_ref, out_ref, back_ref
):
    normed = normed_ref[...]
    gate = dot_tt(normed, wg_ref[...], NORMAL)
    up = dot_tt(normed, wu_ref[...], NORMAL)
    hidden_grad = dot_tt(grad_ref[...], wd_ref[...], NORMAL)
    sigmoid = jax.nn.sigmoid(gate)
    silu = gate * sigmoid
    hidden_ref[...] = (silu * up).astype(jnp.bfloat16)
    du_ref[...] = (hidden_grad * silu).astype(jnp.bfloat16)
    dg_ref[...] = (hidden_grad * up * (sigmoid * (1.0 + gate * (1.0 - sigmoid)))).astype(
        jnp.bfloat16
    )
    out = dot_tt(hidden_ref[...], wd_ref[...], RIGHT_T)
    back = dot_tt(dg_ref[...], wg_ref[...], RIGHT_T) + dot_tt(du_ref[...], wu_ref[...], RIGHT_T)

    @pl.when(pl.program_id(0) == 0)
    def _():
        out_ref[...] = out
        back_ref[...] = back

    @pl.when(pl.program_id(0) > 0)
    def _():
        out_ref[...] += out
        back_ref[...] += back


def feed_forward(normed, grad, wg, wu, wd, block=1024):
    tokens, width = normed.shape
    units = wg.shape[1]
    fixed = pl.BlockSpec((tokens, width), lambda b: (0, 0))
    weight = pl.BlockSpec((width, block), lambda b: (0, b))
    moving = pl.BlockSpec((tokens, block), lambda b: (0, b))
    return pl.pallas_call(
        feed_kernel,
        grid=(units // block,),
        out_shape=[jax.ShapeDtypeStruct((tokens, units), jnp.bfloat16)] * 3
        + [jax.ShapeDtypeStruct((tokens, width), jnp.float32)] * 2,
        in_specs=[fixed, fixed, weight, weight, weight],
        out_specs=[moving, moving, moving, fixed, fixed],
        compiler_params=pltpu.CompilerParams(vmem_limit_bytes=60000000),
        name="feed_forward",
    )(normed, grad, wg, wu, wd)


def order_matrix(width):
    rows = width // 8
    d = lax.axis_index("dp")
    owner = jnp.concatenate([jnp.full((rows,), mask, jnp.int32) for mask in RELATIVE])
    feature = (d ^ owner) * rows + jnp.arange(width, dtype=jnp.int32) % rows
    return (jnp.arange(width, dtype=jnp.int32)[:, None] == feature[None, :]).astype(jnp.bfloat16)


def group_body(
    block_input,
    lengths,
    out_grad,
    w_query,
    w_key,
    w_value,
    w_out,
    w_gate,
    w_up,
    w_down,
    attn_gain,
    ffn_gain,
):
    micro, _, groups, width = block_input.shape
    unit_cols = w_query.shape[1]
    bf16 = jnp.bfloat16
    f32 = jnp.float32
    contract = ((1,), (0,))
    contract_t = ((1,), (1,))
    own_lengths = lax.dynamic_slice_in_dim(
        lengths.reshape(micro * groups, 3), lax.axis_index("tensor"), 1, 0
    )
    rows = attn_gain.shape[0]
    gain_tile = jnp.zeros((8, 256), f32).at[0, :rows].set(attn_gain).at[1, :rows].set(ffn_gain)
    w_qkv, wo, x_box, gain_box = gather_weights(
        (jnp.concatenate([w_query, w_key, w_value], axis=1), w_out.T),
        to_parcels(block_input),
        gain_tile,
        ((0,), (1,)),
    )
    gains = gain_box[:, :2, :rows].transpose(1, 0, 2).reshape(2, width)
    order = order_matrix(width)
    tokens_in = dot_tt(x_box.reshape(GTOK, width), order, contract)
    gain_one = gains[0]
    gain_two = gains[1]

    segment, cos_table, sin_table = layout_tables(own_lengths)
    seg = segment[:, 0]
    cos_wide = jnp.tile(cos_table[:, 0], (1, 4))
    sin_wide = jnp.tile(sin_table[:, 0], (1, 4))
    index = jnp.arange(GTOK, dtype=jnp.int32)
    allowed = (index[None, :] <= index[:, None]) & (
        (seg[None, :] == 0) | (seg[None, :] == seg[:, None])
    )
    bias = jnp.where(allowed, 0.0, MASKED).astype(f32)
    residual = tokens_in
    scale_one = rms_scale(residual)
    unit_one = residual * scale_one
    normed_one = (unit_one * gain_one).astype(bf16)
    joint, mix, logs, attn_sum, wg, wu, wd, dy_box = attend(
        normed_one,
        w_qkv,
        wo,
        cos_wide,
        sin_wide,
        bias,
        (w_gate, w_up, w_down.T),
        to_parcels(out_grad),
        ((0, 1), (2,)),
    )
    upstream = dot_tt(dy_box.reshape(GTOK, width), order, contract).astype(bf16)
    middle = residual + attn_sum
    scale_two = rms_scale(middle)
    unit_two = middle * scale_two
    normed_two = (unit_two * gain_two).astype(bf16)
    hidden, gate_grad, up_grad, ffn_sum, normed_two_grad = feed_forward(
        normed_two, upstream, wg, wu, wd
    )
    output = (middle + ffn_sum).astype(bf16)
    out_parcels = dot_tt(output, order, contract_t).astype(bf16).reshape(x_box.shape)
    gain_two_grad = jnp.sum(normed_two_grad * unit_two, axis=0)
    middle_grad = upstream.astype(f32) + norm_back(
        normed_two_grad, unit_two, gain_two, scale_two
    )
    attn_grad = middle_grad.astype(bf16)
    joint_grad, normed_one_grad, share_gate, share_up, out_box = attend_back(
        attn_grad,
        w_qkv,
        wo,
        joint,
        logs.transpose(0, 2, 1),
        cos_wide,
        sin_wide,
        bias.T,
        (grad_dot(normed_two, gate_grad), grad_dot(normed_two, up_grad)),
        out_parcels,
    )
    gain_one_grad = jnp.sum(normed_one_grad * unit_one, axis=0)
    input_grad = (
        middle_grad + norm_back(normed_one_grad, unit_one, gain_one, scale_one)
    ).astype(bf16)
    in_parcels = dot_tt(input_grad, order, contract_t).astype(bf16).reshape(x_box.shape)
    gain_parts = jnp.stack([gain_one_grad, gain_two_grad]).reshape(2, 8, rows).transpose(1, 0, 2)
    gain_parts = jnp.pad(gain_parts, ((0, 0), (0, 6), (0, 256 - rows)))
    share_joint, share_down, share_out, own_gains, in_box = scatter_grads(
        ((normed_one, joint_grad), (upstream, hidden), (attn_grad, mix)),
        gain_parts,
        in_parcels,
    )
    return (
        from_box(out_box, micro, groups),
        from_box(in_box, micro, groups),
        share_joint[:, :unit_cols],
        share_joint[:, unit_cols : 2 * unit_cols],
        share_joint[:, 2 * unit_cols :],
        share_out.T,
        share_gate,
        share_up,
        share_down.T,
        own_gains[0, :rows],
        own_gains[1, :rows],
    )


def body(*operands):
    micro, _, groups, _ = operands[0].shape
    if lax.axis_size("dp") == 8 and micro * groups == lax.axis_size("tensor") == 4:
        return group_body(*operands)
    return sharded_body(*operands)


def solution(mesh):
    placed = (
        P(None, "tensor", "dp", None),
        P(None, "dp", None),
        P(None, "tensor", "dp", None),
        P("dp", "tensor"),
        P("dp", "tensor"),
        P("dp", "tensor"),
        P("tensor", "dp"),
        P("dp", "tensor"),
        P("dp", "tensor"),
        P("tensor", "dp"),
        P("dp"),
        P("dp"),
    )
    return jax.shard_map(
        body,
        mesh=mesh,
        in_specs=placed,
        out_specs=(
            P(None, "tensor", "dp", None),
            P(None, "tensor", "dp", None),
            P("dp", "tensor"),
            P("dp", "tensor"),
            P("dp", "tensor"),
            P("tensor", "dp"),
            P("dp", "tensor"),
            P("dp", "tensor"),
            P("tensor", "dp"),
            P("dp"),
            P("dp"),
        ),
        check_vma=False,
    )
```

```python
import functools
import math

import jax
import jax.numpy as jnp
from jax import lax
from jax.experimental import pallas as pl
from jax.experimental.pallas import tpu as pltpu
from jax.sharding import PartitionSpec as P


HD = 64
GTOK = 512


EPSILON = 1e-05
MASKED = -1e30


def layout_tables(group_lengths):
    slot_index = jnp.arange(GTOK, dtype=jnp.int32)[:, None]
    prompt_len = group_lengths[:, 0][None, :]
    first_len = group_lengths[:, 1][None, :]
    segment = jnp.where(
        slot_index < prompt_len, 0, jnp.where(slot_index < prompt_len + first_len, 1, 2)
    ).astype(jnp.int32)
    position = jnp.where(segment == 2, slot_index - first_len, slot_index)
    frequency = jnp.exp(jnp.arange(HD // 2, dtype=jnp.float32) * (-2.0 * math.log(10000.0) / HD))
    angles = position.astype(jnp.float32)[:, :, None] * frequency
    return (segment, jnp.cos(angles), jnp.sin(angles))


def rotate(values, cos_table, sin_table):
    half_size = values.shape[-1] // 2
    first_half = values[..., :half_size]
    second_half = values[..., half_size:]
    cos_wide = cos_table[:, :, None, :]
    sin_wide = sin_table[:, :, None, :]
    return jnp.concatenate(
        [
            first_half * cos_wide - second_half * sin_wide,
            second_half * cos_wide + first_half * sin_wide,
        ],
        axis=-1,
    )


def rotate_back(values, cos_table, sin_table):
    half_size = values.shape[-1] // 2
    first_half = values[..., :half_size]
    second_half = values[..., half_size:]
    cos_wide = cos_table[:, :, None, :]
    sin_wide = sin_table[:, :, None, :]
    return jnp.concatenate(
        [
            first_half * cos_wide + second_half * sin_wide,
            second_half * cos_wide - first_half * sin_wide,
        ],
        axis=-1,
    )


def rms_scale(values):
    return lax.rsqrt(jnp.mean(values * values, axis=-1, keepdims=True) + EPSILON)


def norm_back(upstream, unit_rows, gain_row, scale_rows):
    scaled = upstream * gain_row
    return scale_rows * (scaled - unit_rows * jnp.mean(scaled * unit_rows, axis=-1, keepdims=True))


def attention_scores(queries, key_rows, allowed):
    scores = jnp.einsum(
        "tghe,sghe->ghts", queries, key_rows, preferred_element_type=jnp.float32
    ) * HD ** (-0.5)
    return jnp.where(allowed[:, None], scores, MASKED)


def add_tuples(first_set, second_set):
    return tuple((earlier + later for earlier, later in zip(first_set, second_set)))


def micro_step(inputs, group_lengths, upstream, gathered):
    w_query, w_key, w_value, w_out, w_gate, w_up, w_down, attn_gain, ffn_gain = gathered
    gain_one = attn_gain.astype(jnp.float32)
    gain_two = ffn_gain.astype(jnp.float32)
    group_count = inputs.shape[1]
    head_cols = w_query.shape[1]
    hidden_cols = w_gate.shape[1]
    shape_heads = (GTOK, group_count, head_cols // HD, HD)
    segment, cos_table, sin_table = layout_tables(group_lengths)
    token_index = jnp.arange(GTOK, dtype=jnp.int32)
    seg_groups = segment.T
    allowed = (token_index[None, None, :] <= token_index[None, :, None]) & (
        (seg_groups[:, None, :] == 0) | (seg_groups[:, None, :] == seg_groups[:, :, None])
    )
    residual = inputs.astype(jnp.float32)
    scale_one = rms_scale(residual)
    unit_one = residual * scale_one
    normed_one = (unit_one * gain_one).astype(jnp.bfloat16)
    normed_all = lax.all_gather(normed_one, "tensor", axis=0, tiled=True)
    w_joint = jnp.concatenate([w_query, w_key, w_value], axis=1)
    projected = jnp.einsum("tgd,dc->tgc", normed_all, w_joint, preferred_element_type=jnp.float32)
    queries = rotate(projected[..., :head_cols].reshape(shape_heads), cos_table, sin_table).astype(
        jnp.bfloat16
    )
    key_rows = rotate(
        projected[..., head_cols : 2 * head_cols].reshape(shape_heads), cos_table, sin_table
    ).astype(jnp.bfloat16)
    value_rows = projected[..., 2 * head_cols :].reshape(shape_heads).astype(jnp.bfloat16)
    scores = attention_scores(queries, key_rows, allowed)
    row_max = jnp.max(scores, axis=-1, keepdims=True)
    log_total = row_max + jnp.log(jnp.sum(jnp.exp(scores - row_max), axis=-1, keepdims=True))
    attn_probs = jnp.exp(scores - log_total).astype(jnp.bfloat16)
    attn_mix = (
        jnp.einsum("ghts,sghe->tghe", attn_probs, value_rows, preferred_element_type=jnp.float32)
        .astype(jnp.bfloat16)
        .reshape(GTOK, group_count, head_cols)
    )
    rows_here = attn_mix
    attn_sum = lax.psum_scatter(
        jnp.einsum("tgc,cd->tgd", rows_here, w_out, preferred_element_type=jnp.float32),
        "tensor",
        scatter_dimension=0,
        tiled=True,
    )
    middle = residual + attn_sum
    scale_two = rms_scale(middle)
    unit_two = middle * scale_two
    normed_two = (unit_two * gain_two).astype(jnp.bfloat16)
    normed_more = lax.all_gather(normed_two, "tensor", axis=0, tiled=True)
    w_gate_up = jnp.concatenate([w_gate, w_up], axis=1)
    gate_up = jnp.einsum("tgd,df->tgf", normed_more, w_gate_up, preferred_element_type=jnp.float32)
    gate_vals = gate_up[..., :hidden_cols]
    up_vals = gate_up[..., hidden_cols:]
    sigmoid_gate = jax.nn.sigmoid(gate_vals)
    silu_gate = gate_vals * sigmoid_gate
    hidden = (silu_gate * up_vals).astype(jnp.bfloat16)
    rows_here = hidden
    ffn_sum = lax.psum_scatter(
        jnp.einsum("tgf,fd->tgd", rows_here, w_down, preferred_element_type=jnp.float32).astype(
            jnp.bfloat16
        ),
        "tensor",
        scatter_dimension=0,
        tiled=True,
    ).astype(jnp.float32)
    output = (middle + ffn_sum).astype(jnp.bfloat16)
    upstream_all = lax.all_gather(upstream, "tensor", axis=0, tiled=True)
    hidden_grad = jnp.einsum(
        "tgd,fd->tgf", upstream_all, w_down, preferred_element_type=jnp.float32
    )
    grad_down = jnp.einsum("tgf,tgd->fd", hidden, upstream_all, preferred_element_type=jnp.float32)
    up_grad = hidden_grad * silu_gate
    gate_grad = hidden_grad * up_vals * (sigmoid_gate * (1.0 + gate_vals * (1.0 - sigmoid_gate)))
    gate_up_grad = jnp.concatenate([gate_grad, up_grad], axis=-1).astype(jnp.bfloat16)
    grad_gate_up = jnp.einsum(
        "tgd,tgf->df", normed_more, gate_up_grad, preferred_element_type=jnp.float32
    )
    rows_here = gate_up_grad
    normed_two_grad = lax.psum_scatter(
        jnp.einsum("tgf,df->tgd", rows_here, w_gate_up, preferred_element_type=jnp.float32).astype(
            jnp.bfloat16
        ),
        "tensor",
        scatter_dimension=0,
        tiled=True,
    ).astype(jnp.float32)
    gain_two_grad = jnp.sum(normed_two_grad * unit_two, axis=(0, 1))
    middle_grad = upstream.astype(jnp.float32) + norm_back(
        normed_two_grad, unit_two, gain_two, scale_two
    )
    attn_grad = middle_grad.astype(jnp.bfloat16)
    attn_grad_all = lax.all_gather(attn_grad, "tensor", axis=0, tiled=True)
    mix_grad = (
        jnp.einsum("tgd,cd->tgc", attn_grad_all, w_out, preferred_element_type=jnp.float32)
        .astype(jnp.bfloat16)
        .reshape(shape_heads)
    )
    grad_out = jnp.einsum(
        "tgc,tgd->cd", attn_mix, attn_grad_all, preferred_element_type=jnp.float32
    )
    scores_again = attention_scores(queries, key_rows, allowed)
    probs_full = jnp.exp(scores_again - log_total)
    prob_grad = jnp.einsum(
        "tghe,sghe->ghts", mix_grad, value_rows, preferred_element_type=jnp.float32
    )
    value_grad = jnp.einsum(
        "ghts,tghe->sghe",
        probs_full.astype(jnp.bfloat16),
        mix_grad,
        preferred_element_type=jnp.float32,
    )
    centre = jnp.sum(probs_full * prob_grad, axis=-1, keepdims=True)
    score_grad = (probs_full * (prob_grad - centre)).astype(jnp.bfloat16)
    query_grad = jnp.einsum(
        "ghts,sghe->tghe", score_grad, key_rows, preferred_element_type=jnp.float32
    ) * HD ** (-0.5)
    key_grad = jnp.einsum(
        "ghts,tghe->sghe", score_grad, queries, preferred_element_type=jnp.float32
    ) * HD ** (-0.5)
    flat_shape = (GTOK, group_count, head_cols)
    joint_grad = jnp.concatenate(
        [
            rotate_back(query_grad, cos_table, sin_table).reshape(flat_shape),
            rotate_back(key_grad, cos_table, sin_table).reshape(flat_shape),
            value_grad.reshape(flat_shape),
        ],
        axis=-1,
    ).astype(jnp.bfloat16)
    grad_joint = jnp.einsum(
        "tgd,tgc->dc", normed_all, joint_grad, preferred_element_type=jnp.float32
    )
    rows_here = joint_grad
    normed_one_grad = lax.psum_scatter(
        jnp.einsum("tgc,dc->tgd", rows_here, w_joint, preferred_element_type=jnp.float32).astype(
            jnp.bfloat16
        ),
        "tensor",
        scatter_dimension=0,
        tiled=True,
    ).astype(jnp.float32)
    gain_one_grad = jnp.sum(normed_one_grad * unit_one, axis=(0, 1))
    input_grad = (middle_grad + norm_back(normed_one_grad, unit_one, gain_one, scale_one)).astype(
        jnp.bfloat16
    )
    param_grads = (
        grad_joint[:, :head_cols],
        grad_joint[:, head_cols : 2 * head_cols],
        grad_joint[:, 2 * head_cols :],
        grad_out,
        grad_gate_up[:, :hidden_cols],
        grad_gate_up[:, hidden_cols:],
        grad_down,
        gain_one_grad,
        gain_two_grad,
    )
    return (output, input_grad, param_grads)


def sharded_body(
    block_input,
    lengths,
    out_grad,
    w_query,
    w_key,
    w_value,
    w_out,
    w_gate,
    w_up,
    w_down,
    attn_gain,
    ffn_gain,
):
    outputs = []
    input_grads = []
    totals = None
    shares = None
    for micro_index in range(block_input.shape[0]):
        gathered = (
            lax.all_gather(w_query, "dp", axis=0, tiled=True),
            lax.all_gather(w_key, "dp", axis=0, tiled=True),
            lax.all_gather(w_value, "dp", axis=0, tiled=True),
            lax.all_gather(w_out, "dp", axis=1, tiled=True),
            lax.all_gather(w_gate, "dp", axis=0, tiled=True),
            lax.all_gather(w_up, "dp", axis=0, tiled=True),
            lax.all_gather(w_down, "dp", axis=1, tiled=True),
            lax.all_gather(attn_gain, "dp", axis=0, tiled=True),
            lax.all_gather(ffn_gain, "dp", axis=0, tiled=True),
        )
        output, input_grad, param_grads = micro_step(
            block_input[micro_index], lengths[micro_index], out_grad[micro_index], gathered
        )
        outputs.append(output)
        input_grads.append(input_grad)
        totals = param_grads if totals is None else add_tuples(totals, param_grads)
    shares = (
        lax.psum_scatter(
            totals[0].astype(jnp.bfloat16), "dp", scatter_dimension=0, tiled=True
        ).astype(jnp.float32),
        lax.psum_scatter(
            totals[1].astype(jnp.bfloat16), "dp", scatter_dimension=0, tiled=True
        ).astype(jnp.float32),
        lax.psum_scatter(
            totals[2].astype(jnp.bfloat16), "dp", scatter_dimension=0, tiled=True
        ).astype(jnp.float32),
        lax.psum_scatter(
            totals[3].astype(jnp.bfloat16), "dp", scatter_dimension=1, tiled=True
        ).astype(jnp.float32),
        lax.psum_scatter(
            totals[4].astype(jnp.bfloat16), "dp", scatter_dimension=0, tiled=True
        ).astype(jnp.float32),
        lax.psum_scatter(
            totals[5].astype(jnp.bfloat16), "dp", scatter_dimension=0, tiled=True
        ).astype(jnp.float32),
        lax.psum_scatter(
            totals[6].astype(jnp.bfloat16), "dp", scatter_dimension=1, tiled=True
        ).astype(jnp.float32),
        lax.psum_scatter(
            totals[7].astype(jnp.bfloat16), "dp", scatter_dimension=0, tiled=True
        ).astype(jnp.float32),
        lax.psum_scatter(
            totals[8].astype(jnp.bfloat16), "dp", scatter_dimension=0, tiled=True
        ).astype(jnp.float32),
    )
    gain_one_total, gain_two_total = lax.psum((shares[7], shares[8]), "tensor")
    return (
        jnp.stack(outputs),
        jnp.stack(input_grads),
        shares[0],
        shares[1],
        shares[2],
        shares[3],
        shares[4],
        shares[5],
        shares[6],
        gain_one_total,
        gain_two_total,
    )


MESH = pl.DeviceIdType.MESH
RELATIVE = [4 * ((j // 2) % 2) + 2 * (j % 2) + j // 4 for j in range(8)]


def flip_core(d):
    return d + 1 - 2 * (d % 2)


def flip_x(d):
    return d + 2 - 4 * ((d // 2) % 2)


def flip_y(d):
    return d + 4 - 8 * ((d // 4) % 2)


def flip(d, mask):
    if mask & 1:
        d = flip_core(d)
    if mask & 2:
        d = flip_x(d)
    if mask & 4:
        d = flip_y(d)
    return d


def ring_next(z):
    return (2 * z + 1) % 5


def remote(src, dst, send_sem, recv_sem, peer):
    return pltpu.make_async_remote_copy(
        src_ref=src,
        dst_ref=dst,
        send_sem=send_sem,
        recv_sem=recv_sem,
        device_id=peer,
        device_id_type=MESH,
    )


def greet(d, z):
    barrier = pltpu.get_barrier_semaphore()
    for mask in range(1, 8):
        pl.semaphore_signal(barrier, inc=1, device_id=(flip(d, mask), z), device_id_type=MESH)
    for step in (1, 2, 3):
        pl.semaphore_signal(barrier, inc=1, device_id=(d, (z + step) % 4), device_id_type=MESH)
    pl.semaphore_wait(barrier, 10)


def gather_steps(sets, shards, fulls, sems, box_refs, gain_refs):
    count = len(shards)
    send_sem, recv_sem, local_sem = sems
    d = lax.axis_index("dp")
    z = lax.axis_index("tensor")
    place = {
        "z": (d, ring_next(z)),
        "x": (flip_x(d), z),
        "y": (flip_y(d), z),
        "c": (flip_core(d), z),
    }
    rows = shards[0].shape[0]

    def region(a, k, j, half):
        width = shards[a].shape[1]
        top, size = (j * rows, rows) if half is None else (j * rows + half * (rows // 2), rows // 2)
        return fulls[a].at[pl.ds(top, size), pl.ds(k * width, width)]

    sends = []

    def start(s, way, slot, src, dst, half=None):
        for a in sets[s]:
            source = shards[a] if src == (0, 0) else region(a, *src, half)
            remote(
                source,
                region(a, *dst, half),
                send_sem.at[s, slot],
                recv_sem.at[s, slot],
                place[way],
            ).start()
        sends.append((s, slot, half))

    def bulk(s, slot, half):
        arrs = sets[s]
        size = rows if half is None else rows // 2
        width = sum(shards[a].shape[1] for a in arrs)
        part = fulls[arrs[0]].at[pl.ds(0, size), pl.ds(0, width)]
        return remote(part, part, send_sem.at[s, slot], recv_sem.at[s, slot], place["c"])

    def arrived(s, slot, half=None):
        bulk(s, slot, half).wait_recv()

    ring_slot, x_slot, y_slot, x_relay, y_relay, core_slot = 0, 3, 7, 11, 15, 19

    def core(s, k, j):
        start(s, "c", core_slot + 4 * k + j, (k, j), (k, 4 + j))

    def ring_step(s, k):
        start(s, "z", ring_slot + k, (k, 0), (k + 1, 0))

    def open_unit(s, k):
        if k > 0:
            arrived(s, ring_slot + k - 1)
            if k < 3:
                ring_step(s, k)
        start(s, "x", x_slot + k, (k, 0), (k, 1))
        start(s, "y", y_slot + k, (k, 0), (k, 2))
        core(s, k, 0)

    def close_unit(s, k):
        arrived(s, x_slot + k)
        start(s, "y", y_relay + k, (k, 1), (k, 3), 1)
        core(s, k, 1)
        arrived(s, y_slot + k)
        start(s, "x", x_relay + k, (k, 2), (k, 3), 0)
        core(s, k, 2)

    def last_part(s, k):
        arrived(s, x_relay + k, 0)
        arrived(s, y_relay + k, 1)
        core(s, k, 3)

    def own_copies():
        for a in range(count):
            yield pltpu.make_async_copy(shards[a], region(a, 0, 0, None), local_sem.at[a])
        parcel, box = box_refs[:2]
        yield pltpu.make_async_copy(parcel.at[z], box.at[z], local_sem.at[count])
        if gain_refs:
            gains, gain_box = gain_refs[:2]
            yield pltpu.make_async_copy(gains, gain_box.at[0], local_sem.at[count + 1])

    def box_copy(step):
        parcel, box, box_send, box_recv = box_refs
        other = (z + step) % 4
        return remote(
            parcel.at[other],
            box.at[z],
            box_send.at[step - 1],
            box_recv.at[step - 1],
            (d, other),
        )

    def gain_copy(j):
        gains, gain_box, gain_send, gain_recv = gain_refs
        return remote(
            gains,
            gain_box.at[j],
            gain_send.at[j - 1],
            gain_recv.at[j - 1],
            (flip(d, RELATIVE[j]), z),
        )

    units = [(s, k) for s in range(len(sets)) for k in range(4)]

    def run(i):
        if i == 0:
            greet(d, z)
            if gain_refs:
                for j in range(1, 8):
                    gain_copy(j).start()
            for copy in own_copies():
                copy.start()
            ring_step(0, 0)
            open_unit(*units[0])
        if i < len(units):
            if i + 1 < len(units):
                after = units[i + 1]
                if after[1] == 0:
                    ring_step(after[0], 0)
                open_unit(*after)
            if i == len(units) - 3:
                for step in (1, 2, 3):
                    box_copy(step).start()
            close_unit(*units[i])
        if i > 0:
            last_part(*units[i - 1])
        if i == len(units):
            end()

    def end():
        for s in range(len(sets)):
            for slot in range(core_slot, core_slot + 16):
                arrived(s, slot)
        for step in (1, 2, 3):
            box_copy(step).wait()
        if gain_refs:
            for j in range(1, 8):
                gain_copy(j).wait()
        for s, slot, half in sends:
            bulk(s, slot, half).wait_send()
        for copy in own_copies():
            copy.wait()

    return [functools.partial(run, i) for i in range(len(units) + 1)]


def gather_scratch(sets, count, gains):
    dma = pltpu.SemaphoreType.DMA
    sems = [dma((len(sets), 35)), dma((len(sets), 35)), dma((count + 2,)), dma((3,)), dma((3,))]
    return sems + ([dma((7,)), dma((7,))] if gains else [])


def gather_shapes(shards):
    return [jax.ShapeDtypeStruct((8 * w.shape[0], 4 * w.shape[1]), w.dtype) for w in shards]


def gather_kernel(sets, count, *refs):
    shards = refs[:count]
    parcel, gains = refs[count : count + 2]
    fulls = refs[count + 2 : 2 * count + 2]
    box, gain_box = refs[2 * count + 2 : 2 * count + 4]
    send_sem, recv_sem, local_sem, box_send, box_recv, *gain_sems = refs[2 * count + 4 :]
    for step in gather_steps(
        sets,
        shards,
        fulls,
        (send_sem, recv_sem, local_sem),
        (parcel, box, box_send, box_recv),
        (gains, gain_box, *gain_sems),
    ):
        step()


def gather_weights(shards, parcel, gains, sets):
    count = len(shards)
    vmem = pl.BlockSpec(memory_space=pltpu.VMEM)
    anywhere = pl.BlockSpec(memory_space=pl.ANY)
    return pl.pallas_call(
        functools.partial(gather_kernel, sets, count),
        out_shape=gather_shapes(shards)
        + [jax.ShapeDtypeStruct(parcel.shape, parcel.dtype)]
        + [jax.ShapeDtypeStruct((8, *gains.shape), gains.dtype)],
        in_specs=[vmem] * (count + 2),
        out_specs=[anywhere] * (count + 2),
        scratch_shapes=gather_scratch(sets, count, True),
        compiler_params=pltpu.CompilerParams(collective_id=1, has_side_effects=True),
        name="gather_weights",
    )(*shards, parcel, gains)


def add_rows(target, first, second, chunk=32):
    rows = target.shape[0]

    def step(i, carry):
        at = pl.ds(pl.multiple_of(i * chunk, chunk), chunk)
        target[at, :] = (
            first[at, :].astype(jnp.float32) + second[at, :].astype(jnp.float32)
        ).astype(target.dtype)
        return carry

    lax.fori_loop(0, rows // chunk, step, 0)


def scatter_steps(grads, width, shares, buffers, gain_refs, box_refs, staging=None):
    count = len(grads)
    from_core, from_first, from_second, from_ring = (
        buffers[i * count : (i + 1) * count] for i in range(4)
    )
    total, middle, final, send_sem, recv_sem, load_sem = buffers[4 * count :]
    d = lax.axis_index("dp")
    z = lax.axis_index("tensor")
    core, east, north = (flip_core(d), z), (flip_x(d), z), (flip_y(d), z)
    onward = (d, ring_next(z))
    rows = total.shape[2]
    half = rows // 2
    units = [(g, k) for g in range(count) for k in (1, 2, 3, 0)]

    def send(src, dst, u, slot, peer):
        return remote(src, dst, send_sem.at[u, slot], recv_sem.at[u, slot], peer)

    def gain_copy(j):
        gains, _, gain_box, _, gain_send, gain_recv = gain_refs
        return remote(
            gains.at[j],
            gain_box.at[j],
            gain_send.at[j - 1],
            gain_recv.at[j - 1],
            (flip(d, RELATIVE[j]), z),
        )

    def line_copy(step):
        _, _, _, gain_line, gain_send, gain_recv = gain_refs
        return remote(
            gain_line.at[z],
            gain_line.at[z],
            gain_send.at[6 + step],
            gain_recv.at[6 + step],
            (d, (z + step) % 4),
        )

    def box_copy(step):
        parcel, box, box_send, box_recv, _ = box_refs
        other = (z + step) % 4
        return remote(
            parcel.at[other],
            box.at[z],
            box_send.at[step - 1],
            box_recv.at[step - 1],
            (d, other),
        )

    def own_copy():
        parcel, box, _, _, box_own = box_refs
        return pltpu.make_async_copy(parcel.at[z], box.at[z], box_own)

    def columns(u):
        g, k = units[u]
        return pl.ds(k * width[g], width[g])

    def to_core(u):
        g, k = units[u]
        if staging:
            source = staging[1].at[u % 2, :, :, pl.ds(0, width[g])]
        else:
            source = grads[g].at[pl.ds(4, 4), :, columns(u)]
        return send(source, from_core[g].at[k], u, 0, core)

    def load_right(u):
        g, _ = units[u]
        return pltpu.make_async_copy(
            grads[g][1].at[:, columns(u)],
            staging[0].at[u % 2, :, pl.ds(0, width[g])],
            staging[2].at[u % 2],
        )

    def multiply(u, target, first):
        g, _ = units[u]
        cols = slice(0, width[g])
        for pair in range(2):
            at = slice((first + 2 * pair) * rows, (first + 2 * pair + 2) * rows)
            part = dot_tt(grads[g][0][:, at], staging[0][u % 2, :, cols], ((0,), (0,)))
            target[2 * pair : 2 * pair + 2, :, cols] = part.astype(jnp.bfloat16).reshape(
                2, rows, width[g]
            )

    def far_half(u):
        load_right(u).wait()
        if u >= 2:
            to_core(u - 2).wait_send()
        multiply(u, staging[1].at[u % 2], 4)
        to_core(u).start()

    def near_half(u):
        multiply(u, total.at[u % 3], 0)
        if u + 2 < len(units):
            load_right(u + 2).start()

    def load(u):
        g, _ = units[u]
        return pltpu.make_async_copy(
            grads[g].at[pl.ds(0, 4), :, columns(u)],
            total.at[u % 3, :, :, pl.ds(0, width[g])],
            load_sem.at[u % 3],
        )

    def first_sends(u):
        g, k = units[u]
        t = total.at[u % 3]
        cols = pl.ds(0, width[g])
        return [
            send(t.at[1, pl.ds(0, half), cols], from_first[g].at[k, 0, 0], u, 1, east),
            send(t.at[3, pl.ds(0, half), cols], from_first[g].at[k, 0, 1], u, 2, east),
            send(t.at[2, pl.ds(half, half), cols], from_first[g].at[k, 1, 0], u, 3, north),
            send(t.at[3, pl.ds(half, half), cols], from_first[g].at[k, 1, 1], u, 4, north),
        ]

    def second_sends(u):
        g, k = units[u]
        m = middle.at[u % 2]
        cols = pl.ds(0, width[g])
        return [
            send(m.at[0, :, cols], from_second[g].at[k, 0], u, 5, north),
            send(m.at[1, :, cols], from_second[g].at[k, 1], u, 6, east),
        ]

    def ring_send(u):
        g, k = units[u]
        return send(
            final.at[u % 2, :, pl.ds(0, width[g])], from_ring[g].at[k], u, 7, onward
        )

    def first_stage(u):
        g, k = units[u]
        t = total.at[u % 3]
        cols = pl.ds(0, width[g])
        if not staging:
            load(u).wait()
        to_core(u).wait_recv()
        for j in range(4):
            part = t.at[j, :, cols]
            add_rows(part, part, from_core[g].at[k, j])
        for copy in first_sends(u):
            copy.start()

    def second_stage(u):
        g, k = units[u]
        t = total.at[u % 3]
        m = middle.at[u % 2]
        cols = pl.ds(0, width[g])
        if u >= 2:
            for copy in second_sends(u - 2):
                copy.wait_send()
        sends = first_sends(u)
        sends[1].wait_recv()
        add_rows(m.at[0, :, cols], t.at[2, pl.ds(0, half), cols], from_first[g].at[k, 0, 1])
        sends[3].wait_recv()
        add_rows(m.at[1, :, cols], t.at[1, pl.ds(half, half), cols], from_first[g].at[k, 1, 1])
        for copy in second_sends(u):
            copy.start()
        sends[0].wait_recv()
        upper = t.at[0, pl.ds(0, half), cols]
        add_rows(upper, upper, from_first[g].at[k, 0, 0])
        sends[2].wait_recv()
        lower = t.at[0, pl.ds(half, half), cols]
        add_rows(lower, lower, from_first[g].at[k, 1, 0])

    def third_stage(u):
        g, k = units[u]
        t = total.at[u % 3]
        cols = pl.ds(0, width[g])
        for side, copy in enumerate(second_sends(u)):
            copy.wait_recv()
            part = t.at[0, pl.ds(side * half, half), cols]
            if k == 1:
                if side == 0 and u >= 2:
                    wait_ring(u - 2)
                add_rows(
                    final.at[u % 2, pl.ds(side * half, half), cols],
                    part,
                    from_second[g].at[k, side],
                )
            else:
                add_rows(part, part, from_second[g].at[k, side])
        if k != 1:
            ring_send(u - 1).wait_recv()
            if u >= 2:
                wait_ring(u - 2)
            if k == 0:
                add_rows(shares[g], t.at[0, :, cols], from_ring[g].at[3])
            else:
                add_rows(final.at[u % 2, :, cols], t.at[0, :, cols], from_ring[g].at[k - 1])
        if k != 0:
            ring_send(u).start()
        for copy in first_sends(u):
            copy.wait_send()

    def wait_ring(u):
        if units[u][1] != 0:
            ring_send(u).wait_send()

    n = len(units)

    def begin():
        greet(d, z)
        if gain_refs:
            for j in range(1, 8):
                gain_copy(j).start()
        own_copy().start()
        for hop in (1, 2, 3):
            box_copy(hop).start()
        if staging:
            load_right(0).start()
            load_right(1).start()
            far_half(0)
            near_half(0)
            far_half(1)
        else:
            for u in range(n):
                to_core(u).start()
                if u < 3:
                    load(u).start()

    def run(step):
        if step == 0:
            begin()
        if step < n:
            first_stage(step)
        if 0 <= step - 1 < n:
            second_stage(step - 1)
        if 0 <= step - 2:
            third_stage(step - 2)
            if step + 1 < n and not staging:
                load(step + 1).start()
        if staging and step + 1 < n:
            near_half(step + 1)
            if step + 2 < n:
                far_half(step + 2)
        if step == 2 and gain_refs:
            gains, _, gain_box, gain_line, _, _ = gain_refs
            for j in range(1, 8):
                gain_copy(j).wait()
            gain_line[z] = gains[0] + sum(gain_box[j] for j in range(1, 8))
            for hop in (1, 2, 3):
                line_copy(hop).start()
        if step == n + 1:
            end()

    def end():
        if gain_refs:
            _, gain_share, _, gain_line, _, _ = gain_refs
            for hop in (1, 2, 3):
                line_copy(hop).wait()
            gain_share[...] = gain_line[0] + gain_line[1] + gain_line[2] + gain_line[3]
        for hop in (1, 2, 3):
            box_copy(hop).wait()
        own_copy().wait()
        for u in range(n):
            if u >= n - 2 or not staging:
                to_core(u).wait_send()
            if u >= n - 2:
                for copy in second_sends(u):
                    copy.wait_send()
                wait_ring(u)

    return [functools.partial(run, step) for step in range(n + 2)]


def scatter_scratch(rows, widths):
    bf16 = jnp.bfloat16
    half = rows // 2
    widest = max(widths)
    dma = pltpu.SemaphoreType.DMA
    return (
        [pltpu.VMEM((4, 4, rows, w), bf16) for w in widths]
        + [pltpu.VMEM((4, 2, 2, half, w), bf16) for w in widths]
        + [pltpu.VMEM((4, 2, half, w), bf16) for w in widths]
        + [pltpu.VMEM((4, rows, w), bf16) for w in widths]
        + [
            pltpu.VMEM((3, 4, rows, widest), bf16),
            pltpu.VMEM((2, 2, half, widest), bf16),
            pltpu.VMEM((2, rows, widest), bf16),
            dma((4 * len(widths), 8)),
            dma((4 * len(widths), 8)),
            dma((3,)),
        ]
    )


def scatter_kernel(width, *refs):
    count = len(width)
    grads = [(refs[g], refs[count + g]) for g in range(count)]
    refs = refs[2 * count :]
    gains, parcel = refs[:2]
    shares = refs[2 : count + 2]
    gain_share, box = refs[count + 2 : count + 4]
    rest = refs[count + 4 :]
    buffers = rest[: 4 * count + 6]
    gain_box, gain_line, gain_send, gain_recv = rest[4 * count + 6 : 4 * count + 10]
    box_sems = rest[4 * count + 10 : 4 * count + 13]
    for step in scatter_steps(
        grads,
        width,
        shares,
        buffers,
        (gains, gain_share, gain_box, gain_line, gain_send, gain_recv),
        (parcel, box, *box_sems),
        rest[4 * count + 13 :],
    ):
        step()


def scatter_grads(pairs, gains, parcel):
    lefts = [left for left, _ in pairs]
    rights = [right for _, right in pairs]
    tokens = lefts[0].shape[0]
    rows = lefts[0].shape[1] // 8
    widths = [right.shape[1] // 4 for right in rights]
    widest = max(widths)
    count = len(pairs)
    dma = pltpu.SemaphoreType.DMA
    vmem = pl.BlockSpec(memory_space=pltpu.VMEM)
    anywhere = pl.BlockSpec(memory_space=pl.ANY)
    return pl.pallas_call(
        functools.partial(scatter_kernel, widths),
        out_shape=[jax.ShapeDtypeStruct((rows, w), jnp.float32) for w in widths]
        + [jax.ShapeDtypeStruct(gains.shape[1:], jnp.float32)]
        + [jax.ShapeDtypeStruct(parcel.shape, parcel.dtype)],
        in_specs=[vmem] * count + [anywhere] * count + [vmem] * 2,
        out_specs=[vmem] * (count + 1) + [anywhere],
        scratch_shapes=scatter_scratch(rows, widths)
        + [
            pltpu.VMEM(gains.shape, jnp.float32),
            pltpu.VMEM((4, *gains.shape[1:]), jnp.float32),
            dma((10,)),
            dma((10,)),
            dma((3,)),
            dma((3,)),
            dma(()),
            pltpu.VMEM((2, tokens, widest), jnp.bfloat16),
            pltpu.VMEM((2, 4, rows, widest), jnp.bfloat16),
            dma((2,)),
        ],
        compiler_params=pltpu.CompilerParams(
            collective_id=2, has_side_effects=True, vmem_limit_bytes=66000000
        ),
        name="scatter_grads",
    )(*lefts, *rights, gains, parcel)


def grad_dot(left, right):
    return dot_tt(left, right, ((0,), (0,))).astype(jnp.bfloat16)


def to_parcels(values):
    micro, rows, groups, width = values.shape
    return values.transpose(0, 2, 1, 3).reshape(micro * groups, rows, width)


def from_box(box, micro, groups):
    return box.reshape(micro, groups, *box.shape[1:]).transpose(0, 2, 1, 3)


def dot_tt(left, right, dims):
    return lax.dot_general(left, right, (dims, ((), ())), preferred_element_type=jnp.float32)


ROWS = 128
PAIR = 2 * HD
NORMAL = ((1,), (0,))
RIGHT_T = ((1,), (1,))
LEFT_T = ((0,), (0,))


def head_masks(scale):
    lane = lax.broadcasted_iota(jnp.int32, (1, PAIR), 1)
    return [jnp.where((lane // HD) == h, scale, 0.0).astype(jnp.bfloat16) for h in range(2)]


def spin(values, cos_table, sin_table, sign):
    lane = lax.broadcasted_iota(jnp.int32, values.shape, 1)
    ahead = pltpu.roll(values, PAIR - HD // 2, 1)
    behind = pltpu.roll(values, HD // 2, 1)
    turned = jnp.where(lane % HD < HD // 2, -ahead, behind)
    return values * cos_table + (sign * turned) * sin_table


def attend_kernel(sets, count, normed_ref, w_ref, wo_ref, cos_ref, sin_ref, bias_ref, *refs):
    shards = refs[:count]
    parcel, joint_ref, mix_ref, log_ref, sum_ref = refs[count : count + 5]
    fulls = refs[count + 5 : 2 * count + 5]
    box, proj_ref, send_sem, recv_sem, local_sem, box_send, box_recv = refs[2 * count + 5 :]
    turns = gather_steps(
        sets,
        shards,
        fulls,
        (send_sem, recv_sem, local_sem),
        (parcel, box, box_send, box_recv),
        None,
    )
    phase = pl.program_id(0)

    def talk(slot):
        for p in range(4):
            if slot == 0 or p < 2:

                @pl.when(phase == p)
                def _():
                    turns[p + min(p, 2) + slot]()

    talk(0)
    tokens = normed_ref.shape[0]
    cols = wo_ref.shape[1]
    pairs = cols // PAIR
    proj_ref[...] = dot_tt(normed_ref[...], w_ref[...], NORMAL)
    for c in range(3 * pairs):
        at = slice(c * PAIR, (c + 1) * PAIR)
        part = proj_ref[:, at]
        if c < 2 * pairs:
            part = spin(part, cos_ref[...], sin_ref[...], 1.0)
        joint_ref[:, at] = part.astype(jnp.bfloat16)
    masks = head_masks(HD ** (-0.5))
    lane = lax.broadcasted_iota(jnp.int32, (ROWS, PAIR), 1)
    for pair in range(pairs):
        if pair == 1:
            talk(1)
        for i in range(tokens // ROWS):
            rows = slice(i * ROWS, (i + 1) * ROWS)
            size = (i + 1) * ROWS
            q = joint_ref[rows, pair * PAIR : (pair + 1) * PAIR]
            k = joint_ref[:size, cols + pair * PAIR : cols + (pair + 1) * PAIR]
            v = joint_ref[:size, 2 * cols + pair * PAIR : 2 * cols + (pair + 1) * PAIR]
            both = jnp.concatenate([q * masks[0], q * masks[1]], axis=0)
            bias = bias_ref[rows, :size]
            scores = dot_tt(both, k, RIGHT_T) + jnp.concatenate([bias, bias], axis=0)
            top = jnp.max(scores, axis=1, keepdims=True)
            powers = jnp.exp(scores - top)
            norm = jnp.sum(powers, axis=1, keepdims=True)
            probs = (powers * (1.0 / norm)).astype(jnp.bfloat16)
            mixed = dot_tt(probs, v, NORMAL)
            mix_ref[rows, pair * PAIR : (pair + 1) * PAIR] = jnp.where(
                lane < HD, mixed[:ROWS], mixed[ROWS:]
            ).astype(jnp.bfloat16)
            log_norm = top + jnp.log(norm)
            log_ref[0, rows, 2 * pair : 2 * pair + 1] = log_norm[:ROWS]
            log_ref[0, rows, 2 * pair + 1 : 2 * pair + 2] = log_norm[ROWS:]
    projected = dot_tt(mix_ref[...], wo_ref[...], RIGHT_T)

    @pl.when(phase == 0)
    def _():
        sum_ref[...] = projected

    @pl.when(phase > 0)
    def _():
        sum_ref[...] += projected

    @pl.when(phase == 3)
    def _():
        for step in turns[6:]:
            step()


def attend(normed, w_qkv, wo, cos_wide, sin_wide, bias, shards, parcel, sets):
    tokens, width = normed.shape
    count = len(shards)
    blocks = 4
    cols = wo.shape[1] // blocks
    vmem = pl.BlockSpec(memory_space=pltpu.VMEM)
    anywhere = pl.BlockSpec(memory_space=pl.ANY)
    moving = lambda k: (0, k)
    return pl.pallas_call(
        functools.partial(attend_kernel, sets, count),
        grid=(blocks,),
        out_shape=[
            jax.ShapeDtypeStruct((tokens, 3 * blocks * cols), jnp.bfloat16),
            jax.ShapeDtypeStruct((tokens, blocks * cols), jnp.bfloat16),
            jax.ShapeDtypeStruct((blocks, tokens, 8), jnp.float32),
            jax.ShapeDtypeStruct((tokens, width), jnp.float32),
        ]
        + gather_shapes(shards)
        + [jax.ShapeDtypeStruct(parcel.shape, parcel.dtype)],
        in_specs=[
            vmem,
            pl.BlockSpec((width, 3 * cols), moving),
            pl.BlockSpec((width, cols), moving),
            vmem,
            vmem,
            vmem,
        ]
        + [vmem] * (count + 1),
        out_specs=[
            pl.BlockSpec((tokens, 3 * cols), moving),
            pl.BlockSpec((tokens, cols), moving),
            pl.BlockSpec((1, tokens, 8), lambda k: (k, 0, 0)),
            vmem,
        ]
        + [anywhere] * (count + 1),
        scratch_shapes=[pltpu.VMEM((tokens, 3 * cols), jnp.float32)]
        + gather_scratch(sets, count, False),
        compiler_params=pltpu.CompilerParams(
            collective_id=4, has_side_effects=True, vmem_limit_bytes=60000000
        ),
        name="attend",
    )(normed, w_qkv, wo, cos_wide, sin_wide, bias, *shards, parcel)


def attend_back_kernel(
    count,
    grad_ref,
    w_ref,
    wo_ref,
    joint_ref,
    log_ref,
    cos_ref,
    sin_ref,
    bias_ref,
    *refs,
):
    grads = [(refs[0], right) for right in refs[1 : count + 1]]
    refs = refs[1:]
    parcel, out_ref, sum_ref = refs[count : count + 3]
    shares = refs[count + 3 : 2 * count + 3]
    box, mix_grad, q_grad, k_grad, v_grad = refs[2 * count + 3 : 2 * count + 8]
    buffers = refs[2 * count + 8 : 6 * count + 14]
    box_sems = refs[6 * count + 14 : 6 * count + 17]
    width = [share.shape[1] for share in shares]
    turns = scatter_steps(
        grads,
        width,
        shares,
        buffers,
        None,
        (parcel, box, *box_sems),
        refs[6 * count + 17 :],
    )
    phase = pl.program_id(0)

    def talk(slot):
        for p in range(4):
            if slot == 0 or p < 2:

                @pl.when(phase == p)
                def _():
                    turns[p + min(p, 2) + slot]()

    tokens = grad_ref.shape[0]
    cols = wo_ref.shape[1]
    pairs = cols // PAIR
    talk(0)
    mix_grad[...] = dot_tt(grad_ref[...], wo_ref[...], NORMAL).astype(jnp.bfloat16)
    scale = HD ** (-0.5)
    masks = head_masks(scale)
    ones = head_masks(1.0)
    lane = lax.broadcasted_iota(jnp.int32, (ROWS, PAIR), 1)
    last = tokens // ROWS - 1
    for pair in range(pairs):
        if pair == 1:
            talk(1)
        for i in range(last, -1, -1):
            rows = slice(i * ROWS, (i + 1) * ROWS)
            size = (i + 1) * ROWS
            q = joint_ref[rows, pair * PAIR : (pair + 1) * PAIR]
            k = joint_ref[:size, cols + pair * PAIR : cols + (pair + 1) * PAIR]
            v = joint_ref[:size, 2 * cols + pair * PAIR : 2 * cols + (pair + 1) * PAIR]
            g = mix_grad[rows, pair * PAIR : (pair + 1) * PAIR]
            q_both = jnp.concatenate([q * masks[0], q * masks[1]], axis=0)
            g_both = jnp.concatenate([g * ones[0], g * ones[1]], axis=0)
            bias = bias_ref[:size, rows]
            logs = jnp.concatenate(
                [log_ref[0, 2 * pair : 2 * pair + 1, rows], log_ref[0, 2 * pair + 1 : 2 * pair + 2, rows]],
                axis=1,
            )
            scores = dot_tt(k, q_both, RIGHT_T) + jnp.concatenate([bias, bias], axis=1)
            probs = jnp.exp(scores - logs)
            prob_grad = dot_tt(v, g_both, RIGHT_T)
            centre = jnp.sum(probs * prob_grad, axis=0, keepdims=True)
            score_grad = (probs * (prob_grad - centre)).astype(jnp.bfloat16)
            k_part = dot_tt(score_grad, q_both, NORMAL)
            v_part = dot_tt(probs.astype(jnp.bfloat16), g_both, NORMAL)
            if i == last:
                k_grad[...] = k_part
                v_grad[...] = v_part
            else:
                k_grad[:size, :] += k_part
                v_grad[:size, :] += v_part
            q_part = dot_tt(score_grad, k, LEFT_T)
            q_grad[rows, :] = jnp.where(lane < HD, q_part[:ROWS], q_part[ROWS:]) * scale
        cos_table = cos_ref[...]
        sin_table = sin_ref[...]
        out_ref[:, pair * PAIR : (pair + 1) * PAIR] = spin(
            q_grad[...], cos_table, sin_table, -1.0
        ).astype(jnp.bfloat16)
        out_ref[:, cols + pair * PAIR : cols + (pair + 1) * PAIR] = spin(
            k_grad[...], cos_table, sin_table, -1.0
        ).astype(jnp.bfloat16)
        out_ref[:, 2 * cols + pair * PAIR : 2 * cols + (pair + 1) * PAIR] = v_grad[...].astype(
            jnp.bfloat16
        )
    projected = dot_tt(out_ref[...], w_ref[...], RIGHT_T)

    @pl.when(phase == 0)
    def _():
        sum_ref[...] = projected

    @pl.when(phase > 0)
    def _():
        sum_ref[...] += projected

    @pl.when(phase == 3)
    def _():
        for step in turns[6:]:
            step()


def attend_back(grad, w_qkv, wo, joint, logs, cos_wide, sin_wide, bias_t, left, rights, parcel):
    tokens, width = grad.shape
    count = len(rights)
    rows = width // 8
    widths = [right.shape[1] // 4 for right in rights]
    blocks = 4
    cols = wo.shape[1] // blocks
    dma = pltpu.SemaphoreType.DMA
    vmem = pl.BlockSpec(memory_space=pltpu.VMEM)
    anywhere = pl.BlockSpec(memory_space=pl.ANY)
    moving = lambda k: (0, k)
    single = pl.Buffered(1)
    return pl.pallas_call(
        functools.partial(attend_back_kernel, count),
        grid=(blocks,),
        out_shape=[
            jax.ShapeDtypeStruct((tokens, 3 * blocks * cols), jnp.bfloat16),
            jax.ShapeDtypeStruct((tokens, width), jnp.float32),
        ]
        + [jax.ShapeDtypeStruct((rows, w), jnp.float32) for w in widths]
        + [jax.ShapeDtypeStruct(parcel.shape, parcel.dtype)],
        in_specs=[
            vmem,
            pl.BlockSpec((width, 3 * cols), moving, pipeline_mode=single),
            pl.BlockSpec((width, cols), moving, pipeline_mode=single),
            pl.BlockSpec((tokens, 3 * cols), moving, pipeline_mode=single),
            pl.BlockSpec((1, 8, tokens), lambda k: (k, 0, 0)),
            vmem,
            vmem,
            vmem,
            vmem,
        ]
        + [anywhere] * (count + 1),
        out_specs=[pl.BlockSpec((tokens, 3 * cols), moving), vmem] + [vmem] * count + [anywhere],
        scratch_shapes=[
            pltpu.VMEM((tokens, cols), jnp.bfloat16),
            pltpu.VMEM((tokens, PAIR), jnp.float32),
            pltpu.VMEM((tokens, PAIR), jnp.float32),
            pltpu.VMEM((tokens, PAIR), jnp.float32),
        ]
        + scatter_scratch(rows, widths)
        + [
            dma((3,)),
            dma((3,)),
            dma(()),
            pltpu.VMEM((2, tokens, max(widths)), jnp.bfloat16),
            pltpu.VMEM((2, 4, rows, max(widths)), jnp.bfloat16),
            dma((2,)),
        ],
        compiler_params=pltpu.CompilerParams(
            collective_id=3, has_side_effects=True, vmem_limit_bytes=66500000
        ),
        name="attend_back",
    )(grad, w_qkv, wo, joint, logs, cos_wide, sin_wide, bias_t, left, *rights, parcel)


def feed_kernel(
    normed_ref, grad_ref, wg_ref, wu_ref, wd_ref, hidden_ref, dg_ref, du_ref, out_ref, back_ref
):
    normed = normed_ref[...]
    gate = dot_tt(normed, wg_ref[...], NORMAL)
    up = dot_tt(normed, wu_ref[...], NORMAL)
    hidden_grad = dot_tt(grad_ref[...], wd_ref[...], NORMAL)
    sigmoid = jax.nn.sigmoid(gate)
    silu = gate * sigmoid
    hidden_ref[...] = (silu * up).astype(jnp.bfloat16)
    du_ref[...] = (hidden_grad * silu).astype(jnp.bfloat16)
    dg_ref[...] = (hidden_grad * up * (sigmoid * (1.0 + gate * (1.0 - sigmoid)))).astype(
        jnp.bfloat16
    )
    out = dot_tt(hidden_ref[...], wd_ref[...], RIGHT_T)
    back = dot_tt(dg_ref[...], wg_ref[...], RIGHT_T) + dot_tt(du_ref[...], wu_ref[...], RIGHT_T)

    @pl.when(pl.program_id(0) == 0)
    def _():
        out_ref[...] = out
        back_ref[...] = back

    @pl.when(pl.program_id(0) > 0)
    def _():
        out_ref[...] += out
        back_ref[...] += back


def feed_forward(normed, grad, wg, wu, wd, block=1024):
    tokens, width = normed.shape
    units = wg.shape[1]
    fixed = pl.BlockSpec((tokens, width), lambda b: (0, 0))
    weight = pl.BlockSpec((width, block), lambda b: (0, b))
    moving = pl.BlockSpec((tokens, block), lambda b: (0, b))
    return pl.pallas_call(
        feed_kernel,
        grid=(units // block,),
        out_shape=[jax.ShapeDtypeStruct((tokens, units), jnp.bfloat16)] * 3
        + [jax.ShapeDtypeStruct((tokens, width), jnp.float32)] * 2,
        in_specs=[fixed, fixed, weight, weight, weight],
        out_specs=[moving, moving, moving, fixed, fixed],
        compiler_params=pltpu.CompilerParams(vmem_limit_bytes=60000000),
        name="feed_forward",
    )(normed, grad, wg, wu, wd)


def order_matrix(width):
    rows = width // 8
    d = lax.axis_index("dp")
    owner = jnp.concatenate([jnp.full((rows,), mask, jnp.int32) for mask in RELATIVE])
    feature = (d ^ owner) * rows + jnp.arange(width, dtype=jnp.int32) % rows
    return (jnp.arange(width, dtype=jnp.int32)[:, None] == feature[None, :]).astype(jnp.bfloat16)


def group_body(
    block_input,
    lengths,
    out_grad,
    w_query,
    w_key,
    w_value,
    w_out,
    w_gate,
    w_up,
    w_down,
    attn_gain,
    ffn_gain,
):
    micro, _, groups, width = block_input.shape
    unit_cols = w_query.shape[1]
    bf16 = jnp.bfloat16
    f32 = jnp.float32
    contract = ((1,), (0,))
    contract_t = ((1,), (1,))
    own_lengths = lax.dynamic_slice_in_dim(
        lengths.reshape(micro * groups, 3), lax.axis_index("tensor"), 1, 0
    )
    rows = attn_gain.shape[0]
    gain_tile = jnp.zeros((8, 256), f32).at[0, :rows].set(attn_gain).at[1, :rows].set(ffn_gain)
    w_qkv, wo, x_box, gain_box = gather_weights(
        (jnp.concatenate([w_query, w_key, w_value], axis=1), w_out.T),
        to_parcels(block_input),
        gain_tile,
        ((0, 1),),
    )
    gains = gain_box[:, :2, :rows].transpose(1, 0, 2).reshape(2, width)
    order = order_matrix(width)
    tokens_in = dot_tt(x_box.reshape(GTOK, width), order, contract)
    gain_one = gains[0]
    gain_two = gains[1]

    segment, cos_table, sin_table = layout_tables(own_lengths)
    seg = segment[:, 0]
    cos_wide = jnp.tile(cos_table[:, 0], (1, 4))
    sin_wide = jnp.tile(sin_table[:, 0], (1, 4))
    index = jnp.arange(GTOK, dtype=jnp.int32)
    allowed = (index[None, :] <= index[:, None]) & (
        (seg[None, :] == 0) | (seg[None, :] == seg[:, None])
    )
    bias = jnp.where(allowed, 0.0, MASKED).astype(f32)
    residual = tokens_in
    scale_one = rms_scale(residual)
    unit_one = residual * scale_one
    normed_one = (unit_one * gain_one).astype(bf16)
    joint, mix, logs, attn_sum, wg, wu, wd, dy_box = attend(
        normed_one,
        w_qkv,
        wo,
        cos_wide,
        sin_wide,
        bias,
        (w_gate, w_up, w_down.T),
        to_parcels(out_grad),
        ((0, 1), (2,)),
    )
    upstream = dot_tt(dy_box.reshape(GTOK, width), order, contract).astype(bf16)
    middle = residual + attn_sum
    scale_two = rms_scale(middle)
    unit_two = middle * scale_two
    normed_two = (unit_two * gain_two).astype(bf16)
    hidden, gate_grad, up_grad, ffn_sum, normed_two_grad = feed_forward(
        normed_two, upstream, wg, wu, wd
    )
    output = (middle + ffn_sum).astype(bf16)
    out_parcels = dot_tt(output, order, contract_t).astype(bf16).reshape(x_box.shape)
    gain_two_grad = jnp.sum(normed_two_grad * unit_two, axis=0)
    middle_grad = upstream.astype(f32) + norm_back(
        normed_two_grad, unit_two, gain_two, scale_two
    )
    attn_grad = middle_grad.astype(bf16)
    joint_grad, normed_one_grad, share_gate, share_up, out_box = attend_back(
        attn_grad,
        w_qkv,
        wo,
        joint,
        logs.transpose(0, 2, 1),
        cos_wide,
        sin_wide,
        bias.T,
        normed_two,
        (gate_grad, up_grad),
        out_parcels,
    )
    gain_one_grad = jnp.sum(normed_one_grad * unit_one, axis=0)
    input_grad = (
        middle_grad + norm_back(normed_one_grad, unit_one, gain_one, scale_one)
    ).astype(bf16)
    in_parcels = dot_tt(input_grad, order, contract_t).astype(bf16).reshape(x_box.shape)
    gain_parts = jnp.stack([gain_one_grad, gain_two_grad]).reshape(2, 8, rows).transpose(1, 0, 2)
    gain_parts = jnp.pad(gain_parts, ((0, 0), (0, 6), (0, 256 - rows)))
    share_joint, share_down, share_out, own_gains, in_box = scatter_grads(
        ((normed_one, joint_grad), (upstream, hidden), (attn_grad, mix)),
        gain_parts,
        in_parcels,
    )
    return (
        from_box(out_box, micro, groups),
        from_box(in_box, micro, groups),
        share_joint[:, :unit_cols],
        share_joint[:, unit_cols : 2 * unit_cols],
        share_joint[:, 2 * unit_cols :],
        share_out.T,
        share_gate,
        share_up,
        share_down.T,
        own_gains[0, :rows],
        own_gains[1, :rows],
    )


def body(*operands):
    micro, _, groups, _ = operands[0].shape
    if lax.axis_size("dp") == 8 and micro * groups == lax.axis_size("tensor") == 4:
        return group_body(*operands)
    return sharded_body(*operands)


def solution(mesh):
    placed = (
        P(None, "tensor", "dp", None),
        P(None, "dp", None),
        P(None, "tensor", "dp", None),
        P("dp", "tensor"),
        P("dp", "tensor"),
        P("dp", "tensor"),
        P("tensor", "dp"),
        P("dp", "tensor"),
        P("dp", "tensor"),
        P("tensor", "dp"),
        P("dp"),
        P("dp"),
    )
    return jax.shard_map(
        body,
        mesh=mesh,
        in_specs=placed,
        out_specs=(
            P(None, "tensor", "dp", None),
            P(None, "tensor", "dp", None),
            P("dp", "tensor"),
            P("dp", "tensor"),
            P("dp", "tensor"),
            P("tensor", "dp"),
            P("dp", "tensor"),
            P("dp", "tensor"),
            P("tensor", "dp"),
            P("dp"),
            P("dp"),
        ),
        check_vma=False,
    )
```
